32 devices in a mesh: pipe: 2 (over core), dp: 4 (over y, x), tensor: 4 (over z).
Axes of the slice: x: 2, y: 2, z: 4, core: 2. Of those that a mesh axis runs over, the one named last changes fastest.
Arguments:
- enc_input: bfloat16 [8, 2048, 1024], P('dp', 'tensor'), may hold values from -6 to 6
- dec_input: bfloat16 [8, 256, 1024], P('dp', 'tensor'), may hold values from -6 to 6
- dec_cotangent: bfloat16 [8, 256, 1024], P('dp', 'tensor'), may hold values from -6 to 6
- enc_lengths: int32 [8, 3], P('dp'), may hold values from 1 to 1024, 2048 in all within a row
- dec_lengths: int32 [8, 3], P('dp'), may hold values from 1 to 128, 256 in all within a row
- attn_weights: float32 [2, 1024, 4, 1024], P('pipe', None, None, 'tensor'), as said below
- cross_weights: float32 [2, 1024, 2, 1024], P('pipe', None, None, 'tensor'), as said below
- ffn_weights: float32 [2, 1024, 2, 4096], P('pipe', None, None, 'tensor'), may hold values from -0.1875 to 0.1875
- norm_gains: float32 [2, 3, 1024], P('pipe'), may hold values from 0.25 to 1.75
- norm_biases: float32 [2, 3, 1024], P('pipe'), may hold values from -2.5 to 2.5
Outputs:
- dec_output: bfloat16 [8, 256, 1024], P('dp', 'tensor', 'pipe')
- enc_input_grad: float32 [8, 2048, 1024], P('dp', 'tensor', 'pipe')
- dec_input_grad: float32 [8, 256, 1024], P('dp', 'tensor', 'pipe')
- attn_weights_grad: float32 [2, 1024, 4, 1024], P('pipe', 'dp', None, 'tensor')
- cross_weights_grad: float32 [2, 1024, 2, 1024], P('pipe', 'dp', None, 'tensor')
- ffn_weights_grad: float32 [2, 1024, 2, 4096], P('pipe', 'dp', None, 'tensor')
- norm_gains_grad: float32 [2, 3, 1024], P('pipe', None, ('dp', 'tensor'))
- norm_biases_grad: float32 [2, 3, 1024], P('pipe', None, ('dp', 'tensor'))
The draws below stay inside these ranges and needn't reach their ends.
Inputs may be any that keep to these rules, and one draw needn't show every extreme that they name: `enc_lengths`: each row sums to 2048; entry j is the encoder length of table j. `dec_lengths`: each row sums to 256; entry j is the decoder length of table j. `attn_weights`: independent entries. `cross_weights`: independent entries.
All inputs are finite; a program needn't handle non-finite values.
Results may differ from the reference program's by a relative error of at most 0.034.
Values may be sent and summed in bfloat16 or wider, within the bound.
A program may use at most 320 MiB of HBM per device.

```python
import math
import jax
import jax.numpy as jnp
import numpy as np
from jax import lax

D = 1024
HEADS = 16
HEAD = 64
FF = 4096
TABLES_MB = 3
LEN_ENC = 1024
ENC_SLOTS = 2048
LEN_DEC = 128
DEC_SLOTS = 256
MB_TOTAL = 8


def draw_attn_weights(key, part):
    base = jax.random.truncated_normal(key, -4.0, 4.0, (2, D, 4, D), jnp.float32)
    factors = jnp.array([[1.0, 1.0, 1.0, 0.5 * math.sqrt(LEN_ENC)], [1.0, 1.0, 1.0, 0.35 * math.sqrt(LEN_DEC)]], jnp.float32)
    return base * D ** (-0.5) * factors[:, None, :, None]


def draw_cross_weights(key, part):
    base = jax.random.truncated_normal(key, -4.0, 4.0, (2, D, 2, D), jnp.float32)
    factors = jnp.array([[1.0, 1.0], [1.0, 0.5 * math.sqrt(LEN_ENC)]], jnp.float32)
    return base * D ** (-0.5) * factors[:, None, :, None]


def strengthened(values, key, source, target, shards_of, factor):
    owner, partner = [(jnp.arange(values.shape[axis_at]) // (values.shape[axis_at] // shards_of)).reshape([-1 if axis == axis_at else 1 for axis in range(values.ndim)]) for axis_at in (source, target)]
    chosen = jax.random.permutation(key, shards_of)[partner]
    strong = (owner == chosen) | (owner == (partner + shards_of // 2) % shards_of)
    return jnp.where(strong, factor * values, values)


def steps_of(stream_key, shape, cuts, least, largest):
    gain, own = 1.0, jax.random.fold_in(stream_key, 6)
    for dim, parts in cuts:
        steps = jnp.exp(jax.random.uniform(jax.random.fold_in(own, dim), (parts,), jnp.float32, least / len(cuts), largest / len(cuts)))
        gain = gain * jnp.repeat(steps, shape[dim] // parts).reshape([-1 if axis == dim else 1 for axis in range(len(shape))])
    return gain


def split_up(count, total, most, skew):
    weights = [(1 << 20) // math.isqrt(grade ** skew) + 1 for grade in range(2, count + 1)]
    surplus, given = total - most - (count - 1), [1] * (count - 1)
    while surplus > 0:
        movable = [i for i in range(count - 1) if given[i] < most]
        mass, left = sum([weights[i] for i in movable]), surplus
        for i in movable:
            addition = min(most - given[i], max(1, left * weights[i] // mass), surplus)
            given[i] = given[i] + addition
            surplus = surplus - addition
    return np.array([most] + given)


def ragged_sizes(key, number_of, total, reach, skew):
    if number_of == 2:
        one = jax.random.randint(key, (), max(1, total - reach), min(reach, total - 1) + 1)
        return jnp.stack([one, total - one])
    sizes = jnp.asarray(split_up(number_of, total, reach, skew), jnp.int32)
    pairs = (number_of - 1) // 2
    giver, sink = sizes[1:1 + 2 * pairs:2], sizes[2:2 + 2 * pairs:2]
    margin = jnp.minimum(giver - 1, reach - sink)
    passed = jax.random.randint(jax.random.fold_in(key, 1), (pairs,), 0, 1 << 20) % (margin + 1)
    sizes = sizes.at[1:1 + 2 * pairs:2].set(giver - passed).at[2:2 + 2 * pairs:2].set(sink + passed)
    return sizes[jax.random.permutation(jax.random.fold_in(key, 2), number_of)]


def bell_draw(key, extent, scale, bound, split=(), held_as=jnp.bfloat16):
    loudness = steps_of(key, extent, split, -0.22, 0.18) if split else 1.0
    drawn = jax.random.normal(key, extent, jnp.float32) * scale * loudness
    return jnp.minimum(jnp.maximum(drawn, -bound), bound).astype(held_as)


def gaussian_with(stream_key, dims, spread, limit, split, heavy, kind=jnp.bfloat16):
    values = spread * jax.random.normal(stream_key, dims, jnp.float32)
    if split:
        values = values * steps_of(stream_key, dims, split, -0.22, 0.18)
    return jnp.clip(strengthened(values, jax.random.fold_in(stream_key, 3), *heavy), -limit, limit).astype(kind)


def setup_inputs(seed: int = 0) -> dict:
    splits = jax.random.split(jax.random.key(seed), 11)
    enc_input = bell_draw(splits[0], (MB_TOTAL, ENC_SLOTS, D), 1.0, 6.0, ((0, 4), (1, 4)))
    dec_input = bell_draw(splits[1], (MB_TOTAL, DEC_SLOTS, D), 1.0, 6.0, ((0, 4), (1, 4)))
    dec_cotangent = gaussian_with(splits[2], (MB_TOTAL, DEC_SLOTS, D), 1.0, 6.0, ((0, 4), (1, 4)), (0, 2, 4, 2.0))
    enc_lengths = jax.vmap(lambda own: ragged_sizes(own, TABLES_MB, ENC_SLOTS, LEN_ENC, 2))(jax.random.split(splits[3], MB_TOTAL)).reshape((MB_TOTAL, TABLES_MB)).astype(jnp.int32)
    dec_lengths = jax.vmap(lambda own: ragged_sizes(own, TABLES_MB, DEC_SLOTS, LEN_DEC, 2))(jax.random.split(splits[4], MB_TOTAL)).reshape((MB_TOTAL, TABLES_MB)).astype(jnp.int32)
    attn_weights = draw_attn_weights(jax.random.fold_in(splits[10], 71), 0)
    cross_weights = draw_cross_weights(jax.random.fold_in(splits[10], 71), 0)
    ffn_weights = bell_draw(splits[7], (2, D, 2, FF), D ** -0.5, 0.1875, ((0, 2), (3, 4)), jnp.float32)
    norm_gains = jnp.clip(1.0 + 0.15 * jax.random.normal(splits[8], (2, 3, D), jnp.float32), 0.25, 1.75)
    norm_biases = bell_draw(splits[9], (2, 3, D), 0.3, 2.5, ((0, 2),), jnp.float32)
    return {"enc_input": enc_input, "dec_input": dec_input, "dec_cotangent": dec_cotangent, "enc_lengths": enc_lengths, "dec_lengths": dec_lengths, "attn_weights": attn_weights, "cross_weights": cross_weights, "ffn_weights": ffn_weights, "norm_gains": norm_gains, "norm_biases": norm_biases}


@jax.custom_vjp
def low(v):
    return lax.optimization_barrier(v.astype(jnp.bfloat16)).astype(jnp.float32)

@jax.custom_vjp
def low_back(v):
    return v

def low_keep(v):
    return (low(v), None)

def low_pass(kept, grad):
    return (grad,)

def back_keep(v):
    return (v, None)

def back_low(kept, grad):
    return (low(grad),)
low.defvjp(low_keep, low_pass)
low_back.defvjp(back_keep, back_low)
EPSILON = 1e-05
NEGATIVE = -1e+30
HIGHEST = lax.Precision.HIGHEST

def norm_apply(values, gain_vec, bias_vec):
    center = values - lax.optimization_barrier(jnp.mean(values, axis=-1, keepdims=True))
    inv_scale = lax.rsqrt(lax.optimization_barrier(jnp.mean(center * center, axis=-1, keepdims=True)) + EPSILON)
    return center * inv_scale * gain_vec + bias_vec

def product(left, right):
    return jnp.dot(left, right, precision=HIGHEST)

def rounded(values):
    return low(low_back(values))

def segments(lengths, row_count):
    seg_ends = jnp.cumsum(lengths).astype(jnp.int32)
    places = jnp.arange(row_count, dtype=jnp.int32)
    return lax.optimization_barrier(jnp.sum((places[None, :] >= seg_ends[:, None]).astype(jnp.int32), axis=0)).astype(jnp.int32)

def attention(queries, key_vecs, value_vecs, allowed):
    row_count = queries.shape[0]
    key_count = key_vecs.shape[0]
    query_heads = queries.reshape(row_count, HEADS, HEAD)
    key_heads = key_vecs.reshape(key_count, HEADS, HEAD)
    value_heads = value_vecs.reshape(key_count, HEADS, HEAD)
    raw_scores = jnp.einsum('qhd,khd->hqk', query_heads, key_heads, precision=HIGHEST)
    scores = jnp.where(allowed[None], low_back(raw_scores) * HEAD ** (-0.5), NEGATIVE)
    row_top = lax.optimization_barrier(jnp.max(scores, axis=-1, keepdims=True))
    expo_vals = jnp.exp(scores - row_top)
    probabilities = expo_vals / lax.optimization_barrier(jnp.sum(expo_vals, axis=-1, keepdims=True))
    head_out = jnp.einsum('hqk,khd->qhd', low(probabilities), value_heads, precision=HIGHEST)
    return head_out.reshape(row_count, HEADS * HEAD)

def micro_batch(weights, batch_args):
    attn_w, cross_w, ffn_w, gains, biases = weights
    enc_rows, dec_rows, enc_len, dec_len = batch_args
    enc_seg = segments(enc_len, ENC_SLOTS)
    dec_seg = segments(dec_len, DEC_SLOTS)
    places = jnp.arange(DEC_SLOTS, dtype=jnp.int32)
    enc_mask = enc_seg[:, None] == enc_seg[None, :]
    dec_mask = (dec_seg[:, None] == dec_seg[None, :]) & (places[:, None] >= places[None, :])
    cross_mask = dec_seg[:, None] == enc_seg[None, :]

    def self_block(inputs, section, allowed):
        inputs_low = low(inputs)
        queries = rounded(product(inputs_low, attn_w[section, :, 0]))
        key_vecs = rounded(product(inputs_low, attn_w[section, :, 1]))
        value_vecs = rounded(product(inputs_low, attn_w[section, :, 2]))
        head_out = rounded(attention(queries, key_vecs, value_vecs, allowed))
        return low_back(product(head_out, attn_w[section, :, 3].T))

    def ffn_block(inputs, section):
        hidden = low_back(product(low(inputs), ffn_w[section, :, 0]))
        active = low(jax.nn.gelu(hidden, approximate=False))
        return low_back(product(active, ffn_w[section, :, 1].T))
    embed = norm_apply(enc_rows, gains[0, 0], biases[0, 0])
    attn_norm = norm_apply(embed + self_block(embed, 0, enc_mask), gains[0, 1], biases[0, 1])
    memory = norm_apply(attn_norm + ffn_block(attn_norm, 0), gains[0, 2], biases[0, 2])
    memory_low = low(memory)
    cross_keys = rounded(product(memory_low, cross_w[0, :, 0]))
    cross_values = rounded(product(memory_low, cross_w[0, :, 1]))
    decoded = norm_apply(dec_rows + self_block(dec_rows, 1, dec_mask), gains[1, 0], biases[1, 0])
    cross_query = rounded(product(low(decoded), cross_w[1, :, 0]))
    cross_heads = rounded(attention(cross_query, cross_keys, cross_values, cross_mask))
    crossed = norm_apply(decoded + low_back(product(cross_heads, cross_w[1, :, 1].T)), gains[1, 1], biases[1, 1])
    return norm_apply(crossed + ffn_block(crossed, 1), gains[1, 2], biases[1, 2])

def reference(enc_input, dec_input, dec_cotangent, enc_lengths, dec_lengths, attn_weights, cross_weights, ffn_weights, norm_gains, norm_biases):
    per_batch = jax.checkpoint(micro_batch)

    def forward(enc_rows, dec_rows, attn_w, cross_w, ffn_w, gains, biases):
        weights = (low(attn_w), low(cross_w), low(ffn_w), gains, biases)
        return lax.map(lambda batch_args: per_batch(weights, batch_args), (enc_rows, dec_rows, enc_lengths, dec_lengths))
    result, pullback = jax.vjp(forward, enc_input.astype(jnp.float32), dec_input.astype(jnp.float32), attn_weights, cross_weights, ffn_weights, norm_gains, norm_biases)
    grads = pullback(dec_cotangent.astype(jnp.float32))
    return (result.astype(jnp.bfloat16), grads[0], grads[1], grads[2], grads[3], grads[4], grads[5], grads[6])
```

```python
from functools import partial

import jax
import jax.numpy as jnp
from jax import lax
from jax.experimental import pallas as pl
from jax.experimental.pallas import tpu as pltpu
from jax.sharding import PartitionSpec as P

HEAD = 64
LANES = 128
EPSILON = 1e-05
NEGATIVE = -1e30
HALF = jnp.bfloat16
WIDE = jnp.float32
VMEM_LIMIT = 56 << 20
MESH = pl.DeviceIdType.MESH
TILE_Q = 512
TILE_K = 512


def dot(left, right):
    return jnp.dot(left, right, preferred_element_type=WIDE)


def dot_bt(left, right):
    return lax.dot_general(left, right, (((1,), (1,)), ((), ())), preferred_element_type=WIDE)


def dot_ta(left, right):
    return lax.dot_general(left, right, (((0,), (0,)), ((), ())), preferred_element_type=WIDE)


def swap(value, axis, mask):
    return lax.ppermute(value, axis, [(i, i ^ mask) for i in range(lax.axis_size(axis))])


def joint(value, pairs):
    count = lax.axis_size("tensor")
    return lax.ppermute(
        value,
        ("pipe", "tensor"),
        [(a[0] * count + a[1], b[0] * count + b[1]) for a, b in pairs],
    )


def after(value, *earlier):
    return lax.optimization_barrier((value, *earlier))[0]


def swap_columns(value, axis, mask, difference):
    got = swap(value, axis, mask).reshape(value.shape[0], -1, LANES)
    order = [b ^ difference for b in range(got.shape[1])]
    return jnp.concatenate([got[:, b] for b in order], axis=1)


def table_of(places, lengths):
    total = jnp.zeros((), jnp.int32)
    table = jnp.zeros(places.shape, jnp.int32)
    for j in range(lengths.shape[0]):
        total = total + lengths[j]
        table = table + (places >= total).astype(jnp.int32)
    return table


def norm_forward(values, gain, bias):
    center = values - jnp.mean(values, axis=-1, keepdims=True)
    inv_scale = lax.rsqrt(jnp.mean(center * center, axis=-1, keepdims=True) + EPSILON)
    normed = center * inv_scale
    return normed * gain + bias, normed, inv_scale


def norm_backward(grad_out, normed, inv_scale, gain):
    grad_gain = jnp.sum(grad_out * normed, axis=0)
    grad_bias = jnp.sum(grad_out, axis=0)
    grad_normed = grad_out * gain
    grad_in = inv_scale * (
        grad_normed
        - jnp.mean(grad_normed, axis=-1, keepdims=True)
        - normed * jnp.mean(grad_normed * normed, axis=-1, keepdims=True)
    )
    return grad_in, grad_gain, grad_bias


def gelu(hidden):
    return 0.5 * hidden * (1.0 + lax.erf(hidden * (2.0**-0.5)))


def gelu_slope(hidden):
    density = jnp.exp(-0.5 * hidden * hidden) * 0.3989422804014327
    return 0.5 * (1.0 + lax.erf(hidden * (2.0**-0.5))) + hidden * density


def _allowed(seg_k, seg_q, causal, col0, row0):
    ok = seg_k == seg_q
    if causal:
        keys = col0 + lax.broadcasted_iota(jnp.int32, ok.shape, 0)
        queries = row0 + lax.broadcasted_iota(jnp.int32, ok.shape, 1)
        ok = ok & (queries >= keys)
    return ok


def _tile_loop(act, chunks, c, nq, nk, tq, tk, body):
    def step(i, carry):
        iq, ik = i // nk, i % nk

        @pl.when(act[iq * (chunks * nk) + c * nk + ik] > 0)
        def _():
            body(iq * tq, ik * tk, pl.ds(pl.multiple_of(iq * tq, tq), tq), pl.ds(pl.multiple_of(ik * tk, tk), tk))

        return carry

    lax.fori_loop(0, nq * nk, step, 0)


def _head_lanes(shape, head):
    lanes = lax.broadcasted_iota(jnp.int32, shape, 1)
    return (lanes < HEAD) if head == 0 else (lanes >= HEAD)


def _attend_kernel(chunks, tq, tk, causal, act, seg_q, seg_k, q, *refs):
    keys, values = refs[:chunks], refs[chunks : 2 * chunks]
    out, lse, top, total, acc = refs[2 * chunks :]
    rows = q.shape[0]
    nq, nk = rows // tq, keys[0].shape[0] // tk
    top[...] = jnp.full(top.shape, NEGATIVE, WIDE)
    total[...] = jnp.zeros(total.shape, WIDE)
    acc[...] = jnp.zeros(acc.shape, WIDE)
    for c in range(chunks):

        def tile(row0, col0, r, s, c=c):
            qs = q[r, :] * jnp.asarray(HEAD**-0.5, HALF)
            kk, vt = keys[c][s, :], values[c][s, :].T
            ok = _allowed(seg_k[c, s, 0:1], seg_q[0:1, r], causal, col0, row0)
            for h in range(2):
                qh = jnp.where(_head_lanes(qs.shape, h), qs, jnp.zeros_like(qs))
                sc = jnp.where(ok, dot_bt(kk, qh), NEGATIVE)
                before = top[h : h + 1, r]
                after = jnp.maximum(before, jnp.max(sc, axis=0, keepdims=True))
                pr = jnp.exp(sc - after).astype(HALF)
                fade = jnp.exp(before - after)
                total[h : h + 1, r] = total[h : h + 1, r] * fade + jnp.sum(
                    pr.astype(WIDE), axis=0, keepdims=True
                )
                span = slice(h * HEAD, (h + 1) * HEAD)
                acc[span, r] = acc[span, r] * fade + dot(vt[span, :], pr)
                top[h : h + 1, r] = after

        _tile_loop(act, chunks, c, nq, nk, tq, tk, tile)
    count = total[...]
    count = jnp.where(count > 0.0, count, 1.0)
    lse[0] = top[...] + jnp.log(count)
    whole = jnp.concatenate([acc[:HEAD, :] / count[0:1, :], acc[HEAD:, :] / count[1:2, :]], axis=0)
    out[...] = whole.T.astype(out.dtype)


def _attend_back_kernel(chunks, tq, tk, causal, own_delta, act, seg_q, seg_k, q, *refs):
    keys, values = refs[:chunks], refs[chunks : 2 * chunks]
    grad_out, stats = refs[2 * chunks : 2 * chunks + 2]
    refs = refs[2 * chunks + 2 :]
    extra, grad_q, *refs = refs
    grad_kv, (delta, dq, dkv) = refs[:chunks], refs[chunks:]
    rows = q.shape[0]
    nq, nk = rows // tq, keys[0].shape[0] // tk
    if own_delta:
        product = grad_out[...].astype(WIDE) * extra[...].astype(WIDE)
        pick = (
            lax.broadcasted_iota(jnp.int32, (8, LANES), 1) // HEAD
            == lax.broadcasted_iota(jnp.int32, (8, LANES), 0)
        ).astype(WIDE)
        delta[...] = lax.dot_general(
            pick, product, (((1,), (1,)), ((), ())), precision=lax.Precision.HIGHEST, preferred_element_type=WIDE
        )
    else:
        delta[0:2, :] = stats[0, 2:4, :]
    dq[...] = jnp.zeros(dq.shape, WIDE)
    for c in range(chunks):
        dkv[...] = jnp.zeros(dkv.shape, WIDE)

        def tile(row0, col0, r, s, c=c):
            qs = q[r, :] * jnp.asarray(HEAD**-0.5, HALF)
            go = grad_out[r, :]
            kk, vv = keys[c][s, :], values[c][s, :]
            ok = _allowed(seg_k[c, s, 0:1], seg_q[0:1, r], causal, col0, row0)
            for h in range(2):
                mine, mine_k = _head_lanes(qs.shape, h), _head_lanes(kk.shape, h)
                qh = jnp.where(mine, qs, jnp.zeros_like(qs))
                gh = jnp.where(mine, go, jnp.zeros_like(go))
                kh = jnp.where(mine_k, kk if own_delta else extra[s, :], jnp.zeros_like(kk))
                sc = jnp.where(ok, dot_bt(kk, qh), NEGATIVE)
                pr = jnp.exp(sc - stats[0, h : h + 1, r])
                ds = (pr * (dot_bt(vv, gh) - delta[h : h + 1, r])).astype(HALF)
                pr = pr.astype(HALF)
                dq[r, :] = dq[r, :] + dot_ta(ds, kh)
                dkv[0, s, :] = dkv[0, s, :] + dot(ds, qh)
                dkv[1, s, :] = dkv[1, s, :] + dot(pr, gh)

        _tile_loop(act, chunks, c, nq, nk, tq, tk, tile)
        grad_kv[c][...] = dkv[...].astype(grad_kv[c].dtype)
    grad_q[...] = (dq[...] * HEAD**-0.5).astype(grad_q.dtype)


def _tile_sizes(rows, keys):
    return min(TILE_Q, rows), min(TILE_K, keys)


def _activity(seg_q, seg_k, tq, tk):
    qt = seg_q.reshape(-1, tq)
    kt = seg_k.reshape(-1, tk)
    hit = (qt[:, :1] <= kt[:, -1][None]) & (kt[:, 0][None] <= qt[:, -1:])
    return hit.astype(jnp.int32).reshape(-1)


def tables(seg_q, seg_k):
    rows, (chunks, span) = seg_q.shape[0], seg_k.shape
    tq, tk = _tile_sizes(rows, span)
    return (
        _activity(seg_q, seg_k, tq, tk),
        jnp.broadcast_to(seg_q[None], (8, rows)),
        jnp.broadcast_to(seg_k[:, :, None], (chunks, span, LANES)),
    )


def _specs(rows, span, chunks, masks, blocked):
    row_block = pl.BlockSpec((rows, LANES), lambda h, act: (0, h))
    if blocked:
        row_block = pl.BlockSpec((None, rows, LANES), lambda h, act: (h, 0, 0))
    stat_block = pl.BlockSpec((1, 8, rows), lambda h, act: (h, 0, 0))
    heads = [
        pl.BlockSpec((8, rows), lambda h, act: (0, 0)),
        pl.BlockSpec((chunks, span, LANES), lambda h, act: (0, 0, 0)),
        row_block,
    ]
    for part in range(2):
        heads += [
            pl.BlockSpec((None, span, LANES), lambda h, act, m=m, part=part: (part, 0, h ^ m)) for m in masks
        ]
    return row_block, stat_block, heads


def attend(q, key_values, segs, masks, causal=False, out_type=WIDE):
    blocked = q.ndim == 3
    rows, width = (q.shape[1], q.shape[0] * LANES) if blocked else q.shape
    span = key_values[0].shape[1]
    chunks, blocks = len(key_values), width // LANES
    tq, tk = _tile_sizes(rows, span)
    row_block, stat_block, specs = _specs(rows, span, chunks, masks, blocked)
    pairs = rows * span * chunks
    return pl.pallas_call(
        partial(_attend_kernel, chunks, tq, tk, causal),
        out_shape=(
            jax.ShapeDtypeStruct(q.shape, out_type),
            jax.ShapeDtypeStruct((blocks, 8, rows), WIDE),
        ),
        grid_spec=pltpu.PrefetchScalarGridSpec(
            num_scalar_prefetch=1,
            grid=(blocks,),
            in_specs=specs,
            out_specs=[row_block, stat_block],
            scratch_shapes=[
                pltpu.VMEM((8, rows), WIDE),
                pltpu.VMEM((8, rows), WIDE),
                pltpu.VMEM((LANES, rows), WIDE),
            ],
        ),
        compiler_params=pltpu.CompilerParams(vmem_limit_bytes=VMEM_LIMIT),
        cost_estimate=pl.CostEstimate(
            flops=4 * pairs * width, transcendentals=pairs * width // HEAD, bytes_accessed=rows * width * 20
        ),
        name="attend",
    )(*segs, q, *key_values, *key_values)


def attend_back(q, key_values, grad_out, stats, extra, segs, masks, causal=False, own_delta=True):
    blocked = q.ndim == 3
    rows, width = (q.shape[1], q.shape[0] * LANES) if blocked else q.shape
    span = key_values[0].shape[1]
    chunks, blocks = len(key_values), width // LANES
    tq, tk = _tile_sizes(rows, span)
    row_block, stat_block, specs = _specs(rows, span, chunks, masks, blocked)
    kv_out = [pl.BlockSpec((2, span, LANES), lambda h, act, m=m: (0, 0, h ^ m)) for m in masks]
    pairs = rows * span * chunks
    extra_block = row_block if own_delta else pl.BlockSpec((span, LANES), lambda h, act: (0, h))
    outs = pl.pallas_call(
        partial(_attend_back_kernel, chunks, tq, tk, causal, own_delta),
        out_shape=[jax.ShapeDtypeStruct(q.shape, HALF)]
        + [jax.ShapeDtypeStruct((2, span, width), HALF)] * chunks,
        grid_spec=pltpu.PrefetchScalarGridSpec(
            num_scalar_prefetch=1,
            grid=(blocks,),
            in_specs=specs + [row_block, stat_block, extra_block],
            out_specs=[row_block] + kv_out,
            scratch_shapes=[
                pltpu.VMEM((8, rows), WIDE),
                pltpu.VMEM((rows, LANES), WIDE),
                pltpu.VMEM((2, span, LANES), WIDE),
            ],
        ),
        compiler_params=pltpu.CompilerParams(vmem_limit_bytes=VMEM_LIMIT),
        cost_estimate=pl.CostEstimate(
            flops=10 * pairs * width, transcendentals=pairs * width // HEAD, bytes_accessed=rows * width * 40
        ),
        name="attend_back",
    )(*segs, q, *key_values, *key_values, grad_out, stats, extra)
    return outs[0], outs[1:]


def _row_mean(values):
    return jnp.mean(values, axis=-1, keepdims=True)


def _norm_rows(values, gain, bias):
    center = values - _row_mean(values)
    inv_scale = lax.rsqrt(_row_mean(center * center) + EPSILON)
    normed = center * inv_scale
    return normed * gain + bias, normed, inv_scale


def _norm_rows_back(grad_out, normed, inv_scale, gain):
    grad_normed = grad_out * gain
    grad_in = inv_scale * (
        grad_normed - _row_mean(grad_normed) - normed * _row_mean(grad_normed * normed)
    )
    return (
        grad_in,
        jnp.sum(grad_out * normed, axis=0, keepdims=True),
        jnp.sum(grad_out, axis=0, keepdims=True),
    )


def _forward_rows(total, ins, outs):
    resid, gain, bias = ins
    value, normed, inv_scale = _norm_rows(total + resid[...], gain[...], bias[...])
    outs[0][...] = value
    outs[1][...] = normed
    outs[2][...] = jnp.broadcast_to(inv_scale, outs[2].shape)
    return value


def _turn_rows(total, ins, outs):
    resid, gain, bias, cotangent = ins
    value, normed, inv_scale = _norm_rows(total + resid[...], gain[...], bias[...])
    outs[0][...] = value.astype(outs[0].dtype)
    grad, grad_gain, grad_bias = _norm_rows_back(
        cotangent[...].astype(WIDE), normed, inv_scale, gain[...]
    )
    outs[1][...] = grad
    outs[2][0:1, :] = grad_gain
    outs[2][1:2, :] = grad_bias
    return grad


def _backward_rows(total, ins, outs):
    resid, normed, inv_scale, gain = ins
    grad, grad_gain, grad_bias = _norm_rows_back(
        total + resid[...], normed[...], inv_scale[:, 0:1], gain[...]
    )
    outs[0][...] = grad
    outs[1][0:1, :] = grad_gain
    outs[1][1:2, :] = grad_bias
    return grad


def _last_rows(total, ins, outs):
    outs[0][...] = total + ins[0][...]


def _rows_kernel(count, scatter, gather, middle, n_in, n_out, *refs):
    refs = list(refs)
    part = refs.pop(0) if scatter else None
    ins, refs = refs[:n_in], refs[n_in:]
    outs, refs = refs[:n_out], refs[n_out:]
    full = refs.pop(0) if gather else None
    landed = refs.pop(0) if scatter else None
    send_sem, recv_sem = refs[:2]
    me = lax.axis_index("tensor")
    steps = range(1, count)
    peers = [lax.rem(me + s, count) for s in steps]
    barrier = pltpu.get_barrier_semaphore()
    for peer in peers:
        pl.semaphore_signal(barrier, inc=1, device_id={"tensor": peer}, device_id_type=MESH)
    pl.semaphore_wait(barrier, count - 1)
    total = None
    if scatter:
        rows = part.shape[0] // count
        copies = []
        for s, peer in zip(steps, peers):
            copy = pltpu.make_async_remote_copy(
                src_ref=part.at[pl.ds(pl.multiple_of(peer * rows, rows), rows)],
                dst_ref=landed.at[s - 1],
                send_sem=send_sem.at[0, s - 1],
                recv_sem=recv_sem.at[0, s - 1],
                device_id={"tensor": peer},
                device_id_type=MESH,
            )
            copy.start()
            copies.append(copy)
        total = part[pl.ds(pl.multiple_of(me * rows, rows), rows), :].astype(WIDE)
        for s, copy in zip(steps, copies):
            copy.wait_recv()
            total = total + landed[s - 1].astype(WIDE)
        for copy in copies:
            copy.wait_send()
    sent = middle(total, ins, outs)
    if gather:
        rows = full.shape[0] // count
        own = pl.ds(pl.multiple_of(me * rows, rows), rows)
        full[own, :] = sent.astype(full.dtype)
        copies = []
        for s, peer in zip(steps, peers):
            copy = pltpu.make_async_remote_copy(
                src_ref=full.at[own],
                dst_ref=full.at[own],
                send_sem=send_sem.at[1, s - 1],
                recv_sem=recv_sem.at[1, s - 1],
                device_id={"tensor": peer},
                device_id_type=MESH,
            )
            copy.start()
            copies.append(copy)
        for copy in copies:
            copy.wait()


def rows_call(middle, number, part, ins, outs, gather=True):
    count = lax.axis_size("tensor")
    scatter = part is not None
    width = (part if scatter else ins[0]).shape[1]
    rows = part.shape[0] // count if scatter else ins[0].shape[0]
    shapes = [jax.ShapeDtypeStruct(shape, kind) for shape, kind in outs]
    if gather:
        shapes.append(jax.ShapeDtypeStruct((rows * count, width), HALF))
    whole = pl.BlockSpec(memory_space=pltpu.VMEM)
    operands = ([part] if scatter else []) + list(ins)
    got = pl.pallas_call(
        partial(_rows_kernel, count, scatter, gather, middle, len(ins), len(outs)),
        out_shape=shapes,
        in_specs=[whole] * len(operands),
        out_specs=[whole] * len(shapes),
        scratch_shapes=([pltpu.VMEM((count - 1, rows, width), HALF)] if scatter else [])
        + [pltpu.SemaphoreType.DMA((2, count - 1))] * 2,
        compiler_params=pltpu.CompilerParams(
            collective_id=number, has_side_effects=True, vmem_limit_bytes=VMEM_LIMIT
        ),
        cost_estimate=pl.CostEstimate(
            flops=10 * rows * width, transcendentals=0, bytes_accessed=64 * rows * width
        ),
        name=middle.__name__.strip("_"),
    )(*operands)
    return got


def _differ(a, b, count):
    total, bit = 0, 1
    while bit < count:
        total = total + lax.rem(lax.rem(a // bit, 2) + lax.rem(b // bit, 2), 2) * bit
        bit *= 2
    return total


def _slot(difference, count):
    top = count // 2
    return 2 * lax.rem(difference, top) + difference // top


def _enter(peers):
    barrier = pltpu.get_barrier_semaphore()
    for peer in peers:
        pl.semaphore_signal(barrier, inc=1, device_id=peer, device_id_type=MESH)
    pl.semaphore_wait(barrier, len(peers))


def _send(source, dest, send_sem, recv_sem, peer):
    copy = pltpu.make_async_remote_copy(
        src_ref=source,
        dst_ref=dest,
        send_sem=send_sem,
        recv_sem=recv_sem,
        device_id=peer,
        device_id_type=MESH,
    )
    copy.start()
    return copy


def _to_encoder_kernel(count, with_stats, *refs):
    if with_stats:
        value, out, lse, full, stats, own, own_stats, held, other, other_stats, send_sem, recv_sem = refs
    else:
        value, full, own, other, send_sem, recv_sem = refs
    core, me = lax.axis_index("pipe"), lax.axis_index("tensor")
    group = me // (count // 2)
    chips = [lax.rem(me + s, count) for s in range(1, count)]
    _enter([{"tensor": chip} for chip in chips] + [{"pipe": 1 - core}])
    sets = [(value, own, other, full)]
    if with_stats:
        for h in range(2):
            product = value[h].astype(WIDE) * out[h]
            pick = (
                lax.broadcasted_iota(jnp.int32, (8, product.shape[1]), 1) // HEAD
                == lax.broadcasted_iota(jnp.int32, (8, product.shape[1]), 0) - 2
            ).astype(WIDE)
            held[h] = lax.dot_general(
                pick,
                product,
                (((1,), (1,)), ((), ())),
                precision=lax.Precision.HIGHEST,
                preferred_element_type=WIDE,
            )
            held[h, 0:2, :] = lse[h, 0:2, :]
        sets.append((held, own_stats, other_stats, stats))
    copies = []
    for s, chip in enumerate(chips):
        place = _slot(_differ(chip, me, count), count)
        for h in range(2):
            at = lax.rem(h + core, 2) * count + place
            for i, (source, dest, _, _) in enumerate(sets):
                sems = (send_sem.at[i, s, h], recv_sem.at[i, s, h])
                copies.append(_send(source.at[h], dest.at[at], *sems, {"tensor": chip}))
    for h in range(2):
        for source, dest, _, _ in sets:
            dest[lax.rem(h + core, 2) * count] = source[h]
    for copy in copies:
        copy.wait()
    copies = []
    for g in range(2):
        for i, (_, source, dest, _) in enumerate(sets):
            here, there = pl.ds(g * count, count), pl.ds((1 - g) * count, count)
            sems = (send_sem.at[i, count - 1, g], recv_sem.at[i, count - 1, g])
            copies.append(_send(source.at[here], dest.at[there], *sems, {"pipe": 1 - core}))
    for copy in copies:
        copy.wait()
    for _, mine, theirs, dest in sets:

        @pl.when(core == group)
        def _(mine=mine, dest=dest):
            dest[...] = mine[...]

        @pl.when(core != group)
        def _(theirs=theirs, dest=dest):
            dest[...] = theirs[...]


def to_encoder(value, number, out=None, lse=None):
    count = lax.axis_size("tensor")
    _, rows, wide = value.shape
    shapes = [((2 * count, rows, wide), HALF)]
    if out is not None:
        shapes.append(((2 * count, 8, rows), WIDE))
    scratch = [pltpu.VMEM(*s) for s in shapes]
    if out is not None:
        scratch.append(pltpu.VMEM((2, 8, rows), WIDE))
    scratch += [pltpu.VMEM(*s) for s in shapes]
    whole = pl.BlockSpec(memory_space=pltpu.VMEM)
    operands = (value,) if out is None else (value, out, lse)
    return pl.pallas_call(
        partial(_to_encoder_kernel, count, out is not None),
        out_shape=[jax.ShapeDtypeStruct(*s) for s in shapes],
        in_specs=[whole] * len(operands),
        out_specs=[whole] * len(shapes),
        scratch_shapes=scratch + [pltpu.SemaphoreType.DMA((len(shapes), count, 2))] * 2,
        compiler_params=pltpu.CompilerParams(
            collective_id=number, has_side_effects=True, vmem_limit_bytes=VMEM_LIMIT
        ),
        name="to_encoder",
    )(*operands)


def _over_lanes(weights, wide):
    lanes = lax.broadcasted_iota(jnp.int32, (8, wide), 1) // HEAD
    pick = (lanes == lax.broadcasted_iota(jnp.int32, (8, wide), 0)).astype(HALF)
    high = weights.astype(HALF)
    low = (weights - high.astype(WIDE)).astype(HALF)
    return dot_ta(jnp.concatenate([high, low], axis=0), jnp.concatenate([pick, pick], axis=0))


def _to_decoder_kernel(count, *refs):
    part, lse, heads, out, out_lse = refs[:5]
    other, other_lse, both, both_lse, landed, landed_lse, send_sem, recv_sem = refs[5:]
    core, me = lax.axis_index("pipe"), lax.axis_index("tensor")
    top = count // 2
    chips = [lax.rem(me + s, count) for s in range(1, count)]
    _enter([{"tensor": chip} for chip in chips] + [{"pipe": 1 - core}])
    copies = []
    for g in range(2):
        here, there = pl.ds(g * count, count), pl.ds((1 - g) * count, count)
        for i, (source, dest) in enumerate(((part, other), (lse, other_lse))):
            sems = (send_sem.at[i, count - 1, g], recv_sem.at[i, count - 1, g])
            copies.append(_send(source.at[here], dest.at[there], *sems, {"pipe": 1 - core}))
    for copy in copies:
        copy.wait()
    wide = part.shape[2]
    for i in range(2 * count):
        first, second = lse[i], other_lse[i]
        peak = jnp.maximum(first, second)
        a, b = jnp.exp(first - peak), jnp.exp(second - peak)
        both_lse[i] = peak + jnp.log(a + b)
        share = _over_lanes(b / (a + b), wide)
        mine = part[i].astype(WIDE)
        both[i] = (mine + share * (other[i].astype(WIDE) - mine)).astype(HALF)
    copies = []
    for s, chip in enumerate(chips):
        place = _slot(_differ(chip, me, count), count)
        for h in range(2):
            at = lax.rem(h + core, 2) * count + place
            for i, (source, dest) in enumerate(((both, landed), (both_lse, landed_lse))):
                sems = (send_sem.at[i, s, h], recv_sem.at[i, s, h])
                copies.append(_send(source.at[at], dest.at[s, h], *sems, {"tensor": chip}))
    for copy in copies:
        copy.wait()
    for h in range(2):
        at = lax.rem(h + core, 2) * count
        terms = [(me, both[at], both_lse[at])]
        for s in range(count - 1):
            terms.append((lax.rem(me - s - 1 + count, count), landed[s, h], landed_lse[s, h]))
        logs = [jnp.where(chip // top == core, log, NEGATIVE) for chip, _, log in terms]
        peak = logs[0]
        for log in logs[1:]:
            peak = jnp.maximum(peak, log)
        weights = [jnp.exp(log - peak) for log in logs]
        weights = [
            jnp.where(chip // top == core, w, 0.0) for (chip, _, _), w in zip(terms, weights)
        ]
        total = sum(weights)
        out_lse[h] = peak + jnp.log(total)
        shares = [_over_lanes(w / total, wide) for w in weights]
        value = sum(c * term.astype(WIDE) for c, (_, term, _) in zip(shares, terms)) / sum(shares)
        out[h] = value
        heads[:, h * wide : (h + 1) * wide] = value.astype(HALF)


def to_decoder(part, lse, number):
    count = lax.axis_size("tensor")
    slots, rows, wide = part.shape
    whole = pl.BlockSpec(memory_space=pltpu.VMEM)
    return pl.pallas_call(
        partial(_to_decoder_kernel, count),
        out_shape=[
            jax.ShapeDtypeStruct((rows, 2 * wide), HALF),
            jax.ShapeDtypeStruct((2, rows, wide), WIDE),
            jax.ShapeDtypeStruct((2, 8, rows), WIDE),
        ],
        in_specs=[whole] * 2,
        out_specs=[whole] * 3,
        scratch_shapes=[
            pltpu.VMEM((slots, rows, wide), HALF),
            pltpu.VMEM((slots, 8, rows), WIDE),
            pltpu.VMEM((slots, rows, wide), HALF),
            pltpu.VMEM((slots, 8, rows), WIDE),
            pltpu.VMEM((count - 1, 2, rows, wide), HALF),
            pltpu.VMEM((count - 1, 2, 8, rows), WIDE),
        ]
        + [pltpu.SemaphoreType.DMA((2, count, 2))] * 2,
        compiler_params=pltpu.CompilerParams(
            collective_id=number, has_side_effects=True, vmem_limit_bytes=VMEM_LIMIT
        ),
        name="to_decoder",
    )(part, lse)


def to_pairs(value):
    slots, rows, wide = value.shape
    each = LANES // wide
    if each == 1:
        return value
    value = value.reshape(slots // each, each, rows, wide)
    return value.transpose(0, 2, 1, 3).reshape(slots // each, rows, LANES)


def from_pairs(value, wide):
    blocks, rows, _ = value.shape
    each = LANES // wide
    if each == 1:
        return value
    value = value.reshape(blocks, rows, each, wide)
    return value.transpose(0, 2, 1, 3).reshape(blocks * each, rows, wide)


def stats_to_pairs(stats, wide):
    each = LANES // wide
    if each == 1:
        return stats
    slots, _, rows = stats.shape
    stats = stats.reshape(slots // each, each, 8, rows)
    return jnp.concatenate(
        [stats[:, :, 0], stats[:, :, 2], jnp.zeros((slots // each, 4, rows), WIDE)], axis=1
    )


def stats_from_pairs(stats, wide):
    each = LANES // wide
    if each == 1:
        return stats
    blocks, _, rows = stats.shape
    value = stats[:, :each].reshape(blocks * each, 1, rows)
    return jnp.concatenate([value, jnp.zeros((blocks * each, 7, rows), WIDE)], axis=1)


def slot_bits():
    count = lax.axis_size("tensor")
    bits, bit = [count // 2], 1
    while bit < count // 2:
        bits.append(bit)
        bit *= 2
    return [b for b in bits if b > 0]


def in_column_halves(values):
    wide = values.shape[2] // 2
    return jnp.stack(
        [
            jnp.concatenate(
                [values[:, k, h * wide : (h + 1) * wide] for k in range(values.shape[1])], axis=1
            ).astype(HALF)
            for h in range(2)
        ]
    )


def _gather_kernel(bits, count, planes, *refs):
    own, refs = refs[:3], refs[3:]
    leaving, dec_rows, *refs = refs
    full, enc_cross, enc_ffn, *refs = refs
    dec, refs = refs[:3], refs[3:]
    rests, refs = refs[:2], refs[2:]
    coming, dec_full, send_sem, recv_sem, local_sem = refs
    core, place, me = lax.axis_index("pipe"), lax.axis_index("dp"), lax.axis_index("tensor")
    wide = own[0].shape[2]
    block = own[0].shape[1] // planes
    sibling = {"pipe": 1 - core}
    chips = {bit: {"tensor": _differ(me, bit, count)} for bit in bits}
    line = [{"tensor": _differ(me, s, count)} for s in range(1, count)]
    dp_bits = [1 << i for i in range(planes.bit_length() - 1)]
    others = {bit: {"dp": _differ(place, bit, planes)} for bit in dp_bits}
    _enter([sibling, *line, *others.values()])
    made = [0]

    def push(source, dest, peer):
        i = made[0]
        made[0] += 1
        return _send(source, dest, send_sem.at[i], recv_sem.at[i], peer)

    def rows_of(difference):
        return pl.ds(pl.multiple_of(_differ(place, difference, planes) * block, block), block)

    enc = [full.at[:, :, pl.ds(0, wide)], enc_cross, enc_ffn]
    shown = []
    for a in range(3):
        i = made[0]
        made[0] += 2
        shown.append(i)

        @pl.when(core == 0)
        def _(a=a, i=i):
            for h in range(2):
                _send(own[a].at[h], enc[a].at[1 - h], send_sem.at[i + h], recv_sem.at[i + h], sibling)
                pltpu.make_async_copy(own[a].at[h], enc[a].at[h], local_sem.at[a, h]).start()

        @pl.when(core == 1)
        def _(a=a, i=i):
            for h in range(2):
                _send(own[a].at[h], dec[a].at[h], send_sem.at[i + h], recv_sem.at[i + h], sibling)
                pltpu.make_async_copy(own[a].at[h], dec[a].at[h], local_sem.at[a, h]).start()

    def arrived(a):
        i = shown[a]
        for h in range(2):
            pltpu.make_async_copy(own[a].at[h], enc[a].at[h], local_sem.at[a, h]).wait()
            pltpu.make_async_copy(own[a].at[h], enc[a].at[h], recv_sem.at[i + h]).wait()

    def line_step(a, n, bit):
        here, size = rows_of(0), own[a].shape[2]
        if a == 0:
            source = full.at[0, here, pl.ds(0, n * size)]
            return [push(source, full.at[0, here, pl.ds(n * size, n * size)], chips[bit])]
        rest = rests[a - 1]
        copies = [
            push(enc[a].at[0, here], rest.at[:, pl.ds((n - 1) * size, size)], chips[bit])
        ]
        if n > 1:
            source = rest.at[:, pl.ds(0, (n - 1) * size)]
            copies.append(push(source, rest.at[:, pl.ds(n * size, (n - 1) * size)], chips[bit]))
        return copies

    def wait(copies):
        for copy in copies:
            copy.wait()

    def advance(chain):
        wait(chain["now"])
        chain["now"] = line_step(chain["array"], *chain["todo"].pop(0)) if chain["todo"] else []

    def columns(part):
        return pl.ds(wide + part * half, half)

    def plane_step(j):
        copies = []
        for part, order in enumerate(orders):
            for m in held[part]:
                at = full.at[0, rows_of(m), columns(part)]
                copies.append((part, m ^ order[j], push(at, at, others[order[j]])))
        return copies

    def share(part, m):
        here = rows_of(m)
        source = full.at[0, here, columns(part)]
        return push(source, full.at[1, here, columns(part)], sibling)

    steps = [(1 << i, bit) for i, bit in enumerate(bits)]
    for_attn, for_cross, for_ffn = [{"array": a, "todo": list(steps), "now": []} for a in range(3)]
    arrived(0)
    advance(for_attn)
    arrived(2)
    advance(for_attn)
    advance(for_ffn)
    while for_attn["now"]:
        advance(for_attn)
    token_sem = made[0]
    made[0] += 1

    @pl.when(core == 1)
    def _():
        _send(leaving, coming, send_sem.at[token_sem], recv_sem.at[token_sem], chips[bits[0]])

    at = pl.ds(pl.multiple_of(me * dec_rows.shape[0], dec_rows.shape[0]), dec_rows.shape[0])
    dec_full[at, :] = dec_rows[...]
    dec_sent = [push(dec_full.at[at], dec_full.at[at], peer) for peer in line]
    half = (count - 1) * wide // 2
    orders, held = (dp_bits, dp_bits[::-1]), ([0], [0])
    moving = plane_step(0)
    shared = [share(part, 0) for part in range(2)]
    advance(for_ffn)
    arrived(1)
    for j in range(len(dp_bits)):
        for _, _, copy in moving:
            copy.wait()
        for part, order in enumerate(orders):
            held[part].extend([m ^ order[j] for m in held[part]])
        following = plane_step(j + 1) if j + 1 < len(dp_bits) else []
        shared += [share(part, m) for part, m, _ in moving]
        moving = following
        advance(for_cross)
    while for_ffn["now"]:
        advance(for_ffn)
    while for_cross["now"]:
        advance(for_cross)

    @pl.when(core == 1)
    def _():
        pltpu.make_async_copy(leaving, leaving, send_sem.at[token_sem]).wait()
        pltpu.make_async_copy(leaving, coming, recv_sem.at[token_sem]).wait()

    wait(dec_sent)
    wait(shared)
    for a in range(3):
        for h in range(2):
            pltpu.make_async_copy(own[a].at[h], own[a].at[h], send_sem.at[shown[a] + h]).wait()


def gather_weights(attn, cross, ffn, leaving, dec_rows):
    own = (attn, cross, ffn)
    count, planes = lax.axis_size("tensor"), lax.axis_size("dp")
    depth = attn.shape[1]
    shapes = [(2, depth, count * attn.shape[2]), cross.shape, ffn.shape]
    shapes += [v.shape for v in own]
    shapes += [(depth // planes, (count - 1) * v.shape[2]) for v in (cross, ffn)]
    shapes += [leaving.shape, (count * dec_rows.shape[0], dec_rows.shape[1])]
    hbm, vmem = pl.BlockSpec(memory_space=pl.ANY), pl.BlockSpec(memory_space=pltpu.VMEM)
    return pl.pallas_call(
        partial(_gather_kernel, slot_bits(), count, planes),
        out_shape=[jax.ShapeDtypeStruct(shape, HALF) for shape in shapes],
        in_specs=[vmem] * 3 + [hbm, vmem],
        out_specs=[hbm] * (len(shapes) - 1) + [vmem],
        scratch_shapes=[pltpu.SemaphoreType.DMA((64,))] * 2 + [pltpu.SemaphoreType.DMA((3, 2))],
        compiler_params=pltpu.CompilerParams(
            collective_id=9, has_side_effects=True, vmem_limit_bytes=VMEM_LIMIT
        ),
        name="gather_weights",
    )(*own, leaving, dec_rows)


def gather_planes(rest):
    return lax.all_gather(rest, "dp", axis=0, tiled=True)


def fold_cores(mine, other):
    return (mine.astype(WIDE) + swap(other, "pipe", 1).astype(WIDE)).astype(HALF)


def fold_planes(term):
    return lax.psum_scatter(term, "dp", scatter_dimension=0, tiled=True)


def fold_chips(rows, kinds):
    for bit in reversed(slot_bits()):
        keep, send = jnp.split(rows, 2, axis=1)
        rows = (keep.astype(WIDE) + swap(send, "tensor", bit).astype(WIDE)).astype(HALF)
    return rows.reshape(rows.shape[0], kinds, -1)


def scatter_local(terms):
    core = lax.axis_index("pipe")
    wide = terms[0].shape[1] // 2
    pick = partial(lax.dynamic_slice_in_dim, slice_size=wide, axis=1)
    mine = jnp.concatenate([pick(v.astype(HALF), core * wide) for v in terms], axis=1)
    other = jnp.concatenate([pick(v.astype(HALF), (1 - core) * wide) for v in terms], axis=1)
    term = fold_cores(mine, other)
    rows = fold_planes(term)
    return rows.reshape(rows.shape[0], len(terms), wide), term


def reduce_norms(enc_terms, dec_terms):
    core = lax.axis_index("pipe")
    value = jnp.where(core == 0, enc_terms, dec_terms) + swap(
        jnp.where(core == 0, dec_terms, enc_terms), "pipe", 1
    )
    for axis in ("dp", "tensor"):
        bit = lax.axis_size(axis) // 2
        while bit >= 1:
            parts = value.reshape(value.shape[0], 2, -1)
            mine = lax.rem(lax.axis_index(axis) // bit, 2)
            keep = lax.dynamic_index_in_dim(parts, mine, 1, False)
            send = lax.dynamic_index_in_dim(parts, 1 - mine, 1, False)
            value = keep + swap(send, axis, bit)
            bit //= 2
    return value


def _blocks_of(weights, kinds):
    wide = weights.shape[2] // (lax.axis_size("tensor") * kinds)
    each = LANES // wide
    blocks = lax.axis_size("tensor") // each
    spec = pl.BlockSpec(
        (None, weights.shape[1], each * kinds * wide), lambda i: (i // blocks, 0, lax.rem(i, blocks))
    )
    return wide, each, blocks, spec


def _piece(weights, kinds, wide, each, k):
    parts = [weights[:, (j * kinds + k) * wide : (j * kinds + k + 1) * wide] for j in range(each)]
    return parts[0] if each == 1 else jnp.concatenate(parts, axis=1)


def _store_grads(refs, i, blocks, pieces, wide, each):
    columns = [p[:, j * wide : (j + 1) * wide] for j in range(each) for p in pieces]
    for ref, when in zip(refs, (i < blocks, i >= blocks)):

        @pl.when(when)
        def _(ref=ref):
            for n, column in enumerate(columns):
                ref[:, n * wide : (n + 1) * wide] = column.astype(ref.dtype)


def _grad_specs(depth, columns, blocks):
    return [
        pl.BlockSpec((depth, columns), lambda i: (0, jnp.minimum(i, blocks - 1))),
        pl.BlockSpec((depth, columns), lambda i: (0, jnp.maximum(i - blocks, 0))),
    ]


def _spread_kernel(kinds, use, wide, each, blocks, with_grad, pair, x, weights, *refs):
    left = x[...]
    values = [dot(left, _piece(weights, kinds, wide, each, k)) for k in use]
    if with_grad:
        y, *refs = refs
        i = pl.program_id(0)
        _store_grads(refs[-2:], i, blocks, [dot_ta(left, y[...].astype(HALF))], wide, each)
    if pair:
        refs[-1][0] = values[-2].astype(HALF)
        refs[-1][1] = values[-1].astype(HALF)
        values = values[:-2]
    for ref, value in zip(refs, values):
        ref[...] = value.astype(HALF)


def spread(x, weights, kinds, use, y=None, pair=False):
    rows, width = x.shape
    wide, each, blocks, spec = _blocks_of(weights, kinds)
    column = pl.BlockSpec((rows, LANES), lambda i: (0, i))
    single = len(use) - (2 if pair else 0)
    shapes, specs = [((rows, width), HALF)] * single, [column] * single
    if pair:
        shapes.append(((2, rows, width), HALF))
        specs.append(pl.BlockSpec((2, rows, LANES), lambda i: (0, 0, i)))
    if y is not None:
        shapes += [((width, width // 2), HALF)] * 2
        specs += _grad_specs(width, LANES, blocks)
    return pl.pallas_call(
        partial(_spread_kernel, kinds, use, wide, each, blocks, y is not None, pair),
        out_shape=[jax.ShapeDtypeStruct(*s) for s in shapes],
        grid=(2 * blocks,),
        in_specs=[pl.BlockSpec((rows, width), lambda i: (0, 0)), spec] + [column] * (y is not None),
        out_specs=specs,
        compiler_params=pltpu.CompilerParams(vmem_limit_bytes=VMEM_LIMIT),
        cost_estimate=pl.CostEstimate(
            flops=2 * rows * width * width * (len(use) + (y is not None)),
            transcendentals=0,
            bytes_accessed=2 * width * width * kinds,
        ),
        name="spread",
    )(x, weights, *([] if y is None else [y]))


def _collect_kernel(kinds, use, wide, each, blocks, n_y, with_grad, ending, n_extra, *refs):
    refs = list(refs)
    ys, refs = refs[:n_y], refs[n_y:]
    weights, refs = refs[0], refs[1:]
    x = refs.pop(0) if with_grad else None
    extra, refs = refs[:n_extra], refs[n_extra:]
    acc = refs.pop()
    grads = [refs.pop(), refs.pop()][::-1] if with_grad else []
    i = pl.program_id(0)

    @pl.when(i == 0)
    def _():
        acc[...] = jnp.zeros(acc.shape, WIDE)

    values = []
    for y in ys:
        values += [y[...]] if len(y.shape) == 2 else [y[0], y[1]]
    values = [v.astype(HALF) for v in values]
    for value, k in zip(values, use):
        acc[...] += dot_bt(value, _piece(weights, kinds, wide, each, k))
    if with_grad:
        left = x[...]
        _store_grads(grads, i, blocks, [dot_ta(left, v) for v in values], wide, each)

    @pl.when(i == 2 * blocks - 1)
    def _():
        ending(acc[...], extra, refs)


def collect(ys, weights, kinds, use, ending, extra, outs, x=None):
    rows, width = ys[0].shape[-2:]
    wide, each, blocks, spec = _blocks_of(weights, kinds)
    y_specs = [
        pl.BlockSpec((rows, LANES), lambda i: (0, i))
        if y.ndim == 2
        else pl.BlockSpec((2, rows, LANES), lambda i: (0, 0, i))
        for y in ys
    ]
    fixed = [pl.BlockSpec(v.shape, lambda i: (0, 0)) for v in ([] if x is None else [x]) + extra]
    shapes = list(outs)
    specs = [pl.BlockSpec(shape, lambda i: (0, 0)) for shape, _ in outs]
    if x is not None:
        shapes += [((width, len(use) * width // 2), HALF)] * 2
        specs += _grad_specs(width, len(use) * LANES, blocks)
    return pl.pallas_call(
        partial(
            _collect_kernel, kinds, use, wide, each, blocks, len(ys), x is not None, ending, len(extra)
        ),
        out_shape=[jax.ShapeDtypeStruct(*s) for s in shapes],
        grid=(2 * blocks,),
        in_specs=y_specs + [spec] + fixed,
        out_specs=specs,
        scratch_shapes=[pltpu.VMEM((rows, width), WIDE)],
        compiler_params=pltpu.CompilerParams(vmem_limit_bytes=VMEM_LIMIT),
        cost_estimate=pl.CostEstimate(
            flops=2 * rows * width * width * len(use) * (1 + (x is not None)),
            transcendentals=0,
            bytes_accessed=2 * width * width * kinds,
        ),
        name="collect",
    )(*ys, weights, *([] if x is None else [x]), *extra)


def _end_norm(total, ins, outs):
    resid, gain, bias = ins
    value, normed, inv_scale = _norm_rows(total + resid[...], gain[...], bias[...])
    outs[0][...] = value
    outs[1][...] = value.astype(HALF)
    outs[2][...] = normed
    outs[3][...] = jnp.broadcast_to(inv_scale, outs[3].shape)


def _end_norm_back(total, ins, outs):
    *resid, normed, inv_scale, gain = ins
    total = total + resid[0][...] if resid else total
    grad, grad_gain, grad_bias = _norm_rows_back(total, normed[...], inv_scale[:, 0:1], gain[...])
    outs[0][...] = grad
    outs[1][...] = grad.astype(HALF)
    outs[2][0:1, :] = grad_gain
    outs[2][1:2, :] = grad_bias


def _ffn_parts(count, own, mine, other):
    depth, wide = own.shape[1], own.shape[2] // 2
    specs = []
    for k in range(2):
        specs.append(pl.BlockSpec((None, depth, wide), lambda i, k=k: (i // count, 0, k)))
        for first in (0, count):
            specs.append(
                pl.BlockSpec(
                    (depth, wide),
                    lambda i, k=k, first=first: (0, 2 * jnp.clip(i - first - 1, 0, count - 2) + k),
                )
            )
    return wide, specs


def _ffn_cases(count, i, ins, outs):
    local = lax.rem(i, count) == 0
    return [
        (local, ins[0], outs[0]),
        (jnp.logical_and(~local, i < count), ins[1], outs[1]),
        (jnp.logical_and(~local, i > count), ins[2], outs[2]),
    ]


def _ffn_kernel(count, x, resid, gain, bias, *refs):
    ins, outs, refs = refs[:3], refs[3:6], refs[6:]
    value, value_low, normed, inv_scale, active, slope, acc = refs
    i = pl.program_id(0)

    @pl.when(i == 0)
    def _():
        acc[...] = jnp.zeros(acc.shape, WIDE)

    for condition, first, second in _ffn_cases(count, i, ins, outs):

        @pl.when(condition)
        def _(first=first, second=second):
            hidden = dot(x[...], first[...])
            below = 0.5 * (1.0 + lax.erf(hidden * (2.0**-0.5)))
            density = jnp.exp(-0.5 * hidden * hidden) * 0.3989422804014327
            act = (hidden * below).astype(HALF)
            active[...] = act
            slope[...] = (below + hidden * density).astype(HALF)
            acc[...] += dot_bt(act, second[...])

    @pl.when(i == 2 * count - 1)
    def _():
        _end_norm(acc[...], (resid, gain, bias), (value, value_low, normed, inv_scale))


def feed_forward(x, resid, gain, bias, own, mine, other):
    count = lax.axis_size("tensor")
    rows, width = x.shape
    wide, specs = _ffn_parts(count, own, mine, other)
    units = 2 * count * wide
    fixed = [pl.BlockSpec(v.shape, lambda i: (0, 0)) for v in (x, resid, gain, bias)]
    shapes = [((rows, width), WIDE), ((rows, width), HALF), ((rows, width), WIDE), ((rows, LANES), WIDE)]
    column = pl.BlockSpec((rows, wide), lambda i: (0, i))
    return pl.pallas_call(
        partial(_ffn_kernel, count),
        out_shape=[jax.ShapeDtypeStruct(*s) for s in shapes]
        + [jax.ShapeDtypeStruct((rows, units), HALF)] * 2,
        grid=(2 * count,),
        in_specs=fixed + specs,
        out_specs=[pl.BlockSpec(s, lambda i: (0, 0)) for s, _ in shapes] + [column] * 2,
        scratch_shapes=[pltpu.VMEM((rows, width), WIDE)],
        compiler_params=pltpu.CompilerParams(vmem_limit_bytes=VMEM_LIMIT),
        cost_estimate=pl.CostEstimate(
            flops=4 * rows * width * units, transcendentals=2 * rows * units, bytes_accessed=4 * width * units
        ),
        name="feed_forward",
    )(x, resid, gain, bias, own, mine, other, own, mine, other)


def _ffn_back_kernel(count, x, grad, resid, normed, inv_scale, gain, active, slope, *refs):
    ins, outs, refs = refs[:3], refs[3:6], refs[6:]
    result, result_low, terms, *grads, acc = refs
    i = pl.program_id(0)

    @pl.when(i == 0)
    def _():
        acc[...] = jnp.zeros(acc.shape, WIDE)

    for condition, first, second in _ffn_cases(count, i, ins, outs):

        @pl.when(condition)
        def _(first=first, second=second):
            hidden = (dot(grad[...], second[...]) * slope[...].astype(WIDE)).astype(HALF)
            acc[...] += dot_bt(hidden, first[...])
            f1 = dot_ta(x[...], hidden).astype(HALF)
            f2 = dot_ta(grad[...], active[...]).astype(HALF)
            for half, when in enumerate((i < count, i >= count)):

                @pl.when(when)
                def _(half=half):
                    grads[half][...] = f1
                    grads[2 + half][...] = f2

    @pl.when(i == 2 * count - 1)
    def _():
        _end_norm_back(acc[...], (resid, normed, inv_scale, gain), (result, result_low, terms))


def feed_forward_back(x, grad, resid, normed, inv_scale, gain, active, slope, own, mine, other):
    count = lax.axis_size("tensor")
    rows, width = x.shape
    wide, specs = _ffn_parts(count, own, mine, other)
    column = pl.BlockSpec((rows, wide), lambda i: (0, i))
    fixed = [pl.BlockSpec(v.shape, lambda i: (0, 0)) for v in (x, grad, resid, normed, inv_scale, gain)]
    shapes = [((rows, width), WIDE), ((rows, width), HALF), ((8, width), WIDE)]
    grad_specs = [
        pl.BlockSpec((width, wide), lambda i: (0, jnp.minimum(i, count - 1))),
        pl.BlockSpec((width, wide), lambda i: (0, jnp.maximum(i - count, 0))),
    ]
    return pl.pallas_call(
        partial(_ffn_back_kernel, count),
        out_shape=[jax.ShapeDtypeStruct(*s) for s in shapes]
        + [jax.ShapeDtypeStruct((width, count * wide), HALF)] * 4,
        grid=(2 * count,),
        in_specs=fixed + [column] * 2 + specs,
        out_specs=[pl.BlockSpec(s, lambda i: (0, 0)) for s, _ in shapes] + grad_specs * 2,
        scratch_shapes=[pltpu.VMEM((rows, width), WIDE)],
        compiler_params=pltpu.CompilerParams(vmem_limit_bytes=VMEM_LIMIT),
        cost_estimate=pl.CostEstimate(
            flops=16 * rows * width * count * wide, transcendentals=0, bytes_accessed=16 * width * count * wide
        ),
        name="feed_forward_back",
    )(x, grad, resid, normed, inv_scale, gain, active, slope, own, mine, other, own, mine, other)


def per_device(
    enc_input,
    dec_input,
    dec_cotangent,
    enc_lengths,
    dec_lengths,
    attn_weights,
    cross_weights,
    ffn_weights,
    norm_gains,
    norm_biases,
):
    core, place = lax.axis_index("pipe"), lax.axis_index("tensor")
    count = lax.axis_size("tensor")
    top_bit = count // 2
    group = place // top_bit
    block = jnp.where(core == 0, place, place ^ top_bit)
    span, width = enc_input.shape[1:]
    dec_span = dec_input.shape[1]
    local_width = attn_weights.shape[3]
    is_first = core == 0
    chips = range(count)
    half = width // 2
    half_local = local_width // 2

    def owner(t):
        return t // top_bit

    pick = partial(lax.dynamic_index_in_dim, index=core, axis=0, keepdims=False)
    start_low = pick(dec_input)
    (
        w_attn,
        own_cross,
        own_ffn,
        dec_attn_halves,
        dec_cross_halves,
        dec_ffn_halves,
        cross_rest,
        ffn_rest,
        got,
        start_full,
    ) = gather_weights(
        *[in_column_halves(v[0]) for v in (attn_weights, cross_weights, ffn_weights)],
        lax.dynamic_index_in_dim(enc_input, 1 - group, 0, False),
        start_low,
    )
    kept = lax.dynamic_index_in_dim(enc_input, group, 0, False)
    tokens = jnp.where(is_first, kept, got).astype(WIDE)
    mine_ffn = gather_planes(ffn_rest)

    def natural(halves, kinds):
        wide = halves.shape[2] // kinds
        return [
            jnp.concatenate([halves[h][:, k * wide : (k + 1) * wide] for h in range(2)], axis=1)
            for k in range(kinds)
        ]

    dec_attn, dec_cross, dec_ffn = [
        natural(v, k) for v, k in ((dec_attn_halves, 4), (dec_cross_halves, 2), (dec_ffn_halves, 2))
    ]
    norms = jnp.concatenate([norm_gains[0], norm_biases[0]], axis=0)
    norms_other = swap(norms, "pipe", 1)
    enc_norms = jnp.where(is_first, norms, norms_other)
    dec_norms = jnp.where(is_first, norms_other, norms)
    eg, eb, dg, db = enc_norms[:3], enc_norms[3:], dec_norms[:3], dec_norms[3:]

    enc_row = lax.dynamic_index_in_dim(enc_lengths, group, 0, False)
    dec_row_of_group = lax.dynamic_index_in_dim(dec_lengths, group, 0, False)
    dec_row = lax.dynamic_index_in_dim(dec_lengths, core, 0, False)
    spots = jnp.arange(span, dtype=jnp.int32)
    sources = [(s // top_bit, s % top_bit) for s in range(2 * top_bit)]
    own_seg = table_of(block * span + spots, enc_row)
    key_seg = jnp.stack(
        [table_of((block ^ (a * top_bit) ^ c) * span + spots, enc_row) for a, c in sources]
    )
    blocks = width // LANES
    masks = [a * (blocks // 2) + c * (blocks // 2 // top_bit) for a, c in sources]
    dec_spots = jnp.arange(dec_span * count, dtype=jnp.int32)
    dec_seg = table_of(dec_spots, dec_row)
    enc_segs = tables(own_seg, key_seg)
    dec_segs = tables(dec_seg, dec_seg[None])
    cross_segs = tables(table_of(dec_spots, dec_row_of_group), own_seg[None])

    def gain_of(i):
        return enc_norms[i : i + 1]

    def bias_of(i):
        return enc_norms[3 + i : 4 + i]

    embed, start_normed, start_scale = norm_forward(tokens, eg[0], eb[0])
    start_scale = jnp.broadcast_to(start_scale, (span, LANES))
    embed_low = embed.astype(HALF)
    query, key_value = spread(embed_low, w_attn, 4, (0, 1, 2), pair=True)

    def exchange(value):
        held = [value]
        bit = 1
        while bit < top_bit:
            held = held + [swap(v, "tensor", bit) for v in held]
            bit *= 2
        return held + [swap(v, "pipe", 1) for v in held]

    key_values = exchange(key_value)
    mine_cross = gather_planes(after(cross_rest, query))

    start_full = after(start_full, key_value)
    start = start_low.astype(WIDE)
    rows_full = dec_span * count
    wide_rows = ((dec_span, width), WIDE)
    kept_rows = [wide_rows, wide_rows, ((dec_span, LANES), WIDE)]
    norm_terms = ((8, width), WIDE)
    dec_in_w = [dec_attn[k] for k in range(3)]
    dec_query = dot(start_full, dec_in_w[0]).astype(HALF)
    dec_kv = jnp.stack([dot(start_full, w).astype(HALF) for w in dec_in_w[1:]])
    dec_heads_wide, dec_lse = attend(dec_query, [dec_kv], dec_segs, [0], True)
    dec_heads = dec_heads_wide.astype(HALF)
    self_norm, self_normed, self_scale, self_full = rows_call(
        _forward_rows,
        2,
        dot_bt(dec_heads, dec_attn[3]).astype(HALF),
        [start, dg[0:1], db[0:1]],
        kept_rows,
    )
    cross_query = dot(self_full, dec_cross[0]).astype(HALF)

    def in_halves(value):
        return jnp.stack([value[:, :half_local], value[:, half_local:]])

    [cross_q_enc] = to_encoder(in_halves(cross_query), 6)
    cross_q_enc = to_pairs(cross_q_enc)
    mine_ffn = after(mine_ffn, cross_q_enc)
    other_ffn = swap(mine_ffn, "pipe", 1)

    heads_wide, lse = attend(query, key_values, enc_segs, masks)
    heads = heads_wide.astype(HALF)
    mine_cross = after(mine_cross, heads)
    w_cross = jnp.stack(
        [
            jnp.concatenate([own_cross[0], mine_cross], axis=1),
            jnp.concatenate([own_cross[1], swap(mine_cross, "pipe", 1)], axis=1),
        ]
    )
    kept_tokens = [((span, width), WIDE), ((span, width), HALF), ((span, width), WIDE), ((span, LANES), WIDE)]
    attn_norm, attn_norm_low, attn_normed, attn_scale = collect(
        [heads], w_attn, 4, (3,), _end_norm, [embed, gain_of(1), bias_of(1)], kept_tokens
    )
    _, memory_low, mem_normed, mem_scale, active, slope = feed_forward(
        attn_norm_low, attn_norm, gain_of(2), bias_of(2), own_ffn, mine_ffn, other_ffn
    )
    [cross_kv] = spread(memory_low, w_cross, 2, (0, 1), pair=True)

    tables_of_keys = enc_lengths.shape[1]
    at_table = (own_seg[:, None] == jnp.arange(tables_of_keys)[None]).astype(HALF)
    sums = dot_ta(at_table, cross_kv[0])
    bit = 1
    while bit < top_bit:
        sums = sums + swap_columns(sums, "tensor", bit, masks[bit])
        bit *= 2
    sums = sums + swap_columns(sums, "pipe", 1, masks[top_bit])
    means = sums / enc_row.astype(WIDE)[:, None]
    centers = sum(
        jnp.where((own_seg == j)[:, None], means[j : j + 1], 0.0) for j in range(tables_of_keys)
    )
    centered = (cross_kv[0].astype(WIDE) - centers).astype(HALF)

    part_out, part_lse = attend(cross_q_enc, [cross_kv], cross_segs, [0], False, HALF)
    cross_heads, cross_out_wide, cross_lse = to_decoder(
        from_pairs(part_out, half_local), stats_from_pairs(part_lse, half_local), 7
    )
    cross_norm, cross_normed, cross_scale, cross_full = rows_call(
        _forward_rows,
        2,
        dot_bt(cross_heads, dec_cross[1]).astype(HALF),
        [self_norm, dg[1:2], db[1:2]],
        kept_rows,
    )
    dec_hidden = dot(cross_full, dec_ffn[0])
    dec_active = gelu(dec_hidden).astype(HALF)
    result, resid, dec_terms2, grad_full = rows_call(
        _turn_rows,
        3,
        dot_bt(dec_active, dec_ffn[1]).astype(HALF),
        [cross_norm, dg[2:3], db[2:3], pick(dec_cotangent)],
        [((dec_span, width), HALF), wide_rows, norm_terms],
    )
    grad_hidden = (dot(grad_full, dec_ffn[1]) * gelu_slope(dec_hidden)).astype(HALF)
    resid, dec_terms1, cross_grad_full = rows_call(
        _backward_rows,
        4,
        dot_bt(grad_hidden, dec_ffn[0]).astype(HALF),
        [resid, cross_normed, cross_scale, dg[1:2]],
        [wide_rows, norm_terms],
    )
    cross_heads_grad = dot(cross_grad_full, dec_cross[1]).astype(HALF)
    heads_grad_enc, stats_enc = to_encoder(
        in_halves(cross_heads_grad), 8, cross_out_wide, cross_lse
    )
    cross_q_term, [cross_kv_grad] = attend_back(
        cross_q_enc,
        [cross_kv],
        to_pairs(heads_grad_enc),
        stats_to_pairs(stats_enc, half_local),
        centered,
        cross_segs,
        [0],
        False,
        False,
    )
    dec_f2_grad = dot_ta(grad_full, dec_active)
    dec_f1_grad = dot_ta(cross_full, grad_hidden)
    dec_ffn_half, _ = scatter_local([dec_f1_grad, dec_f2_grad])

    back_tokens = [((span, width), WIDE), ((span, width), HALF), ((8, width), WIDE)]
    resid_enc, resid_low, enc_terms2, *cross_grads = collect(
        [cross_kv_grad],
        w_cross,
        2,
        (0, 1),
        _end_norm_back,
        [mem_normed, mem_scale, gain_of(2)],
        back_tokens,
        memory_low,
    )
    enc_ckv = fold_planes(fold_cores(*cross_grads))
    resid_enc, resid_low, enc_terms1, *ffn_grads = feed_forward_back(
        attn_norm_low,
        resid_low,
        resid_enc,
        attn_normed,
        attn_scale,
        gain_of(1),
        active,
        slope,
        own_ffn,
        mine_ffn,
        other_ffn,
    )
    enc_f2 = fold_planes(after(fold_cores(*ffn_grads[2:]), dec_ffn_half, enc_ckv))
    enc_f1 = fold_planes(fold_cores(*ffn_grads[:2]))
    heads_grad, *out_grads = spread(resid_low, w_attn, 4, (3,), heads)
    q_grad, kv_grads = attend_back(
        query, key_values, heads_grad, lse, heads_wide, enc_segs, masks
    )

    def join(a, b):
        return (a.astype(WIDE) + b.astype(WIDE)).astype(HALF)

    held = [join(a, swap(b, "pipe", 1)) for a, b in zip(kv_grads[:top_bit], kv_grads[top_bit:])]
    bit = top_bit // 2
    while bit >= 1:
        held = [join(a, swap(b, "tensor", bit)) for a, b in zip(held[:bit], held[bit:])]
        bit //= 2
    kv_grad = held[0]

    def to_owner(value):
        theirs = joint(value, [((1 - owner(t), t), (owner(t), t)) for t in chips])
        theirs = theirs.reshape(2, count, *theirs.shape[1:])
        chip = value.reshape(theirs.shape).astype(WIDE) + theirs[::-1].astype(WIDE)
        chip = jnp.where(is_first, chip, chip[::-1]).astype(HALF)
        terms = []
        for s in range(top_bit):
            near, far = 2 * s, 2 * s + 1
            near_pairs = [((owner(t), t), (owner(t), t ^ s)) for t in chips]
            far_pairs = [((owner(t), t), (owner(t), t ^ s ^ top_bit)) for t in chips]
            near_got = chip[:, near] if s == 0 else joint(chip[:, near], near_pairs)
            far_got = joint(chip[:, far], far_pairs)
            terms.append(jnp.where(core == group, near_got, far_got).astype(WIDE))
        return sum(terms)

    cross_q_grad = after(to_owner(from_pairs(cross_q_term, half_local)).astype(HALF), q_grad)
    cross_q_grad = jnp.concatenate([cross_q_grad[0], cross_q_grad[1]], axis=1)
    resid, dec_terms0, self_grad_full = rows_call(
        _backward_rows,
        4,
        dot_bt(cross_q_grad, dec_cross[0]).astype(HALF),
        [resid, self_normed, self_scale, dg[0:1]],
        [wide_rows, norm_terms],
    )
    dec_heads_grad = dot(self_grad_full, dec_attn[3]).astype(HALF)
    dec_q_grad, [dec_kv_grad] = attend_back(
        dec_query, [dec_kv], dec_heads_grad, dec_lse, dec_heads_wide, dec_segs, [0], True
    )
    dec_proj_grad = [dec_q_grad, dec_kv_grad[0], dec_kv_grad[1]]
    [dec_grad] = rows_call(
        _last_rows,
        5,
        sum(dot_bt(g, w) for g, w in zip(dec_proj_grad, dec_in_w)).astype(HALF),
        [resid],
        [wide_rows],
        False,
    )
    dec_left = [start_full] * 3 + [self_grad_full, self_full, cross_grad_full]
    dec_right = dec_proj_grad + [dec_heads, cross_q_grad, cross_heads]
    dec_small = [dot_ta(a, b) for a, b in zip(dec_left, dec_right)]
    dec_small_half, dec_small_term = scatter_local(dec_small)
    kv_grad = after(kv_grad, dec_small_term)

    enc_grad, _, enc_terms0, *in_grads = collect(
        [q_grad, kv_grad],
        w_attn,
        4,
        (0, 1, 2),
        _end_norm_back,
        [resid_enc, start_normed, start_scale, gain_of(0)],
        back_tokens,
        embed_low,
    )
    enc_in, enc_out = fold_cores(*in_grads), fold_cores(*out_grads)
    enc_attn_rows = fold_planes(jnp.concatenate([enc_in, enc_out], axis=1))
    enc_ffn_half = jnp.concatenate([fold_chips(enc_f1, 1), fold_chips(enc_f2, 1)], axis=1)
    enc_cross_half = fold_chips(enc_ckv, 2)
    enc_terms = [enc_terms0, enc_terms1, enc_terms2]

    def section(enc_half, dec_half):
        keep = jnp.where(is_first, enc_half, dec_half)
        got = swap(jnp.where(is_first, dec_half, enc_half), "pipe", 1)
        pair = jnp.where(is_first, jnp.stack([keep, got], axis=2), jnp.stack([got, keep], axis=2))
        return pair.reshape(*pair.shape[:2], -1)[None].astype(WIDE)

    ffn_out_grad = section(enc_ffn_half, dec_ffn_half)
    enc_attn_rows = after(enc_attn_rows, ffn_out_grad, enc_cross_half, dec_grad)
    in_columns = enc_in.shape[1]
    enc_attn_half = jnp.concatenate(
        [fold_chips(enc_attn_rows[:, :in_columns], 3), fold_chips(enc_attn_rows[:, in_columns:], 1)], axis=1
    )
    attn_out = section(enc_attn_half, dec_small_half[:, :4])
    cross_out = section(enc_cross_half, dec_small_half[:, 4:])
    dec_terms = [dec_terms0, dec_terms1, dec_terms2]
    norm_sums = reduce_norms(
        jnp.stack([v[i] for i in range(2) for v in enc_terms]),
        jnp.stack([v[i] for i in range(2) for v in dec_terms]),
    )

    dec_pair = jnp.stack([result, dec_grad.astype(HALF)])
    dec_halves = dec_pair.reshape(2, dec_span, 2, half)
    dec_got = swap(lax.dynamic_index_in_dim(dec_halves, 1 - core, 2, False), "pipe", 1)
    own_result = lax.dynamic_slice_in_dim(result, core * half, half, 1)
    own_grad = lax.dynamic_slice_in_dim(dec_grad, core * half, half, 1)
    dec_output = jnp.where(
        is_first, jnp.stack([own_result, dec_got[0]]), jnp.stack([dec_got[0], own_result])
    )
    got_grad = dec_got[1].astype(WIDE)
    dec_input_grad = jnp.where(
        is_first, jnp.stack([own_grad, got_grad]), jnp.stack([got_grad, own_grad])
    )

    enc_low = enc_grad.astype(HALF)
    far_first = joint(enc_low[:, :half], [((1, t), (0, t ^ top_bit)) for t in chips])
    far_second = joint(enc_low[:, half:], [((1, t), (1, t ^ top_bit)) for t in chips])
    near_second = joint(enc_low[:, half:], [((0, t), (1, t)) for t in chips])
    here = jnp.where(is_first, enc_grad[:, :half], near_second.astype(WIDE))
    there = jnp.where(is_first, far_first, far_second).astype(WIDE)
    enc_input_grad = jnp.where(group == 0, jnp.stack([here, there]), jnp.stack([there, here]))
    return (
        dec_output,
        enc_input_grad,
        dec_input_grad,
        attn_out,
        cross_out,
        ffn_out_grad,
        norm_sums[None, :3],
        norm_sums[None, 3:],
    )


def solution(mesh):
    rows = P("dp", "tensor", None)
    weights = P("pipe", None, None, "tensor")
    half_rows = P("dp", "tensor", "pipe")
    weight_grads = P("pipe", "dp", None, "tensor")
    norm_grads = P("pipe", None, ("dp", "tensor"))
    return jax.shard_map(
        per_device,
        mesh=mesh,
        in_specs=(rows, rows, rows, P("dp", None), P("dp", None))
        + (weights,) * 3
        + (P("pipe", None, None),) * 2,
        out_specs=(half_rows,) * 3 + (weight_grads,) * 3 + (norm_grads,) * 2,
        check_vma=False,
    )
```

```python
from functools import partial

import jax
import jax.numpy as jnp
from jax import lax
from jax.experimental import pallas as pl
from jax.experimental.pallas import tpu as pltpu
from jax.sharding import PartitionSpec as P

HEAD = 64
LANES = 128
EPSILON = 1e-05
NEGATIVE = -1e30
HALF = jnp.bfloat16
WIDE = jnp.float32
VMEM_LIMIT = 56 << 20
MESH = pl.DeviceIdType.MESH
TILE_Q = 512
TILE_K = 512


def dot(left, right):
    return jnp.dot(left, right, preferred_element_type=WIDE)


def dot_bt(left, right):
    return lax.dot_general(left, right, (((1,), (1,)), ((), ())), preferred_element_type=WIDE)


def dot_ta(left, right):
    return lax.dot_general(left, right, (((0,), (0,)), ((), ())), preferred_element_type=WIDE)


def swap(value, axis, mask):
    return lax.ppermute(value, axis, [(i, i ^ mask) for i in range(lax.axis_size(axis))])


def joint(value, pairs):
    count = lax.axis_size("tensor")
    return lax.ppermute(
        value,
        ("pipe", "tensor"),
        [(a[0] * count + a[1], b[0] * count + b[1]) for a, b in pairs],
    )


def after(value, *earlier):
    return lax.optimization_barrier((value, *earlier))[0]


def swap_columns(value, axis, mask, difference):
    got = swap(value, axis, mask).reshape(value.shape[0], -1, LANES)
    order = [b ^ difference for b in range(got.shape[1])]
    return jnp.concatenate([got[:, b] for b in order], axis=1)


def table_of(places, lengths):
    total = jnp.zeros((), jnp.int32)
    table = jnp.zeros(places.shape, jnp.int32)
    for j in range(lengths.shape[0]):
        total = total + lengths[j]
        table = table + (places >= total).astype(jnp.int32)
    return table


def norm_forward(values, gain, bias):
    center = values - jnp.mean(values, axis=-1, keepdims=True)
    inv_scale = lax.rsqrt(jnp.mean(center * center, axis=-1, keepdims=True) + EPSILON)
    normed = center * inv_scale
    return normed * gain + bias, normed, inv_scale


def norm_backward(grad_out, normed, inv_scale, gain):
    grad_gain = jnp.sum(grad_out * normed, axis=0)
    grad_bias = jnp.sum(grad_out, axis=0)
    grad_normed = grad_out * gain
    grad_in = inv_scale * (
        grad_normed
        - jnp.mean(grad_normed, axis=-1, keepdims=True)
        - normed * jnp.mean(grad_normed * normed, axis=-1, keepdims=True)
    )
    return grad_in, grad_gain, grad_bias


def gelu(hidden):
    return 0.5 * hidden * (1.0 + lax.erf(hidden * (2.0**-0.5)))


def gelu_slope(hidden):
    density = jnp.exp(-0.5 * hidden * hidden) * 0.3989422804014327
    return 0.5 * (1.0 + lax.erf(hidden * (2.0**-0.5))) + hidden * density


def _allowed(seg_k, seg_q, causal, col0, row0):
    ok = seg_k == seg_q
    if causal:
        keys = col0 + lax.broadcasted_iota(jnp.int32, ok.shape, 0)
        queries = row0 + lax.broadcasted_iota(jnp.int32, ok.shape, 1)
        ok = ok & (queries >= keys)
    return ok


def _tile_loop(act, chunks, c, nq, nk, tq, tk, body):
    def step(i, carry):
        iq, ik = i // nk, i % nk

        @pl.when(act[iq * (chunks * nk) + c * nk + ik] > 0)
        def _():
            body(iq * tq, ik * tk, pl.ds(pl.multiple_of(iq * tq, tq), tq), pl.ds(pl.multiple_of(ik * tk, tk), tk))

        return carry

    lax.fori_loop(0, nq * nk, step, 0)


def _head_lanes(shape, head):
    lanes = lax.broadcasted_iota(jnp.int32, shape, 1)
    return (lanes < HEAD) if head == 0 else (lanes >= HEAD)


def _attend_kernel(chunks, tq, tk, causal, act, seg_q, seg_k, q, *refs):
    keys, values = refs[:chunks], refs[chunks : 2 * chunks]
    out, lse, top, total, acc = refs[-5:]
    rows = q.shape[0]
    nq, nk = rows // tq, keys[0].shape[0] // tk
    top[...] = jnp.full(top.shape, NEGATIVE, WIDE)
    total[...] = jnp.zeros(total.shape, WIDE)
    acc[...] = jnp.zeros(acc.shape, WIDE)
    for c in range(chunks):

        def tile(row0, col0, r, s, c=c):
            qs = q[r, :] * jnp.asarray(HEAD**-0.5, HALF)
            kk, vt = keys[c][s, :], values[c][s, :].T
            ok = _allowed(seg_k[c, s, 0:1], seg_q[0:1, r], causal, col0, row0)
            for h in range(2):
                qh = jnp.where(_head_lanes(qs.shape, h), qs, jnp.zeros_like(qs))
                sc = jnp.where(ok, dot_bt(kk, qh), NEGATIVE)
                before = top[h : h + 1, r]
                after = jnp.maximum(before, jnp.max(sc, axis=0, keepdims=True))
                pr = jnp.exp(sc - after).astype(HALF)
                fade = jnp.exp(before - after)
                total[h : h + 1, r] = total[h : h + 1, r] * fade + jnp.sum(
                    pr.astype(WIDE), axis=0, keepdims=True
                )
                span = slice(h * HEAD, (h + 1) * HEAD)
                acc[span, r] = acc[span, r] * fade + dot(vt[span, :], pr)
                top[h : h + 1, r] = after

        _tile_loop(act, chunks, c, nq, nk, tq, tk, tile)
    count = total[...]
    count = jnp.where(count > 0.0, count, 1.0)
    lse[0] = top[...] + jnp.log(count)
    whole = jnp.concatenate([acc[:HEAD, :] / count[0:1, :], acc[HEAD:, :] / count[1:2, :]], axis=0)
    out[...] = whole.T.astype(out.dtype)


def _attend_back_kernel(chunks, tq, tk, causal, own_delta, act, seg_q, seg_k, q, *refs):
    keys, values = refs[:chunks], refs[chunks : 2 * chunks]
    grad_out, stats = refs[2 * chunks : 2 * chunks + 2]
    refs = refs[2 * chunks + 2 :]
    extra, (grad_q, *grad_kv, delta, dq, dkv) = refs[0], refs[-(chunks + 4) :]
    rows = q.shape[0]
    nq, nk = rows // tq, keys[0].shape[0] // tk
    if own_delta:
        product = grad_out[...].astype(WIDE) * extra[...].astype(WIDE)
        pick = (
            lax.broadcasted_iota(jnp.int32, (8, LANES), 1) // HEAD
            == lax.broadcasted_iota(jnp.int32, (8, LANES), 0)
        ).astype(WIDE)
        delta[...] = lax.dot_general(
            pick, product, (((1,), (1,)), ((), ())), precision=lax.Precision.HIGHEST, preferred_element_type=WIDE
        )
    else:
        delta[0:2, :] = stats[0, 2:4, :]
    dq[...] = jnp.zeros(dq.shape, WIDE)
    for c in range(chunks):
        dkv[...] = jnp.zeros(dkv.shape, WIDE)

        def tile(row0, col0, r, s, c=c):
            qs = q[r, :] * jnp.asarray(HEAD**-0.5, HALF)
            go = grad_out[r, :]
            kk, vv = keys[c][s, :], values[c][s, :]
            ok = _allowed(seg_k[c, s, 0:1], seg_q[0:1, r], causal, col0, row0)
            for h in range(2):
                mine, mine_k = _head_lanes(qs.shape, h), _head_lanes(kk.shape, h)
                qh = jnp.where(mine, qs, jnp.zeros_like(qs))
                gh = jnp.where(mine, go, jnp.zeros_like(go))
                kh = jnp.where(mine_k, kk if own_delta else extra[s, :], jnp.zeros_like(kk))
                sc = jnp.where(ok, dot_bt(kk, qh), NEGATIVE)
                pr = jnp.exp(sc - stats[0, h : h + 1, r])
                ds = (pr * (dot_bt(vv, gh) - delta[h : h + 1, r])).astype(HALF)
                pr = pr.astype(HALF)
                dq[r, :] = dq[r, :] + dot_ta(ds, kh)
                dkv[0, s, :] = dkv[0, s, :] + dot(ds, qh)
                dkv[1, s, :] = dkv[1, s, :] + dot(pr, gh)

        _tile_loop(act, chunks, c, nq, nk, tq, tk, tile)
        grad_kv[c][...] = dkv[...].astype(grad_kv[c].dtype)
    grad_q[...] = (dq[...] * HEAD**-0.5).astype(grad_q.dtype)


def _tile_sizes(rows, keys):
    return min(TILE_Q, rows), min(TILE_K, keys)


def _activity(seg_q, seg_k, tq, tk):
    qt = seg_q.reshape(-1, tq)
    kt = seg_k.reshape(-1, tk)
    hit = (qt[:, :1] <= kt[:, -1][None]) & (kt[:, 0][None] <= qt[:, -1:])
    return hit.astype(jnp.int32).reshape(-1)


def tables(seg_q, seg_k):
    rows, (chunks, span) = seg_q.shape[0], seg_k.shape
    tq, tk = _tile_sizes(rows, span)
    return (
        _activity(seg_q, seg_k, tq, tk),
        jnp.broadcast_to(seg_q[None], (8, rows)),
        jnp.broadcast_to(seg_k[:, :, None], (chunks, span, LANES)),
    )


def _specs(rows, span, chunks, masks, blocked, part):
    def block(h):
        return h if part is None else 2 * h + part

    row_block = pl.BlockSpec((rows, LANES), lambda h, act: (0, block(h)))
    if blocked:
        row_block = pl.BlockSpec((None, rows, LANES), lambda h, act: (block(h), 0, 0))
    stat_block = pl.BlockSpec((1, 8, rows), lambda h, act: (block(h), 0, 0))
    heads = [
        pl.BlockSpec((8, rows), lambda h, act: (0, 0)),
        pl.BlockSpec((chunks, span, LANES), lambda h, act: (0, 0, 0)),
        row_block,
    ]
    for side in range(2):
        heads += [
            pl.BlockSpec((None, span, LANES), lambda h, act, m=m, side=side: (side, 0, h ^ m)) for m in masks
        ]
    return row_block, stat_block, heads


def _dimensions(q, key_values, masks, part):
    blocked = q.ndim == 3
    rows, width = (q.shape[1], q.shape[0] * LANES) if blocked else q.shape
    span, chunks, blocks = key_values[0].shape[1], len(key_values), width // LANES
    if part is not None:
        blocks, masks = blocks // 2, [m // 2 for m in masks]
    row_block, stat_block, specs = _specs(rows, span, chunks, masks, blocked, part)
    return rows, span, chunks, blocks, masks, _tile_sizes(rows, span), row_block, stat_block, specs


def attend(q, key_values, segs, masks, causal=False, out_type=WIDE, part=None, into=()):
    rows, span, chunks, blocks, masks, (tq, tk), row_block, stat_block, specs = _dimensions(
        q, key_values, masks, part
    )
    pairs = rows * span * chunks * blocks * LANES
    kept = 4 + 2 * chunks
    stat_blocks = blocks if part is None else 2 * blocks
    return pl.pallas_call(
        partial(_attend_kernel, chunks, tq, tk, causal),
        out_shape=(
            jax.ShapeDtypeStruct(q.shape, out_type),
            jax.ShapeDtypeStruct((stat_blocks, 8, rows), WIDE),
        ),
        grid_spec=pltpu.PrefetchScalarGridSpec(
            num_scalar_prefetch=1,
            grid=(blocks,),
            in_specs=specs + [pl.BlockSpec(memory_space=pl.ANY)] * len(into),
            out_specs=[row_block, stat_block],
            scratch_shapes=[
                pltpu.VMEM((8, rows), WIDE),
                pltpu.VMEM((8, rows), WIDE),
                pltpu.VMEM((LANES, rows), WIDE),
            ],
        ),
        input_output_aliases={kept + i: i for i in range(len(into))},
        compiler_params=pltpu.CompilerParams(vmem_limit_bytes=VMEM_LIMIT),
        cost_estimate=pl.CostEstimate(
            flops=48 * pairs, transcendentals=pairs // HEAD, bytes_accessed=rows * blocks * LANES * 20
        ),
        name="attend",
    )(*segs, q, *key_values, *key_values, *into)


def attend_back(
    q, key_values, grad_out, stats, extra, segs, masks, causal=False, own_delta=True, part=None, into=()
):
    rows, span, chunks, blocks, masks, (tq, tk), row_block, stat_block, specs = _dimensions(
        q, key_values, masks, part
    )
    kv_out = [pl.BlockSpec((2, span, LANES), lambda h, act, m=m: (0, 0, h ^ m)) for m in masks]
    pairs = rows * span * chunks * blocks * LANES
    extra_block = row_block if own_delta else pl.BlockSpec((span, LANES), lambda h, act: (0, h))
    kept = 7 + 2 * chunks
    outs = pl.pallas_call(
        partial(_attend_back_kernel, chunks, tq, tk, causal, own_delta),
        out_shape=[jax.ShapeDtypeStruct(q.shape, HALF)]
        + [jax.ShapeDtypeStruct((2, span, blocks * LANES), HALF)] * chunks,
        grid_spec=pltpu.PrefetchScalarGridSpec(
            num_scalar_prefetch=1,
            grid=(blocks,),
            in_specs=specs
            + [row_block, stat_block, extra_block]
            + [pl.BlockSpec(memory_space=pl.ANY)] * len(into),
            out_specs=[row_block] + kv_out,
            scratch_shapes=[
                pltpu.VMEM((8, rows), WIDE),
                pltpu.VMEM((rows, LANES), WIDE),
                pltpu.VMEM((2, span, LANES), WIDE),
            ],
        ),
        input_output_aliases={kept + i: i for i in range(len(into))},
        compiler_params=pltpu.CompilerParams(vmem_limit_bytes=VMEM_LIMIT),
        cost_estimate=pl.CostEstimate(
            flops=80 * pairs, transcendentals=pairs // HEAD, bytes_accessed=rows * blocks * LANES * 40
        ),
        name="attend_back",
    )(*segs, q, *key_values, *key_values, grad_out, stats, extra, *into)
    return outs[0], outs[1:]


def _row_mean(values):
    return jnp.mean(values, axis=-1, keepdims=True)


def _norm_rows(values, gain, bias):
    center = values - _row_mean(values)
    inv_scale = lax.rsqrt(_row_mean(center * center) + EPSILON)
    normed = center * inv_scale
    return normed * gain + bias, normed, inv_scale


def _norm_rows_back(grad_out, normed, inv_scale, gain):
    grad_normed = grad_out * gain
    grad_in = inv_scale * (
        grad_normed - _row_mean(grad_normed) - normed * _row_mean(grad_normed * normed)
    )
    return (
        grad_in,
        jnp.sum(grad_out * normed, axis=0, keepdims=True),
        jnp.sum(grad_out, axis=0, keepdims=True),
    )


def _forward_rows(total, ins, outs):
    resid, gain, bias = ins
    value, normed, inv_scale = _norm_rows(total + resid[...], gain[...], bias[...])
    outs[0][...] = value
    outs[1][...] = normed
    outs[2][...] = jnp.broadcast_to(inv_scale, outs[2].shape)
    return value


def _turn_rows(total, ins, outs):
    resid, gain, bias, cotangent = ins
    value, normed, inv_scale = _norm_rows(total + resid[...], gain[...], bias[...])
    outs[0][...] = value.astype(outs[0].dtype)
    grad, grad_gain, grad_bias = _norm_rows_back(
        cotangent[...].astype(WIDE), normed, inv_scale, gain[...]
    )
    outs[1][...] = grad
    outs[2][0:1, :] = grad_gain
    outs[2][1:2, :] = grad_bias
    return grad


def _backward_rows(total, ins, outs):
    resid, normed, inv_scale, gain = ins
    grad, grad_gain, grad_bias = _norm_rows_back(
        total + resid[...], normed[...], inv_scale[:, 0:1], gain[...]
    )
    outs[0][...] = grad
    outs[1][0:1, :] = grad_gain
    outs[1][1:2, :] = grad_bias
    return grad


def _rows_kernel(count, scatter, gather, middle, n_in, n_out, *refs):
    refs = list(refs)
    part = refs.pop(0) if scatter else None
    ins, refs = refs[:n_in], refs[n_in:]
    outs, refs = refs[:n_out], refs[n_out:]
    full = refs.pop(0) if gather else None
    landed = refs.pop(0) if scatter else None
    send_sem, recv_sem = refs[:2]
    me = lax.axis_index("tensor")
    steps = range(1, count)
    peers = [lax.rem(me + s, count) for s in steps]
    barrier = pltpu.get_barrier_semaphore()
    for peer in peers:
        pl.semaphore_signal(barrier, inc=1, device_id={"tensor": peer}, device_id_type=MESH)
    pl.semaphore_wait(barrier, count - 1)
    total = None
    if scatter:
        rows = part.shape[0] // count
        copies = []
        for s, peer in zip(steps, peers):
            copy = pltpu.make_async_remote_copy(
                src_ref=part.at[pl.ds(pl.multiple_of(peer * rows, rows), rows)],
                dst_ref=landed.at[s - 1],
                send_sem=send_sem.at[0, s - 1],
                recv_sem=recv_sem.at[0, s - 1],
                device_id={"tensor": peer},
                device_id_type=MESH,
            )
            copy.start()
            copies.append(copy)
        total = part[pl.ds(pl.multiple_of(me * rows, rows), rows), :].astype(WIDE)
        for s, copy in zip(steps, copies):
            copy.wait_recv()
            total = total + landed[s - 1].astype(WIDE)
        for copy in copies:
            copy.wait_send()
    sent = middle(total, ins, outs)
    if gather:
        rows = full.shape[0] // count
        own = pl.ds(pl.multiple_of(me * rows, rows), rows)
        full[own, :] = sent.astype(full.dtype)
        copies = []
        for s, peer in zip(steps, peers):
            copy = pltpu.make_async_remote_copy(
                src_ref=full.at[own],
                dst_ref=full.at[own],
                send_sem=send_sem.at[1, s - 1],
                recv_sem=recv_sem.at[1, s - 1],
                device_id={"tensor": peer},
                device_id_type=MESH,
            )
            copy.start()
            copies.append(copy)
        for copy in copies:
            copy.wait()


def rows_call(middle, number, part, ins, outs, gather=True):
    count = lax.axis_size("tensor")
    scatter = part is not None
    width = (part if scatter else ins[0]).shape[1]
    rows = part.shape[0] // count if scatter else ins[0].shape[0]
    shapes = [jax.ShapeDtypeStruct(shape, kind) for shape, kind in outs]
    if gather:
        shapes.append(jax.ShapeDtypeStruct((rows * count, width), HALF))
    whole = pl.BlockSpec(memory_space=pltpu.VMEM)
    operands = ([part] if scatter else []) + list(ins)
    got = pl.pallas_call(
        partial(_rows_kernel, count, scatter, gather, middle, len(ins), len(outs)),
        out_shape=shapes,
        in_specs=[whole] * len(operands),
        out_specs=[whole] * len(shapes),
        scratch_shapes=([pltpu.VMEM((count - 1, rows, width), HALF)] if scatter else [])
        + [pltpu.SemaphoreType.DMA((2, count - 1))] * 2,
        compiler_params=pltpu.CompilerParams(
            collective_id=number, has_side_effects=True, vmem_limit_bytes=VMEM_LIMIT
        ),
        cost_estimate=pl.CostEstimate(
            flops=0, transcendentals=0, bytes_accessed=1400 * rows * width
        ),
        name=middle.__name__.strip("_"),
    )(*operands)
    return got


def _differ(a, b, count):
    total, bit = 0, 1
    while bit < count:
        total = total + lax.rem(lax.rem(a // bit, 2) + lax.rem(b // bit, 2), 2) * bit
        bit *= 2
    return total


def _slot(difference, count):
    top = count // 2
    return 2 * lax.rem(difference, top) + difference // top


def _enter(peers):
    barrier = pltpu.get_barrier_semaphore()
    for peer in peers:
        pl.semaphore_signal(barrier, inc=1, device_id=peer, device_id_type=MESH)
    pl.semaphore_wait(barrier, len(peers))


def _send(source, dest, send_sem, recv_sem, peer):
    copy = pltpu.make_async_remote_copy(
        src_ref=source,
        dst_ref=dest,
        send_sem=send_sem,
        recv_sem=recv_sem,
        device_id=peer,
        device_id_type=MESH,
    )
    copy.start()
    return copy


def _to_encoder_kernel(count, with_stats, *refs):
    if with_stats:
        value, out, lse, full, stats, own, own_stats, held, other, other_stats, send_sem, recv_sem = refs
    else:
        value, full, own, other, send_sem, recv_sem = refs
    core, me = lax.axis_index("pipe"), lax.axis_index("tensor")
    group = me // (count // 2)
    chips = [lax.rem(me + s, count) for s in range(1, count)]
    _enter([{"tensor": chip} for chip in chips] + [{"pipe": 1 - core}])
    sets = [(value, own, other, full)]
    if with_stats:
        for h in range(2):
            product = value[h].astype(WIDE) * out[h]
            pick = (
                lax.broadcasted_iota(jnp.int32, (8, product.shape[1]), 1) // HEAD
                == lax.broadcasted_iota(jnp.int32, (8, product.shape[1]), 0) - 2
            ).astype(WIDE)
            held[h] = lax.dot_general(
                pick,
                product,
                (((1,), (1,)), ((), ())),
                precision=lax.Precision.HIGHEST,
                preferred_element_type=WIDE,
            )
            held[h, 0:2, :] = lse[h, 0:2, :]
        sets.append((held, own_stats, other_stats, stats))
    copies = []
    for s, chip in enumerate(chips):
        place = _slot(_differ(chip, me, count), count)
        for h in range(2):
            at = lax.rem(h + core, 2) * count + place
            for i, (source, dest, _, _) in enumerate(sets):
                sems = (send_sem.at[i, s, h], recv_sem.at[i, s, h])
                copies.append(_send(source.at[h], dest.at[at], *sems, {"tensor": chip}))
    for h in range(2):
        for source, dest, _, _ in sets:
            dest[lax.rem(h + core, 2) * count] = source[h]
    for copy in copies:
        copy.wait()
    copies = []
    for g in range(2):
        for i, (_, source, dest, _) in enumerate(sets):
            here, there = pl.ds(g * count, count), pl.ds((1 - g) * count, count)
            sems = (send_sem.at[i, count - 1, g], recv_sem.at[i, count - 1, g])
            copies.append(_send(source.at[here], dest.at[there], *sems, {"pipe": 1 - core}))
    for copy in copies:
        copy.wait()
    for _, mine, theirs, dest in sets:

        @pl.when(core == group)
        def _(mine=mine, dest=dest):
            dest[...] = mine[...]

        @pl.when(core != group)
        def _(theirs=theirs, dest=dest):
            dest[...] = theirs[...]


def to_encoder(value, number, out=None, lse=None):
    count = lax.axis_size("tensor")
    _, rows, wide = value.shape
    shapes = [((2 * count, rows, wide), HALF)]
    if out is not None:
        shapes.append(((2 * count, 8, rows), WIDE))
    scratch = [pltpu.VMEM(*s) for s in shapes]
    if out is not None:
        scratch.append(pltpu.VMEM((2, 8, rows), WIDE))
    scratch += [pltpu.VMEM(*s) for s in shapes]
    whole = pl.BlockSpec(memory_space=pltpu.VMEM)
    operands = (value,) if out is None else (value, out, lse)
    return pl.pallas_call(
        partial(_to_encoder_kernel, count, out is not None),
        out_shape=[jax.ShapeDtypeStruct(*s) for s in shapes],
        in_specs=[whole] * len(operands),
        out_specs=[whole] * len(shapes),
        scratch_shapes=scratch + [pltpu.SemaphoreType.DMA((len(shapes), count, 2))] * 2,
        compiler_params=pltpu.CompilerParams(
            collective_id=number, has_side_effects=True, vmem_limit_bytes=VMEM_LIMIT
        ),
        cost_estimate=pl.CostEstimate(flops=0, transcendentals=0, bytes_accessed=60 << 20),
        name="to_encoder",
    )(*operands)


def _over_lanes(weights, wide):
    lanes = lax.broadcasted_iota(jnp.int32, (8, wide), 1) // HEAD
    pick = (lanes == lax.broadcasted_iota(jnp.int32, (8, wide), 0)).astype(HALF)
    high = weights.astype(HALF)
    low = (weights - high.astype(WIDE)).astype(HALF)
    return dot_ta(jnp.concatenate([high, low], axis=0), jnp.concatenate([pick, pick], axis=0))


def _to_decoder_kernel(count, *refs):
    part, lse, heads, out, out_lse = refs[:5]
    other, other_lse, both, both_lse, landed, landed_lse, send_sem, recv_sem = refs[5:]
    core, me = lax.axis_index("pipe"), lax.axis_index("tensor")
    top = count // 2
    chips = [lax.rem(me + s, count) for s in range(1, count)]
    _enter([{"tensor": chip} for chip in chips] + [{"pipe": 1 - core}])
    copies = []
    for g in range(2):
        here, there = pl.ds(g * count, count), pl.ds((1 - g) * count, count)
        for i, (source, dest) in enumerate(((part, other), (lse, other_lse))):
            sems = (send_sem.at[i, count - 1, g], recv_sem.at[i, count - 1, g])
            copies.append(_send(source.at[here], dest.at[there], *sems, {"pipe": 1 - core}))
    for copy in copies:
        copy.wait()
    wide = part.shape[2]
    for i in range(2 * count):
        first, second = lse[i], other_lse[i]
        peak = jnp.maximum(first, second)
        a, b = jnp.exp(first - peak), jnp.exp(second - peak)
        both_lse[i] = peak + jnp.log(a + b)
        share = _over_lanes(b / (a + b), wide)
        mine = part[i].astype(WIDE)
        both[i] = (mine + share * (other[i].astype(WIDE) - mine)).astype(HALF)
    copies = []
    for s, chip in enumerate(chips):
        place = _slot(_differ(chip, me, count), count)
        for h in range(2):
            at = lax.rem(h + core, 2) * count + place
            for i, (source, dest) in enumerate(((both, landed), (both_lse, landed_lse))):
                sems = (send_sem.at[i, s, h], recv_sem.at[i, s, h])
                copies.append(_send(source.at[at], dest.at[s, h], *sems, {"tensor": chip}))
    for copy in copies:
        copy.wait()
    for h in range(2):
        at = lax.rem(h + core, 2) * count
        terms = [(me, both[at], both_lse[at])]
        for s in range(count - 1):
            terms.append((lax.rem(me - s - 1 + count, count), landed[s, h], landed_lse[s, h]))
        logs = [jnp.where(chip // top == core, log, NEGATIVE) for chip, _, log in terms]
        peak = logs[0]
        for log in logs[1:]:
            peak = jnp.maximum(peak, log)
        weights = [jnp.exp(log - peak) for log in logs]
        weights = [
            jnp.where(chip // top == core, w, 0.0) for (chip, _, _), w in zip(terms, weights)
        ]
        total = sum(weights)
        out_lse[h] = peak + jnp.log(total)
        shares = [_over_lanes(w / total, wide) for w in weights]
        value = sum(c * term.astype(WIDE) for c, (_, term, _) in zip(shares, terms)) / sum(shares)
        out[h] = value
        heads[:, h * wide : (h + 1) * wide] = value.astype(HALF)


def to_decoder(part, lse, number):
    count = lax.axis_size("tensor")
    slots, rows, wide = part.shape
    whole = pl.BlockSpec(memory_space=pltpu.VMEM)
    return pl.pallas_call(
        partial(_to_decoder_kernel, count),
        out_shape=[
            jax.ShapeDtypeStruct((rows, 2 * wide), HALF),
            jax.ShapeDtypeStruct((2, rows, wide), WIDE),
            jax.ShapeDtypeStruct((2, 8, rows), WIDE),
        ],
        in_specs=[whole] * 2,
        out_specs=[whole] * 3,
        scratch_shapes=[
            pltpu.VMEM((slots, rows, wide), HALF),
            pltpu.VMEM((slots, 8, rows), WIDE),
            pltpu.VMEM((slots, rows, wide), HALF),
            pltpu.VMEM((slots, 8, rows), WIDE),
            pltpu.VMEM((count - 1, 2, rows, wide), HALF),
            pltpu.VMEM((count - 1, 2, 8, rows), WIDE),
        ]
        + [pltpu.SemaphoreType.DMA((2, count, 2))] * 2,
        compiler_params=pltpu.CompilerParams(
            collective_id=number, has_side_effects=True, vmem_limit_bytes=VMEM_LIMIT
        ),
        cost_estimate=pl.CostEstimate(flops=0, transcendentals=0, bytes_accessed=60 << 20),
        name="to_decoder",
    )(part, lse)


def to_pairs(value):
    slots, rows, wide = value.shape
    each = LANES // wide
    if each == 1:
        return value
    value = value.reshape(slots // each, each, rows, wide)
    return value.transpose(0, 2, 1, 3).reshape(slots // each, rows, LANES)


def from_pairs(value, wide):
    blocks, rows, _ = value.shape
    each = LANES // wide
    if each == 1:
        return value
    value = value.reshape(blocks, rows, each, wide)
    return value.transpose(0, 2, 1, 3).reshape(blocks * each, rows, wide)


def stats_to_pairs(stats, wide):
    each = LANES // wide
    if each == 1:
        return stats
    slots, _, rows = stats.shape
    stats = stats.reshape(slots // each, each, 8, rows)
    return jnp.concatenate(
        [stats[:, :, 0], stats[:, :, 2], jnp.zeros((slots // each, 4, rows), WIDE)], axis=1
    )


def stats_from_pairs(stats, wide):
    each = LANES // wide
    if each == 1:
        return stats
    blocks, _, rows = stats.shape
    value = stats[:, :each].reshape(blocks * each, 1, rows)
    return jnp.concatenate([value, jnp.zeros((blocks * each, 7, rows), WIDE)], axis=1)


def slot_bits():
    count = lax.axis_size("tensor")
    bits, bit = [count // 2], 1
    while bit < count // 2:
        bits.append(bit)
        bit *= 2
    return [b for b in bits if b > 0]


def in_column_halves(values):
    wide = values.shape[2] // 2
    return jnp.stack(
        [
            jnp.concatenate(
                [values[:, k, h * wide : (h + 1) * wide] for k in range(values.shape[1])], axis=1
            ).astype(HALF)
            for h in range(2)
        ]
    )


def _gather_kernel(bits, count, planes, *refs):
    own, refs = refs[:3], refs[3:]
    leaving, dec_rows, *refs = refs
    full, enc_cross, enc_ffn, *refs = refs
    dec, refs = refs[:3], refs[3:]
    rests, refs = refs[:2], refs[2:]
    coming, dec_full, send_sem, recv_sem, local_sem = refs
    core, place, me = lax.axis_index("pipe"), lax.axis_index("dp"), lax.axis_index("tensor")
    wide = own[0].shape[2]
    block = own[0].shape[1] // planes
    sibling = {"pipe": 1 - core}
    chips = {bit: {"tensor": _differ(me, bit, count)} for bit in bits}
    line = [{"tensor": _differ(me, s, count)} for s in range(1, count)]
    dp_bits = [1 << i for i in range(planes.bit_length() - 1)]
    others = {bit: {"dp": _differ(place, bit, planes)} for bit in dp_bits}
    _enter([sibling, *line, *others.values()])
    made = [0]

    def push(source, dest, peer):
        i = made[0]
        made[0] += 1
        return _send(source, dest, send_sem.at[i], recv_sem.at[i], peer)

    def rows_of(difference):
        return pl.ds(pl.multiple_of(_differ(place, difference, planes) * block, block), block)

    enc = [full.at[:, :, pl.ds(0, wide)], enc_cross, enc_ffn]
    shown = []
    for a in range(3):
        i = made[0]
        made[0] += 2
        shown.append(i)

        @pl.when(core == 0)
        def _(a=a, i=i):
            for h in range(2):
                _send(own[a].at[h], enc[a].at[1 - h], send_sem.at[i + h], recv_sem.at[i + h], sibling)
                pltpu.make_async_copy(own[a].at[h], enc[a].at[h], local_sem.at[a, h]).start()

        @pl.when(core == 1)
        def _(a=a, i=i):
            for h in range(2):
                _send(own[a].at[h], dec[a].at[h], send_sem.at[i + h], recv_sem.at[i + h], sibling)
                pltpu.make_async_copy(own[a].at[h], dec[a].at[h], local_sem.at[a, h]).start()

    def arrived(a):
        i = shown[a]
        for h in range(2):
            pltpu.make_async_copy(own[a].at[h], enc[a].at[h], local_sem.at[a, h]).wait()
            pltpu.make_async_copy(own[a].at[h], enc[a].at[h], recv_sem.at[i + h]).wait()

    def line_step(a, n, bit):
        here, size = rows_of(0), own[a].shape[2]
        if a == 0:
            source = full.at[0, here, pl.ds(0, n * size)]
            return [push(source, full.at[0, here, pl.ds(n * size, n * size)], chips[bit])]
        rest = rests[a - 1]
        copies = [
            push(enc[a].at[0, here], rest.at[:, pl.ds((n - 1) * size, size)], chips[bit])
        ]
        if n > 1:
            source = rest.at[:, pl.ds(0, (n - 1) * size)]
            copies.append(push(source, rest.at[:, pl.ds(n * size, (n - 1) * size)], chips[bit]))
        return copies

    def wait(copies):
        for copy in copies:
            copy.wait()

    def advance(chain):
        wait(chain["now"])
        chain["now"] = line_step(chain["array"], *chain["todo"].pop(0)) if chain["todo"] else []

    def columns(part):
        return pl.ds(wide + part * half, half)

    def plane_step(j):
        copies = []
        for part, order in enumerate(orders):
            for m in held[part]:
                at = full.at[0, rows_of(m), columns(part)]
                copies.append((part, m ^ order[j], push(at, at, others[order[j]])))
        return copies

    def share(part, m):
        here = rows_of(m)
        source = full.at[0, here, columns(part)]
        return push(source, full.at[1, here, columns(part)], sibling)

    steps = [(1 << i, bit) for i, bit in enumerate(bits)]
    for_attn, for_cross, for_ffn = [{"array": a, "todo": list(steps), "now": []} for a in range(3)]
    arrived(0)
    advance(for_attn)
    arrived(2)
    advance(for_attn)
    advance(for_ffn)
    while for_attn["now"]:
        advance(for_attn)
    token_sem = made[0]
    made[0] += 1

    @pl.when(core == 1)
    def _():
        _send(leaving, coming, send_sem.at[token_sem], recv_sem.at[token_sem], chips[bits[0]])

    at = pl.ds(pl.multiple_of(me * dec_rows.shape[0], dec_rows.shape[0]), dec_rows.shape[0])
    dec_full[at, :] = dec_rows[...]
    dec_sent = [push(dec_full.at[at], dec_full.at[at], peer) for peer in line]
    half = (count - 1) * wide // 2
    orders, held = (dp_bits, dp_bits[::-1]), ([0], [0])
    moving = plane_step(0)
    shared = [share(part, 0) for part in range(2)]
    advance(for_ffn)
    arrived(1)
    for j in range(len(dp_bits)):
        for _, _, copy in moving:
            copy.wait()
        for part, order in enumerate(orders):
            held[part].extend([m ^ order[j] for m in held[part]])
        following = plane_step(j + 1) if j + 1 < len(dp_bits) else []
        shared += [share(part, m) for part, m, _ in moving]
        moving = following
        advance(for_cross)
    while for_ffn["now"]:
        advance(for_ffn)
    while for_cross["now"]:
        advance(for_cross)

    @pl.when(core == 1)
    def _():
        pltpu.make_async_copy(leaving, leaving, send_sem.at[token_sem]).wait()
        pltpu.make_async_copy(leaving, coming, recv_sem.at[token_sem]).wait()

    wait(dec_sent)
    wait(shared)
    for a in range(3):
        for h in range(2):
            pltpu.make_async_copy(own[a].at[h], own[a].at[h], send_sem.at[shown[a] + h]).wait()


def gather_weights(attn, cross, ffn, leaving, dec_rows):
    own = (attn, cross, ffn)
    count, planes = lax.axis_size("tensor"), lax.axis_size("dp")
    depth = attn.shape[1]
    shapes = [(2, depth, count * attn.shape[2]), cross.shape, ffn.shape]
    shapes += [v.shape for v in own]
    shapes += [(depth // planes, (count - 1) * v.shape[2]) for v in (cross, ffn)]
    shapes += [leaving.shape, (count * dec_rows.shape[0], dec_rows.shape[1])]
    hbm, vmem = pl.BlockSpec(memory_space=pl.ANY), pl.BlockSpec(memory_space=pltpu.VMEM)
    return pl.pallas_call(
        partial(_gather_kernel, slot_bits(), count, planes),
        out_shape=[jax.ShapeDtypeStruct(shape, HALF) for shape in shapes],
        in_specs=[vmem] * 3 + [hbm, vmem],
        out_specs=[hbm] * (len(shapes) - 1) + [vmem],
        scratch_shapes=[pltpu.SemaphoreType.DMA((64,))] * 2 + [pltpu.SemaphoreType.DMA((3, 2))],
        compiler_params=pltpu.CompilerParams(
            collective_id=9, has_side_effects=True, vmem_limit_bytes=VMEM_LIMIT
        ),
        cost_estimate=pl.CostEstimate(flops=0, transcendentals=0, bytes_accessed=280 << 20),
        name="gather_weights",
    )(*own, leaving, dec_rows)


def gather_planes(rest):
    return lax.all_gather(rest, "dp", axis=0, tiled=True)


def fold_cores(mine, other):
    return (mine.astype(WIDE) + swap(other, "pipe", 1).astype(WIDE)).astype(HALF)


def fold_line(rows, bits):
    for bit in bits:
        keep, send = jnp.split(rows, 2, axis=1)
        rows = (keep.astype(WIDE) + swap(send, "tensor", bit).astype(WIDE)).astype(HALF)
    return rows


def fold_planes(term):
    return lax.psum_scatter(term, "dp", scatter_dimension=0, tiled=True)


def scatter_local(terms):
    core = lax.axis_index("pipe")
    wide = terms[0].shape[1] // 2
    pick = partial(lax.dynamic_slice_in_dim, slice_size=wide, axis=1)
    mine = jnp.concatenate([pick(v.astype(HALF), core * wide) for v in terms], axis=1)
    other = jnp.concatenate([pick(v.astype(HALF), (1 - core) * wide) for v in terms], axis=1)
    term = fold_cores(mine, other)
    return fold_planes(term), term


def _blocks_of(weights, kinds):
    wide = weights.shape[2] // (lax.axis_size("tensor") * kinds)
    each = LANES // wide
    blocks = lax.axis_size("tensor") // each
    spec = pl.BlockSpec(
        (None, weights.shape[1], each * kinds * wide), lambda i: (i // blocks, 0, lax.rem(i, blocks))
    )
    return wide, each, blocks, spec


def _piece(weights, kinds, wide, each, k):
    parts = [weights[:, (j * kinds + k) * wide : (j * kinds + k + 1) * wide] for j in range(each)]
    return parts[0] if each == 1 else jnp.concatenate(parts, axis=1)


def _store_grads(refs, i, blocks, pieces, wide, each):
    columns = [p[:, j * wide : (j + 1) * wide] for j in range(each) for p in pieces]
    for ref, when in zip(refs, (i < blocks, i >= blocks)):

        @pl.when(when)
        def _(ref=ref):
            for n, column in enumerate(columns):
                ref[:, n * wide : (n + 1) * wide] = column.astype(ref.dtype)


def _grad_specs(depth, columns, blocks):
    return [
        pl.BlockSpec((depth, columns), lambda i: (0, jnp.minimum(i, blocks - 1))),
        pl.BlockSpec((depth, columns), lambda i: (0, jnp.maximum(i - blocks, 0))),
    ]


def _spread_kernel(kinds, use, wide, each, blocks, with_grad, pair, x, weights, *refs):
    left = x[...]
    values = [dot(left, _piece(weights, kinds, wide, each, k)) for k in use]
    if with_grad:
        y, *refs = refs
        i = pl.program_id(0)
        _store_grads(refs[-2:], i, blocks, [dot_ta(left, y[...].astype(HALF))], wide, each)
    for n in range(pair):
        ref = refs[len(refs) - pair + n]

        @pl.when(lax.rem(pl.program_id(0), pair) == n)
        def _(ref=ref):
            ref[0] = values[-2].astype(HALF)
            ref[1] = values[-1].astype(HALF)

    values = values[:-2] if pair else values
    for ref, value in zip(refs, values):
        ref[...] = value.astype(HALF)


def spread(x, weights, kinds, use, y=None, pair=0):
    rows, width = x.shape
    wide, each, blocks, spec = _blocks_of(weights, kinds)
    column = pl.BlockSpec((rows, LANES), lambda i: (0, i))
    single = len(use) - (2 if pair else 0)
    shapes, specs = [((rows, width), HALF)] * single, [column] * single
    for _ in range(pair):
        shapes.append(((2, rows, width // pair), HALF))
        specs.append(pl.BlockSpec((2, rows, LANES), lambda i: (0, 0, i // pair)))
    if y is not None:
        shapes += [((width, width // 2), HALF)] * 2
        specs += _grad_specs(width, LANES, blocks)
    return pl.pallas_call(
        partial(_spread_kernel, kinds, use, wide, each, blocks, y is not None, pair),
        out_shape=[jax.ShapeDtypeStruct(*s) for s in shapes],
        grid=(2 * blocks,),
        in_specs=[pl.BlockSpec((rows, width), lambda i: (0, 0)), spec] + [column] * (y is not None),
        out_specs=specs,
        compiler_params=pltpu.CompilerParams(vmem_limit_bytes=VMEM_LIMIT),
        cost_estimate=pl.CostEstimate(
            flops=8 * rows * width * width * (len(use) + (y is not None)),
            transcendentals=0,
            bytes_accessed=2 * width * width * kinds,
        ),
        name="spread",
    )(x, weights, *([] if y is None else [y]))


def _collect_kernel(kinds, use, wide, each, blocks, n_y, split, with_grad, ending, n_extra, *refs):
    refs = list(refs)
    ys, refs = refs[:n_y], refs[n_y:]
    weights, refs = refs[0], refs[1:]
    x = refs.pop(0) if with_grad else None
    extra, refs = refs[:n_extra], refs[n_extra:]
    acc = refs.pop()
    grads = [refs.pop(), refs.pop()][::-1] if with_grad else []
    i = pl.program_id(0)

    @pl.when(i == 0)
    def _():
        acc[...] = jnp.zeros(acc.shape, WIDE)

    values, ys = [], list(ys)
    while ys:
        y = ys.pop(0)
        if len(y.shape) == 2:
            values.append(y[...])
        elif split:
            odd = ys.pop(0)
            values += [jnp.where(lax.rem(i, 2) == 0, y[n], odd[n]) for n in range(2)]
        else:
            values += [y[0], y[1]]
    values = [v.astype(HALF) for v in values]
    for value, k in zip(values, use):
        acc[...] += dot_bt(value, _piece(weights, kinds, wide, each, k))
    if with_grad:
        left = x[...]
        _store_grads(grads, i, blocks, [dot_ta(left, v) for v in values], wide, each)

    @pl.when(i == 2 * blocks - 1)
    def _():
        ending(acc[...], extra, refs)


def collect(ys, weights, kinds, use, ending, extra, outs, x=None):
    rows, width = ys[0].shape[-2], weights.shape[1]
    split = any(y.ndim == 3 and y.shape[2] < width for y in ys)
    wide, each, blocks, spec = _blocks_of(weights, kinds)
    y_specs = [
        pl.BlockSpec((rows, LANES), lambda i: (0, i))
        if y.ndim == 2
        else pl.BlockSpec((2, rows, LANES), lambda i: (0, 0, i // (2 if split else 1)))
        for y in ys
    ]
    fixed = [pl.BlockSpec(v.shape, lambda i: (0, 0)) for v in ([] if x is None else [x]) + extra]
    shapes = list(outs)
    specs = [pl.BlockSpec(shape, lambda i: (0, 0)) for shape, _ in outs]
    if x is not None:
        shapes += [((width, len(use) * width // 2), HALF)] * 2
        specs += _grad_specs(width, len(use) * LANES, blocks)
    return pl.pallas_call(
        partial(
            _collect_kernel, kinds, use, wide, each, blocks, len(ys), split, x is not None, ending, len(extra)
        ),
        out_shape=[jax.ShapeDtypeStruct(*s) for s in shapes],
        grid=(2 * blocks,),
        in_specs=y_specs + [spec] + fixed,
        out_specs=specs,
        scratch_shapes=[pltpu.VMEM((rows, width), WIDE)],
        compiler_params=pltpu.CompilerParams(vmem_limit_bytes=VMEM_LIMIT),
        cost_estimate=pl.CostEstimate(
            flops=8 * rows * width * width * len(use) * (1 + (x is not None)),
            transcendentals=0,
            bytes_accessed=2 * width * width * kinds,
        ),
        name="collect",
    )(*ys, weights, *([] if x is None else [x]), *extra)


def _end_norm(total, ins, outs):
    resid, gain, bias = ins
    value, normed, inv_scale = _norm_rows(total + resid[...], gain[...], bias[...])
    outs[0][...] = value
    outs[1][...] = value.astype(HALF)
    outs[2][...] = normed
    outs[3][...] = jnp.broadcast_to(inv_scale, outs[3].shape)


def _end_norm_back(total, ins, outs):
    *resid, normed, inv_scale, gain = ins
    total = total + resid[0][...] if resid else total
    grad, grad_gain, grad_bias = _norm_rows_back(total, normed[...], inv_scale[:, 0:1], gain[...])
    outs[0][...] = grad
    outs[1][...] = grad.astype(HALF)
    outs[2][0:1, :] = grad_gain
    outs[2][1:2, :] = grad_bias


def _ffn_parts(count, own, mine, other):
    depth, wide = own.shape[1], own.shape[2] // 2
    specs = []
    for k in range(2):
        specs.append(pl.BlockSpec((None, depth, wide), lambda i, k=k: (i // count, 0, k)))
        for first in (0, count):
            specs.append(
                pl.BlockSpec(
                    (depth, wide),
                    lambda i, k=k, first=first: (0, 2 * jnp.clip(i - first - 1, 0, count - 2) + k),
                )
            )
    return wide, specs


def _ffn_cases(count, i, ins, outs):
    local = lax.rem(i, count) == 0
    return [
        (local, ins[0], outs[0]),
        (jnp.logical_and(~local, i < count), ins[1], outs[1]),
        (jnp.logical_and(~local, i > count), ins[2], outs[2]),
    ]


def _ffn_kernel(count, x, resid, gain, bias, *refs):
    ins, outs, refs = refs[:3], refs[3:6], refs[6:]
    value, value_low, normed, inv_scale, active, slope, acc = refs
    i = pl.program_id(0)

    @pl.when(i == 0)
    def _():
        acc[...] = jnp.zeros(acc.shape, WIDE)

    for condition, first, second in _ffn_cases(count, i, ins, outs):

        @pl.when(condition)
        def _(first=first, second=second):
            hidden = dot(x[...], first[...])
            below = 0.5 * (1.0 + lax.erf(hidden * (2.0**-0.5)))
            density = jnp.exp(-0.5 * hidden * hidden) * 0.3989422804014327
            act = (hidden * below).astype(HALF)
            active[...] = act
            slope[...] = (below + hidden * density).astype(HALF)
            acc[...] += dot_bt(act, second[...])

    @pl.when(i == 2 * count - 1)
    def _():
        _end_norm(acc[...], (resid, gain, bias), (value, value_low, normed, inv_scale))


def feed_forward(x, resid, gain, bias, own, mine, other):
    count = lax.axis_size("tensor")
    rows, width = x.shape
    wide, specs = _ffn_parts(count, own, mine, other)
    units = 2 * count * wide
    fixed = [pl.BlockSpec(v.shape, lambda i: (0, 0)) for v in (x, resid, gain, bias)]
    shapes = [((rows, width), WIDE), ((rows, width), HALF), ((rows, width), WIDE), ((rows, LANES), WIDE)]
    column = pl.BlockSpec((rows, wide), lambda i: (0, i))
    return pl.pallas_call(
        partial(_ffn_kernel, count),
        out_shape=[jax.ShapeDtypeStruct(*s) for s in shapes]
        + [jax.ShapeDtypeStruct((rows, units), HALF)] * 2,
        grid=(2 * count,),
        in_specs=fixed + specs,
        out_specs=[pl.BlockSpec(s, lambda i: (0, 0)) for s, _ in shapes] + [column] * 2,
        scratch_shapes=[pltpu.VMEM((rows, width), WIDE)],
        compiler_params=pltpu.CompilerParams(vmem_limit_bytes=VMEM_LIMIT),
        cost_estimate=pl.CostEstimate(
            flops=12 * rows * width * units, transcendentals=2 * rows * units, bytes_accessed=4 * width * units
        ),
        name="feed_forward",
    )(x, resid, gain, bias, own, mine, other, own, mine, other)


def _ffn_back_kernel(count, x, grad, resid, normed, inv_scale, gain, active, slope, *refs):
    ins, outs, refs = refs[:3], refs[3:6], refs[6:]
    result, result_low, terms, *grads, acc = refs
    i = pl.program_id(0)

    @pl.when(i == 0)
    def _():
        acc[...] = jnp.zeros(acc.shape, WIDE)

    for condition, first, second in _ffn_cases(count, i, ins, outs):

        @pl.when(condition)
        def _(first=first, second=second):
            hidden = (dot(grad[...], second[...]) * slope[...].astype(WIDE)).astype(HALF)
            acc[...] += dot_bt(hidden, first[...])
            f1 = dot_ta(x[...], hidden).astype(HALF)
            f2 = dot_ta(grad[...], active[...]).astype(HALF)
            for half, when in enumerate((i < count, i >= count)):

                @pl.when(when)
                def _(half=half):
                    grads[half][...] = f1
                    grads[2 + half][...] = f2

    @pl.when(i == 2 * count - 1)
    def _():
        _end_norm_back(acc[...], (resid, normed, inv_scale, gain), (result, result_low, terms))


def feed_forward_back(x, grad, resid, normed, inv_scale, gain, active, slope, own, mine, other):
    count = lax.axis_size("tensor")
    rows, width = x.shape
    wide, specs = _ffn_parts(count, own, mine, other)
    column = pl.BlockSpec((rows, wide), lambda i: (0, i))
    fixed = [pl.BlockSpec(v.shape, lambda i: (0, 0)) for v in (x, grad, resid, normed, inv_scale, gain)]
    shapes = [((rows, width), WIDE), ((rows, width), HALF), ((8, width), WIDE)]
    grad_specs = [
        pl.BlockSpec((width, wide), lambda i: (0, jnp.minimum(i, count - 1))),
        pl.BlockSpec((width, wide), lambda i: (0, jnp.maximum(i - count, 0))),
    ]
    return pl.pallas_call(
        partial(_ffn_back_kernel, count),
        out_shape=[jax.ShapeDtypeStruct(*s) for s in shapes]
        + [jax.ShapeDtypeStruct((width, count * wide), HALF)] * 4,
        grid=(2 * count,),
        in_specs=fixed + [column] * 2 + specs,
        out_specs=[pl.BlockSpec(s, lambda i: (0, 0)) for s, _ in shapes] + grad_specs * 2,
        scratch_shapes=[pltpu.VMEM((rows, width), WIDE)],
        compiler_params=pltpu.CompilerParams(vmem_limit_bytes=VMEM_LIMIT),
        cost_estimate=pl.CostEstimate(
            flops=32 * rows * width * count * wide, transcendentals=0, bytes_accessed=16 * width * count * wide
        ),
        name="feed_forward_back",
    )(x, grad, resid, normed, inv_scale, gain, active, slope, own, mine, other, own, mine, other)


def _add_rows(dest, first, second):
    rows = 64 if dest.shape[0] % 64 == 0 else dest.shape[0]

    def step(i, carry):
        at = pl.ds(pl.multiple_of(i * rows, rows), rows)
        dest[at, :] = (first[at, :].astype(WIDE) + second[at, :].astype(WIDE)).astype(HALF)
        return carry

    lax.fori_loop(0, dest.shape[0] // rows, step, 0)


def _finish_kernel(bits, count, planes, *refs):
    in_mine, out_mine, in_other, out_other, f1, f2, ckv, dec_ffn, dec_small, tokens, part, resid = refs[:12]
    norm_terms, refs = refs[12:18], refs[18:]
    attn_out, cross_out, ffn_out, far, near, dec_grad, norm_sum = refs[:7]
    land_in, land_out, term, *refs = refs[7:]
    n_steps = planes.bit_length() - 1
    land_planes, refs = refs[:n_steps], refs[n_steps:]
    folded, landed, refs = refs[:3], refs[3:6], refs[6:]
    enc_ffn, enc_small, got_ffn, got_small, land_dec, norm_other, norm_land, send_sem, recv_sem = refs
    core, place, me = lax.axis_index("pipe"), lax.axis_index("dp"), lax.axis_index("tensor")
    sibling = {"pipe": 1 - core}
    line = {s: {"tensor": _differ(me, s, count)} for s in range(1, count)}
    cross_over = {"pipe": 1 - core, "tensor": _differ(me, bits[0], count)}
    dp_bits = [1 << i for i in range(n_steps)]
    others = {bit: {"dp": _differ(place, bit, planes)} for bit in dp_bits}
    _enter([sibling, cross_over, *line.values(), *others.values()])
    made = [0]

    def number():
        made[0] += 1
        return made[0] - 1

    def push(source, dest, peer):
        i = number()
        return _send(source, dest, send_sem.at[i], recv_sem.at[i], peer)

    def wait(copies):
        for copy in copies:
            copy.wait()

    for i in range(3):
        at = slice(2 * i, 2 * i + 2)
        enc, dec = norm_terms[i][0:2, :], norm_terms[3 + i][0:2, :]
        norm_sum[at, :] = jnp.where(core == 0, enc, dec)
        norm_other[at, :] = jnp.where(core == 0, dec, enc)
    norm_sum[6:8, :] = jnp.zeros((2, norm_sum.shape[1]), WIDE)
    norm_other[6:8, :] = jnp.zeros((2, norm_sum.shape[1]), WIDE)
    norm_peers = [*others.values(), *(line[bit] for bit in bits)]
    norm_now = [push(norm_other, norm_land.at[0], sibling)]

    def advance_norms():
        if norm_now:
            norm_now.pop().wait()
            n = n_steps + len(bits) - len(norm_peers)
            norm_sum[...] = norm_sum[...] + norm_land[n]
            if norm_peers:
                norm_now.append(push(norm_sum, norm_land.at[n + 1], norm_peers.pop(0)))

    to_core = [push(in_other, land_in, sibling), push(out_other, land_out, sibling)]

    def chain(source, a, at=slice(None)):
        fold, land = (v if at == slice(None) else v.at[at] for v in (folded[a], landed[a]))
        size = folded[a].shape[1] * 2 // count
        return {
            "source": source,
            "fold": fold,
            "land": land,
            "size": size,
            "slots": count,
            "bits": list(reversed(bits)),
            "now": [],
        }

    def advance(c):
        land, size = c["land"], c["size"]
        if c["now"]:
            wait(c["now"])
            c["now"] = []
            kept = c["slots"] // 2 * size
            offset = (count - c["slots"]) * size
            at = pl.ds(0, kept)
            _add_rows(c["fold"].at[:, at], c["source"].at[:, at], land.at[:, pl.ds(offset, kept)])
            c["source"], c["slots"] = c["fold"], c["slots"] // 2
        if c["bits"]:
            kept = c["slots"] // 2 * size
            offset = (count - c["slots"]) * size
            source = c["source"].at[:, pl.ds(kept, kept)]
            c["now"] = [push(source, land.at[:, pl.ds(offset, kept)], line[c["bits"].pop(0)])]

    chains = [chain(f1, 0), chain(ckv, 1)]
    advance(chains[0])

    half = tokens.shape[1] // 2
    far_sem, near_sem, same_sem = number(), number(), number()

    @pl.when(core == 1)
    def _():
        _send(tokens.at[:, pl.ds(0, half)], far, send_sem.at[far_sem], recv_sem.at[far_sem], cross_over)
        _send(
            tokens.at[:, pl.ds(half, half)], far, send_sem.at[same_sem], recv_sem.at[far_sem], line[bits[0]]
        )

    @pl.when(core == 0)
    def _():
        _send(tokens.at[:, pl.ds(half, half)], near, send_sem.at[near_sem], recv_sem.at[near_sem], sibling)

    rows = dec_grad.shape[0]

    def rows_of_chip(chip):
        return pl.ds(pl.multiple_of(chip * rows, rows), rows)

    dec_sent = [
        push(part.at[rows_of_chip(peer["tensor"])], land_dec.at[s - 1], peer) for s, peer in line.items()
    ]

    wait(to_core)
    block = in_mine.shape[0] // planes
    wide = term.shape[1] // count
    inner = in_mine.shape[1] // count

    def sum_step(i, carry):
        at = pl.ds(pl.multiple_of(i * 64, 64), 64)
        for s in range(count):
            first = in_mine[at, s * inner : (s + 1) * inner].astype(WIDE)
            second = land_in[at, s * inner : (s + 1) * inner].astype(WIDE)
            term[at, s * wide : s * wide + inner] = (first + second).astype(HALF)
            outer = wide - inner
            first = out_mine[at, s * outer : (s + 1) * outer].astype(WIDE)
            second = land_out[at, s * outer : (s + 1) * outer].astype(WIDE)
            term[at, s * wide + inner : (s + 1) * wide] = (first + second).astype(HALF)
        return carry

    lax.fori_loop(0, in_mine.shape[0] // 64, sum_step, 0)

    columns = term.shape[1] // 2
    orders = (dp_bits, dp_bits[::-1])
    held = [[list(range(planes)) for _ in orders] for _ in range(2)]
    piece = block // 2

    def rows_of(difference, r):
        first = _differ(place, difference, planes) * block + r * piece
        return pl.ds(pl.multiple_of(first, piece), piece)

    def at_of(p, m, r):
        return term.at[rows_of(m, r), pl.ds(p * columns, columns)]

    def plane_start(j, r):
        copies = []
        for p, order in enumerate(orders):
            bit = order[j]
            kept = [m for m in held[r][p] if not m & bit]
            for n, m in enumerate(kept):
                dest = land_planes[j].at[p, n, pl.ds(r * piece, piece)]
                copies.append((p, m, dest, push(at_of(p, m ^ bit, r), dest, others[bit])))
            held[r][p] = kept
        return copies

    def plane_finish(copies, r):
        for p, m, dest, copy in copies:
            copy.wait()
            _add_rows(at_of(p, m, r), at_of(p, m, r), dest)

    moving = [plane_start(0, r) for r in range(2)]
    for_attn = []
    for j in range(n_steps):
        for r in range(2):
            advance(chains[min(2 * j + r, 1)])
            advance_norms()
            plane_finish(moving[r], r)
            if j + 1 < n_steps:
                moving[r] = plane_start(j + 1, r)
            else:
                for_attn.append(chain(term.at[rows_of(0, r)], 2, pl.ds(r * piece, piece)))
                advance(for_attn[-1])
    while any(c["now"] or c["bits"] for c in chains + for_attn):
        for c in for_attn + chains:
            advance(c)
        advance_norms()
    while norm_now:
        advance_norms()

    size = [fold.shape[1] * 2 // count for fold in folded]
    enc_ffn[:, : size[0]] = folded[0][:, : size[0]]
    enc_ffn[:, size[0] :] = f2[...]
    enc_small[:, : size[2]] = folded[2][:, : size[2]]
    enc_small[:, size[2] :] = folded[1][:, : size[1]]
    swap_sem = [number(), number()]

    @pl.when(core == 0)
    def _():
        _send(dec_ffn, got_ffn, send_sem.at[swap_sem[0]], recv_sem.at[swap_sem[0]], sibling)
        _send(dec_small, got_small, send_sem.at[swap_sem[1]], recv_sem.at[swap_sem[1]], sibling)

    @pl.when(core == 1)
    def _():
        _send(enc_ffn, got_ffn, send_sem.at[swap_sem[0]], recv_sem.at[swap_sem[0]], sibling)
        _send(enc_small, got_small, send_sem.at[swap_sem[1]], recv_sem.at[swap_sem[1]], sibling)

    wait(dec_sent)
    total = part[rows_of_chip(me), :].astype(WIDE) + resid[...]
    for s in range(count - 1):
        total = total + land_dec[s].astype(WIDE)
    dec_grad[...] = total
    for i, (mine, got) in enumerate(((enc_ffn, got_ffn), (enc_small, got_small))):
        pltpu.make_async_copy(mine, got, send_sem.at[swap_sem[i]]).wait()
        pltpu.make_async_copy(mine, got, recv_sem.at[swap_sem[i]]).wait()

    def write(first, second):
        for h, (ffn, small) in enumerate((first, second)):
            c = ffn.shape[1] // 2
            for k in range(2):
                ffn_out[k, :, h * c : (h + 1) * c] = ffn[:, k * c : (k + 1) * c].astype(WIDE)
            c = small.shape[1] // 6
            for k in range(6):
                dest = attn_out.at[k] if k < 4 else cross_out.at[k - 4]
                dest[:, h * c : (h + 1) * c] = small[:, k * c : (k + 1) * c].astype(WIDE)

    @pl.when(core == 0)
    def _():
        write((enc_ffn, enc_small), (got_ffn, got_small))

    @pl.when(core == 1)
    def _():
        write((got_ffn, got_small), (dec_ffn, dec_small))

    pltpu.make_async_copy(far, far, recv_sem.at[far_sem]).wait()

    @pl.when(core == 1)
    def _():
        pltpu.make_async_copy(far, far, send_sem.at[far_sem]).wait()
        pltpu.make_async_copy(far, far, send_sem.at[same_sem]).wait()
        pltpu.make_async_copy(near, near, recv_sem.at[near_sem]).wait()

    @pl.when(core == 0)
    def _():
        pltpu.make_async_copy(near, near, send_sem.at[near_sem]).wait()


def finish(in_grads, out_grads, f1, f2, ckv, dec_ffn, dec_small, tokens, part, resid, norm_terms):
    count, planes = lax.axis_size("tensor"), lax.axis_size("dp")
    depth = in_grads[0].shape[0]
    rows = depth // planes
    attn_columns = in_grads[0].shape[1] + out_grads[0].shape[1]
    wide = 2 * dec_small.shape[1] // 6
    vmem = pl.BlockSpec(memory_space=pltpu.VMEM)
    operands = (in_grads[0], out_grads[0], in_grads[1], out_grads[1], f1, f2, ckv, dec_ffn, dec_small, tokens, part, resid)
    operands += tuple(norm_terms)
    lines = [f1.shape[1], ckv.shape[1], attn_columns]
    scratch = [in_grads[0].shape, out_grads[0].shape, (depth, attn_columns)]
    blocks = planes // 2
    while blocks >= 1:
        scratch.append((2, blocks, rows, attn_columns // 2))
        blocks //= 2
    scratch += [(rows, c // 2) for c in lines]
    scratch += [(rows, c - c // count) for c in lines]
    scratch += [dec_ffn.shape, dec_small.shape] * 2
    scratch.append((count - 1, *resid.shape))
    norm_steps = count.bit_length() + planes.bit_length() - 1
    norm_shapes = [norm_terms[0].shape, (norm_steps, *norm_terms[0].shape)]
    token_piece = ((tokens.shape[0], tokens.shape[1] // 2), HALF)
    outs = [((4, rows, wide), WIDE), ((2, rows, wide), WIDE), ((2, rows, dec_ffn.shape[1]), WIDE)]
    outs += [token_piece, token_piece, (resid.shape, WIDE), (norm_terms[0].shape, WIDE)]
    return pl.pallas_call(
        partial(_finish_kernel, slot_bits(), count, planes),
        out_shape=[jax.ShapeDtypeStruct(*o) for o in outs],
        in_specs=[vmem] * len(operands),
        out_specs=[vmem] * len(outs),
        scratch_shapes=[pltpu.VMEM(shape, HALF) for shape in scratch]
        + [pltpu.VMEM(shape, WIDE) for shape in norm_shapes]
        + [pltpu.SemaphoreType.DMA((64,))] * 2,
        compiler_params=pltpu.CompilerParams(
            collective_id=5, has_side_effects=True, vmem_limit_bytes=VMEM_LIMIT
        ),
        cost_estimate=pl.CostEstimate(flops=0, transcendentals=0, bytes_accessed=200 << 20),
        name="finish",
    )(*operands)


def per_device(
    enc_input,
    dec_input,
    dec_cotangent,
    enc_lengths,
    dec_lengths,
    attn_weights,
    cross_weights,
    ffn_weights,
    norm_gains,
    norm_biases,
):
    core, place = lax.axis_index("pipe"), lax.axis_index("tensor")
    count = lax.axis_size("tensor")
    top_bit = count // 2
    group = place // top_bit
    block = jnp.where(core == 0, place, place ^ top_bit)
    span, width = enc_input.shape[1:]
    dec_span = dec_input.shape[1]
    local_width = attn_weights.shape[3]
    is_first = core == 0
    chips = range(count)
    sources = [(s // top_bit, s % top_bit) for s in range(2 * top_bit)]
    half = width // 2
    half_local = local_width // 2

    def owner(t):
        return t // top_bit

    norms = jnp.concatenate([norm_gains[0], norm_biases[0]], axis=0)
    norms_other = swap(norms, "pipe", 1)
    enc_norms = jnp.where(is_first, norms, norms_other)
    dec_norms = jnp.where(is_first, norms_other, norms)
    eg, eb, dg, db = enc_norms[:3], enc_norms[3:], dec_norms[:3], dec_norms[3:]

    pick = partial(lax.dynamic_index_in_dim, index=core, axis=0, keepdims=False)
    start_low = pick(dec_input)
    (
        w_attn,
        own_cross,
        own_ffn,
        dec_attn_halves,
        dec_cross_halves,
        dec_ffn_halves,
        cross_rest,
        ffn_rest,
        got,
        start_full,
    ) = gather_weights(
        *[in_column_halves(v[0]) for v in (after(attn_weights, norms_other), cross_weights, ffn_weights)],
        lax.dynamic_index_in_dim(enc_input, 1 - group, 0, False),
        start_low,
    )
    kept = lax.dynamic_index_in_dim(enc_input, group, 0, False)
    tokens = jnp.where(is_first, kept, got).astype(WIDE)
    mine_ffn = gather_planes(ffn_rest)

    def natural(halves, kinds):
        wide = halves.shape[2] // kinds
        return [
            jnp.concatenate([halves[h][:, k * wide : (k + 1) * wide] for h in range(2)], axis=1)
            for k in range(kinds)
        ]

    dec_attn, dec_cross, dec_ffn = [
        natural(v, k) for v, k in ((dec_attn_halves, 4), (dec_cross_halves, 2), (dec_ffn_halves, 2))
    ]
    blocks = width // LANES
    masks = [a * (blocks // 2) + c * (blocks // 2 // top_bit) for a, c in sources]

    def gain_of(i):
        return enc_norms[i : i + 1]

    def bias_of(i):
        return enc_norms[3 + i : 4 + i]

    embed, start_normed, start_scale = norm_forward(tokens, eg[0], eb[0])
    start_scale = jnp.broadcast_to(start_scale, (span, LANES))
    embed_low = embed.astype(HALF)
    parts = 2 if all(m % 2 == 0 for m in masks) else 1
    query, *key_value = spread(embed_low, w_attn, 4, (0, 1, 2), pair=parts)

    def across_chips(value):
        held, bit = [value], 1
        while bit < top_bit:
            held = held + [swap(v, "tensor", bit) for v in held]
            bit *= 2
        return held

    def exchange(held, *earlier):
        if earlier:
            held = after(tuple(held), *earlier)
        return list(held) + [swap(v, "pipe", 1) for v in held]

    key_values = [across_chips(v) for v in key_value]
    mine_cross = gather_planes(after(cross_rest, query))

    enc_lengths, dec_lengths = [after(v, query) for v in (enc_lengths, dec_lengths)]
    enc_row = lax.dynamic_index_in_dim(enc_lengths, group, 0, False)
    dec_row_of_group = lax.dynamic_index_in_dim(dec_lengths, group, 0, False)
    dec_row = lax.dynamic_index_in_dim(dec_lengths, core, 0, False)
    spots = jnp.arange(span, dtype=jnp.int32)
    own_seg = table_of(block * span + spots, enc_row)
    key_seg = jnp.stack(
        [table_of((block ^ (a * top_bit) ^ c) * span + spots, enc_row) for a, c in sources]
    )
    dec_spots = jnp.arange(dec_span * count, dtype=jnp.int32)
    dec_seg = table_of(dec_spots, dec_row)
    enc_segs = tables(own_seg, key_seg)
    dec_segs = tables(dec_seg, dec_seg[None])
    cross_segs = tables(table_of(dec_spots, dec_row_of_group), own_seg[None])

    start_full = after(start_full, key_value)
    start = start_low.astype(WIDE)
    rows_full = dec_span * count
    wide_rows = ((dec_span, width), WIDE)
    kept_rows = [wide_rows, wide_rows, ((dec_span, LANES), WIDE)]
    norm_terms = ((8, width), WIDE)
    dec_in_w = [dec_attn[k] for k in range(3)]
    dec_query = dot(start_full, dec_in_w[0]).astype(HALF)
    dec_kv = jnp.stack([dot(start_full, w).astype(HALF) for w in dec_in_w[1:]])
    dec_heads_wide, dec_lse = attend(dec_query, [dec_kv], dec_segs, [0], True)
    dec_heads = dec_heads_wide.astype(HALF)
    term = dot_bt(dec_heads, dec_attn[3]).astype(HALF)

    attended = ()
    for n in range(parts):
        key_values[n] = exchange(key_values[n], *attended, *((term,) if n else ()))
        attended = attend(
            query, key_values[n], enc_segs, masks, part=n if parts == 2 else None, into=attended
        )
    heads_wide, lse = attended

    def sum_to_owner(term):
        total = after(start, lse)
        for s in range(count):
            rows = lax.dynamic_slice_in_dim(term, (place ^ s) * dec_span, dec_span, 0)
            total = total + (swap(rows, "tensor", s) if s else rows).astype(WIDE)
        return total

    self_norm, self_normed, self_scale = norm_forward(sum_to_owner(term), dg[0:1], db[0:1])
    self_scale = jnp.broadcast_to(self_scale, (dec_span, LANES))
    self_low = self_norm.astype(HALF)
    self_rows = [swap(self_low, "tensor", s) if s else self_low for s in range(count)]

    heads = heads_wide.astype(HALF)
    mine_ffn = after(mine_ffn, heads_wide)
    other_ffn = swap(mine_ffn, "pipe", 1)
    mine_cross = after(mine_cross, other_ffn)
    w_cross = jnp.stack(
        [
            jnp.concatenate([own_cross[0], mine_cross], axis=1),
            jnp.concatenate([own_cross[1], swap(mine_cross, "pipe", 1)], axis=1),
        ]
    )
    kept_tokens = [((span, width), WIDE), ((span, width), HALF), ((span, width), WIDE), ((span, LANES), WIDE)]
    attn_norm, attn_norm_low, attn_normed, attn_scale = collect(
        [heads], w_attn, 4, (3,), _end_norm, [embed, gain_of(1), bias_of(1)], kept_tokens
    )
    _, memory_low, mem_normed, mem_scale, active, slope = feed_forward(
        attn_norm_low, attn_norm, gain_of(2), bias_of(2), own_ffn, mine_ffn, other_ffn
    )
    self_full = after(jnp.zeros((rows_full, width), HALF), mem_scale)
    for s in range(count):
        self_full = lax.dynamic_update_slice_in_dim(self_full, self_rows[s], (place ^ s) * dec_span, 0)
    cross_query = dot(self_full, dec_cross[0]).astype(HALF)

    def in_halves(value):
        return jnp.stack([value[:, :half_local], value[:, half_local:]])

    [cross_q_enc] = to_encoder(in_halves(cross_query), 6)
    cross_q_enc = to_pairs(cross_q_enc)

    [cross_kv] = spread(memory_low, w_cross, 2, (0, 1), pair=1)

    tables_of_keys = enc_lengths.shape[1]
    at_table = (own_seg[:, None] == jnp.arange(tables_of_keys)[None]).astype(HALF)
    sums = dot_ta(at_table, cross_kv[0])
    bit = 1
    while bit < top_bit:
        sums = sums + swap_columns(sums, "tensor", bit, masks[bit])
        bit *= 2
    sums = sums + swap_columns(sums, "pipe", 1, masks[top_bit])
    means = sums / enc_row.astype(WIDE)[:, None]
    centers = sum(
        jnp.where((own_seg == j)[:, None], means[j : j + 1], 0.0) for j in range(tables_of_keys)
    )
    centered = (cross_kv[0].astype(WIDE) - centers).astype(HALF)

    part_out, part_lse = attend(cross_q_enc, [cross_kv], cross_segs, [0], False, HALF)
    cross_heads, cross_out_wide, cross_lse = to_decoder(
        from_pairs(part_out, half_local), stats_from_pairs(part_lse, half_local), 7
    )
    cross_norm, cross_normed, cross_scale, cross_full = rows_call(
        _forward_rows,
        2,
        dot_bt(cross_heads, dec_cross[1]).astype(HALF),
        [self_norm, dg[1:2], db[1:2]],
        kept_rows,
    )
    dec_hidden = dot(cross_full, dec_ffn[0])
    dec_active = gelu(dec_hidden).astype(HALF)
    result, resid, dec_terms2, grad_full = rows_call(
        _turn_rows,
        3,
        dot_bt(dec_active, dec_ffn[1]).astype(HALF),
        [cross_norm, dg[2:3], db[2:3], pick(dec_cotangent)],
        [((dec_span, width), HALF), wide_rows, norm_terms],
    )
    grad_hidden = (dot(grad_full, dec_ffn[1]) * gelu_slope(dec_hidden)).astype(HALF)
    resid, dec_terms1, cross_grad_full = rows_call(
        _backward_rows,
        4,
        dot_bt(grad_hidden, dec_ffn[0]).astype(HALF),
        [resid, cross_normed, cross_scale, dg[1:2]],
        [wide_rows, norm_terms],
    )
    cross_heads_grad = dot(cross_grad_full, dec_cross[1]).astype(HALF)
    heads_grad_enc, stats_enc = to_encoder(
        in_halves(cross_heads_grad), 8, cross_out_wide, cross_lse
    )
    cross_q_term, [cross_kv_grad] = attend_back(
        cross_q_enc,
        [cross_kv],
        to_pairs(heads_grad_enc),
        stats_to_pairs(stats_enc, half_local),
        centered,
        cross_segs,
        [0],
        False,
        False,
    )
    dec_f2_grad = dot_ta(grad_full, dec_active)
    dec_f1_grad = dot_ta(cross_full, grad_hidden)
    dec_ffn_rows, _ = scatter_local([dec_f1_grad, dec_f2_grad])

    def to_chip(value):
        theirs = joint(value, [((1 - owner(t), t), (owner(t), t)) for t in chips])
        theirs = theirs.reshape(2, count, *theirs.shape[1:])
        chip = value.reshape(theirs.shape).astype(WIDE) + theirs[::-1].astype(WIDE)
        return jnp.where(is_first, chip, chip[::-1]).astype(HALF)

    def to_owner(chip):
        terms = []
        for s in range(top_bit):
            near, far = 2 * s, 2 * s + 1
            near_pairs = [((owner(t), t), (owner(t), t ^ s)) for t in chips]
            far_pairs = [((owner(t), t), (owner(t), t ^ s ^ top_bit)) for t in chips]
            near_got = chip[:, near] if s == 0 else joint(chip[:, near], near_pairs)
            far_got = joint(chip[:, far], far_pairs)
            terms.append(jnp.where(core == group, near_got, far_got).astype(WIDE))
        return sum(terms)

    cross_q_chip = to_chip(from_pairs(cross_q_term, half_local))
    cross_q_grad = to_owner(cross_q_chip).astype(HALF)
    cross_q_grad = jnp.concatenate([cross_q_grad[0], cross_q_grad[1]], axis=1)

    back_tokens = [((span, width), WIDE), ((span, width), HALF), ((8, width), WIDE)]
    resid_enc, resid_low, enc_terms2, *cross_grads = collect(
        [cross_kv_grad],
        w_cross,
        2,
        (0, 1),
        _end_norm_back,
        [mem_normed, mem_scale, gain_of(2)],
        back_tokens,
        memory_low,
    )
    ckv_term = fold_cores(*cross_grads)
    enc_ckv = fold_planes(ckv_term)
    resid_enc, resid_low, enc_terms1, *ffn_grads = feed_forward_back(
        attn_norm_low,
        after(resid_low, dec_ffn_rows, cross_q_chip),
        resid_enc,
        attn_normed,
        attn_scale,
        gain_of(1),
        active,
        slope,
        own_ffn,
        mine_ffn,
        other_ffn,
    )
    f2_term = fold_cores(*ffn_grads[2:])
    enc_f2 = fold_planes(f2_term)
    f1_term = fold_cores(*ffn_grads[:2])
    enc_f1 = fold_planes(f1_term)
    heads_grad, *out_grads = spread(after(resid_low, cross_q_grad), w_attn, 4, (3,), heads)
    line_bits = list(reversed(slot_bits()))

    def join(a, b):
        return (a.astype(WIDE) + b.astype(WIDE)).astype(HALF)

    grads_in = after(heads_grad, f1_term, f2_term)
    def send_chips(held):
        pairs, bit = [(v,) for v in held], top_bit // 2
        while bit >= 1:
            held = [join(*v) if len(v) == 2 else v[0] for v in pairs]
            pairs = [(a, swap(b, "tensor", bit)) for a, b in zip(held[:bit], held[bit:])]
            bit //= 2
        return pairs[0]

    def sum_pair(pair, *earlier):
        return join(after(pair[0], *earlier), pair[1]) if len(pair) == 2 else pair[0]

    q_grad, moving, held = (), [], []
    for n in range(parts):
        q_grad, terms = attend_back(
            query,
            key_values[n],
            after(grads_in, *held),
            lse,
            heads_wide,
            enc_segs,
            masks,
            part=n if parts == 2 else None,
            into=q_grad,
        )
        q_grad = (q_grad,)
        if n == 0:
            keep, send = jnp.split(after(enc_f2, terms[0]), 2, axis=1)
            f2_pair = (keep, swap(send, "tensor", line_bits[0]))
        held = [join(a, swap(b, "pipe", 1)) for a, b in zip(terms[:top_bit], terms[top_bit:])]
        moving.append(send_chips(held))
    kv_grad = [sum_pair(pair, terms[0]) for pair in moving[:-1]]
    f2_rows = sum_pair(f2_pair, terms[0])
    f2_half = fold_line(f2_rows, line_bits[1:])
    [q_grad] = q_grad

    cross_q_grad = after(cross_q_grad, *held, enc_f1, f2_rows)
    resid, dec_terms0, self_grad_full = rows_call(
        _backward_rows,
        4,
        dot_bt(cross_q_grad, dec_cross[0]).astype(HALF),
        [resid, self_normed, self_scale, dg[0:1]],
        [wide_rows, norm_terms],
    )
    dec_heads_grad = dot(self_grad_full, dec_attn[3]).astype(HALF)
    dec_q_grad, [dec_kv_grad] = attend_back(
        dec_query, [dec_kv], dec_heads_grad, dec_lse, dec_heads_wide, dec_segs, [0], True
    )
    dec_proj_grad = [dec_q_grad, dec_kv_grad[0], dec_kv_grad[1]]
    dec_part = sum(dot_bt(g, w) for g, w in zip(dec_proj_grad, dec_in_w)).astype(HALF)
    dec_left = [start_full] * 3 + [self_grad_full, self_full, cross_grad_full]
    dec_right = dec_proj_grad + [dec_heads, cross_q_grad, cross_heads]
    dec_small = [dot_ta(a, b) for a, b in zip(dec_left, dec_right)]
    dec_small_rows, dec_small_term = scatter_local(dec_small)
    kv_grad.append(sum_pair(moving[-1], dec_small_term, enc_ckv, f2_half))

    enc_grad, enc_low, enc_terms0, *in_grads = collect(
        [q_grad, *kv_grad],
        w_attn,
        4,
        (0, 1, 2),
        _end_norm_back,
        [resid_enc, start_normed, start_scale, gain_of(0)],
        back_tokens,
        embed_low,
    )
    attn_out, cross_out, ffn_out_grad, there, near_second, dec_grad, norm_sums = finish(
        in_grads,
        out_grads,
        enc_f1,
        f2_half,
        enc_ckv,
        dec_ffn_rows,
        dec_small_rows,
        enc_low,
        dec_part,
        resid,
        [enc_terms0, enc_terms1, enc_terms2, dec_terms0, dec_terms1, dec_terms2],
    )

    attn_out, cross_out, ffn_out_grad = [
        v.transpose(1, 0, 2)[None] for v in (attn_out, cross_out, ffn_out_grad)
    ]
    own_columns = width // (lax.axis_size("dp") * count)
    norm_sums = lax.dynamic_slice_in_dim(
        norm_sums[:6].reshape(3, 2, width), (lax.axis_index("dp") * count + place) * own_columns, own_columns, 2
    )

    dec_pair = jnp.stack([result, dec_grad.astype(HALF)])
    dec_halves = dec_pair.reshape(2, dec_span, 2, half)
    dec_got = swap(lax.dynamic_index_in_dim(dec_halves, 1 - core, 2, False), "pipe", 1)
    own_result = lax.dynamic_slice_in_dim(result, core * half, half, 1)
    own_grad = lax.dynamic_slice_in_dim(dec_grad, core * half, half, 1)
    dec_output = jnp.where(
        is_first, jnp.stack([own_result, dec_got[0]]), jnp.stack([dec_got[0], own_result])
    )
    got_grad = dec_got[1].astype(WIDE)
    dec_input_grad = jnp.where(
        is_first, jnp.stack([own_grad, got_grad]), jnp.stack([got_grad, own_grad])
    )

    here = jnp.where(is_first, enc_grad[:, :half], near_second.astype(WIDE))
    there = there.astype(WIDE)
    enc_input_grad = jnp.where(group == 0, jnp.stack([here, there]), jnp.stack([there, here]))
    return (
        dec_output,
        enc_input_grad,
        dec_input_grad,
        attn_out,
        cross_out,
        ffn_out_grad,
        norm_sums[None, :, 0],
        norm_sums[None, :, 1],
    )


def solution(mesh):
    rows = P("dp", "tensor", None)
    weights = P("pipe", None, None, "tensor")
    half_rows = P("dp", "tensor", "pipe")
    weight_grads = P("pipe", "dp", None, "tensor")
    norm_grads = P("pipe", None, ("dp", "tensor"))
    return jax.shard_map(
        per_device,
        mesh=mesh,
        in_specs=(rows, rows, rows, P("dp", None), P("dp", None))
        + (weights,) * 3
        + (P("pipe", None, None),) * 2,
        out_specs=(half_rows,) * 3 + (weight_grads,) * 3 + (norm_grads,) * 2,
        check_vma=False,
    )
```

```python
from functools import partial

import jax
import jax.numpy as jnp
from jax import lax
from jax.experimental import pallas as pl
from jax.experimental.pallas import tpu as pltpu
from jax.sharding import PartitionSpec as P

HEAD = 64
LANES = 128
EPSILON = 1e-05
NEGATIVE = -1e30
HALF = jnp.bfloat16
WIDE = jnp.float32
VMEM_LIMIT = 56 << 20
MESH = pl.DeviceIdType.MESH
TILE_Q = 256
TILE_K = 512


def dot(left, right):
    return jnp.dot(left, right, preferred_element_type=WIDE)


def dot_bt(left, right):
    return lax.dot_general(left, right, (((1,), (1,)), ((), ())), preferred_element_type=WIDE)


def dot_ta(left, right):
    return lax.dot_general(left, right, (((0,), (0,)), ((), ())), preferred_element_type=WIDE)


def swap(value, axis, mask):
    return lax.ppermute(value, axis, [(i, i ^ mask) for i in range(lax.axis_size(axis))])


def joint(value, pairs):
    count = lax.axis_size("tensor")
    return lax.ppermute(
        value,
        ("pipe", "tensor"),
        [(a[0] * count + a[1], b[0] * count + b[1]) for a, b in pairs],
    )


def after(value, *earlier):
    return lax.optimization_barrier((value, *earlier))[0]


def swap_columns(value, axis, mask, difference):
    got = swap(value, axis, mask).reshape(value.shape[0], -1, LANES)
    order = [b ^ difference for b in range(got.shape[1])]
    return jnp.concatenate([got[:, b] for b in order], axis=1)


def table_of(places, lengths):
    total = jnp.zeros((), jnp.int32)
    table = jnp.zeros(places.shape, jnp.int32)
    for j in range(lengths.shape[0]):
        total = total + lengths[j]
        table = table + (places >= total).astype(jnp.int32)
    return table


def norm_forward(values, gain, bias):
    center = values - jnp.mean(values, axis=-1, keepdims=True)
    inv_scale = lax.rsqrt(jnp.mean(center * center, axis=-1, keepdims=True) + EPSILON)
    normed = center * inv_scale
    return normed * gain + bias, normed, inv_scale


def norm_backward(grad_out, normed, inv_scale, gain):
    grad_gain = jnp.sum(grad_out * normed, axis=0)
    grad_bias = jnp.sum(grad_out, axis=0)
    grad_normed = grad_out * gain
    grad_in = inv_scale * (
        grad_normed
        - jnp.mean(grad_normed, axis=-1, keepdims=True)
        - normed * jnp.mean(grad_normed * normed, axis=-1, keepdims=True)
    )
    return grad_in, grad_gain, grad_bias


def gelu(hidden):
    return 0.5 * hidden * (1.0 + lax.erf(hidden * (2.0**-0.5)))


def gelu_slope(hidden):
    density = jnp.exp(-0.5 * hidden * hidden) * 0.3989422804014327
    return 0.5 * (1.0 + lax.erf(hidden * (2.0**-0.5))) + hidden * density


def _allowed(seg_k, seg_q, causal, col0, row0):
    ok = seg_k == seg_q
    if causal:
        keys = col0 + lax.broadcasted_iota(jnp.int32, ok.shape, 0)
        queries = row0 + lax.broadcasted_iota(jnp.int32, ok.shape, 1)
        ok = ok & (queries >= keys)
    return ok


def _tile_loop(act, chunks, c, nq, nk, tq, tk, body):
    def step(i, carry):
        iq, ik = i // nk, i % nk

        @pl.when(act[iq * (chunks * nk) + c * nk + ik] > 0)
        def _():
            body(iq * tq, ik * tk, pl.ds(pl.multiple_of(iq * tq, tq), tq), pl.ds(pl.multiple_of(ik * tk, tk), tk))

        return carry

    lax.fori_loop(0, nq * nk, step, 0)


def _head_lanes(shape, head):
    lanes = lax.broadcasted_iota(jnp.int32, shape, 1)
    return (lanes < HEAD) if head == 0 else (lanes >= HEAD)


def _attend_kernel(chunks, tq, tk, causal, act, seg_q, seg_k, q, *refs):
    keys, values = refs[:chunks], refs[chunks : 2 * chunks]
    out, lse, top, total, acc = refs[-5:]
    rows = q.shape[0]
    nq, nk = rows // tq, keys[0].shape[0] // tk
    top[...] = jnp.full(top.shape, NEGATIVE, WIDE)
    total[...] = jnp.zeros(total.shape, WIDE)
    acc[...] = jnp.zeros(acc.shape, WIDE)
    for c in range(chunks):

        def tile(row0, col0, r, s, c=c):
            qs = q[r, :] * jnp.asarray(HEAD**-0.5, HALF)
            kk, vt = keys[c][s, :], values[c][s, :].T
            ok = _allowed(seg_k[c, s, 0:1], seg_q[0:1, r], causal, col0, row0)
            ones = jnp.ones((8, vt.shape[1]), HALF)
            heads = range(2)
            raw = [
                dot_bt(kk, jnp.where(_head_lanes(qs.shape, h), qs, jnp.zeros_like(qs))) for h in heads
            ]
            scores = [jnp.where(ok, sc, NEGATIVE) for sc in raw]
            before = [top[h : h + 1, r] for h in heads]
            after_ = [jnp.maximum(b, jnp.max(sc, axis=0, keepdims=True)) for b, sc in zip(before, scores)]
            terms = [jnp.exp(sc - a).astype(HALF) for sc, a in zip(scores, after_)]
            for h in heads:
                fade = jnp.exp(before[h] - after_[h])
                span = slice(h * HEAD, (h + 1) * HEAD)
                sums = dot(jnp.concatenate([vt[span, :], ones], axis=0), terms[h])
                acc[span, r] = acc[span, r] * fade + sums[:HEAD]
                total[h : h + 1, r] = total[h : h + 1, r] * fade + sums[HEAD : HEAD + 1]
                top[h : h + 1, r] = after_[h]

        _tile_loop(act, chunks, c, nq, nk, tq, tk, tile)
    count = total[...]
    count = jnp.where(count > 0.0, count, 1.0)
    lse[0] = top[...] + jnp.log(count)
    whole = jnp.concatenate([acc[:HEAD, :] / count[0:1, :], acc[HEAD:, :] / count[1:2, :]], axis=0)
    out[...] = whole.T.astype(out.dtype)


def _attend_back_kernel(chunks, tq, tk, causal, own_delta, act, seg_q, seg_k, q, *refs):
    keys, values = refs[:chunks], refs[chunks : 2 * chunks]
    grad_out, stats = refs[2 * chunks : 2 * chunks + 2]
    refs = refs[2 * chunks + 2 :]
    extra, (grad_q, *grad_kv, delta, dq, dkv) = refs[0], refs[-(chunks + 4) :]
    rows = q.shape[0]
    nq, nk = rows // tq, keys[0].shape[0] // tk
    if own_delta:
        product = grad_out[...].astype(WIDE) * extra[...].astype(WIDE)
        pick = (
            lax.broadcasted_iota(jnp.int32, (8, LANES), 1) // HEAD
            == lax.broadcasted_iota(jnp.int32, (8, LANES), 0)
        ).astype(WIDE)
        delta[...] = lax.dot_general(
            pick, product, (((1,), (1,)), ((), ())), precision=lax.Precision.HIGHEST, preferred_element_type=WIDE
        )
    else:
        delta[0:2, :] = stats[0, 2:4, :]
    dq[...] = jnp.zeros(dq.shape, WIDE)
    for c in range(chunks):
        dkv[...] = jnp.zeros(dkv.shape, WIDE)

        def tile(row0, col0, r, s, c=c):
            qs = q[r, :] * jnp.asarray(HEAD**-0.5, HALF)
            go = grad_out[r, :]
            kk, vv = keys[c][s, :], values[c][s, :]
            ok = _allowed(seg_k[c, s, 0:1], seg_q[0:1, r], causal, col0, row0)
            heads = range(2)
            mine = [_head_lanes(qs.shape, h) for h in heads]
            mine_k = [_head_lanes(kk.shape, h) for h in heads]
            from_keys = kk if own_delta else extra[s, :]
            qh = [jnp.where(m, qs, jnp.zeros_like(qs)) for m in mine]
            gh = [jnp.where(m, go, jnp.zeros_like(go)) for m in mine]
            kh = [jnp.where(m, from_keys, jnp.zeros_like(kk)) for m in mine_k]
            raw = [dot_bt(kk, v) for v in qh]
            grads = [dot_bt(vv, v) for v in gh]
            pr = [jnp.exp(jnp.where(ok, raw[h], NEGATIVE) - stats[0, h : h + 1, r]) for h in heads]
            ds = [(pr[h] * (grads[h] - delta[h : h + 1, r])).astype(HALF) for h in heads]
            pr = [v.astype(HALF) for v in pr]
            dkv[1, s, :] += dot(pr[0], gh[0]) + dot(pr[1], gh[1])
            dkv[0, s, :] += dot(ds[0], qh[0]) + dot(ds[1], qh[1])
            dq[r, :] += dot_ta(ds[0], kh[0]) + dot_ta(ds[1], kh[1])

        _tile_loop(act, chunks, c, nq, nk, tq, tk, tile)
        grad_kv[c][...] = dkv[...].astype(grad_kv[c].dtype)
    grad_q[...] = (dq[...] * HEAD**-0.5).astype(grad_q.dtype)


def _tile_sizes(rows, keys):
    return min(TILE_Q, rows), min(TILE_K, keys)


def _activity(seg_q, seg_k, tq, tk):
    qt = seg_q.reshape(-1, tq)
    kt = seg_k.reshape(-1, tk)
    hit = (qt[:, :1] <= kt[:, -1][None]) & (kt[:, 0][None] <= qt[:, -1:])
    return hit.astype(jnp.int32).reshape(-1)


def tables(seg_q, seg_k):
    rows, (chunks, span) = seg_q.shape[0], seg_k.shape
    tq, tk = _tile_sizes(rows, span)
    return (
        _activity(seg_q, seg_k, tq, tk),
        jnp.broadcast_to(seg_q[None], (8, rows)),
        jnp.broadcast_to(seg_k[:, :, None], (chunks, span, LANES)),
    )


def _specs(rows, span, chunks, masks, blocked, part):
    def block(h):
        return h if part is None else 2 * h + part

    row_block = pl.BlockSpec((rows, LANES), lambda h, act: (0, block(h)))
    if blocked:
        row_block = pl.BlockSpec((None, rows, LANES), lambda h, act: (block(h), 0, 0))
    stat_block = pl.BlockSpec((1, 8, rows), lambda h, act: (block(h), 0, 0))
    heads = [
        pl.BlockSpec((8, rows), lambda h, act: (0, 0)),
        pl.BlockSpec((chunks, span, LANES), lambda h, act: (0, 0, 0)),
        row_block,
    ]
    for side in range(2):
        heads += [
            pl.BlockSpec((None, span, LANES), lambda h, act, m=m, side=side: (side, 0, h ^ m)) for m in masks
        ]
    return row_block, stat_block, heads


def _dimensions(q, key_values, masks, part):
    blocked = q.ndim == 3
    rows, width = (q.shape[1], q.shape[0] * LANES) if blocked else q.shape
    span, chunks, blocks = key_values[0].shape[1], len(key_values), width // LANES
    if part is not None:
        blocks, masks = blocks // 2, [m // 2 for m in masks]
    row_block, stat_block, specs = _specs(rows, span, chunks, masks, blocked, part)
    return rows, span, chunks, blocks, masks, _tile_sizes(rows, span), row_block, stat_block, specs


def attend(q, key_values, segs, masks, causal=False, out_type=WIDE, part=None, into=()):
    rows, span, chunks, blocks, masks, (tq, tk), row_block, stat_block, specs = _dimensions(
        q, key_values, masks, part
    )
    pairs = rows * span * chunks * blocks * LANES
    kept = 4 + 2 * chunks
    stat_blocks = blocks if part is None else 2 * blocks
    return pl.pallas_call(
        partial(_attend_kernel, chunks, tq, tk, causal),
        out_shape=(
            jax.ShapeDtypeStruct(q.shape, out_type),
            jax.ShapeDtypeStruct((stat_blocks, 8, rows), WIDE),
        ),
        grid_spec=pltpu.PrefetchScalarGridSpec(
            num_scalar_prefetch=1,
            grid=(blocks,),
            in_specs=specs + [pl.BlockSpec(memory_space=pl.ANY)] * len(into),
            out_specs=[row_block, stat_block],
            scratch_shapes=[
                pltpu.VMEM((8, rows), WIDE),
                pltpu.VMEM((8, rows), WIDE),
                pltpu.VMEM((LANES, rows), WIDE),
            ],
        ),
        input_output_aliases={kept + i: i for i in range(len(into))},
        compiler_params=pltpu.CompilerParams(vmem_limit_bytes=VMEM_LIMIT),
        cost_estimate=pl.CostEstimate(
            flops=48 * pairs, transcendentals=pairs // HEAD, bytes_accessed=rows * blocks * LANES * 20
        ),
        name="attend",
    )(*segs, q, *key_values, *key_values, *into)


def attend_back(
    q, key_values, grad_out, stats, extra, segs, masks, causal=False, own_delta=True, part=None, into=()
):
    rows, span, chunks, blocks, masks, (tq, tk), row_block, stat_block, specs = _dimensions(
        q, key_values, masks, part
    )
    kv_out = [pl.BlockSpec((2, span, LANES), lambda h, act, m=m: (0, 0, h ^ m)) for m in masks]
    pairs = rows * span * chunks * blocks * LANES
    extra_block = row_block if own_delta else pl.BlockSpec((span, LANES), lambda h, act: (0, h))
    kept = 7 + 2 * chunks
    outs = pl.pallas_call(
        partial(_attend_back_kernel, chunks, tq, tk, causal, own_delta),
        out_shape=[jax.ShapeDtypeStruct(q.shape, HALF)]
        + [jax.ShapeDtypeStruct((2, span, blocks * LANES), HALF)] * chunks,
        grid_spec=pltpu.PrefetchScalarGridSpec(
            num_scalar_prefetch=1,
            grid=(blocks,),
            in_specs=specs
            + [row_block, stat_block, extra_block]
            + [pl.BlockSpec(memory_space=pl.ANY)] * len(into),
            out_specs=[row_block] + kv_out,
            scratch_shapes=[
                pltpu.VMEM((8, rows), WIDE),
                pltpu.VMEM((rows, LANES), WIDE),
                pltpu.VMEM((2, span, LANES), WIDE),
            ],
        ),
        input_output_aliases={kept + i: i for i in range(len(into))},
        compiler_params=pltpu.CompilerParams(vmem_limit_bytes=VMEM_LIMIT),
        cost_estimate=pl.CostEstimate(
            flops=80 * pairs, transcendentals=pairs // HEAD, bytes_accessed=rows * blocks * LANES * 40
        ),
        name="attend_back",
    )(*segs, q, *key_values, *key_values, grad_out, stats, extra, *into)
    return outs[0], outs[1:]


def _row_mean(values):
    return jnp.mean(values, axis=-1, keepdims=True)


def _norm_rows(values, gain, bias):
    center = values - _row_mean(values)
    inv_scale = lax.rsqrt(_row_mean(center * center) + EPSILON)
    normed = center * inv_scale
    return normed * gain + bias, normed, inv_scale


def _norm_rows_back(grad_out, normed, inv_scale, gain):
    grad_normed = grad_out * gain
    grad_in = inv_scale * (
        grad_normed - _row_mean(grad_normed) - normed * _row_mean(grad_normed * normed)
    )
    return (
        grad_in,
        jnp.sum(grad_out * normed, axis=0, keepdims=True),
        jnp.sum(grad_out, axis=0, keepdims=True),
    )


def _forward_rows(total, ins, outs):
    resid, gain, bias = ins
    value, normed, inv_scale = _norm_rows(total + resid[...], gain[...], bias[...])
    outs[0][...] = value
    outs[1][...] = normed
    outs[2][...] = jnp.broadcast_to(inv_scale, outs[2].shape)
    return value


def _turn_rows(total, ins, outs):
    resid, gain, bias, cotangent = ins
    value, normed, inv_scale = _norm_rows(total + resid[...], gain[...], bias[...])
    outs[0][...] = value.astype(outs[0].dtype)
    grad, grad_gain, grad_bias = _norm_rows_back(
        cotangent[...].astype(WIDE), normed, inv_scale, gain[...]
    )
    outs[1][...] = grad
    outs[2][0:1, :] = grad_gain
    outs[2][1:2, :] = grad_bias
    return grad


def _backward_rows(total, ins, outs):
    resid, normed, inv_scale, gain = ins
    grad, grad_gain, grad_bias = _norm_rows_back(
        total + resid[...], normed[...], inv_scale[:, 0:1], gain[...]
    )
    outs[0][...] = grad
    outs[1][0:1, :] = grad_gain
    outs[1][1:2, :] = grad_bias
    return grad


def _rows_kernel(count, scatter, gather, middle, n_in, n_out, *refs):
    refs = list(refs)
    part = refs.pop(0) if scatter else None
    ins, refs = refs[:n_in], refs[n_in:]
    outs, refs = refs[:n_out], refs[n_out:]
    full = refs.pop(0) if gather else None
    landed = refs.pop(0) if scatter else None
    send_sem, recv_sem = refs[:2]
    me = lax.axis_index("tensor")
    steps = range(1, count)
    peers = [lax.rem(me + s, count) for s in steps]
    barrier = pltpu.get_barrier_semaphore()
    for peer in peers:
        pl.semaphore_signal(barrier, inc=1, device_id={"tensor": peer}, device_id_type=MESH)
    pl.semaphore_wait(barrier, count - 1)
    total = None
    if scatter:
        rows = part.shape[0] // count
        copies = []
        for s, peer in zip(steps, peers):
            copy = pltpu.make_async_remote_copy(
                src_ref=part.at[pl.ds(pl.multiple_of(peer * rows, rows), rows)],
                dst_ref=landed.at[s - 1],
                send_sem=send_sem.at[0, s - 1],
                recv_sem=recv_sem.at[0, s - 1],
                device_id={"tensor": peer},
                device_id_type=MESH,
            )
            copy.start()
            copies.append(copy)
        total = part[pl.ds(pl.multiple_of(me * rows, rows), rows), :].astype(WIDE)
        for s, copy in zip(steps, copies):
            copy.wait_recv()
            total = total + landed[s - 1].astype(WIDE)
        for copy in copies:
            copy.wait_send()
    sent = middle(total, ins, outs)
    if gather:
        rows = full.shape[0] // count
        own = pl.ds(pl.multiple_of(me * rows, rows), rows)
        full[own, :] = sent.astype(full.dtype)
        copies = []
        for s, peer in zip(steps, peers):
            copy = pltpu.make_async_remote_copy(
                src_ref=full.at[own],
                dst_ref=full.at[own],
                send_sem=send_sem.at[1, s - 1],
                recv_sem=recv_sem.at[1, s - 1],
                device_id={"tensor": peer},
                device_id_type=MESH,
            )
            copy.start()
            copies.append(copy)
        for copy in copies:
            copy.wait()


def rows_call(middle, number, part, ins, outs, gather=True):
    count = lax.axis_size("tensor")
    scatter = part is not None
    width = (part if scatter else ins[0]).shape[1]
    rows = part.shape[0] // count if scatter else ins[0].shape[0]
    shapes = [jax.ShapeDtypeStruct(shape, kind) for shape, kind in outs]
    if gather:
        shapes.append(jax.ShapeDtypeStruct((rows * count, width), HALF))
    whole = pl.BlockSpec(memory_space=pltpu.VMEM)
    operands = ([part] if scatter else []) + list(ins)
    got = pl.pallas_call(
        partial(_rows_kernel, count, scatter, gather, middle, len(ins), len(outs)),
        out_shape=shapes,
        in_specs=[whole] * len(operands),
        out_specs=[whole] * len(shapes),
        scratch_shapes=([pltpu.VMEM((count - 1, rows, width), HALF)] if scatter else [])
        + [pltpu.SemaphoreType.DMA((2, count - 1))] * 2,
        compiler_params=pltpu.CompilerParams(
            collective_id=number, has_side_effects=True, vmem_limit_bytes=VMEM_LIMIT
        ),
        cost_estimate=pl.CostEstimate(
            flops=0, transcendentals=0, bytes_accessed=1400 * rows * width
        ),
        name=middle.__name__.strip("_"),
    )(*operands)
    return got


def _differ(a, b, count):
    total, bit = 0, 1
    while bit < count:
        total = total + lax.rem(lax.rem(a // bit, 2) + lax.rem(b // bit, 2), 2) * bit
        bit *= 2
    return total


def _slot(difference, count):
    top = count // 2
    return 2 * lax.rem(difference, top) + difference // top


def _enter(peers):
    barrier = pltpu.get_barrier_semaphore()
    for peer in peers:
        pl.semaphore_signal(barrier, inc=1, device_id=peer, device_id_type=MESH)
    pl.semaphore_wait(barrier, len(peers))


def _send(source, dest, send_sem, recv_sem, peer):
    copy = pltpu.make_async_remote_copy(
        src_ref=source,
        dst_ref=dest,
        send_sem=send_sem,
        recv_sem=recv_sem,
        device_id=peer,
        device_id_type=MESH,
    )
    copy.start()
    return copy


def _to_encoder_kernel(count, with_stats, *refs):
    if with_stats:
        value, out, lse, full, stats, own, own_stats, held, other, other_stats, send_sem, recv_sem = refs
    else:
        value, full, own, other, send_sem, recv_sem = refs
    core, me = lax.axis_index("pipe"), lax.axis_index("tensor")
    group = me // (count // 2)
    chips = [lax.rem(me + s, count) for s in range(1, count)]
    _enter([{"tensor": chip} for chip in chips] + [{"pipe": 1 - core}])
    sets = [(value, own, other, full)]
    if with_stats:
        for h in range(2):
            product = value[h].astype(WIDE) * out[h]
            pick = (
                lax.broadcasted_iota(jnp.int32, (8, product.shape[1]), 1) // HEAD
                == lax.broadcasted_iota(jnp.int32, (8, product.shape[1]), 0) - 2
            ).astype(WIDE)
            held[h] = lax.dot_general(
                pick,
                product,
                (((1,), (1,)), ((), ())),
                precision=lax.Precision.HIGHEST,
                preferred_element_type=WIDE,
            )
            held[h, 0:2, :] = lse[h, 0:2, :]
        sets.append((held, own_stats, other_stats, stats))
    copies = []
    for s, chip in enumerate(chips):
        place = _slot(_differ(chip, me, count), count)
        for h in range(2):
            at = lax.rem(h + core, 2) * count + place
            for i, (source, dest, _, _) in enumerate(sets):
                sems = (send_sem.at[i, s, h], recv_sem.at[i, s, h])
                copies.append(_send(source.at[h], dest.at[at], *sems, {"tensor": chip}))
    for h in range(2):
        for source, dest, _, _ in sets:
            dest[lax.rem(h + core, 2) * count] = source[h]
    for copy in copies:
        copy.wait()
    copies = []
    for g in range(2):
        for i, (_, source, dest, _) in enumerate(sets):
            here, there = pl.ds(g * count, count), pl.ds((1 - g) * count, count)
            sems = (send_sem.at[i, count - 1, g], recv_sem.at[i, count - 1, g])
            copies.append(_send(source.at[here], dest.at[there], *sems, {"pipe": 1 - core}))
    for copy in copies:
        copy.wait()
    for _, mine, theirs, dest in sets:

        @pl.when(core == group)
        def _(mine=mine, dest=dest):
            dest[...] = mine[...]

        @pl.when(core != group)
        def _(theirs=theirs, dest=dest):
            dest[...] = theirs[...]


def to_encoder(value, number, out=None, lse=None):
    count = lax.axis_size("tensor")
    _, rows, wide = value.shape
    shapes = [((2 * count, rows, wide), HALF)]
    if out is not None:
        shapes.append(((2 * count, 8, rows), WIDE))
    scratch = [pltpu.VMEM(*s) for s in shapes]
    if out is not None:
        scratch.append(pltpu.VMEM((2, 8, rows), WIDE))
    scratch += [pltpu.VMEM(*s) for s in shapes]
    whole = pl.BlockSpec(memory_space=pltpu.VMEM)
    operands = (value,) if out is None else (value, out, lse)
    return pl.pallas_call(
        partial(_to_encoder_kernel, count, out is not None),
        out_shape=[jax.ShapeDtypeStruct(*s) for s in shapes],
        in_specs=[whole] * len(operands),
        out_specs=[whole] * len(shapes),
        scratch_shapes=scratch + [pltpu.SemaphoreType.DMA((len(shapes), count, 2))] * 2,
        compiler_params=pltpu.CompilerParams(
            collective_id=number, has_side_effects=True, vmem_limit_bytes=VMEM_LIMIT
        ),
        cost_estimate=pl.CostEstimate(flops=0, transcendentals=0, bytes_accessed=60 << 20),
        name="to_encoder",
    )(*operands)


def _over_lanes(weights, wide):
    lanes = lax.broadcasted_iota(jnp.int32, (8, wide), 1) // HEAD
    pick = (lanes == lax.broadcasted_iota(jnp.int32, (8, wide), 0)).astype(HALF)
    high = weights.astype(HALF)
    low = (weights - high.astype(WIDE)).astype(HALF)
    return dot_ta(jnp.concatenate([high, low], axis=0), jnp.concatenate([pick, pick], axis=0))


def _to_decoder_kernel(count, *refs):
    part, lse, heads, out, out_lse = refs[:5]
    other, other_lse, both, both_lse, landed, landed_lse, send_sem, recv_sem = refs[5:]
    core, me = lax.axis_index("pipe"), lax.axis_index("tensor")
    top = count // 2
    chips = [lax.rem(me + s, count) for s in range(1, count)]
    _enter([{"tensor": chip} for chip in chips] + [{"pipe": 1 - core}])
    copies = []
    for g in range(2):
        here, there = pl.ds(g * count, count), pl.ds((1 - g) * count, count)
        for i, (source, dest) in enumerate(((part, other), (lse, other_lse))):
            sems = (send_sem.at[i, count - 1, g], recv_sem.at[i, count - 1, g])
            copies.append(_send(source.at[here], dest.at[there], *sems, {"pipe": 1 - core}))
    for copy in copies:
        copy.wait()
    wide = part.shape[2]
    for i in range(2 * count):
        first, second = lse[i], other_lse[i]
        peak = jnp.maximum(first, second)
        a, b = jnp.exp(first - peak), jnp.exp(second - peak)
        both_lse[i] = peak + jnp.log(a + b)
        share = _over_lanes(b / (a + b), wide)
        mine = part[i].astype(WIDE)
        both[i] = (mine + share * (other[i].astype(WIDE) - mine)).astype(HALF)
    copies = []
    for s, chip in enumerate(chips):
        place = _slot(_differ(chip, me, count), count)
        for h in range(2):
            at = lax.rem(h + core, 2) * count + place
            for i, (source, dest) in enumerate(((both, landed), (both_lse, landed_lse))):
                sems = (send_sem.at[i, s, h], recv_sem.at[i, s, h])
                copies.append(_send(source.at[at], dest.at[s, h], *sems, {"tensor": chip}))
    for copy in copies:
        copy.wait()
    for h in range(2):
        at = lax.rem(h + core, 2) * count
        terms = [(me, both[at], both_lse[at])]
        for s in range(count - 1):
            terms.append((lax.rem(me - s - 1 + count, count), landed[s, h], landed_lse[s, h]))
        logs = [jnp.where(chip // top == core, log, NEGATIVE) for chip, _, log in terms]
        peak = logs[0]
        for log in logs[1:]:
            peak = jnp.maximum(peak, log)
        weights = [jnp.exp(log - peak) for log in logs]
        weights = [
            jnp.where(chip // top == core, w, 0.0) for (chip, _, _), w in zip(terms, weights)
        ]
        total = sum(weights)
        out_lse[h] = peak + jnp.log(total)
        shares = [_over_lanes(w / total, wide) for w in weights]
        value = sum(c * term.astype(WIDE) for c, (_, term, _) in zip(shares, terms)) / sum(shares)
        out[h] = value
        heads[:, h * wide : (h + 1) * wide] = value.astype(HALF)


def to_decoder(part, lse, number):
    count = lax.axis_size("tensor")
    slots, rows, wide = part.shape
    whole = pl.BlockSpec(memory_space=pltpu.VMEM)
    return pl.pallas_call(
        partial(_to_decoder_kernel, count),
        out_shape=[
            jax.ShapeDtypeStruct((rows, 2 * wide), HALF),
            jax.ShapeDtypeStruct((2, rows, wide), WIDE),
            jax.ShapeDtypeStruct((2, 8, rows), WIDE),
        ],
        in_specs=[whole] * 2,
        out_specs=[whole] * 3,
        scratch_shapes=[
            pltpu.VMEM((slots, rows, wide), HALF),
            pltpu.VMEM((slots, 8, rows), WIDE),
            pltpu.VMEM((slots, rows, wide), HALF),
            pltpu.VMEM((slots, 8, rows), WIDE),
            pltpu.VMEM((count - 1, 2, rows, wide), HALF),
            pltpu.VMEM((count - 1, 2, 8, rows), WIDE),
        ]
        + [pltpu.SemaphoreType.DMA((2, count, 2))] * 2,
        compiler_params=pltpu.CompilerParams(
            collective_id=number, has_side_effects=True, vmem_limit_bytes=VMEM_LIMIT
        ),
        cost_estimate=pl.CostEstimate(flops=0, transcendentals=0, bytes_accessed=60 << 20),
        name="to_decoder",
    )(part, lse)


def to_pairs(value):
    slots, rows, wide = value.shape
    each = LANES // wide
    if each == 1:
        return value
    value = value.reshape(slots // each, each, rows, wide)
    return value.transpose(0, 2, 1, 3).reshape(slots // each, rows, LANES)


def from_pairs(value, wide):
    blocks, rows, _ = value.shape
    each = LANES // wide
    if each == 1:
        return value
    value = value.reshape(blocks, rows, each, wide)
    return value.transpose(0, 2, 1, 3).reshape(blocks * each, rows, wide)


def stats_to_pairs(stats, wide):
    each = LANES // wide
    if each == 1:
        return stats
    slots, _, rows = stats.shape
    stats = stats.reshape(slots // each, each, 8, rows)
    return jnp.concatenate(
        [stats[:, :, 0], stats[:, :, 2], jnp.zeros((slots // each, 4, rows), WIDE)], axis=1
    )


def stats_from_pairs(stats, wide):
    each = LANES // wide
    if each == 1:
        return stats
    blocks, _, rows = stats.shape
    value = stats[:, :each].reshape(blocks * each, 1, rows)
    return jnp.concatenate([value, jnp.zeros((blocks * each, 7, rows), WIDE)], axis=1)


def slot_bits():
    count = lax.axis_size("tensor")
    bits, bit = [count // 2], 1
    while bit < count // 2:
        bits.append(bit)
        bit *= 2
    return [b for b in bits if b > 0]


def in_column_halves(values):
    wide = values.shape[2] // 2
    return jnp.stack(
        [
            jnp.concatenate(
                [values[:, k, h * wide : (h + 1) * wide] for k in range(values.shape[1])], axis=1
            ).astype(HALF)
            for h in range(2)
        ]
    )


def _gather_kernel(bits, count, planes, *refs):
    own, refs = refs[:3], refs[3:]
    leaving, dec_rows, *refs = refs
    full, enc_cross, enc_ffn, *refs = refs
    dec, refs = refs[:3], refs[3:]
    rests, refs = refs[:2], refs[2:]
    coming, dec_full, send_sem, recv_sem, local_sem = refs
    core, place, me = lax.axis_index("pipe"), lax.axis_index("dp"), lax.axis_index("tensor")
    wide = own[0].shape[2]
    block = own[0].shape[1] // planes
    sibling = {"pipe": 1 - core}
    chips = {bit: {"tensor": _differ(me, bit, count)} for bit in bits}
    line = [{"tensor": _differ(me, s, count)} for s in range(1, count)]
    dp_bits = [1 << i for i in range(planes.bit_length() - 1)]
    others = {bit: {"dp": _differ(place, bit, planes)} for bit in dp_bits}
    _enter([sibling, *line, *others.values()])
    made = [0]

    def push(source, dest, peer):
        i = made[0]
        made[0] += 1
        return _send(source, dest, send_sem.at[i], recv_sem.at[i], peer)

    def rows_of(difference):
        return pl.ds(pl.multiple_of(_differ(place, difference, planes) * block, block), block)

    enc = [full.at[:, :, pl.ds(0, wide)], enc_cross, enc_ffn]
    shown = []
    for a in range(3):
        i = made[0]
        made[0] += 2
        shown.append(i)

        @pl.when(core == 0)
        def _(a=a, i=i):
            for h in range(2):
                _send(own[a].at[h], enc[a].at[1 - h], send_sem.at[i + h], recv_sem.at[i + h], sibling)
                pltpu.make_async_copy(own[a].at[h], enc[a].at[h], local_sem.at[a, h]).start()

        @pl.when(core == 1)
        def _(a=a, i=i):
            for h in range(2):
                _send(own[a].at[h], dec[a].at[h], send_sem.at[i + h], recv_sem.at[i + h], sibling)
                pltpu.make_async_copy(own[a].at[h], dec[a].at[h], local_sem.at[a, h]).start()

    def arrived(a):
        i = shown[a]
        for h in range(2):
            pltpu.make_async_copy(own[a].at[h], enc[a].at[h], local_sem.at[a, h]).wait()
            pltpu.make_async_copy(own[a].at[h], enc[a].at[h], recv_sem.at[i + h]).wait()

    def line_step(a, n, bit):
        here, size = rows_of(0), own[a].shape[2]
        if a == 0:
            source = full.at[0, here, pl.ds(0, n * size)]
            return [push(source, full.at[0, here, pl.ds(n * size, n * size)], chips[bit])]
        rest = rests[a - 1]
        copies = [
            push(enc[a].at[0, here], rest.at[:, pl.ds((n - 1) * size, size)], chips[bit])
        ]
        if n > 1:
            source = rest.at[:, pl.ds(0, (n - 1) * size)]
            copies.append(push(source, rest.at[:, pl.ds(n * size, (n - 1) * size)], chips[bit]))
        return copies

    def wait(copies):
        for copy in copies:
            copy.wait()

    def advance(chain):
        wait(chain["now"])
        chain["now"] = line_step(chain["array"], *chain["todo"].pop(0)) if chain["todo"] else []

    def columns(part):
        return pl.ds(wide + part * half, half)

    def plane_step(j):
        copies = []
        for part, order in enumerate(orders):
            for m in held[part]:
                at = full.at[0, rows_of(m), columns(part)]
                copies.append((part, m ^ order[j], push(at, at, others[order[j]])))
        return copies

    def share(part, m):
        here = rows_of(m)
        source = full.at[0, here, columns(part)]
        return push(source, full.at[1, here, columns(part)], sibling)

    steps = [(1 << i, bit) for i, bit in enumerate(bits)]
    for_attn, for_cross, for_ffn = [{"array": a, "todo": list(steps), "now": []} for a in range(3)]
    arrived(0)
    advance(for_attn)
    arrived(2)
    advance(for_attn)
    advance(for_ffn)
    while for_attn["now"]:
        advance(for_attn)
    token_sem = made[0]
    made[0] += 1

    @pl.when(core == 1)
    def _():
        _send(leaving, coming, send_sem.at[token_sem], recv_sem.at[token_sem], chips[bits[0]])

    at = pl.ds(pl.multiple_of(me * dec_rows.shape[0], dec_rows.shape[0]), dec_rows.shape[0])
    dec_full[at, :] = dec_rows[...]
    dec_sent = [push(dec_full.at[at], dec_full.at[at], peer) for peer in line]
    half = (count - 1) * wide // 2
    orders, held = (dp_bits, dp_bits[::-1]), ([0], [0])
    moving = plane_step(0)
    shared = [share(part, 0) for part in range(2)]
    advance(for_ffn)
    arrived(1)
    for j in range(len(dp_bits)):
        for _, _, copy in moving:
            copy.wait()
        for part, order in enumerate(orders):
            held[part].extend([m ^ order[j] for m in held[part]])
        following = plane_step(j + 1) if j + 1 < len(dp_bits) else []
        shared += [share(part, m) for part, m, _ in moving]
        moving = following
        advance(for_cross)
    while for_ffn["now"]:
        advance(for_ffn)
    while for_cross["now"]:
        advance(for_cross)

    @pl.when(core == 1)
    def _():
        pltpu.make_async_copy(leaving, leaving, send_sem.at[token_sem]).wait()
        pltpu.make_async_copy(leaving, coming, recv_sem.at[token_sem]).wait()

    wait(dec_sent)
    wait(shared)
    for a in range(3):
        for h in range(2):
            pltpu.make_async_copy(own[a].at[h], own[a].at[h], send_sem.at[shown[a] + h]).wait()


def gather_weights(attn, cross, ffn, leaving, dec_rows):
    own = (attn, cross, ffn)
    count, planes = lax.axis_size("tensor"), lax.axis_size("dp")
    depth = attn.shape[1]
    shapes = [(2, depth, count * attn.shape[2]), cross.shape, ffn.shape]
    shapes += [v.shape for v in own]
    shapes += [(depth // planes, (count - 1) * v.shape[2]) for v in (cross, ffn)]
    shapes += [leaving.shape, (count * dec_rows.shape[0], dec_rows.shape[1])]
    hbm, vmem = pl.BlockSpec(memory_space=pl.ANY), pl.BlockSpec(memory_space=pltpu.VMEM)
    return pl.pallas_call(
        partial(_gather_kernel, slot_bits(), count, planes),
        out_shape=[jax.ShapeDtypeStruct(shape, HALF) for shape in shapes],
        in_specs=[vmem] * 3 + [hbm, vmem],
        out_specs=[hbm] * (len(shapes) - 1) + [vmem],
        scratch_shapes=[pltpu.SemaphoreType.DMA((64,))] * 2 + [pltpu.SemaphoreType.DMA((3, 2))],
        compiler_params=pltpu.CompilerParams(
            collective_id=9, has_side_effects=True, vmem_limit_bytes=VMEM_LIMIT
        ),
        cost_estimate=pl.CostEstimate(flops=0, transcendentals=0, bytes_accessed=280 << 20),
        name="gather_weights",
    )(*own, leaving, dec_rows)


def gather_planes(rest):
    return lax.all_gather(rest, "dp", axis=0, tiled=True)


def fold_cores(mine, other):
    return (mine.astype(WIDE) + swap(other, "pipe", 1).astype(WIDE)).astype(HALF)


def fold_planes(term):
    return lax.psum_scatter(term, "dp", scatter_dimension=0, tiled=True)


def scatter_local(terms):
    core = lax.axis_index("pipe")
    wide = terms[0].shape[1] // 2
    pick = partial(lax.dynamic_slice_in_dim, slice_size=wide, axis=1)
    mine = jnp.concatenate([pick(v.astype(HALF), core * wide) for v in terms], axis=1)
    other = jnp.concatenate([pick(v.astype(HALF), (1 - core) * wide) for v in terms], axis=1)
    term = fold_cores(mine, other)
    return fold_planes(term), term


def _blocks_of(weights, kinds):
    wide = weights.shape[2] // (lax.axis_size("tensor") * kinds)
    each = LANES // wide
    blocks = lax.axis_size("tensor") // each
    spec = pl.BlockSpec(
        (None, weights.shape[1], each * kinds * wide), lambda i: (i // blocks, 0, lax.rem(i, blocks))
    )
    return wide, each, blocks, spec


def _piece(weights, kinds, wide, each, k):
    parts = [weights[:, (j * kinds + k) * wide : (j * kinds + k + 1) * wide] for j in range(each)]
    return parts[0] if each == 1 else jnp.concatenate(parts, axis=1)


def _store_grads(refs, i, blocks, pieces, wide, each):
    columns = [p[:, j * wide : (j + 1) * wide] for j in range(each) for p in pieces]
    for ref, when in zip(refs, (i < blocks, i >= blocks)):

        @pl.when(when)
        def _(ref=ref):
            for n, column in enumerate(columns):
                ref[:, n * wide : (n + 1) * wide] = column.astype(ref.dtype)


def _grad_specs(depth, columns, blocks):
    return [
        pl.BlockSpec((depth, columns), lambda i: (0, jnp.minimum(i, blocks - 1))),
        pl.BlockSpec((depth, columns), lambda i: (0, jnp.maximum(i - blocks, 0))),
    ]


def _spread_kernel(kinds, use, wide, each, blocks, with_grad, pair, x, weights, *refs):
    left = x[...]
    values = [dot(left, _piece(weights, kinds, wide, each, k)) for k in use]
    if with_grad:
        y, *refs = refs
        i = pl.program_id(0)
        _store_grads(refs[-2:], i, blocks, [dot_ta(left, y[...].astype(HALF))], wide, each)
    for n in range(pair):
        ref = refs[len(refs) - pair + n]

        @pl.when(lax.rem(pl.program_id(0), pair) == n)
        def _(ref=ref):
            ref[0] = values[-2].astype(HALF)
            ref[1] = values[-1].astype(HALF)

    values = values[:-2] if pair else values
    for ref, value in zip(refs, values):
        ref[...] = value.astype(HALF)


def spread(x, weights, kinds, use, y=None, pair=0):
    rows, width = x.shape
    wide, each, blocks, spec = _blocks_of(weights, kinds)
    column = pl.BlockSpec((rows, LANES), lambda i: (0, i))
    single = len(use) - (2 if pair else 0)
    shapes, specs = [((rows, width), HALF)] * single, [column] * single
    for _ in range(pair):
        shapes.append(((2, rows, width // pair), HALF))
        specs.append(pl.BlockSpec((2, rows, LANES), lambda i: (0, 0, i // pair)))
    if y is not None:
        shapes += [((width, width // 2), HALF)] * 2
        specs += _grad_specs(width, LANES, blocks)
    return pl.pallas_call(
        partial(_spread_kernel, kinds, use, wide, each, blocks, y is not None, pair),
        out_shape=[jax.ShapeDtypeStruct(*s) for s in shapes],
        grid=(2 * blocks,),
        in_specs=[pl.BlockSpec((rows, width), lambda i: (0, 0)), spec] + [column] * (y is not None),
        out_specs=specs,
        compiler_params=pltpu.CompilerParams(vmem_limit_bytes=VMEM_LIMIT),
        cost_estimate=pl.CostEstimate(
            flops=8 * rows * width * width * (len(use) + (y is not None)),
            transcendentals=0,
            bytes_accessed=2 * width * width * kinds,
        ),
        name="spread",
    )(x, weights, *([] if y is None else [y]))


def _collect_kernel(kinds, use, wide, each, blocks, n_y, split, with_grad, ending, n_extra, *refs):
    refs = list(refs)
    ys, refs = refs[:n_y], refs[n_y:]
    weights, refs = refs[0], refs[1:]
    x = refs.pop(0) if with_grad else None
    extra, refs = refs[:n_extra], refs[n_extra:]
    acc = refs.pop()
    grads = [refs.pop(), refs.pop()][::-1] if with_grad else []
    i = pl.program_id(0)

    @pl.when(i == 0)
    def _():
        acc[...] = jnp.zeros(acc.shape, WIDE)

    values, ys = [], list(ys)
    while ys:
        y = ys.pop(0)
        if len(y.shape) == 2:
            values.append(y[...])
        elif split:
            odd = ys.pop(0)
            values += [jnp.where(lax.rem(i, 2) == 0, y[n], odd[n]) for n in range(2)]
        else:
            values += [y[0], y[1]]
    values = [v.astype(HALF) for v in values]
    for value, k in zip(values, use):
        acc[...] += dot_bt(value, _piece(weights, kinds, wide, each, k))
    if with_grad:
        left = x[...]
        _store_grads(grads, i, blocks, [dot_ta(left, v) for v in values], wide, each)

    @pl.when(i == 2 * blocks - 1)
    def _():
        ending(acc[...], extra, refs)


def collect(ys, weights, kinds, use, ending, extra, outs, x=None):
    rows, width = ys[0].shape[-2], weights.shape[1]
    split = any(y.ndim == 3 and y.shape[2] < width for y in ys)
    wide, each, blocks, spec = _blocks_of(weights, kinds)
    y_specs = [
        pl.BlockSpec((rows, LANES), lambda i: (0, i))
        if y.ndim == 2
        else pl.BlockSpec((2, rows, LANES), lambda i: (0, 0, i // (2 if split else 1)))
        for y in ys
    ]
    fixed = [pl.BlockSpec(v.shape, lambda i: (0, 0)) for v in ([] if x is None else [x]) + extra]
    shapes = list(outs)
    specs = [pl.BlockSpec(shape, lambda i: (0, 0)) for shape, _ in outs]
    if x is not None:
        shapes += [((width, len(use) * width // 2), HALF)] * 2
        specs += _grad_specs(width, len(use) * LANES, blocks)
    return pl.pallas_call(
        partial(
            _collect_kernel, kinds, use, wide, each, blocks, len(ys), split, x is not None, ending, len(extra)
        ),
        out_shape=[jax.ShapeDtypeStruct(*s) for s in shapes],
        grid=(2 * blocks,),
        in_specs=y_specs + [spec] + fixed,
        out_specs=specs,
        scratch_shapes=[pltpu.VMEM((rows, width), WIDE)],
        compiler_params=pltpu.CompilerParams(vmem_limit_bytes=VMEM_LIMIT),
        cost_estimate=pl.CostEstimate(
            flops=8 * rows * width * width * len(use) * (1 + (x is not None)),
            transcendentals=0,
            bytes_accessed=2 * width * width * kinds,
        ),
        name="collect",
    )(*ys, weights, *([] if x is None else [x]), *extra)


def _end_norm(total, ins, outs):
    resid, gain, bias = ins
    value, normed, inv_scale = _norm_rows(total + resid[...], gain[...], bias[...])
    outs[0][...] = value
    outs[1][...] = value.astype(HALF)
    outs[2][...] = normed
    outs[3][...] = jnp.broadcast_to(inv_scale, outs[3].shape)


def _end_norm_back(total, ins, outs):
    *resid, normed, inv_scale, gain = ins
    total = total + resid[0][...] if resid else total
    grad, grad_gain, grad_bias = _norm_rows_back(total, normed[...], inv_scale[:, 0:1], gain[...])
    outs[0][...] = grad
    outs[1][...] = grad.astype(HALF)
    outs[2][0:1, :] = grad_gain
    outs[2][1:2, :] = grad_bias


def _ffn_parts(count, own, mine, other):
    depth, wide = own.shape[1], own.shape[2] // 2
    specs = []
    for k in range(2):
        specs.append(pl.BlockSpec((None, depth, wide), lambda i, k=k: (i // count, 0, k)))
        for first in (0, count):
            specs.append(
                pl.BlockSpec(
                    (depth, wide),
                    lambda i, k=k, first=first: (0, 2 * jnp.clip(i - first - 1, 0, count - 2) + k),
                )
            )
    return wide, specs


def _ffn_cases(count, i, ins, outs):
    local = lax.rem(i, count) == 0
    return [
        (local, ins[0], outs[0]),
        (jnp.logical_and(~local, i < count), ins[1], outs[1]),
        (jnp.logical_and(~local, i > count), ins[2], outs[2]),
    ]


def _ffn_kernel(count, x, resid, gain, bias, *refs):
    ins, outs, refs = refs[:3], refs[3:6], refs[6:]
    value, value_low, normed, inv_scale, active, slope, acc = refs
    i = pl.program_id(0)

    @pl.when(i == 0)
    def _():
        acc[...] = jnp.zeros(acc.shape, WIDE)

    for condition, first, second in _ffn_cases(count, i, ins, outs):

        @pl.when(condition)
        def _(first=first, second=second):
            hidden = dot(x[...], first[...])
            below = 0.5 * (1.0 + lax.erf(hidden * (2.0**-0.5)))
            density = jnp.exp(-0.5 * hidden * hidden) * 0.3989422804014327
            act = (hidden * below).astype(HALF)
            active[...] = act
            slope[...] = (below + hidden * density).astype(HALF)
            acc[...] += dot_bt(act, second[...])

    @pl.when(i == 2 * count - 1)
    def _():
        _end_norm(acc[...], (resid, gain, bias), (value, value_low, normed, inv_scale))


def feed_forward(x, resid, gain, bias, own, mine, other):
    count = lax.axis_size("tensor")
    rows, width = x.shape
    wide, specs = _ffn_parts(count, own, mine, other)
    units = 2 * count * wide
    fixed = [pl.BlockSpec(v.shape, lambda i: (0, 0)) for v in (x, resid, gain, bias)]
    shapes = [((rows, width), WIDE), ((rows, width), HALF), ((rows, width), WIDE), ((rows, LANES), WIDE)]
    column = pl.BlockSpec((rows, wide), lambda i: (0, i))
    return pl.pallas_call(
        partial(_ffn_kernel, count),
        out_shape=[jax.ShapeDtypeStruct(*s) for s in shapes]
        + [jax.ShapeDtypeStruct((rows, units), HALF)] * 2,
        grid=(2 * count,),
        in_specs=fixed + specs,
        out_specs=[pl.BlockSpec(s, lambda i: (0, 0)) for s, _ in shapes] + [column] * 2,
        scratch_shapes=[pltpu.VMEM((rows, width), WIDE)],
        compiler_params=pltpu.CompilerParams(vmem_limit_bytes=VMEM_LIMIT),
        cost_estimate=pl.CostEstimate(
            flops=12 * rows * width * units, transcendentals=2 * rows * units, bytes_accessed=4 * width * units
        ),
        name="feed_forward",
    )(x, resid, gain, bias, own, mine, other, own, mine, other)


def _ffn_back_kernel(count, x, grad, resid, normed, inv_scale, gain, active, slope, *refs):
    ins, outs, refs = refs[:3], refs[3:6], refs[6:]
    result, result_low, terms, *grads, acc = refs
    i = pl.program_id(0)

    @pl.when(i == 0)
    def _():
        acc[...] = jnp.zeros(acc.shape, WIDE)

    for condition, first, second in _ffn_cases(count, i, ins, outs):

        @pl.when(condition)
        def _(first=first, second=second):
            hidden = (dot(grad[...], second[...]) * slope[...].astype(WIDE)).astype(HALF)
            acc[...] += dot_bt(hidden, first[...])
            f1 = dot_ta(x[...], hidden).astype(HALF)
            f2 = dot_ta(grad[...], active[...]).astype(HALF)
            for half, when in enumerate((i < count, i >= count)):

                @pl.when(when)
                def _(half=half):
                    grads[half][...] = f1
                    grads[2 + half][...] = f2

    @pl.when(i == 2 * count - 1)
    def _():
        _end_norm_back(acc[...], (resid, normed, inv_scale, gain), (result, result_low, terms))


def feed_forward_back(x, grad, resid, normed, inv_scale, gain, active, slope, own, mine, other):
    count = lax.axis_size("tensor")
    rows, width = x.shape
    wide, specs = _ffn_parts(count, own, mine, other)
    column = pl.BlockSpec((rows, wide), lambda i: (0, i))
    fixed = [pl.BlockSpec(v.shape, lambda i: (0, 0)) for v in (x, grad, resid, normed, inv_scale, gain)]
    shapes = [((rows, width), WIDE), ((rows, width), HALF), ((8, width), WIDE)]
    grad_specs = [
        pl.BlockSpec((width, wide), lambda i: (0, jnp.minimum(i, count - 1))),
        pl.BlockSpec((width, wide), lambda i: (0, jnp.maximum(i - count, 0))),
    ]
    return pl.pallas_call(
        partial(_ffn_back_kernel, count),
        out_shape=[jax.ShapeDtypeStruct(*s) for s in shapes]
        + [jax.ShapeDtypeStruct((width, count * wide), HALF)] * 4,
        grid=(2 * count,),
        in_specs=fixed + [column] * 2 + specs,
        out_specs=[pl.BlockSpec(s, lambda i: (0, 0)) for s, _ in shapes] + grad_specs * 2,
        scratch_shapes=[pltpu.VMEM((rows, width), WIDE)],
        compiler_params=pltpu.CompilerParams(vmem_limit_bytes=VMEM_LIMIT),
        cost_estimate=pl.CostEstimate(
            flops=32 * rows * width * count * wide, transcendentals=0, bytes_accessed=16 * width * count * wide
        ),
        name="feed_forward_back",
    )(x, grad, resid, normed, inv_scale, gain, active, slope, own, mine, other, own, mine, other)


def _add_rows(dest, first, second):
    rows = 64 if dest.shape[0] % 64 == 0 else dest.shape[0]

    def step(i, carry):
        at = pl.ds(pl.multiple_of(i * rows, rows), rows)
        dest[at, :] = (first[at, :].astype(WIDE) + second[at, :].astype(WIDE)).astype(HALF)
        return carry

    lax.fori_loop(0, dest.shape[0] // rows, step, 0)


def _finish_kernel(bits, count, planes, *refs):
    in_mine, out_mine, in_other, out_other, f1, f2, ckv, dec_ffn, dec_small, tokens = refs[:10]
    norm_terms, refs = refs[10:16], refs[16:]
    attn_out, cross_out, ffn_out, far, near, norm_sum = refs[:6]
    land_in, land_out, term, *refs = refs[6:]
    n_steps = planes.bit_length() - 1
    land_planes, refs = refs[:n_steps], refs[n_steps:]
    folded, landed, refs = refs[:4], refs[4:8], refs[8:]
    enc_ffn, enc_small, got_ffn, got_small, norm_other, norm_land, send_sem, recv_sem = refs
    core, place, me = lax.axis_index("pipe"), lax.axis_index("dp"), lax.axis_index("tensor")
    sibling = {"pipe": 1 - core}
    line = {s: {"tensor": _differ(me, s, count)} for s in range(1, count)}
    cross_over = {"pipe": 1 - core, "tensor": _differ(me, bits[0], count)}
    dp_bits = [1 << i for i in range(n_steps)]
    others = {bit: {"dp": _differ(place, bit, planes)} for bit in dp_bits}
    _enter([sibling, cross_over, *line.values(), *others.values()])
    made = [0]

    def number():
        made[0] += 1
        return made[0] - 1

    def push(source, dest, peer):
        i = number()
        return _send(source, dest, send_sem.at[i], recv_sem.at[i], peer)

    def wait(copies):
        for copy in copies:
            copy.wait()

    for i in range(3):
        at = slice(2 * i, 2 * i + 2)
        enc, dec = norm_terms[i][0:2, :], norm_terms[3 + i][0:2, :]
        norm_sum[at, :] = jnp.where(core == 0, enc, dec)
        norm_other[at, :] = jnp.where(core == 0, dec, enc)
    norm_sum[6:8, :] = jnp.zeros((2, norm_sum.shape[1]), WIDE)
    norm_other[6:8, :] = jnp.zeros((2, norm_sum.shape[1]), WIDE)
    norm_peers = [*others.values(), *(line[bit] for bit in bits)]
    norm_now = [push(norm_other, norm_land.at[0], sibling)]

    def advance_norms():
        if norm_now:
            norm_now.pop().wait()
            n = n_steps + len(bits) - len(norm_peers)
            norm_sum[...] = norm_sum[...] + norm_land[n]
            if norm_peers:
                norm_now.append(push(norm_sum, norm_land.at[n + 1], norm_peers.pop(0)))

    to_core = [push(in_other, land_in, sibling), push(out_other, land_out, sibling)]

    def chain(source, a, at=slice(None)):
        fold, land = (v if at == slice(None) else v.at[at] for v in (folded[a], landed[a]))
        size = folded[a].shape[1] * 2 // count
        return {
            "source": source,
            "fold": fold,
            "land": land,
            "size": size,
            "slots": count,
            "bits": list(reversed(bits)),
            "now": [],
        }

    def advance(c):
        land, size = c["land"], c["size"]
        if c["now"]:
            wait(c["now"])
            c["now"] = []
            kept = c["slots"] // 2 * size
            offset = (count - c["slots"]) * size
            at = pl.ds(0, kept)
            _add_rows(c["fold"].at[:, at], c["source"].at[:, at], land.at[:, pl.ds(offset, kept)])
            c["source"], c["slots"] = c["fold"], c["slots"] // 2
        if c["bits"]:
            kept = c["slots"] // 2 * size
            offset = (count - c["slots"]) * size
            source = c["source"].at[:, pl.ds(kept, kept)]
            c["now"] = [push(source, land.at[:, pl.ds(offset, kept)], line[c["bits"].pop(0)])]

    chains = [chain(f2, 0), chain(f1, 1), chain(ckv, 2)]
    advance(chains[0])

    half = tokens.shape[1] // 2
    far_sem, near_sem, same_sem = number(), number(), number()

    @pl.when(core == 1)
    def _():
        _send(tokens.at[:, pl.ds(0, half)], far, send_sem.at[far_sem], recv_sem.at[far_sem], cross_over)
        _send(
            tokens.at[:, pl.ds(half, half)], far, send_sem.at[same_sem], recv_sem.at[far_sem], line[bits[0]]
        )

    @pl.when(core == 0)
    def _():
        _send(tokens.at[:, pl.ds(half, half)], near, send_sem.at[near_sem], recv_sem.at[near_sem], sibling)

    wait(to_core)
    block = in_mine.shape[0] // planes
    wide = term.shape[1] // count
    inner = in_mine.shape[1] // count

    def sum_step(i, carry):
        at = pl.ds(pl.multiple_of(i * 64, 64), 64)
        for s in range(count):
            first = in_mine[at, s * inner : (s + 1) * inner].astype(WIDE)
            second = land_in[at, s * inner : (s + 1) * inner].astype(WIDE)
            term[at, s * wide : s * wide + inner] = (first + second).astype(HALF)
            outer = wide - inner
            first = out_mine[at, s * outer : (s + 1) * outer].astype(WIDE)
            second = land_out[at, s * outer : (s + 1) * outer].astype(WIDE)
            term[at, s * wide + inner : (s + 1) * wide] = (first + second).astype(HALF)
        return carry

    lax.fori_loop(0, in_mine.shape[0] // 64, sum_step, 0)

    columns = term.shape[1] // 2
    orders = (dp_bits, dp_bits[::-1])
    held = [[list(range(planes)) for _ in orders] for _ in range(2)]
    piece = block // 2

    def rows_of(difference, r):
        first = _differ(place, difference, planes) * block + r * piece
        return pl.ds(pl.multiple_of(first, piece), piece)

    def at_of(p, m, r):
        return term.at[rows_of(m, r), pl.ds(p * columns, columns)]

    def plane_start(j, r):
        copies = []
        for p, order in enumerate(orders):
            bit = order[j]
            kept = [m for m in held[r][p] if not m & bit]
            for n, m in enumerate(kept):
                dest = land_planes[j].at[p, n, pl.ds(r * piece, piece)]
                copies.append((p, m, dest, push(at_of(p, m ^ bit, r), dest, others[bit])))
            held[r][p] = kept
        return copies

    def plane_finish(copies, r):
        for p, m, dest, copy in copies:
            copy.wait()
            _add_rows(at_of(p, m, r), at_of(p, m, r), dest)

    moving = [plane_start(0, r) for r in range(2)]
    for_attn = []
    for j in range(n_steps):
        for r in range(2):
            advance(chains[min(2 * j + r, 2)])
            advance_norms()
            plane_finish(moving[r], r)
            if j + 1 < n_steps:
                moving[r] = plane_start(j + 1, r)
            else:
                for_attn.append(chain(term.at[rows_of(0, r)], 3, pl.ds(r * piece, piece)))
                advance(for_attn[-1])
    while any(c["now"] or c["bits"] for c in chains + for_attn):
        for c in for_attn + chains:
            advance(c)
        advance_norms()
    while norm_now:
        advance_norms()

    size = [fold.shape[1] * 2 // count for fold in folded]
    enc_ffn[:, : size[1]] = folded[1][:, : size[1]]
    enc_ffn[:, size[1] :] = folded[0][:, : size[0]]
    enc_small[:, : size[3]] = folded[3][:, : size[3]]
    enc_small[:, size[3] :] = folded[2][:, : size[2]]
    swap_sem = [number(), number()]

    @pl.when(core == 0)
    def _():
        _send(dec_ffn, got_ffn, send_sem.at[swap_sem[0]], recv_sem.at[swap_sem[0]], sibling)
        _send(dec_small, got_small, send_sem.at[swap_sem[1]], recv_sem.at[swap_sem[1]], sibling)

    @pl.when(core == 1)
    def _():
        _send(enc_ffn, got_ffn, send_sem.at[swap_sem[0]], recv_sem.at[swap_sem[0]], sibling)
        _send(enc_small, got_small, send_sem.at[swap_sem[1]], recv_sem.at[swap_sem[1]], sibling)

    for i, (mine, got) in enumerate(((enc_ffn, got_ffn), (enc_small, got_small))):
        pltpu.make_async_copy(mine, got, send_sem.at[swap_sem[i]]).wait()
        pltpu.make_async_copy(mine, got, recv_sem.at[swap_sem[i]]).wait()

    def write(first, second):
        for h, (ffn, small) in enumerate((first, second)):
            c = ffn.shape[1] // 2
            for k in range(2):
                ffn_out[k, :, h * c : (h + 1) * c] = ffn[:, k * c : (k + 1) * c].astype(WIDE)
            c = small.shape[1] // 6
            for k in range(6):
                dest = attn_out.at[k] if k < 4 else cross_out.at[k - 4]
                dest[:, h * c : (h + 1) * c] = small[:, k * c : (k + 1) * c].astype(WIDE)

    @pl.when(core == 0)
    def _():
        write((enc_ffn, enc_small), (got_ffn, got_small))

    @pl.when(core == 1)
    def _():
        write((got_ffn, got_small), (dec_ffn, dec_small))

    pltpu.make_async_copy(far, far, recv_sem.at[far_sem]).wait()

    @pl.when(core == 1)
    def _():
        pltpu.make_async_copy(far, far, send_sem.at[far_sem]).wait()
        pltpu.make_async_copy(far, far, send_sem.at[same_sem]).wait()
        pltpu.make_async_copy(near, near, recv_sem.at[near_sem]).wait()

    @pl.when(core == 0)
    def _():
        pltpu.make_async_copy(near, near, send_sem.at[near_sem]).wait()


def finish(in_grads, out_grads, f1, f2, ckv, dec_ffn, dec_small, tokens, norm_terms):
    count, planes = lax.axis_size("tensor"), lax.axis_size("dp")
    depth = in_grads[0].shape[0]
    rows = depth // planes
    attn_columns = in_grads[0].shape[1] + out_grads[0].shape[1]
    wide = 2 * dec_small.shape[1] // 6
    vmem = pl.BlockSpec(memory_space=pltpu.VMEM)
    operands = (in_grads[0], out_grads[0], in_grads[1], out_grads[1], f1, f2, ckv, dec_ffn, dec_small, tokens)
    operands += tuple(norm_terms)
    lines = [f2.shape[1], f1.shape[1], ckv.shape[1], attn_columns]
    scratch = [in_grads[0].shape, out_grads[0].shape, (depth, attn_columns)]
    blocks = planes // 2
    while blocks >= 1:
        scratch.append((2, blocks, rows, attn_columns // 2))
        blocks //= 2
    scratch += [(rows, c // 2) for c in lines]
    scratch += [(rows, c - c // count) for c in lines]
    scratch += [dec_ffn.shape, dec_small.shape] * 2
    norm_steps = count.bit_length() + planes.bit_length() - 1
    norm_shapes = [norm_terms[0].shape, (norm_steps, *norm_terms[0].shape)]
    token_piece = ((tokens.shape[0], tokens.shape[1] // 2), HALF)
    outs = [((4, rows, wide), WIDE), ((2, rows, wide), WIDE), ((2, rows, dec_ffn.shape[1]), WIDE)]
    outs += [token_piece, token_piece, (norm_terms[0].shape, WIDE)]
    return pl.pallas_call(
        partial(_finish_kernel, slot_bits(), count, planes),
        out_shape=[jax.ShapeDtypeStruct(*o) for o in outs],
        in_specs=[vmem] * len(operands),
        out_specs=[vmem] * len(outs),
        scratch_shapes=[pltpu.VMEM(shape, HALF) for shape in scratch]
        + [pltpu.VMEM(shape, WIDE) for shape in norm_shapes]
        + [pltpu.SemaphoreType.DMA((64,))] * 2,
        compiler_params=pltpu.CompilerParams(
            collective_id=5, has_side_effects=True, vmem_limit_bytes=VMEM_LIMIT
        ),
        cost_estimate=pl.CostEstimate(flops=0, transcendentals=0, bytes_accessed=200 << 20),
        name="finish",
    )(*operands)


def per_device(
    enc_input,
    dec_input,
    dec_cotangent,
    enc_lengths,
    dec_lengths,
    attn_weights,
    cross_weights,
    ffn_weights,
    norm_gains,
    norm_biases,
):
    core, place = lax.axis_index("pipe"), lax.axis_index("tensor")
    count = lax.axis_size("tensor")
    top_bit = count // 2
    group = place // top_bit
    block = jnp.where(core == 0, place, place ^ top_bit)
    span, width = enc_input.shape[1:]
    dec_span = dec_input.shape[1]
    local_width = attn_weights.shape[3]
    is_first = core == 0
    chips = range(count)
    sources = [(s // top_bit, s % top_bit) for s in range(2 * top_bit)]
    half = width // 2
    half_local = local_width // 2

    def owner(t):
        return t // top_bit

    norms = jnp.concatenate([norm_gains[0], norm_biases[0]], axis=0)
    norms_other = swap(norms, "pipe", 1)
    enc_norms = jnp.where(is_first, norms, norms_other)
    dec_norms = jnp.where(is_first, norms_other, norms)
    eg, eb, dg, db = enc_norms[:3], enc_norms[3:], dec_norms[:3], dec_norms[3:]

    pick = partial(lax.dynamic_index_in_dim, index=core, axis=0, keepdims=False)
    start_low = pick(dec_input)
    (
        w_attn,
        own_cross,
        own_ffn,
        dec_attn_halves,
        dec_cross_halves,
        dec_ffn_halves,
        cross_rest,
        ffn_rest,
        got,
        start_full,
    ) = gather_weights(
        *[in_column_halves(v[0]) for v in (after(attn_weights, norms_other), cross_weights, ffn_weights)],
        lax.dynamic_index_in_dim(enc_input, 1 - group, 0, False),
        start_low,
    )
    kept = lax.dynamic_index_in_dim(enc_input, group, 0, False)
    tokens = jnp.where(is_first, kept, got).astype(WIDE)
    mine_ffn = gather_planes(ffn_rest)

    def natural(halves, kinds):
        wide = halves.shape[2] // kinds
        return [
            jnp.concatenate([halves[h][:, k * wide : (k + 1) * wide] for h in range(2)], axis=1)
            for k in range(kinds)
        ]

    dec_attn, dec_cross, dec_ffn = [
        natural(v, k) for v, k in ((dec_attn_halves, 4), (dec_cross_halves, 2), (dec_ffn_halves, 2))
    ]
    blocks = width // LANES
    masks = [a * (blocks // 2) + c * (blocks // 2 // top_bit) for a, c in sources]

    def gain_of(i):
        return enc_norms[i : i + 1]

    def bias_of(i):
        return enc_norms[3 + i : 4 + i]

    embed, start_normed, start_scale = norm_forward(tokens, eg[0], eb[0])
    start_scale = jnp.broadcast_to(start_scale, (span, LANES))
    embed_low = embed.astype(HALF)
    parts = 2 if all(m % 2 == 0 for m in masks) else 1
    query, *key_value = spread(embed_low, w_attn, 4, (0, 1, 2), pair=parts)

    def across_chips(value):
        held, bit = [value], 1
        while bit < top_bit:
            held = held + [swap(v, "tensor", bit) for v in held]
            bit *= 2
        return held

    def exchange(held, *earlier):
        if earlier:
            held = after(tuple(held), *earlier)
        return list(held) + [swap(v, "pipe", 1) for v in held]

    key_values = [across_chips(v) for v in key_value]
    mine_cross = gather_planes(after(cross_rest, query))

    enc_lengths, dec_lengths = [after(v, query) for v in (enc_lengths, dec_lengths)]
    enc_row = lax.dynamic_index_in_dim(enc_lengths, group, 0, False)
    dec_row_of_group = lax.dynamic_index_in_dim(dec_lengths, group, 0, False)
    dec_row = lax.dynamic_index_in_dim(dec_lengths, core, 0, False)
    spots = jnp.arange(span, dtype=jnp.int32)
    own_seg = table_of(block * span + spots, enc_row)
    key_seg = jnp.stack(
        [table_of((block ^ (a * top_bit) ^ c) * span + spots, enc_row) for a, c in sources]
    )
    dec_spots = jnp.arange(dec_span * count, dtype=jnp.int32)
    dec_seg = table_of(dec_spots, dec_row)
    enc_segs = tables(own_seg, key_seg)
    dec_segs = tables(dec_seg, dec_seg[None])
    cross_segs = tables(table_of(dec_spots, dec_row_of_group), own_seg[None])

    start_full = after(start_full, key_value)
    start = start_low.astype(WIDE)
    rows_full = dec_span * count
    wide_rows = ((dec_span, width), WIDE)
    kept_rows = [wide_rows, wide_rows, ((dec_span, LANES), WIDE)]
    norm_terms = ((8, width), WIDE)
    dec_in_w = [dec_attn[k] for k in range(3)]
    dec_query = dot(start_full, dec_in_w[0]).astype(HALF)
    dec_kv = jnp.stack([dot(start_full, w).astype(HALF) for w in dec_in_w[1:]])
    dec_heads_wide, dec_lse = attend(dec_query, [dec_kv], dec_segs, [0], True)
    dec_heads = dec_heads_wide.astype(HALF)
    term = dot_bt(dec_heads, dec_attn[3]).astype(HALF)

    attended = ()
    for n in range(parts):
        key_values[n] = exchange(key_values[n], *attended, *((term,) if n else ()))
        attended = attend(
            query, key_values[n], enc_segs, masks, part=n if parts == 2 else None, into=attended
        )
    heads_wide, lse = attended

    def sum_to_owner(term, resid, *earlier):
        total = after(resid, *earlier)
        for s in range(count):
            rows = lax.dynamic_slice_in_dim(term, (place ^ s) * dec_span, dec_span, 0)
            total = total + (swap(rows, "tensor", s) if s else rows).astype(WIDE)
        return total

    self_norm, self_normed, self_scale = norm_forward(sum_to_owner(term, start, lse), dg[0:1], db[0:1])
    self_scale = jnp.broadcast_to(self_scale, (dec_span, LANES))
    self_low = self_norm.astype(HALF)
    self_rows = [swap(self_low, "tensor", s) if s else self_low for s in range(count)]

    heads = heads_wide.astype(HALF)
    mine_ffn = after(mine_ffn, heads_wide)
    other_ffn = swap(mine_ffn, "pipe", 1)
    mine_cross = after(mine_cross, other_ffn)
    w_cross = jnp.stack(
        [
            jnp.concatenate([own_cross[0], mine_cross], axis=1),
            jnp.concatenate([own_cross[1], swap(mine_cross, "pipe", 1)], axis=1),
        ]
    )
    kept_tokens = [((span, width), WIDE), ((span, width), HALF), ((span, width), WIDE), ((span, LANES), WIDE)]
    attn_norm, attn_norm_low, attn_normed, attn_scale = collect(
        [heads], w_attn, 4, (3,), _end_norm, [embed, gain_of(1), bias_of(1)], kept_tokens
    )
    _, memory_low, mem_normed, mem_scale, active, slope = feed_forward(
        attn_norm_low, attn_norm, gain_of(2), bias_of(2), own_ffn, mine_ffn, other_ffn
    )
    self_full = after(jnp.zeros((rows_full, width), HALF), mem_scale)
    for s in range(count):
        self_full = lax.dynamic_update_slice_in_dim(self_full, self_rows[s], (place ^ s) * dec_span, 0)
    cross_query = dot(self_full, dec_cross[0]).astype(HALF)

    def in_halves(value):
        return jnp.stack([value[:, :half_local], value[:, half_local:]])

    [cross_q_enc] = to_encoder(in_halves(cross_query), 6)
    cross_q_enc = to_pairs(cross_q_enc)

    [cross_kv] = spread(memory_low, w_cross, 2, (0, 1), pair=1)

    tables_of_keys = enc_lengths.shape[1]
    at_table = (own_seg[:, None] == jnp.arange(tables_of_keys)[None]).astype(HALF)
    sums = dot_ta(at_table, cross_kv[0])
    bit = 1
    while bit < top_bit:
        sums = sums + swap_columns(sums, "tensor", bit, masks[bit])
        bit *= 2
    sums = sums + swap_columns(sums, "pipe", 1, masks[top_bit])
    means = sums / enc_row.astype(WIDE)[:, None]
    centers = sum(
        jnp.where((own_seg == j)[:, None], means[j : j + 1], 0.0) for j in range(tables_of_keys)
    )
    centered = (cross_kv[0].astype(WIDE) - centers).astype(HALF)

    part_out, part_lse = attend(cross_q_enc, [cross_kv], cross_segs, [0], False, HALF)
    cross_heads, cross_out_wide, cross_lse = to_decoder(
        from_pairs(part_out, half_local), stats_from_pairs(part_lse, half_local), 7
    )
    cross_norm, cross_normed, cross_scale, cross_full = rows_call(
        _forward_rows,
        2,
        dot_bt(cross_heads, dec_cross[1]).astype(HALF),
        [self_norm, dg[1:2], db[1:2]],
        kept_rows,
    )
    dec_hidden = dot(cross_full, dec_ffn[0])
    dec_active = gelu(dec_hidden).astype(HALF)
    result, resid, dec_terms2, grad_full = rows_call(
        _turn_rows,
        3,
        dot_bt(dec_active, dec_ffn[1]).astype(HALF),
        [cross_norm, dg[2:3], db[2:3], pick(dec_cotangent)],
        [((dec_span, width), HALF), wide_rows, norm_terms],
    )
    grad_hidden = (dot(grad_full, dec_ffn[1]) * gelu_slope(dec_hidden)).astype(HALF)
    resid, dec_terms1, cross_grad_full = rows_call(
        _backward_rows,
        4,
        dot_bt(grad_hidden, dec_ffn[0]).astype(HALF),
        [resid, cross_normed, cross_scale, dg[1:2]],
        [wide_rows, norm_terms],
    )
    cross_heads_grad = dot(cross_grad_full, dec_cross[1]).astype(HALF)
    heads_grad_enc, stats_enc = to_encoder(
        in_halves(cross_heads_grad), 8, cross_out_wide, cross_lse
    )
    cross_q_term, [cross_kv_grad] = attend_back(
        cross_q_enc,
        [cross_kv],
        to_pairs(heads_grad_enc),
        stats_to_pairs(stats_enc, half_local),
        centered,
        cross_segs,
        [0],
        False,
        False,
    )
    dec_f2_grad = dot_ta(grad_full, dec_active)
    dec_f1_grad = dot_ta(cross_full, grad_hidden)
    dec_ffn_rows, _ = scatter_local([dec_f1_grad, dec_f2_grad])

    def to_chip(value):
        theirs = joint(value, [((1 - owner(t), t), (owner(t), t)) for t in chips])
        theirs = theirs.reshape(2, count, *theirs.shape[1:])
        chip = value.reshape(theirs.shape).astype(WIDE) + theirs[::-1].astype(WIDE)
        return jnp.where(is_first, chip, chip[::-1]).astype(HALF)

    def to_owner(chip):
        terms = []
        for s in range(top_bit):
            near, far = 2 * s, 2 * s + 1
            near_pairs = [((owner(t), t), (owner(t), t ^ s)) for t in chips]
            far_pairs = [((owner(t), t), (owner(t), t ^ s ^ top_bit)) for t in chips]
            near_got = chip[:, near] if s == 0 else joint(chip[:, near], near_pairs)
            far_got = joint(chip[:, far], far_pairs)
            terms.append(jnp.where(core == group, near_got, far_got).astype(WIDE))
        return sum(terms)

    cross_q_chip = to_chip(from_pairs(cross_q_term, half_local))
    cross_q_grad = to_owner(cross_q_chip).astype(HALF)
    cross_q_grad = jnp.concatenate([cross_q_grad[0], cross_q_grad[1]], axis=1)

    back_tokens = [((span, width), WIDE), ((span, width), HALF), ((8, width), WIDE)]
    resid_enc, resid_low, enc_terms2, *cross_grads = collect(
        [cross_kv_grad],
        w_cross,
        2,
        (0, 1),
        _end_norm_back,
        [mem_normed, mem_scale, gain_of(2)],
        back_tokens,
        memory_low,
    )
    ckv_term = fold_cores(*cross_grads)
    enc_ckv = fold_planes(ckv_term)
    resid_enc, resid_low, enc_terms1, *ffn_grads = feed_forward_back(
        attn_norm_low,
        after(resid_low, dec_ffn_rows, cross_q_chip),
        resid_enc,
        attn_normed,
        attn_scale,
        gain_of(1),
        active,
        slope,
        own_ffn,
        mine_ffn,
        other_ffn,
    )
    heads_grad, *out_grads = spread(resid_low, w_attn, 4, (3,), heads)
    f2_term = fold_cores(after(ffn_grads[2], heads_grad), ffn_grads[3])
    enc_f2 = fold_planes(f2_term)
    f1_term = fold_cores(*ffn_grads[:2])
    enc_f1 = fold_planes(f1_term)
    def join(a, b):
        return (a.astype(WIDE) + b.astype(WIDE)).astype(HALF)

    grads_in = after(heads_grad, f1_term, f2_term, cross_q_grad)
    def send_chips(held):
        pairs, bit = [(v,) for v in held], top_bit // 2
        while bit >= 1:
            held = [join(*v) if len(v) == 2 else v[0] for v in pairs]
            pairs = [(a, swap(b, "tensor", bit)) for a, b in zip(held[:bit], held[bit:])]
            bit //= 2
        return pairs[0]

    def sum_pair(pair, *earlier):
        return join(after(pair[0], *earlier), pair[1]) if len(pair) == 2 else pair[0]

    q_grad, moving, held = (), [], []
    for n in range(parts):
        q_grad, terms = attend_back(
            query,
            key_values[n],
            after(grads_in, *held),
            lse,
            heads_wide,
            enc_segs,
            masks,
            part=n if parts == 2 else None,
            into=q_grad,
        )
        q_grad = (q_grad,)
        held = [join(a, swap(b, "pipe", 1)) for a, b in zip(terms[:top_bit], terms[top_bit:])]
        moving.append(send_chips(held))
    kv_grad = [sum_pair(pair, terms[0]) for pair in moving[:-1]]
    [q_grad] = q_grad

    cross_q_grad = after(cross_q_grad, *held, enc_f1)
    resid, dec_terms0, self_grad_full = rows_call(
        _backward_rows,
        4,
        dot_bt(cross_q_grad, dec_cross[0]).astype(HALF),
        [resid, self_normed, self_scale, dg[0:1]],
        [wide_rows, norm_terms],
    )
    kv_grad.append(sum_pair(moving[-1], self_grad_full))
    dec_heads_grad = dot(after(self_grad_full, kv_grad[-1]), dec_attn[3]).astype(HALF)
    dec_q_grad, [dec_kv_grad] = attend_back(
        dec_query, [dec_kv], dec_heads_grad, dec_lse, dec_heads_wide, dec_segs, [0], True
    )
    dec_proj_grad = [dec_q_grad, dec_kv_grad[0], dec_kv_grad[1]]
    dec_part = sum(dot_bt(g, w) for g, w in zip(dec_proj_grad, dec_in_w)).astype(HALF)
    dec_left = [start_full] * 3 + [self_grad_full, self_full, cross_grad_full]
    dec_right = dec_proj_grad + [dec_heads, cross_q_grad, cross_heads]
    dec_small = [dot_ta(a, b) for a, b in zip(dec_left, dec_right)]
    dec_small_rows, dec_small_term = scatter_local(dec_small)
    kv_grad[-1] = after(kv_grad[-1], dec_small_term, enc_ckv)

    enc_grad, enc_low, enc_terms0, *in_grads = collect(
        [q_grad, *kv_grad],
        w_attn,
        4,
        (0, 1, 2),
        _end_norm_back,
        [resid_enc, start_normed, start_scale, gain_of(0)],
        back_tokens,
        embed_low,
    )
    dec_grad = sum_to_owner(dec_part, resid, enc_low)
    attn_out, cross_out, ffn_out_grad, there, near_second, norm_sums = finish(
        in_grads,
        out_grads,
        enc_f1,
        enc_f2,
        enc_ckv,
        dec_ffn_rows,
        dec_small_rows,
        after(enc_low, dec_grad),
        [enc_terms0, enc_terms1, enc_terms2, dec_terms0, dec_terms1, dec_terms2],
    )

    attn_out, cross_out, ffn_out_grad = [
        v.transpose(1, 0, 2)[None] for v in (attn_out, cross_out, ffn_out_grad)
    ]
    own_columns = width // (lax.axis_size("dp") * count)
    norm_sums = lax.dynamic_slice_in_dim(
        norm_sums[:6].reshape(3, 2, width), (lax.axis_index("dp") * count + place) * own_columns, own_columns, 2
    )

    dec_pair = jnp.stack([result, dec_grad.astype(HALF)])
    dec_halves = dec_pair.reshape(2, dec_span, 2, half)
    dec_got = swap(lax.dynamic_index_in_dim(dec_halves, 1 - core, 2, False), "pipe", 1)
    own_result = lax.dynamic_slice_in_dim(result, core * half, half, 1)
    own_grad = lax.dynamic_slice_in_dim(dec_grad, core * half, half, 1)
    dec_output = jnp.where(
        is_first, jnp.stack([own_result, dec_got[0]]), jnp.stack([dec_got[0], own_result])
    )
    got_grad = dec_got[1].astype(WIDE)
    dec_input_grad = jnp.where(
        is_first, jnp.stack([own_grad, got_grad]), jnp.stack([got_grad, own_grad])
    )

    here = jnp.where(is_first, enc_grad[:, :half], near_second.astype(WIDE))
    there = there.astype(WIDE)
    enc_input_grad = jnp.where(group == 0, jnp.stack([here, there]), jnp.stack([there, here]))
    return (
        dec_output,
        enc_input_grad,
        dec_input_grad,
        attn_out,
        cross_out,
        ffn_out_grad,
        norm_sums[None, :, 0],
        norm_sums[None, :, 1],
    )


def solution(mesh):
    rows = P("dp", "tensor", None)
    weights = P("pipe", None, None, "tensor")
    half_rows = P("dp", "tensor", "pipe")
    weight_grads = P("pipe", "dp", None, "tensor")
    norm_grads = P("pipe", None, ("dp", "tensor"))
    return jax.shard_map(
        per_device,
        mesh=mesh,
        in_specs=(rows, rows, rows, P("dp", None), P("dp", None))
        + (weights,) * 3
        + (P("pipe", None, None),) * 2,
        out_specs=(half_rows,) * 3 + (weight_grads,) * 3 + (norm_grads,) * 2,
        check_vma=False,
    )
```

```python
from functools import partial

import jax
import jax.numpy as jnp
from jax import lax
from jax.experimental import pallas as pl
from jax.experimental.pallas import tpu as pltpu
from jax.sharding import PartitionSpec as P

HEAD = 64
LANES = 128
EPSILON = 1e-05
NEGATIVE = -1e30
HALF = jnp.bfloat16
WIDE = jnp.float32
VMEM_LIMIT = 56 << 20
MESH = pl.DeviceIdType.MESH
TILE_Q = 256
TILE_K = 512


def dot(left, right):
    return jnp.dot(left, right, preferred_element_type=WIDE)


def dot_bt(left, right):
    return lax.dot_general(left, right, (((1,), (1,)), ((), ())), preferred_element_type=WIDE)


def dot_ta(left, right):
    return lax.dot_general(left, right, (((0,), (0,)), ((), ())), preferred_element_type=WIDE)


def swap(value, axis, mask):
    return lax.ppermute(value, axis, [(i, i ^ mask) for i in range(lax.axis_size(axis))])


def joint(value, pairs):
    count = lax.axis_size("tensor")
    return lax.ppermute(
        value,
        ("pipe", "tensor"),
        [(a[0] * count + a[1], b[0] * count + b[1]) for a, b in pairs],
    )


def after(value, *earlier):
    return lax.optimization_barrier((value, *earlier))[0]


def swap_columns(value, axis, mask, difference):
    got = swap(value, axis, mask).reshape(value.shape[0], -1, LANES)
    order = [b ^ difference for b in range(got.shape[1])]
    return jnp.concatenate([got[:, b] for b in order], axis=1)


def table_of(places, lengths):
    total = jnp.zeros((), jnp.int32)
    table = jnp.zeros(places.shape, jnp.int32)
    for j in range(lengths.shape[0]):
        total = total + lengths[j]
        table = table + (places >= total).astype(jnp.int32)
    return table


def norm_forward(values, gain, bias):
    center = values - jnp.mean(values, axis=-1, keepdims=True)
    inv_scale = lax.rsqrt(jnp.mean(center * center, axis=-1, keepdims=True) + EPSILON)
    normed = center * inv_scale
    return normed * gain + bias, normed, inv_scale


def norm_backward(grad_out, normed, inv_scale, gain):
    grad_gain = jnp.sum(grad_out * normed, axis=0)
    grad_bias = jnp.sum(grad_out, axis=0)
    grad_normed = grad_out * gain
    grad_in = inv_scale * (
        grad_normed
        - jnp.mean(grad_normed, axis=-1, keepdims=True)
        - normed * jnp.mean(grad_normed * normed, axis=-1, keepdims=True)
    )
    return grad_in, grad_gain, grad_bias


def gelu(hidden):
    return 0.5 * hidden * (1.0 + lax.erf(hidden * (2.0**-0.5)))


def gelu_slope(hidden):
    density = jnp.exp(-0.5 * hidden * hidden) * 0.3989422804014327
    return 0.5 * (1.0 + lax.erf(hidden * (2.0**-0.5))) + hidden * density


def _allowed(seg_k, seg_q, causal, col0, row0):
    ok = seg_k == seg_q
    if causal:
        keys = col0 + lax.broadcasted_iota(jnp.int32, ok.shape, 0)
        queries = row0 + lax.broadcasted_iota(jnp.int32, ok.shape, 1)
        ok = ok & (queries >= keys)
    return ok


def _tile_loop(act, chunks, c, nq, nk, tq, tk, body):
    def step(i, carry):
        iq, ik = i // nk, i % nk

        @pl.when(act[iq * (chunks * nk) + c * nk + ik] > 0)
        def _():
            body(iq * tq, ik * tk, pl.ds(pl.multiple_of(iq * tq, tq), tq), pl.ds(pl.multiple_of(ik * tk, tk), tk))

        return carry

    lax.fori_loop(0, nq * nk, step, 0)


def _head_lanes(shape, head):
    lanes = lax.broadcasted_iota(jnp.int32, shape, 1)
    return (lanes < HEAD) if head == 0 else (lanes >= HEAD)


def _attend_kernel(chunks, tq, tk, causal, act, seg_q, seg_k, q, *refs):
    keys, values = refs[:chunks], refs[chunks : 2 * chunks]
    out, lse, top, total, acc = refs[-5:]
    rows = q.shape[0]
    nq, nk = rows // tq, keys[0].shape[0] // tk
    top[...] = jnp.full(top.shape, NEGATIVE, WIDE)
    total[...] = jnp.zeros(total.shape, WIDE)
    acc[...] = jnp.zeros(acc.shape, WIDE)
    for c in range(chunks):

        def tile(row0, col0, r, s, c=c):
            qs = q[r, :] * jnp.asarray(HEAD**-0.5, HALF)
            kk, vt = keys[c][s, :], values[c][s, :].T
            ok = _allowed(seg_k[c, s, 0:1], seg_q[0:1, r], causal, col0, row0)
            ones = jnp.ones((8, vt.shape[1]), HALF)
            heads = range(2)
            raw = [
                dot_bt(kk, jnp.where(_head_lanes(qs.shape, h), qs, jnp.zeros_like(qs))) for h in heads
            ]
            scores = [jnp.where(ok, sc, NEGATIVE) for sc in raw]
            before = [top[h : h + 1, r] for h in heads]
            after_ = [jnp.maximum(b, jnp.max(sc, axis=0, keepdims=True)) for b, sc in zip(before, scores)]
            terms = [jnp.exp(sc - a).astype(HALF) for sc, a in zip(scores, after_)]
            for h in heads:
                fade = jnp.exp(before[h] - after_[h])
                span = slice(h * HEAD, (h + 1) * HEAD)
                sums = dot(jnp.concatenate([vt[span, :], ones], axis=0), terms[h])
                acc[span, r] = acc[span, r] * fade + sums[:HEAD]
                total[h : h + 1, r] = total[h : h + 1, r] * fade + sums[HEAD : HEAD + 1]
                top[h : h + 1, r] = after_[h]

        _tile_loop(act, chunks, c, nq, nk, tq, tk, tile)
    count = total[...]
    count = jnp.where(count > 0.0, count, 1.0)
    lse[0] = top[...] + jnp.log(count)
    whole = jnp.concatenate([acc[:HEAD, :] / count[0:1, :], acc[HEAD:, :] / count[1:2, :]], axis=0)
    out[...] = whole.T.astype(out.dtype)


def _attend_back_kernel(chunks, tq, tk, causal, own_delta, act, seg_q, seg_k, q, *refs):
    keys, values = refs[:chunks], refs[chunks : 2 * chunks]
    grad_out, stats = refs[2 * chunks : 2 * chunks + 2]
    refs = refs[2 * chunks + 2 :]
    extra, (grad_q, *grad_kv, delta, dq, dkv) = refs[0], refs[-(chunks + 4) :]
    rows = q.shape[0]
    nq, nk = rows // tq, keys[0].shape[0] // tk
    if own_delta:
        product = grad_out[...].astype(WIDE) * extra[...].astype(WIDE)
        pick = (
            lax.broadcasted_iota(jnp.int32, (8, LANES), 1) // HEAD
            == lax.broadcasted_iota(jnp.int32, (8, LANES), 0)
        ).astype(WIDE)
        delta[...] = lax.dot_general(
            pick, product, (((1,), (1,)), ((), ())), precision=lax.Precision.HIGHEST, preferred_element_type=WIDE
        )
    else:
        delta[0:2, :] = stats[0, 2:4, :]
    dq[...] = jnp.zeros(dq.shape, WIDE)
    for c in range(chunks):
        dkv[...] = jnp.zeros(dkv.shape, WIDE)

        def tile(row0, col0, r, s, c=c):
            qs = q[r, :] * jnp.asarray(HEAD**-0.5, HALF)
            go = grad_out[r, :]
            kk, vv = keys[c][s, :], values[c][s, :]
            ok = _allowed(seg_k[c, s, 0:1], seg_q[0:1, r], causal, col0, row0)
            heads = range(2)
            mine = [_head_lanes(qs.shape, h) for h in heads]
            mine_k = [_head_lanes(kk.shape, h) for h in heads]
            from_keys = kk if own_delta else extra[s, :]
            qh = [jnp.where(m, qs, jnp.zeros_like(qs)) for m in mine]
            gh = [jnp.where(m, go, jnp.zeros_like(go)) for m in mine]
            kh = [jnp.where(m, from_keys, jnp.zeros_like(kk)) for m in mine_k]
            raw = [dot_bt(kk, v) for v in qh]
            grads = [dot_bt(vv, v) for v in gh]
            pr = [jnp.exp(jnp.where(ok, raw[h], NEGATIVE) - stats[0, h : h + 1, r]) for h in heads]
            ds = [(pr[h] * (grads[h] - delta[h : h + 1, r])).astype(HALF) for h in heads]
            pr = [v.astype(HALF) for v in pr]
            dkv[1, s, :] += dot(pr[0], gh[0]) + dot(pr[1], gh[1])
            dkv[0, s, :] += dot(ds[0], qh[0]) + dot(ds[1], qh[1])
            dq[r, :] += dot_ta(ds[0], kh[0]) + dot_ta(ds[1], kh[1])

        _tile_loop(act, chunks, c, nq, nk, tq, tk, tile)
        grad_kv[c][...] = dkv[...].astype(grad_kv[c].dtype)
    grad_q[...] = (dq[...] * HEAD**-0.5).astype(grad_q.dtype)


def _tile_sizes(rows, keys):
    return min(TILE_Q, rows), min(TILE_K, keys)


def _activity(seg_q, seg_k, tq, tk):
    qt = seg_q.reshape(-1, tq)
    kt = seg_k.reshape(-1, tk)
    hit = (qt[:, :1] <= kt[:, -1][None]) & (kt[:, 0][None] <= qt[:, -1:])
    return hit.astype(jnp.int32).reshape(-1)


def tables(seg_q, seg_k):
    rows, (chunks, span) = seg_q.shape[0], seg_k.shape
    tq, tk = _tile_sizes(rows, span)
    return (
        _activity(seg_q, seg_k, tq, tk),
        jnp.broadcast_to(seg_q[None], (8, rows)),
        jnp.broadcast_to(seg_k[:, :, None], (chunks, span, LANES)),
    )


def _specs(rows, span, chunks, masks, blocked, part):
    def block(h):
        return h if part is None else 2 * h + part

    row_block = pl.BlockSpec((rows, LANES), lambda h, act: (0, block(h)))
    if blocked:
        row_block = pl.BlockSpec((None, rows, LANES), lambda h, act: (block(h), 0, 0))
    stat_block = pl.BlockSpec((1, 8, rows), lambda h, act: (block(h), 0, 0))
    heads = [
        pl.BlockSpec((8, rows), lambda h, act: (0, 0)),
        pl.BlockSpec((chunks, span, LANES), lambda h, act: (0, 0, 0)),
        row_block,
    ]
    for side in range(2):
        heads += [
            pl.BlockSpec((None, span, LANES), lambda h, act, m=m, side=side: (side, 0, h ^ m)) for m in masks
        ]
    return row_block, stat_block, heads


def _dimensions(q, key_values, masks, part):
    blocked = q.ndim == 3
    rows, width = (q.shape[1], q.shape[0] * LANES) if blocked else q.shape
    span, chunks, blocks = key_values[0].shape[1], len(key_values), width // LANES
    if part is not None:
        blocks, masks = blocks // 2, [m // 2 for m in masks]
    row_block, stat_block, specs = _specs(rows, span, chunks, masks, blocked, part)
    return rows, span, chunks, blocks, masks, _tile_sizes(rows, span), row_block, stat_block, specs


def attend(q, key_values, segs, masks, causal=False, out_type=WIDE, part=None, into=()):
    rows, span, chunks, blocks, masks, (tq, tk), row_block, stat_block, specs = _dimensions(
        q, key_values, masks, part
    )
    pairs = rows * span * chunks * blocks * LANES
    kept = 4 + 2 * chunks
    stat_blocks = blocks if part is None else 2 * blocks
    return pl.pallas_call(
        partial(_attend_kernel, chunks, tq, tk, causal),
        out_shape=(
            jax.ShapeDtypeStruct(q.shape, out_type),
            jax.ShapeDtypeStruct((stat_blocks, 8, rows), WIDE),
        ),
        grid_spec=pltpu.PrefetchScalarGridSpec(
            num_scalar_prefetch=1,
            grid=(blocks,),
            in_specs=specs + [pl.BlockSpec(memory_space=pl.ANY)] * len(into),
            out_specs=[row_block, stat_block],
            scratch_shapes=[
                pltpu.VMEM((8, rows), WIDE),
                pltpu.VMEM((8, rows), WIDE),
                pltpu.VMEM((LANES, rows), WIDE),
            ],
        ),
        input_output_aliases={kept + i: i for i in range(len(into))},
        compiler_params=pltpu.CompilerParams(vmem_limit_bytes=VMEM_LIMIT),
        cost_estimate=pl.CostEstimate(
            flops=48 * pairs, transcendentals=pairs // HEAD, bytes_accessed=rows * blocks * LANES * 20
        ),
        name="attend",
    )(*segs, q, *key_values, *key_values, *into)


def attend_back(
    q, key_values, grad_out, stats, extra, segs, masks, causal=False, own_delta=True, part=None, into=()
):
    rows, span, chunks, blocks, masks, (tq, tk), row_block, stat_block, specs = _dimensions(
        q, key_values, masks, part
    )
    kv_out = [pl.BlockSpec((2, span, LANES), lambda h, act, m=m: (0, 0, h ^ m)) for m in masks]
    pairs = rows * span * chunks * blocks * LANES
    extra_block = row_block if own_delta else pl.BlockSpec((span, LANES), lambda h, act: (0, h))
    kept = 7 + 2 * chunks
    outs = pl.pallas_call(
        partial(_attend_back_kernel, chunks, tq, tk, causal, own_delta),
        out_shape=[jax.ShapeDtypeStruct(q.shape, HALF)]
        + [jax.ShapeDtypeStruct((2, span, blocks * LANES), HALF)] * chunks,
        grid_spec=pltpu.PrefetchScalarGridSpec(
            num_scalar_prefetch=1,
            grid=(blocks,),
            in_specs=specs
            + [row_block, stat_block, extra_block]
            + [pl.BlockSpec(memory_space=pl.ANY)] * len(into),
            out_specs=[row_block] + kv_out,
            scratch_shapes=[
                pltpu.VMEM((8, rows), WIDE),
                pltpu.VMEM((rows, LANES), WIDE),
                pltpu.VMEM((2, span, LANES), WIDE),
            ],
        ),
        input_output_aliases={kept + i: i for i in range(len(into))},
        compiler_params=pltpu.CompilerParams(vmem_limit_bytes=VMEM_LIMIT),
        cost_estimate=pl.CostEstimate(
            flops=80 * pairs, transcendentals=pairs // HEAD, bytes_accessed=rows * blocks * LANES * 40
        ),
        name="attend_back",
    )(*segs, q, *key_values, *key_values, grad_out, stats, extra, *into)
    return outs[0], outs[1:]


def _row_mean(values):
    return jnp.mean(values, axis=-1, keepdims=True)


def _norm_rows(values, gain, bias):
    center = values - _row_mean(values)
    inv_scale = lax.rsqrt(_row_mean(center * center) + EPSILON)
    normed = center * inv_scale
    return normed * gain + bias, normed, inv_scale


def _norm_rows_back(grad_out, normed, inv_scale, gain):
    grad_normed = grad_out * gain
    grad_in = inv_scale * (
        grad_normed - _row_mean(grad_normed) - normed * _row_mean(grad_normed * normed)
    )
    return (
        grad_in,
        jnp.sum(grad_out * normed, axis=0, keepdims=True),
        jnp.sum(grad_out, axis=0, keepdims=True),
    )


def _forward_rows(total, ins, outs):
    resid, gain, bias = ins
    value, normed, inv_scale = _norm_rows(total + resid[...], gain[...], bias[...])
    outs[0][...] = value
    outs[1][...] = normed
    outs[2][...] = jnp.broadcast_to(inv_scale, outs[2].shape)
    return value


def _turn_rows(total, ins, outs):
    resid, gain, bias, cotangent = ins
    value, normed, inv_scale = _norm_rows(total + resid[...], gain[...], bias[...])
    outs[0][...] = value.astype(outs[0].dtype)
    grad, grad_gain, grad_bias = _norm_rows_back(
        cotangent[...].astype(WIDE), normed, inv_scale, gain[...]
    )
    outs[1][...] = grad
    outs[2][0:1, :] = grad_gain
    outs[2][1:2, :] = grad_bias
    return grad


def _backward_rows(total, ins, outs):
    resid, normed, inv_scale, gain = ins
    grad, grad_gain, grad_bias = _norm_rows_back(
        total + resid[...], normed[...], inv_scale[:, 0:1], gain[...]
    )
    outs[0][...] = grad
    outs[1][0:1, :] = grad_gain
    outs[1][1:2, :] = grad_bias
    return grad


def _rows_kernel(count, scatter, gather, middle, n_in, n_out, *refs):
    refs = list(refs)
    part = refs.pop(0) if scatter else None
    ins, refs = refs[:n_in], refs[n_in:]
    outs, refs = refs[:n_out], refs[n_out:]
    full = refs.pop(0) if gather else None
    landed = refs.pop(0) if scatter else None
    send_sem, recv_sem = refs[:2]
    me = lax.axis_index("tensor")
    steps = range(1, count)
    peers = [lax.rem(me + s, count) for s in steps]
    barrier = pltpu.get_barrier_semaphore()
    for peer in peers:
        pl.semaphore_signal(barrier, inc=1, device_id={"tensor": peer}, device_id_type=MESH)
    pl.semaphore_wait(barrier, count - 1)
    total = None
    if scatter:
        rows = part.shape[0] // count
        copies = []
        for s, peer in zip(steps, peers):
            copy = pltpu.make_async_remote_copy(
                src_ref=part.at[pl.ds(pl.multiple_of(peer * rows, rows), rows)],
                dst_ref=landed.at[s - 1],
                send_sem=send_sem.at[0, s - 1],
                recv_sem=recv_sem.at[0, s - 1],
                device_id={"tensor": peer},
                device_id_type=MESH,
            )
            copy.start()
            copies.append(copy)
        total = part[pl.ds(pl.multiple_of(me * rows, rows), rows), :].astype(WIDE)
        for s, copy in zip(steps, copies):
            copy.wait_recv()
            total = total + landed[s - 1].astype(WIDE)
        for copy in copies:
            copy.wait_send()
    sent = middle(total, ins, outs)
    if gather:
        rows = full.shape[0] // count
        own = pl.ds(pl.multiple_of(me * rows, rows), rows)
        full[own, :] = sent.astype(full.dtype)
        copies = []
        for s, peer in zip(steps, peers):
            copy = pltpu.make_async_remote_copy(
                src_ref=full.at[own],
                dst_ref=full.at[own],
                send_sem=send_sem.at[1, s - 1],
                recv_sem=recv_sem.at[1, s - 1],
                device_id={"tensor": peer},
                device_id_type=MESH,
            )
            copy.start()
            copies.append(copy)
        for copy in copies:
            copy.wait()


def rows_call(middle, number, part, ins, outs, gather=True):
    count = lax.axis_size("tensor")
    scatter = part is not None
    width = (part if scatter else ins[0]).shape[1]
    rows = part.shape[0] // count if scatter else ins[0].shape[0]
    shapes = [jax.ShapeDtypeStruct(shape, kind) for shape, kind in outs]
    if gather:
        shapes.append(jax.ShapeDtypeStruct((rows * count, width), HALF))
    whole = pl.BlockSpec(memory_space=pltpu.VMEM)
    operands = ([part] if scatter else []) + list(ins)
    got = pl.pallas_call(
        partial(_rows_kernel, count, scatter, gather, middle, len(ins), len(outs)),
        out_shape=shapes,
        in_specs=[whole] * len(operands),
        out_specs=[whole] * len(shapes),
        scratch_shapes=([pltpu.VMEM((count - 1, rows, width), HALF)] if scatter else [])
        + [pltpu.SemaphoreType.DMA((2, count - 1))] * 2,
        compiler_params=pltpu.CompilerParams(
            collective_id=number, has_side_effects=True, vmem_limit_bytes=VMEM_LIMIT
        ),
        cost_estimate=pl.CostEstimate(
            flops=0, transcendentals=0, bytes_accessed=1400 * rows * width
        ),
        name=middle.__name__.strip("_"),
    )(*operands)
    return got


def _differ(a, b, count):
    total, bit = 0, 1
    while bit < count:
        total = total + lax.rem(lax.rem(a // bit, 2) + lax.rem(b // bit, 2), 2) * bit
        bit *= 2
    return total


def _slot(difference, count):
    top = count // 2
    return 2 * lax.rem(difference, top) + difference // top


def _enter(peers):
    barrier = pltpu.get_barrier_semaphore()
    for peer in peers:
        pl.semaphore_signal(barrier, inc=1, device_id=peer, device_id_type=MESH)
    pl.semaphore_wait(barrier, len(peers))


def _send(source, dest, send_sem, recv_sem, peer):
    copy = pltpu.make_async_remote_copy(
        src_ref=source,
        dst_ref=dest,
        send_sem=send_sem,
        recv_sem=recv_sem,
        device_id=peer,
        device_id_type=MESH,
    )
    copy.start()
    return copy


def _to_encoder_kernel(count, with_stats, *refs):
    if with_stats:
        value, out, lse, full, stats, own, own_stats, held, other, other_stats, send_sem, recv_sem = refs
    else:
        value, full, own, other, send_sem, recv_sem = refs
    core, me = lax.axis_index("pipe"), lax.axis_index("tensor")
    group = me // (count // 2)
    chips = [lax.rem(me + s, count) for s in range(1, count)]
    _enter([{"tensor": chip} for chip in chips] + [{"pipe": 1 - core}])
    sets = [(value, own, other, full)]
    if with_stats:
        for h in range(2):
            product = value[h].astype(WIDE) * out[h]
            pick = (
                lax.broadcasted_iota(jnp.int32, (8, product.shape[1]), 1) // HEAD
                == lax.broadcasted_iota(jnp.int32, (8, product.shape[1]), 0) - 2
            ).astype(WIDE)
            held[h] = lax.dot_general(
                pick,
                product,
                (((1,), (1,)), ((), ())),
                precision=lax.Precision.HIGHEST,
                preferred_element_type=WIDE,
            )
            held[h, 0:2, :] = lse[h, 0:2, :]
        sets.append((held, own_stats, other_stats, stats))
    copies = []
    for s, chip in enumerate(chips):
        place = _slot(_differ(chip, me, count), count)
        for h in range(2):
            at = lax.rem(h + core, 2) * count + place
            for i, (source, dest, _, _) in enumerate(sets):
                sems = (send_sem.at[i, s, h], recv_sem.at[i, s, h])
                copies.append(_send(source.at[h], dest.at[at], *sems, {"tensor": chip}))
    for h in range(2):
        for source, dest, _, _ in sets:
            dest[lax.rem(h + core, 2) * count] = source[h]
    for copy in copies:
        copy.wait()
    copies = []
    for g in range(2):
        for i, (_, source, dest, _) in enumerate(sets):
            here, there = pl.ds(g * count, count), pl.ds((1 - g) * count, count)
            sems = (send_sem.at[i, count - 1, g], recv_sem.at[i, count - 1, g])
            copies.append(_send(source.at[here], dest.at[there], *sems, {"pipe": 1 - core}))
    for copy in copies:
        copy.wait()
    for _, mine, theirs, dest in sets:

        @pl.when(core == group)
        def _(mine=mine, dest=dest):
            dest[...] = mine[...]

        @pl.when(core != group)
        def _(theirs=theirs, dest=dest):
            dest[...] = theirs[...]


def to_encoder(value, number, out=None, lse=None):
    count = lax.axis_size("tensor")
    _, rows, wide = value.shape
    shapes = [((2 * count, rows, wide), HALF)]
    if out is not None:
        shapes.append(((2 * count, 8, rows), WIDE))
    scratch = [pltpu.VMEM(*s) for s in shapes]
    if out is not None:
        scratch.append(pltpu.VMEM((2, 8, rows), WIDE))
    scratch += [pltpu.VMEM(*s) for s in shapes]
    whole = pl.BlockSpec(memory_space=pltpu.VMEM)
    operands = (value,) if out is None else (value, out, lse)
    return pl.pallas_call(
        partial(_to_encoder_kernel, count, out is not None),
        out_shape=[jax.ShapeDtypeStruct(*s) for s in shapes],
        in_specs=[whole] * len(operands),
        out_specs=[whole] * len(shapes),
        scratch_shapes=scratch + [pltpu.SemaphoreType.DMA((len(shapes), count, 2))] * 2,
        compiler_params=pltpu.CompilerParams(
            collective_id=number, has_side_effects=True, vmem_limit_bytes=VMEM_LIMIT
        ),
        cost_estimate=pl.CostEstimate(flops=0, transcendentals=0, bytes_accessed=60 << 20),
        name="to_encoder",
    )(*operands)


def _over_lanes(weights, wide):
    lanes = lax.broadcasted_iota(jnp.int32, (8, wide), 1) // HEAD
    pick = (lanes == lax.broadcasted_iota(jnp.int32, (8, wide), 0)).astype(HALF)
    high = weights.astype(HALF)
    low = (weights - high.astype(WIDE)).astype(HALF)
    return dot_ta(jnp.concatenate([high, low], axis=0), jnp.concatenate([pick, pick], axis=0))


def _to_decoder_kernel(count, *refs):
    part, lse, heads, out, out_lse = refs[:5]
    other, other_lse, both, both_lse, landed, landed_lse, send_sem, recv_sem = refs[5:]
    core, me = lax.axis_index("pipe"), lax.axis_index("tensor")
    top = count // 2
    chips = [lax.rem(me + s, count) for s in range(1, count)]
    _enter([{"tensor": chip} for chip in chips] + [{"pipe": 1 - core}])
    copies = []
    for g in range(2):
        here, there = pl.ds(g * count, count), pl.ds((1 - g) * count, count)
        for i, (source, dest) in enumerate(((part, other), (lse, other_lse))):
            sems = (send_sem.at[i, count - 1, g], recv_sem.at[i, count - 1, g])
            copies.append(_send(source.at[here], dest.at[there], *sems, {"pipe": 1 - core}))
    for copy in copies:
        copy.wait()
    wide = part.shape[2]
    for i in range(2 * count):
        first, second = lse[i], other_lse[i]
        peak = jnp.maximum(first, second)
        a, b = jnp.exp(first - peak), jnp.exp(second - peak)
        both_lse[i] = peak + jnp.log(a + b)
        share = _over_lanes(b / (a + b), wide)
        mine = part[i].astype(WIDE)
        both[i] = (mine + share * (other[i].astype(WIDE) - mine)).astype(HALF)
    copies = []
    for s, chip in enumerate(chips):
        place = _slot(_differ(chip, me, count), count)
        for h in range(2):
            at = lax.rem(h + core, 2) * count + place
            for i, (source, dest) in enumerate(((both, landed), (both_lse, landed_lse))):
                sems = (send_sem.at[i, s, h], recv_sem.at[i, s, h])
                copies.append(_send(source.at[at], dest.at[s, h], *sems, {"tensor": chip}))
    for copy in copies:
        copy.wait()
    for h in range(2):
        at = lax.rem(h + core, 2) * count
        terms = [(me, both[at], both_lse[at])]
        for s in range(count - 1):
            terms.append((lax.rem(me - s - 1 + count, count), landed[s, h], landed_lse[s, h]))
        logs = [jnp.where(chip // top == core, log, NEGATIVE) for chip, _, log in terms]
        peak = logs[0]
        for log in logs[1:]:
            peak = jnp.maximum(peak, log)
        weights = [jnp.exp(log - peak) for log in logs]
        weights = [
            jnp.where(chip // top == core, w, 0.0) for (chip, _, _), w in zip(terms, weights)
        ]
        total = sum(weights)
        out_lse[h] = peak + jnp.log(total)
        shares = [_over_lanes(w / total, wide) for w in weights]
        value = sum(c * term.astype(WIDE) for c, (_, term, _) in zip(shares, terms)) / sum(shares)
        out[h] = value
        heads[:, h * wide : (h + 1) * wide] = value.astype(HALF)


def to_decoder(part, lse, number):
    count = lax.axis_size("tensor")
    slots, rows, wide = part.shape
    whole = pl.BlockSpec(memory_space=pltpu.VMEM)
    return pl.pallas_call(
        partial(_to_decoder_kernel, count),
        out_shape=[
            jax.ShapeDtypeStruct((rows, 2 * wide), HALF),
            jax.ShapeDtypeStruct((2, rows, wide), WIDE),
            jax.ShapeDtypeStruct((2, 8, rows), WIDE),
        ],
        in_specs=[whole] * 2,
        out_specs=[whole] * 3,
        scratch_shapes=[
            pltpu.VMEM((slots, rows, wide), HALF),
            pltpu.VMEM((slots, 8, rows), WIDE),
            pltpu.VMEM((slots, rows, wide), HALF),
            pltpu.VMEM((slots, 8, rows), WIDE),
            pltpu.VMEM((count - 1, 2, rows, wide), HALF),
            pltpu.VMEM((count - 1, 2, 8, rows), WIDE),
        ]
        + [pltpu.SemaphoreType.DMA((2, count, 2))] * 2,
        compiler_params=pltpu.CompilerParams(
            collective_id=number, has_side_effects=True, vmem_limit_bytes=VMEM_LIMIT
        ),
        cost_estimate=pl.CostEstimate(flops=0, transcendentals=0, bytes_accessed=60 << 20),
        name="to_decoder",
    )(part, lse)


def to_pairs(value):
    slots, rows, wide = value.shape
    each = LANES // wide
    if each == 1:
        return value
    value = value.reshape(slots // each, each, rows, wide)
    return value.transpose(0, 2, 1, 3).reshape(slots // each, rows, LANES)


def from_pairs(value, wide):
    blocks, rows, _ = value.shape
    each = LANES // wide
    if each == 1:
        return value
    value = value.reshape(blocks, rows, each, wide)
    return value.transpose(0, 2, 1, 3).reshape(blocks * each, rows, wide)


def stats_to_pairs(stats, wide):
    each = LANES // wide
    if each == 1:
        return stats
    slots, _, rows = stats.shape
    stats = stats.reshape(slots // each, each, 8, rows)
    return jnp.concatenate(
        [stats[:, :, 0], stats[:, :, 2], jnp.zeros((slots // each, 4, rows), WIDE)], axis=1
    )


def stats_from_pairs(stats, wide):
    each = LANES // wide
    if each == 1:
        return stats
    blocks, _, rows = stats.shape
    value = stats[:, :each].reshape(blocks * each, 1, rows)
    return jnp.concatenate([value, jnp.zeros((blocks * each, 7, rows), WIDE)], axis=1)


def slot_bits():
    count = lax.axis_size("tensor")
    bits, bit = [count // 2], 1
    while bit < count // 2:
        bits.append(bit)
        bit *= 2
    return [b for b in bits if b > 0]


def in_column_halves(values):
    wide = values.shape[2] // 2
    return jnp.stack(
        [
            jnp.concatenate(
                [values[:, k, h * wide : (h + 1) * wide] for k in range(values.shape[1])], axis=1
            ).astype(HALF)
            for h in range(2)
        ]
    )


def _gather_kernel(bits, count, planes, *refs):
    own, refs = refs[:3], refs[3:]
    leaving, dec_rows, *refs = refs
    full, enc_cross, enc_ffn, *refs = refs
    dec, refs = refs[:3], refs[3:]
    rests, refs = refs[:2], refs[2:]
    coming, dec_full, send_sem, recv_sem, local_sem = refs
    core, place, me = lax.axis_index("pipe"), lax.axis_index("dp"), lax.axis_index("tensor")
    wide = own[0].shape[2]
    block = own[0].shape[1] // planes
    sibling = {"pipe": 1 - core}
    chips = {bit: {"tensor": _differ(me, bit, count)} for bit in bits}
    line = [{"tensor": _differ(me, s, count)} for s in range(1, count)]
    dp_bits = [1 << i for i in range(planes.bit_length() - 1)]
    others = {bit: {"dp": _differ(place, bit, planes)} for bit in dp_bits}
    _enter([sibling, *line, *others.values()])
    made = [0]

    def push(source, dest, peer):
        i = made[0]
        made[0] += 1
        return _send(source, dest, send_sem.at[i], recv_sem.at[i], peer)

    def rows_of(difference):
        return pl.ds(pl.multiple_of(_differ(place, difference, planes) * block, block), block)

    enc = [full.at[:, :, pl.ds(0, wide)], enc_cross, enc_ffn]
    shown = []
    for a in range(3):
        i = made[0]
        made[0] += 2
        shown.append(i)

        @pl.when(core == 0)
        def _(a=a, i=i):
            for h in range(2):
                _send(own[a].at[h], enc[a].at[1 - h], send_sem.at[i + h], recv_sem.at[i + h], sibling)
                pltpu.make_async_copy(own[a].at[h], enc[a].at[h], local_sem.at[a, h]).start()

        @pl.when(core == 1)
        def _(a=a, i=i):
            for h in range(2):
                _send(own[a].at[h], dec[a].at[h], send_sem.at[i + h], recv_sem.at[i + h], sibling)
                pltpu.make_async_copy(own[a].at[h], dec[a].at[h], local_sem.at[a, h]).start()

    def arrived(a):
        i = shown[a]
        for h in range(2):
            pltpu.make_async_copy(own[a].at[h], enc[a].at[h], local_sem.at[a, h]).wait()
            pltpu.make_async_copy(own[a].at[h], enc[a].at[h], recv_sem.at[i + h]).wait()

    def line_step(a, n, bit):
        here, size = rows_of(0), own[a].shape[2]
        if a == 0:
            source = full.at[0, here, pl.ds(0, n * size)]
            return [push(source, full.at[0, here, pl.ds(n * size, n * size)], chips[bit])]
        rest = rests[a - 1]
        copies = [
            push(enc[a].at[0, here], rest.at[:, pl.ds((n - 1) * size, size)], chips[bit])
        ]
        if n > 1:
            source = rest.at[:, pl.ds(0, (n - 1) * size)]
            copies.append(push(source, rest.at[:, pl.ds(n * size, (n - 1) * size)], chips[bit]))
        return copies

    def wait(copies):
        for copy in copies:
            copy.wait()

    def advance(chain):
        wait(chain["now"])
        chain["now"] = line_step(chain["array"], *chain["todo"].pop(0)) if chain["todo"] else []

    def columns(part):
        return pl.ds(wide + part * half, half)

    def plane_step(j):
        copies = []
        for part, order in enumerate(orders):
            for m in held[part]:
                at = full.at[0, rows_of(m), columns(part)]
                copies.append((part, m ^ order[j], push(at, at, others[order[j]])))
        return copies

    def share(part, m):
        here = rows_of(m)
        source = full.at[0, here, columns(part)]
        return push(source, full.at[1, here, columns(part)], sibling)

    steps = [(1 << i, bit) for i, bit in enumerate(bits)]
    for_attn, for_cross, for_ffn = [{"array": a, "todo": list(steps), "now": []} for a in range(3)]
    arrived(0)
    advance(for_attn)
    arrived(2)
    advance(for_attn)
    advance(for_ffn)
    while for_attn["now"]:
        advance(for_attn)
    token_sem = made[0]
    made[0] += 1

    @pl.when(core == 1)
    def _():
        _send(leaving, coming, send_sem.at[token_sem], recv_sem.at[token_sem], chips[bits[0]])

    at = pl.ds(pl.multiple_of(me * dec_rows.shape[0], dec_rows.shape[0]), dec_rows.shape[0])
    dec_full[at, :] = dec_rows[...]
    dec_sent = [push(dec_full.at[at], dec_full.at[at], peer) for peer in line]
    half = (count - 1) * wide // 2
    orders, held = (dp_bits, dp_bits[::-1]), ([0], [0])
    moving = plane_step(0)
    shared = [share(part, 0) for part in range(2)]
    advance(for_ffn)
    arrived(1)
    for j in range(len(dp_bits)):
        for _, _, copy in moving:
            copy.wait()
        for part, order in enumerate(orders):
            held[part].extend([m ^ order[j] for m in held[part]])
        following = plane_step(j + 1) if j + 1 < len(dp_bits) else []
        shared += [share(part, m) for part, m, _ in moving]
        moving = following
        advance(for_cross)
    while for_ffn["now"]:
        advance(for_ffn)
    while for_cross["now"]:
        advance(for_cross)

    @pl.when(core == 1)
    def _():
        pltpu.make_async_copy(leaving, leaving, send_sem.at[token_sem]).wait()
        pltpu.make_async_copy(leaving, coming, recv_sem.at[token_sem]).wait()

    wait(dec_sent)
    wait(shared)
    for a in range(3):
        for h in range(2):
            pltpu.make_async_copy(own[a].at[h], own[a].at[h], send_sem.at[shown[a] + h]).wait()


def gather_weights(attn, cross, ffn, leaving, dec_rows):
    own = (attn, cross, ffn)
    count, planes = lax.axis_size("tensor"), lax.axis_size("dp")
    depth = attn.shape[1]
    shapes = [(2, depth, count * attn.shape[2]), cross.shape, ffn.shape]
    shapes += [v.shape for v in own]
    shapes += [(depth // planes, (count - 1) * v.shape[2]) for v in (cross, ffn)]
    shapes += [leaving.shape, (count * dec_rows.shape[0], dec_rows.shape[1])]
    hbm, vmem = pl.BlockSpec(memory_space=pl.ANY), pl.BlockSpec(memory_space=pltpu.VMEM)
    return pl.pallas_call(
        partial(_gather_kernel, slot_bits(), count, planes),
        out_shape=[jax.ShapeDtypeStruct(shape, HALF) for shape in shapes],
        in_specs=[vmem] * 3 + [hbm, vmem],
        out_specs=[hbm] * (len(shapes) - 1) + [vmem],
        scratch_shapes=[pltpu.SemaphoreType.DMA((64,))] * 2 + [pltpu.SemaphoreType.DMA((3, 2))],
        compiler_params=pltpu.CompilerParams(
            collective_id=9, has_side_effects=True, vmem_limit_bytes=VMEM_LIMIT
        ),
        cost_estimate=pl.CostEstimate(flops=0, transcendentals=0, bytes_accessed=280 << 20),
        name="gather_weights",
    )(*own, leaving, dec_rows)


def gather_planes(rest):
    return lax.all_gather(rest, "dp", axis=0, tiled=True)


def fold_cores(mine, other):
    return (mine.astype(WIDE) + swap(other, "pipe", 1).astype(WIDE)).astype(HALF)


def fold_planes(term):
    return lax.psum_scatter(term, "dp", scatter_dimension=0, tiled=True)


def scatter_local(terms):
    core = lax.axis_index("pipe")
    wide = terms[0].shape[1] // 2
    pick = partial(lax.dynamic_slice_in_dim, slice_size=wide, axis=1)
    mine = jnp.concatenate([pick(v.astype(HALF), core * wide) for v in terms], axis=1)
    other = jnp.concatenate([pick(v.astype(HALF), (1 - core) * wide) for v in terms], axis=1)
    term = fold_cores(mine, other)
    return fold_planes(term), term


def _blocks_of(weights, kinds):
    wide = weights.shape[2] // (lax.axis_size("tensor") * kinds)
    each = LANES // wide
    blocks = lax.axis_size("tensor") // each
    spec = pl.BlockSpec(
        (None, weights.shape[1], each * kinds * wide), lambda i: (i // blocks, 0, lax.rem(i, blocks))
    )
    return wide, each, blocks, spec


def _piece(weights, kinds, wide, each, k):
    parts = [weights[:, (j * kinds + k) * wide : (j * kinds + k + 1) * wide] for j in range(each)]
    return parts[0] if each == 1 else jnp.concatenate(parts, axis=1)


def _store_grads(refs, i, blocks, pieces, wide, each):
    columns = [p[:, j * wide : (j + 1) * wide] for j in range(each) for p in pieces]
    for ref, when in zip(refs, (i < blocks, i >= blocks)):

        @pl.when(when)
        def _(ref=ref):
            for n, column in enumerate(columns):
                ref[:, n * wide : (n + 1) * wide] = column.astype(ref.dtype)


def _grad_specs(depth, columns, blocks):
    return [
        pl.BlockSpec((depth, columns), lambda i: (0, jnp.minimum(i, blocks - 1))),
        pl.BlockSpec((depth, columns), lambda i: (0, jnp.maximum(i - blocks, 0))),
    ]


def _spread_kernel(kinds, use, wide, each, blocks, with_grad, pair, x, weights, *refs):
    left = x[...]
    values = [dot(left, _piece(weights, kinds, wide, each, k)) for k in use]
    if with_grad:
        y, *refs = refs
        i = pl.program_id(0)
        _store_grads(refs[-2:], i, blocks, [dot_ta(left, y[...].astype(HALF))], wide, each)
    for n in range(pair):
        ref = refs[len(refs) - pair + n]

        @pl.when(lax.rem(pl.program_id(0), pair) == n)
        def _(ref=ref):
            ref[0] = values[-2].astype(HALF)
            ref[1] = values[-1].astype(HALF)

    values = values[:-2] if pair else values
    for ref, value in zip(refs, values):
        ref[...] = value.astype(HALF)


def spread(x, weights, kinds, use, y=None, pair=0):
    rows, width = x.shape
    wide, each, blocks, spec = _blocks_of(weights, kinds)
    column = pl.BlockSpec((rows, LANES), lambda i: (0, i))
    single = len(use) - (2 if pair else 0)
    shapes, specs = [((rows, width), HALF)] * single, [column] * single
    for _ in range(pair):
        shapes.append(((2, rows, width // pair), HALF))
        specs.append(pl.BlockSpec((2, rows, LANES), lambda i: (0, 0, i // pair)))
    if y is not None:
        shapes += [((width, width // 2), HALF)] * 2
        specs += _grad_specs(width, LANES, blocks)
    return pl.pallas_call(
        partial(_spread_kernel, kinds, use, wide, each, blocks, y is not None, pair),
        out_shape=[jax.ShapeDtypeStruct(*s) for s in shapes],
        grid=(2 * blocks,),
        in_specs=[pl.BlockSpec((rows, width), lambda i: (0, 0)), spec] + [column] * (y is not None),
        out_specs=specs,
        compiler_params=pltpu.CompilerParams(vmem_limit_bytes=VMEM_LIMIT),
        cost_estimate=pl.CostEstimate(
            flops=8 * rows * width * width * (len(use) + (y is not None)),
            transcendentals=0,
            bytes_accessed=2 * width * width * kinds,
        ),
        name="spread",
    )(x, weights, *([] if y is None else [y]))


def _collect_kernel(kinds, use, wide, each, blocks, n_y, split, with_grad, ending, n_extra, *refs):
    refs = list(refs)
    ys, refs = refs[:n_y], refs[n_y:]
    weights, refs = refs[0], refs[1:]
    x = refs.pop(0) if with_grad else None
    extra, refs = refs[:n_extra], refs[n_extra:]
    acc = refs.pop()
    grads = [refs.pop(), refs.pop()][::-1] if with_grad else []
    i = pl.program_id(0)

    @pl.when(i == 0)
    def _():
        acc[...] = jnp.zeros(acc.shape, WIDE)

    values, ys = [], list(ys)
    while ys:
        y = ys.pop(0)
        if len(y.shape) == 2:
            values.append(y[...])
        elif split:
            odd = ys.pop(0)
            values += [jnp.where(lax.rem(i, 2) == 0, y[n], odd[n]) for n in range(2)]
        else:
            values += [y[0], y[1]]
    values = [v.astype(HALF) for v in values]
    for value, k in zip(values, use):
        acc[...] += dot_bt(value, _piece(weights, kinds, wide, each, k))
    if with_grad:
        left = x[...]
        _store_grads(grads, i, blocks, [dot_ta(left, v) for v in values], wide, each)

    @pl.when(i == 2 * blocks - 1)
    def _():
        ending(acc[...], extra, refs)


def collect(ys, weights, kinds, use, ending, extra, outs, x=None):
    rows, width = ys[0].shape[-2], weights.shape[1]
    split = any(y.ndim == 3 and y.shape[2] < width for y in ys)
    wide, each, blocks, spec = _blocks_of(weights, kinds)
    y_specs = [
        pl.BlockSpec((rows, LANES), lambda i: (0, i))
        if y.ndim == 2
        else pl.BlockSpec((2, rows, LANES), lambda i: (0, 0, i // (2 if split else 1)))
        for y in ys
    ]
    fixed = [pl.BlockSpec(v.shape, lambda i: (0, 0)) for v in ([] if x is None else [x]) + extra]
    shapes = list(outs)
    specs = [pl.BlockSpec(shape, lambda i: (0, 0)) for shape, _ in outs]
    if x is not None:
        shapes += [((width, len(use) * width // 2), HALF)] * 2
        specs += _grad_specs(width, len(use) * LANES, blocks)
    return pl.pallas_call(
        partial(
            _collect_kernel, kinds, use, wide, each, blocks, len(ys), split, x is not None, ending, len(extra)
        ),
        out_shape=[jax.ShapeDtypeStruct(*s) for s in shapes],
        grid=(2 * blocks,),
        in_specs=y_specs + [spec] + fixed,
        out_specs=specs,
        scratch_shapes=[pltpu.VMEM((rows, width), WIDE)],
        compiler_params=pltpu.CompilerParams(vmem_limit_bytes=VMEM_LIMIT),
        cost_estimate=pl.CostEstimate(
            flops=8 * rows * width * width * len(use) * (1 + (x is not None)),
            transcendentals=0,
            bytes_accessed=2 * width * width * kinds,
        ),
        name="collect",
    )(*ys, weights, *([] if x is None else [x]), *extra)


def _end_norm(total, ins, outs):
    resid, gain, bias = ins
    value, normed, inv_scale = _norm_rows(total + resid[...], gain[...], bias[...])
    outs[0][...] = value
    outs[1][...] = value.astype(HALF)
    outs[2][...] = normed
    outs[3][...] = jnp.broadcast_to(inv_scale, outs[3].shape)


def _end_norm_back(total, ins, outs):
    *resid, normed, inv_scale, gain = ins
    total = total + resid[0][...] if resid else total
    grad, grad_gain, grad_bias = _norm_rows_back(total, normed[...], inv_scale[:, 0:1], gain[...])
    outs[0][...] = grad
    outs[1][...] = grad.astype(HALF)
    outs[2][0:1, :] = grad_gain
    outs[2][1:2, :] = grad_bias


def _ffn_parts(count, own, mine, other):
    depth, wide = own.shape[1], own.shape[2] // 2
    specs = []
    for k in range(2):
        specs.append(pl.BlockSpec((None, depth, wide), lambda i, k=k: (i // count, 0, k)))
        for first in (0, count):
            specs.append(
                pl.BlockSpec(
                    (depth, wide),
                    lambda i, k=k, first=first: (0, 2 * jnp.clip(i - first - 1, 0, count - 2) + k),
                )
            )
    return wide, specs


def _ffn_cases(count, i, ins, outs):
    local = lax.rem(i, count) == 0
    return [
        (local, ins[0], outs[0]),
        (jnp.logical_and(~local, i < count), ins[1], outs[1]),
        (jnp.logical_and(~local, i > count), ins[2], outs[2]),
    ]


def _ffn_kernel(count, x, resid, gain, bias, *refs):
    ins, outs, refs = refs[:3], refs[3:6], refs[6:]
    value, value_low, normed, inv_scale, active, slope, acc = refs
    i = pl.program_id(0)

    @pl.when(i == 0)
    def _():
        acc[...] = jnp.zeros(acc.shape, WIDE)

    for condition, first, second in _ffn_cases(count, i, ins, outs):

        @pl.when(condition)
        def _(first=first, second=second):
            hidden = dot(x[...], first[...])
            below = 0.5 * (1.0 + lax.erf(hidden * (2.0**-0.5)))
            density = jnp.exp(-0.5 * hidden * hidden) * 0.3989422804014327
            act = (hidden * below).astype(HALF)
            active[...] = act
            slope[...] = (below + hidden * density).astype(HALF)
            acc[...] += dot_bt(act, second[...])

    @pl.when(i == 2 * count - 1)
    def _():
        _end_norm(acc[...], (resid, gain, bias), (value, value_low, normed, inv_scale))


def feed_forward(x, resid, gain, bias, own, mine, other):
    count = lax.axis_size("tensor")
    rows, width = x.shape
    wide, specs = _ffn_parts(count, own, mine, other)
    units = 2 * count * wide
    fixed = [pl.BlockSpec(v.shape, lambda i: (0, 0)) for v in (x, resid, gain, bias)]
    shapes = [((rows, width), WIDE), ((rows, width), HALF), ((rows, width), WIDE), ((rows, LANES), WIDE)]
    column = pl.BlockSpec((rows, wide), lambda i: (0, i))
    return pl.pallas_call(
        partial(_ffn_kernel, count),
        out_shape=[jax.ShapeDtypeStruct(*s) for s in shapes]
        + [jax.ShapeDtypeStruct((rows, units), HALF)] * 2,
        grid=(2 * count,),
        in_specs=fixed + specs,
        out_specs=[pl.BlockSpec(s, lambda i: (0, 0)) for s, _ in shapes] + [column] * 2,
        scratch_shapes=[pltpu.VMEM((rows, width), WIDE)],
        compiler_params=pltpu.CompilerParams(vmem_limit_bytes=VMEM_LIMIT),
        cost_estimate=pl.CostEstimate(
            flops=12 * rows * width * units, transcendentals=2 * rows * units, bytes_accessed=4 * width * units
        ),
        name="feed_forward",
    )(x, resid, gain, bias, own, mine, other, own, mine, other)


def _ffn_back_kernel(count, x, grad, resid, normed, inv_scale, gain, active, slope, *refs):
    ins, outs, refs = refs[:3], refs[3:6], refs[6:]
    result, result_low, terms, *grads, acc = refs
    i = pl.program_id(0)

    @pl.when(i == 0)
    def _():
        acc[...] = jnp.zeros(acc.shape, WIDE)

    for condition, first, second in _ffn_cases(count, i, ins, outs):

        @pl.when(condition)
        def _(first=first, second=second):
            hidden = (dot(grad[...], second[...]) * slope[...].astype(WIDE)).astype(HALF)
            acc[...] += dot_bt(hidden, first[...])
            f1 = dot_ta(x[...], hidden).astype(HALF)
            f2 = dot_ta(grad[...], active[...]).astype(HALF)
            for half, when in enumerate((i < count, i >= count)):

                @pl.when(when)
                def _(half=half):
                    grads[half][...] = f1
                    grads[2 + half][...] = f2

    @pl.when(i == 2 * count - 1)
    def _():
        _end_norm_back(acc[...], (resid, normed, inv_scale, gain), (result, result_low, terms))


def feed_forward_back(x, grad, resid, normed, inv_scale, gain, active, slope, own, mine, other):
    count = lax.axis_size("tensor")
    rows, width = x.shape
    wide, specs = _ffn_parts(count, own, mine, other)
    column = pl.BlockSpec((rows, wide), lambda i: (0, i))
    fixed = [pl.BlockSpec(v.shape, lambda i: (0, 0)) for v in (x, grad, resid, normed, inv_scale, gain)]
    shapes = [((rows, width), WIDE), ((rows, width), HALF), ((8, width), WIDE)]
    grad_specs = [
        pl.BlockSpec((width, wide), lambda i: (0, jnp.minimum(i, count - 1))),
        pl.BlockSpec((width, wide), lambda i: (0, jnp.maximum(i - count, 0))),
    ]
    return pl.pallas_call(
        partial(_ffn_back_kernel, count),
        out_shape=[jax.ShapeDtypeStruct(*s) for s in shapes]
        + [jax.ShapeDtypeStruct((width, count * wide), HALF)] * 4,
        grid=(2 * count,),
        in_specs=fixed + [column] * 2 + specs,
        out_specs=[pl.BlockSpec(s, lambda i: (0, 0)) for s, _ in shapes] + grad_specs * 2,
        scratch_shapes=[pltpu.VMEM((rows, width), WIDE)],
        compiler_params=pltpu.CompilerParams(vmem_limit_bytes=VMEM_LIMIT),
        cost_estimate=pl.CostEstimate(
            flops=32 * rows * width * count * wide, transcendentals=0, bytes_accessed=16 * width * count * wide
        ),
        name="feed_forward_back",
    )(x, grad, resid, normed, inv_scale, gain, active, slope, own, mine, other, own, mine, other)


def _add_rows(dest, first, second):
    rows = 64 if dest.shape[0] % 64 == 0 else dest.shape[0]

    def step(i, carry):
        at = pl.ds(pl.multiple_of(i * rows, rows), rows)
        dest[at, :] = (first[at, :].astype(WIDE) + second[at, :].astype(WIDE)).astype(HALF)
        return carry

    lax.fori_loop(0, dest.shape[0] // rows, step, 0)


def _finish_kernel(bits, count, planes, *refs):
    in_mine, out_mine, in_other, out_other, f1, f2, ckv, dec_ffn, dec_small, tokens = refs[:10]
    norm_terms, refs = refs[10:16], refs[16:]
    attn_out, cross_out, ffn_out, far, near, norm_sum = refs[:6]
    land_in, land_out, term, *refs = refs[6:]
    n_steps = planes.bit_length() - 1
    land_planes, refs = refs[:n_steps], refs[n_steps:]
    folded, landed, refs = refs[:4], refs[4:8], refs[8:]
    enc_ffn, enc_small, got_ffn, got_small, norm_other, norm_land, send_sem, recv_sem = refs
    core, place, me = lax.axis_index("pipe"), lax.axis_index("dp"), lax.axis_index("tensor")
    sibling = {"pipe": 1 - core}
    line = {s: {"tensor": _differ(me, s, count)} for s in range(1, count)}
    cross_over = {"pipe": 1 - core, "tensor": _differ(me, bits[0], count)}
    dp_bits = [1 << i for i in range(n_steps)]
    others = {bit: {"dp": _differ(place, bit, planes)} for bit in dp_bits}
    _enter([sibling, cross_over, *line.values(), *others.values()])
    made = [0]

    def number():
        made[0] += 1
        return made[0] - 1

    def push(source, dest, peer):
        i = number()
        return _send(source, dest, send_sem.at[i], recv_sem.at[i], peer)

    def wait(copies):
        for copy in copies:
            copy.wait()

    for i in range(3):
        at = slice(2 * i, 2 * i + 2)
        enc, dec = norm_terms[i][0:2, :], norm_terms[3 + i][0:2, :]
        norm_sum[at, :] = jnp.where(core == 0, enc, dec)
        norm_other[at, :] = jnp.where(core == 0, dec, enc)
    norm_sum[6:8, :] = jnp.zeros((2, norm_sum.shape[1]), WIDE)
    norm_other[6:8, :] = jnp.zeros((2, norm_sum.shape[1]), WIDE)
    norm_peers = [*others.values(), *(line[bit] for bit in bits)]
    norm_now = [push(norm_other, norm_land.at[0], sibling)]

    def advance_norms():
        if norm_now:
            norm_now.pop().wait()
            n = n_steps + len(bits) - len(norm_peers)
            norm_sum[...] = norm_sum[...] + norm_land[n]
            if norm_peers:
                norm_now.append(push(norm_sum, norm_land.at[n + 1], norm_peers.pop(0)))

    to_core = [push(in_other, land_in, sibling), push(out_other, land_out, sibling)]

    def chain(source, a, at=slice(None)):
        fold, land = (v if at == slice(None) else v.at[at] for v in (folded[a], landed[a]))
        size = folded[a].shape[1] * 2 // count
        return {
            "source": source,
            "fold": fold,
            "land": land,
            "size": size,
            "slots": count,
            "bits": list(reversed(bits)),
            "now": [],
        }

    def advance(c):
        land, size = c["land"], c["size"]
        if c["now"]:
            wait(c["now"])
            c["now"] = []
            kept = c["slots"] // 2 * size
            offset = (count - c["slots"]) * size
            at = pl.ds(0, kept)
            _add_rows(c["fold"].at[:, at], c["source"].at[:, at], land.at[:, pl.ds(offset, kept)])
            c["source"], c["slots"] = c["fold"], c["slots"] // 2
        if c["bits"]:
            kept = c["slots"] // 2 * size
            offset = (count - c["slots"]) * size
            source = c["source"].at[:, pl.ds(kept, kept)]
            c["now"] = [push(source, land.at[:, pl.ds(offset, kept)], line[c["bits"].pop(0)])]

    chains = [chain(f2, 0), chain(f1, 1), chain(ckv, 2)]
    advance(chains[0])

    half = tokens.shape[1] // 2
    far_sem, near_sem, same_sem = number(), number(), number()

    @pl.when(core == 1)
    def _():
        _send(tokens.at[:, pl.ds(0, half)], far, send_sem.at[far_sem], recv_sem.at[far_sem], cross_over)
        _send(
            tokens.at[:, pl.ds(half, half)], far, send_sem.at[same_sem], recv_sem.at[far_sem], line[bits[0]]
        )

    @pl.when(core == 0)
    def _():
        _send(tokens.at[:, pl.ds(half, half)], near, send_sem.at[near_sem], recv_sem.at[near_sem], sibling)

    wait(to_core)
    block = in_mine.shape[0] // planes
    wide = term.shape[1] // count
    inner = in_mine.shape[1] // count

    def sum_step(i, carry):
        at = pl.ds(pl.multiple_of(i * 64, 64), 64)
        for s in range(count):
            first = in_mine[at, s * inner : (s + 1) * inner].astype(WIDE)
            second = land_in[at, s * inner : (s + 1) * inner].astype(WIDE)
            term[at, s * wide : s * wide + inner] = (first + second).astype(HALF)
            outer = wide - inner
            first = out_mine[at, s * outer : (s + 1) * outer].astype(WIDE)
            second = land_out[at, s * outer : (s + 1) * outer].astype(WIDE)
            term[at, s * wide + inner : (s + 1) * wide] = (first + second).astype(HALF)
        return carry

    lax.fori_loop(0, in_mine.shape[0] // 64, sum_step, 0)

    columns = term.shape[1] // 2
    orders = (dp_bits, dp_bits[::-1])
    held = [[list(range(planes)) for _ in orders] for _ in range(2)]
    piece = block // 2

    def rows_of(difference, r):
        first = _differ(place, difference, planes) * block + r * piece
        return pl.ds(pl.multiple_of(first, piece), piece)

    def at_of(p, m, r):
        return term.at[rows_of(m, r), pl.ds(p * columns, columns)]

    def plane_start(j, r):
        copies = []
        for p, order in enumerate(orders):
            bit = order[j]
            kept = [m for m in held[r][p] if not m & bit]
            for n, m in enumerate(kept):
                dest = land_planes[j].at[p, n, pl.ds(r * piece, piece)]
                copies.append((p, m, dest, push(at_of(p, m ^ bit, r), dest, others[bit])))
            held[r][p] = kept
        return copies

    def plane_finish(copies, r):
        for p, m, dest, copy in copies:
            copy.wait()
            _add_rows(at_of(p, m, r), at_of(p, m, r), dest)

    moving = [plane_start(0, r) for r in range(2)]
    for_attn = []
    for j in range(n_steps):
        for r in range(2):
            advance(chains[min(2 * j + r, 2)])
            advance_norms()
            plane_finish(moving[r], r)
            if j + 1 < n_steps:
                moving[r] = plane_start(j + 1, r)
            else:
                for_attn.append(chain(term.at[rows_of(0, r)], 3, pl.ds(r * piece, piece)))
                advance(for_attn[-1])
    while any(c["now"] or c["bits"] for c in chains + for_attn):
        for c in for_attn + chains:
            advance(c)
        advance_norms()
    while norm_now:
        advance_norms()

    size = [fold.shape[1] * 2 // count for fold in folded]
    enc_ffn[:, : size[1]] = folded[1][:, : size[1]]
    enc_ffn[:, size[1] :] = folded[0][:, : size[0]]
    enc_small[:, : size[3]] = folded[3][:, : size[3]]
    enc_small[:, size[3] :] = folded[2][:, : size[2]]
    swap_sem = [number(), number()]

    @pl.when(core == 0)
    def _():
        _send(dec_ffn, got_ffn, send_sem.at[swap_sem[0]], recv_sem.at[swap_sem[0]], sibling)
        _send(dec_small, got_small, send_sem.at[swap_sem[1]], recv_sem.at[swap_sem[1]], sibling)

    @pl.when(core == 1)
    def _():
        _send(enc_ffn, got_ffn, send_sem.at[swap_sem[0]], recv_sem.at[swap_sem[0]], sibling)
        _send(enc_small, got_small, send_sem.at[swap_sem[1]], recv_sem.at[swap_sem[1]], sibling)

    for i, (mine, got) in enumerate(((enc_ffn, got_ffn), (enc_small, got_small))):
        pltpu.make_async_copy(mine, got, send_sem.at[swap_sem[i]]).wait()
        pltpu.make_async_copy(mine, got, recv_sem.at[swap_sem[i]]).wait()

    def write(first, second):
        for h, (ffn, small) in enumerate((first, second)):
            c = ffn.shape[1] // 2
            for k in range(2):
                ffn_out[k, :, h * c : (h + 1) * c] = ffn[:, k * c : (k + 1) * c].astype(WIDE)
            c = small.shape[1] // 6
            for k in range(6):
                dest = attn_out.at[k] if k < 4 else cross_out.at[k - 4]
                dest[:, h * c : (h + 1) * c] = small[:, k * c : (k + 1) * c].astype(WIDE)

    @pl.when(core == 0)
    def _():
        write((enc_ffn, enc_small), (got_ffn, got_small))

    @pl.when(core == 1)
    def _():
        write((got_ffn, got_small), (dec_ffn, dec_small))

    pltpu.make_async_copy(far, far, recv_sem.at[far_sem]).wait()

    @pl.when(core == 1)
    def _():
        pltpu.make_async_copy(far, far, send_sem.at[far_sem]).wait()
        pltpu.make_async_copy(far, far, send_sem.at[same_sem]).wait()
        pltpu.make_async_copy(near, near, recv_sem.at[near_sem]).wait()

    @pl.when(core == 0)
    def _():
        pltpu.make_async_copy(near, near, send_sem.at[near_sem]).wait()


def finish(in_grads, out_grads, f1, f2, ckv, dec_ffn, dec_small, tokens, norm_terms):
    count, planes = lax.axis_size("tensor"), lax.axis_size("dp")
    depth = in_grads[0].shape[0]
    rows = depth // planes
    attn_columns = in_grads[0].shape[1] + out_grads[0].shape[1]
    wide = 2 * dec_small.shape[1] // 6
    vmem = pl.BlockSpec(memory_space=pltpu.VMEM)
    operands = (in_grads[0], out_grads[0], in_grads[1], out_grads[1], f1, f2, ckv, dec_ffn, dec_small, tokens)
    operands += tuple(norm_terms)
    lines = [f2.shape[1], f1.shape[1], ckv.shape[1], attn_columns]
    scratch = [in_grads[0].shape, out_grads[0].shape, (depth, attn_columns)]
    blocks = planes // 2
    while blocks >= 1:
        scratch.append((2, blocks, rows, attn_columns // 2))
        blocks //= 2
    scratch += [(rows, c // 2) for c in lines]
    scratch += [(rows, c - c // count) for c in lines]
    scratch += [dec_ffn.shape, dec_small.shape] * 2
    norm_steps = count.bit_length() + planes.bit_length() - 1
    norm_shapes = [norm_terms[0].shape, (norm_steps, *norm_terms[0].shape)]
    token_piece = ((tokens.shape[0], tokens.shape[1] // 2), HALF)
    outs = [((4, rows, wide), WIDE), ((2, rows, wide), WIDE), ((2, rows, dec_ffn.shape[1]), WIDE)]
    outs += [token_piece, token_piece, (norm_terms[0].shape, WIDE)]
    return pl.pallas_call(
        partial(_finish_kernel, slot_bits(), count, planes),
        out_shape=[jax.ShapeDtypeStruct(*o) for o in outs],
        in_specs=[vmem] * len(operands),
        out_specs=[vmem] * len(outs),
        scratch_shapes=[pltpu.VMEM(shape, HALF) for shape in scratch]
        + [pltpu.VMEM(shape, WIDE) for shape in norm_shapes]
        + [pltpu.SemaphoreType.DMA((64,))] * 2,
        compiler_params=pltpu.CompilerParams(
            collective_id=5, has_side_effects=True, vmem_limit_bytes=VMEM_LIMIT
        ),
        cost_estimate=pl.CostEstimate(flops=0, transcendentals=0, bytes_accessed=200 << 20),
        name="finish",
    )(*operands)


def per_device(
    enc_input,
    dec_input,
    dec_cotangent,
    enc_lengths,
    dec_lengths,
    attn_weights,
    cross_weights,
    ffn_weights,
    norm_gains,
    norm_biases,
):
    core, place = lax.axis_index("pipe"), lax.axis_index("tensor")
    count = lax.axis_size("tensor")
    top_bit = count // 2
    group = place // top_bit
    block = jnp.where(core == 0, place, place ^ top_bit)
    span, width = enc_input.shape[1:]
    dec_span = dec_input.shape[1]
    local_width = attn_weights.shape[3]
    is_first = core == 0
    chips = range(count)
    sources = [(s // top_bit, s % top_bit) for s in range(2 * top_bit)]
    half = width // 2
    half_local = local_width // 2

    def owner(t):
        return t // top_bit

    norms = jnp.concatenate([norm_gains[0], norm_biases[0]], axis=0)
    norms_other = swap(norms, "pipe", 1)
    enc_norms = jnp.where(is_first, norms, norms_other)
    dec_norms = jnp.where(is_first, norms_other, norms)
    eg, eb, dg, db = enc_norms[:3], enc_norms[3:], dec_norms[:3], dec_norms[3:]

    pick = partial(lax.dynamic_index_in_dim, index=core, axis=0, keepdims=False)
    start_low = pick(dec_input)
    (
        w_attn,
        own_cross,
        own_ffn,
        dec_attn_halves,
        dec_cross_halves,
        dec_ffn_halves,
        cross_rest,
        ffn_rest,
        got,
        start_full,
    ) = gather_weights(
        *[in_column_halves(v[0]) for v in (after(attn_weights, norms_other), cross_weights, ffn_weights)],
        lax.dynamic_index_in_dim(enc_input, 1 - group, 0, False),
        start_low,
    )
    kept = lax.dynamic_index_in_dim(enc_input, group, 0, False)
    tokens = jnp.where(is_first, kept, got).astype(WIDE)
    mine_ffn = gather_planes(ffn_rest)

    def natural(halves, kinds):
        wide = halves.shape[2] // kinds
        return [
            jnp.concatenate([halves[h][:, k * wide : (k + 1) * wide] for h in range(2)], axis=1)
            for k in range(kinds)
        ]

    dec_attn, dec_cross, dec_ffn = [
        natural(v, k) for v, k in ((dec_attn_halves, 4), (dec_cross_halves, 2), (dec_ffn_halves, 2))
    ]
    blocks = width // LANES
    masks = [a * (blocks // 2) + c * (blocks // 2 // top_bit) for a, c in sources]

    def gain_of(i):
        return enc_norms[i : i + 1]

    def bias_of(i):
        return enc_norms[3 + i : 4 + i]

    embed, start_normed, start_scale = norm_forward(tokens, eg[0], eb[0])
    start_scale = jnp.broadcast_to(start_scale, (span, LANES))
    embed_low = embed.astype(HALF)
    parts = 2 if all(m % 2 == 0 for m in masks) else 1
    query, *key_value = spread(embed_low, w_attn, 4, (0, 1, 2), pair=parts)

    def across_chips(value):
        held, bit = [value], 1
        while bit < top_bit:
            held = held + [swap(v, "tensor", bit) for v in held]
            bit *= 2
        return held

    def exchange(held, *earlier):
        if earlier:
            held = after(tuple(held), *earlier)
        return list(held) + [swap(v, "pipe", 1) for v in held]

    key_values = [across_chips(v) for v in key_value]
    mine_cross = gather_planes(after(cross_rest, query))

    enc_lengths, dec_lengths = [after(v, query) for v in (enc_lengths, dec_lengths)]
    enc_row = lax.dynamic_index_in_dim(enc_lengths, group, 0, False)
    dec_row_of_group = lax.dynamic_index_in_dim(dec_lengths, group, 0, False)
    dec_row = lax.dynamic_index_in_dim(dec_lengths, core, 0, False)
    spots = jnp.arange(span, dtype=jnp.int32)
    own_seg = table_of(block * span + spots, enc_row)
    key_seg = jnp.stack(
        [table_of((block ^ (a * top_bit) ^ c) * span + spots, enc_row) for a, c in sources]
    )
    dec_spots = jnp.arange(dec_span * count, dtype=jnp.int32)
    dec_seg = table_of(dec_spots, dec_row)
    enc_segs = tables(own_seg, key_seg)
    dec_segs = tables(dec_seg, dec_seg[None])
    cross_segs = tables(table_of(dec_spots, dec_row_of_group), own_seg[None])

    start_full = after(start_full, key_value)
    start = start_low.astype(WIDE)
    rows_full = dec_span * count
    wide_rows = ((dec_span, width), WIDE)
    kept_rows = [wide_rows, wide_rows, ((dec_span, LANES), WIDE)]
    norm_terms = ((8, width), WIDE)
    dec_in_w = [dec_attn[k] for k in range(3)]
    dec_query = dot(start_full, dec_in_w[0]).astype(HALF)
    dec_kv = jnp.stack([dot(start_full, w).astype(HALF) for w in dec_in_w[1:]])
    dec_heads_wide, dec_lse = attend(dec_query, [dec_kv], dec_segs, [0], True)
    dec_heads = dec_heads_wide.astype(HALF)
    term = dot_bt(dec_heads, dec_attn[3]).astype(HALF)

    attended = ()
    for n in range(parts):
        key_values[n] = exchange(key_values[n], *attended, *((term,) if n else ()))
        attended = attend(
            query, key_values[n], enc_segs, masks, part=n if parts == 2 else None, into=attended
        )
    heads_wide, lse = attended

    def sum_to_owner(term, resid, *earlier):
        total = after(resid, *earlier)
        for s in range(count):
            rows = lax.dynamic_slice_in_dim(term, (place ^ s) * dec_span, dec_span, 0)
            total = total + (swap(rows, "tensor", s) if s else rows).astype(WIDE)
        return total

    self_norm, self_normed, self_scale = norm_forward(sum_to_owner(term, start, lse), dg[0:1], db[0:1])
    self_scale = jnp.broadcast_to(self_scale, (dec_span, LANES))
    self_low = self_norm.astype(HALF)
    self_rows = [swap(self_low, "tensor", s) if s else self_low for s in range(count)]

    heads = heads_wide.astype(HALF)
    mine_ffn = after(mine_ffn, heads_wide)
    other_ffn = swap(mine_ffn, "pipe", 1)
    mine_cross = after(mine_cross, other_ffn)
    w_cross = jnp.stack(
        [
            jnp.concatenate([own_cross[0], mine_cross], axis=1),
            jnp.concatenate([own_cross[1], swap(mine_cross, "pipe", 1)], axis=1),
        ]
    )
    kept_tokens = [((span, width), WIDE), ((span, width), HALF), ((span, width), WIDE), ((span, LANES), WIDE)]
    attn_norm, attn_norm_low, attn_normed, attn_scale = collect(
        [heads], w_attn, 4, (3,), _end_norm, [embed, gain_of(1), bias_of(1)], kept_tokens
    )
    _, memory_low, mem_normed, mem_scale, active, slope = feed_forward(
        attn_norm_low, attn_norm, gain_of(2), bias_of(2), own_ffn, mine_ffn, other_ffn
    )
    self_full = after(jnp.zeros((rows_full, width), HALF), mem_scale)
    for s in range(count):
        self_full = lax.dynamic_update_slice_in_dim(self_full, self_rows[s], (place ^ s) * dec_span, 0)
    cross_query = dot(self_full, dec_cross[0]).astype(HALF)

    def in_halves(value):
        return jnp.stack([value[:, :half_local], value[:, half_local:]])

    [cross_q_enc] = to_encoder(in_halves(cross_query), 6)
    cross_q_enc = to_pairs(cross_q_enc)

    [cross_kv] = spread(memory_low, w_cross, 2, (0, 1), pair=1)

    tables_of_keys = enc_lengths.shape[1]
    at_table = (own_seg[:, None] == jnp.arange(tables_of_keys)[None]).astype(HALF)
    sums = dot_ta(at_table, cross_kv[0])
    bit = 1
    while bit < top_bit:
        sums = sums + swap_columns(sums, "tensor", bit, masks[bit])
        bit *= 2
    sums = sums + swap_columns(sums, "pipe", 1, masks[top_bit])
    means = sums / enc_row.astype(WIDE)[:, None]
    centers = sum(
        jnp.where((own_seg == j)[:, None], means[j : j + 1], 0.0) for j in range(tables_of_keys)
    )
    centered = (cross_kv[0].astype(WIDE) - centers).astype(HALF)

    part_out, part_lse = attend(cross_q_enc, [cross_kv], cross_segs, [0], False, HALF)
    cross_heads, cross_out_wide, cross_lse = to_decoder(
        from_pairs(part_out, half_local), stats_from_pairs(part_lse, half_local), 7
    )
    cross_norm, cross_normed, cross_scale, cross_full = rows_call(
        _forward_rows,
        2,
        dot_bt(cross_heads, dec_cross[1]).astype(HALF),
        [self_norm, dg[1:2], db[1:2]],
        kept_rows,
    )
    dec_hidden = dot(cross_full, dec_ffn[0])
    dec_active = gelu(dec_hidden).astype(HALF)
    result, resid, dec_terms2, grad_full = rows_call(
        _turn_rows,
        3,
        dot_bt(dec_active, dec_ffn[1]).astype(HALF),
        [cross_norm, dg[2:3], db[2:3], pick(dec_cotangent)],
        [((dec_span, width), HALF), wide_rows, norm_terms],
    )
    grad_hidden = (dot(grad_full, dec_ffn[1]) * gelu_slope(dec_hidden)).astype(HALF)
    resid, dec_terms1, cross_grad_full = rows_call(
        _backward_rows,
        4,
        dot_bt(grad_hidden, dec_ffn[0]).astype(HALF),
        [resid, cross_normed, cross_scale, dg[1:2]],
        [wide_rows, norm_terms],
    )
    cross_heads_grad = dot(cross_grad_full, dec_cross[1]).astype(HALF)
    heads_grad_enc, stats_enc = to_encoder(
        in_halves(cross_heads_grad), 8, cross_out_wide, cross_lse
    )
    cross_q_term, [cross_kv_grad] = attend_back(
        cross_q_enc,
        [cross_kv],
        to_pairs(heads_grad_enc),
        stats_to_pairs(stats_enc, half_local),
        centered,
        cross_segs,
        [0],
        False,
        False,
    )
    dec_f2_grad = dot_ta(grad_full, dec_active)
    dec_f1_grad = dot_ta(cross_full, grad_hidden)
    dec_ffn_rows, _ = scatter_local([dec_f1_grad, dec_f2_grad])

    def to_chip(value):
        theirs = joint(value, [((1 - owner(t), t), (owner(t), t)) for t in chips])
        theirs = theirs.reshape(2, count, *theirs.shape[1:])
        chip = value.reshape(theirs.shape).astype(WIDE) + theirs[::-1].astype(WIDE)
        return jnp.where(is_first, chip, chip[::-1]).astype(HALF)

    def to_owner(chip):
        terms = []
        for s in range(top_bit):
            near, far = 2 * s, 2 * s + 1
            near_pairs = [((owner(t), t), (owner(t), t ^ s)) for t in chips]
            far_pairs = [((owner(t), t), (owner(t), t ^ s ^ top_bit)) for t in chips]
            near_got = chip[:, near] if s == 0 else joint(chip[:, near], near_pairs)
            far_got = joint(chip[:, far], far_pairs)
            terms.append(jnp.where(core == group, near_got, far_got).astype(WIDE))
        return sum(terms)

    cross_q_chip = to_chip(from_pairs(cross_q_term, half_local))
    cross_q_grad = to_owner(cross_q_chip).astype(HALF)
    cross_q_grad = jnp.concatenate([cross_q_grad[0], cross_q_grad[1]], axis=1)

    back_tokens = [((span, width), WIDE), ((span, width), HALF), ((8, width), WIDE)]
    resid_enc, resid_low, enc_terms2, *cross_grads = collect(
        [cross_kv_grad],
        w_cross,
        2,
        (0, 1),
        _end_norm_back,
        [mem_normed, mem_scale, gain_of(2)],
        back_tokens,
        memory_low,
    )
    ckv_term = fold_cores(*cross_grads)
    resid_enc, resid_low, enc_terms1, *ffn_grads = feed_forward_back(
        attn_norm_low,
        after(resid_low, dec_ffn_rows, cross_q_chip),
        resid_enc,
        attn_normed,
        attn_scale,
        gain_of(1),
        active,
        slope,
        own_ffn,
        mine_ffn,
        other_ffn,
    )
    heads_grad, *out_grads = spread(resid_low, w_attn, 4, (3,), heads)
    f2_term = fold_cores(after(ffn_grads[2], heads_grad), ffn_grads[3])
    enc_f2 = fold_planes(f2_term)
    f1_term = fold_cores(*ffn_grads[:2])
    enc_f1 = fold_planes(f1_term)
    enc_ckv = fold_planes(ckv_term)
    def join(a, b):
        return (a.astype(WIDE) + b.astype(WIDE)).astype(HALF)

    cross_q_grad = after(cross_q_grad, f2_term)
    resid, dec_terms0, self_grad_full = rows_call(
        _backward_rows,
        4,
        dot_bt(cross_q_grad, dec_cross[0]).astype(HALF),
        [resid, self_normed, self_scale, dg[0:1]],
        [wide_rows, norm_terms],
    )
    dec_heads_grad = dot(self_grad_full, dec_attn[3]).astype(HALF)
    dec_q_grad, [dec_kv_grad] = attend_back(
        dec_query, [dec_kv], dec_heads_grad, dec_lse, dec_heads_wide, dec_segs, [0], True
    )
    dec_proj_grad = [dec_q_grad, dec_kv_grad[0], dec_kv_grad[1]]
    dec_part = sum(dot_bt(g, w) for g, w in zip(dec_proj_grad, dec_in_w)).astype(HALF)
    dec_left = [start_full] * 3 + [self_grad_full, self_full, cross_grad_full]
    dec_right = dec_proj_grad + [dec_heads, cross_q_grad, cross_heads]
    dec_small = [dot_ta(a, b) for a, b in zip(dec_left, dec_right)]
    dec_small_rows, dec_small_term = scatter_local(dec_small)
    grads_in = after(heads_grad, f1_term, dec_small_term)
    def send_chips(held):
        pairs, bit = [(v,) for v in held], top_bit // 2
        while bit >= 1:
            held = [join(*v) if len(v) == 2 else v[0] for v in pairs]
            pairs = [(a, swap(b, "tensor", bit)) for a, b in zip(held[:bit], held[bit:])]
            bit //= 2
        return pairs[0]

    def sum_pair(pair, *earlier):
        return join(after(pair[0], *earlier), pair[1]) if len(pair) == 2 else pair[0]

    q_grad, kv_grad, held = (), [], []
    for n in range(parts):
        q_grad, terms = attend_back(
            query,
            key_values[n],
            after(grads_in, *held),
            lse,
            heads_wide,
            enc_segs,
            masks,
            part=n if parts == 2 else None,
            into=q_grad,
        )
        q_grad = (q_grad,)
        if n:
            kv_grad.append(sum_pair(moving, terms[0]))
            terms = after(tuple(terms), kv_grad[0])
        held = [join(a, swap(b, "pipe", 1)) for a, b in zip(terms[:top_bit], terms[top_bit:])]
        moving = send_chips(held)
    [q_grad] = q_grad

    kv_grad.append(after(sum_pair(moving), enc_ckv, enc_f1, enc_f2))

    enc_grad, enc_low, enc_terms0, *in_grads = collect(
        [q_grad, *kv_grad],
        w_attn,
        4,
        (0, 1, 2),
        _end_norm_back,
        [resid_enc, start_normed, start_scale, gain_of(0)],
        back_tokens,
        embed_low,
    )
    dec_grad = sum_to_owner(after(dec_part, kv_grad[-1]), resid, enc_low)
    attn_out, cross_out, ffn_out_grad, there, near_second, norm_sums = finish(
        in_grads,
        out_grads,
        enc_f1,
        enc_f2,
        enc_ckv,
        dec_ffn_rows,
        dec_small_rows,
        after(enc_low, dec_grad),
        [enc_terms0, enc_terms1, enc_terms2, dec_terms0, dec_terms1, dec_terms2],
    )

    attn_out, cross_out, ffn_out_grad = [
        v.transpose(1, 0, 2)[None] for v in (attn_out, cross_out, ffn_out_grad)
    ]
    own_columns = width // (lax.axis_size("dp") * count)
    norm_sums = lax.dynamic_slice_in_dim(
        norm_sums[:6].reshape(3, 2, width), (lax.axis_index("dp") * count + place) * own_columns, own_columns, 2
    )

    dec_pair = jnp.stack([result, dec_grad.astype(HALF)])
    dec_halves = dec_pair.reshape(2, dec_span, 2, half)
    dec_got = swap(lax.dynamic_index_in_dim(dec_halves, 1 - core, 2, False), "pipe", 1)
    own_result = lax.dynamic_slice_in_dim(result, core * half, half, 1)
    own_grad = lax.dynamic_slice_in_dim(dec_grad, core * half, half, 1)
    dec_output = jnp.where(
        is_first, jnp.stack([own_result, dec_got[0]]), jnp.stack([dec_got[0], own_result])
    )
    got_grad = dec_got[1].astype(WIDE)
    dec_input_grad = jnp.where(
        is_first, jnp.stack([own_grad, got_grad]), jnp.stack([got_grad, own_grad])
    )

    here = jnp.where(is_first, enc_grad[:, :half], near_second.astype(WIDE))
    there = there.astype(WIDE)
    enc_input_grad = jnp.where(group == 0, jnp.stack([here, there]), jnp.stack([there, here]))
    return (
        dec_output,
        enc_input_grad,
        dec_input_grad,
        attn_out,
        cross_out,
        ffn_out_grad,
        norm_sums[None, :, 0],
        norm_sums[None, :, 1],
    )


def solution(mesh):
    rows = P("dp", "tensor", None)
    weights = P("pipe", None, None, "tensor")
    half_rows = P("dp", "tensor", "pipe")
    weight_grads = P("pipe", "dp", None, "tensor")
    norm_grads = P("pipe", None, ("dp", "tensor"))
    return jax.shard_map(
        per_device,
        mesh=mesh,
        in_specs=(rows, rows, rows, P("dp", None), P("dp", None))
        + (weights,) * 3
        + (P("pipe", None, None),) * 2,
        out_specs=(half_rows,) * 3 + (weight_grads,) * 3 + (norm_grads,) * 2,
        check_vma=False,
    )
```

```python
from functools import partial

import jax
import jax.numpy as jnp
from jax import lax
from jax.experimental import pallas as pl
from jax.experimental.pallas import tpu as pltpu
from jax.sharding import PartitionSpec as P

HEAD = 64
LANES = 128
EPSILON = 1e-05
NEGATIVE = -1e30
HALF = jnp.bfloat16
WIDE = jnp.float32
VMEM_LIMIT = 56 << 20
MESH = pl.DeviceIdType.MESH
TILE_Q = 256
TILE_K = 512


def dot(left, right):
    return jnp.dot(left, right, preferred_element_type=WIDE)


def dot_bt(left, right):
    return lax.dot_general(left, right, (((1,), (1,)), ((), ())), preferred_element_type=WIDE)


def dot_ta(left, right):
    return lax.dot_general(left, right, (((0,), (0,)), ((), ())), preferred_element_type=WIDE)


def swap(value, axis, mask):
    return lax.ppermute(value, axis, [(i, i ^ mask) for i in range(lax.axis_size(axis))])


def joint(value, pairs):
    count = lax.axis_size("tensor")
    return lax.ppermute(
        value,
        ("pipe", "tensor"),
        [(a[0] * count + a[1], b[0] * count + b[1]) for a, b in pairs],
    )


def after(value, *earlier):
    return lax.optimization_barrier((value, *earlier))[0]


def swap_columns(value, axis, mask, difference):
    got = swap(value, axis, mask).reshape(value.shape[0], -1, LANES)
    order = [b ^ difference for b in range(got.shape[1])]
    return jnp.concatenate([got[:, b] for b in order], axis=1)


def table_of(places, lengths):
    total = jnp.zeros((), jnp.int32)
    table = jnp.zeros(places.shape, jnp.int32)
    for j in range(lengths.shape[0]):
        total = total + lengths[j]
        table = table + (places >= total).astype(jnp.int32)
    return table


def norm_forward(values, gain, bias):
    center = values - jnp.mean(values, axis=-1, keepdims=True)
    inv_scale = lax.rsqrt(jnp.mean(center * center, axis=-1, keepdims=True) + EPSILON)
    normed = center * inv_scale
    return normed * gain + bias, normed, inv_scale


def norm_backward(grad_out, normed, inv_scale, gain):
    grad_gain = jnp.sum(grad_out * normed, axis=0)
    grad_bias = jnp.sum(grad_out, axis=0)
    grad_normed = grad_out * gain
    grad_in = inv_scale * (
        grad_normed
        - jnp.mean(grad_normed, axis=-1, keepdims=True)
        - normed * jnp.mean(grad_normed * normed, axis=-1, keepdims=True)
    )
    return grad_in, grad_gain, grad_bias


def gelu(hidden):
    return 0.5 * hidden * (1.0 + lax.erf(hidden * (2.0**-0.5)))


def gelu_slope(hidden):
    density = jnp.exp(-0.5 * hidden * hidden) * 0.3989422804014327
    return 0.5 * (1.0 + lax.erf(hidden * (2.0**-0.5))) + hidden * density


def _allowed(seg_k, seg_q, causal, col0, row0):
    ok = seg_k == seg_q
    if causal:
        keys = col0 + lax.broadcasted_iota(jnp.int32, ok.shape, 0)
        queries = row0 + lax.broadcasted_iota(jnp.int32, ok.shape, 1)
        ok = ok & (queries >= keys)
    return ok


def _tile_loop(act, chunks, c, nq, nk, tq, tk, body):
    def step(i, carry):
        iq, ik = i // nk, i % nk

        @pl.when(act[iq * (chunks * nk) + c * nk + ik] > 0)
        def _():
            body(iq * tq, ik * tk, pl.ds(pl.multiple_of(iq * tq, tq), tq), pl.ds(pl.multiple_of(ik * tk, tk), tk))

        return carry

    lax.fori_loop(0, nq * nk, step, 0)


def _head_lanes(shape, head):
    lanes = lax.broadcasted_iota(jnp.int32, shape, 1)
    return (lanes < HEAD) if head == 0 else (lanes >= HEAD)


def _attend_kernel(chunks, tq, tk, causal, act, seg_q, seg_k, q, *refs):
    keys, values = refs[:chunks], refs[chunks : 2 * chunks]
    out, lse, top, total, acc = refs[-5:]
    rows = q.shape[0]
    nq, nk = rows // tq, keys[0].shape[0] // tk
    top[...] = jnp.full(top.shape, NEGATIVE, WIDE)
    total[...] = jnp.zeros(total.shape, WIDE)
    acc[...] = jnp.zeros(acc.shape, WIDE)
    for c in range(chunks):

        def tile(row0, col0, r, s, c=c):
            qs = q[r, :] * jnp.asarray(HEAD**-0.5, HALF)
            kk, vt = keys[c][s, :], values[c][s, :].T
            ok = _allowed(seg_k[c, s, 0:1], seg_q[0:1, r], causal, col0, row0)
            ones = jnp.ones((8, vt.shape[1]), HALF)
            heads = range(2)
            raw = [
                dot_bt(kk, jnp.where(_head_lanes(qs.shape, h), qs, jnp.zeros_like(qs))) for h in heads
            ]
            scores = [jnp.where(ok, sc, NEGATIVE) for sc in raw]
            before = [top[h : h + 1, r] for h in heads]
            after_ = [jnp.maximum(b, jnp.max(sc, axis=0, keepdims=True)) for b, sc in zip(before, scores)]
            terms = [jnp.exp(sc - a).astype(HALF) for sc, a in zip(scores, after_)]
            for h in heads:
                fade = jnp.exp(before[h] - after_[h])
                span = slice(h * HEAD, (h + 1) * HEAD)
                sums = dot(jnp.concatenate([vt[span, :], ones], axis=0), terms[h])
                acc[span, r] = acc[span, r] * fade + sums[:HEAD]
                total[h : h + 1, r] = total[h : h + 1, r] * fade + sums[HEAD : HEAD + 1]
                top[h : h + 1, r] = after_[h]

        _tile_loop(act, chunks, c, nq, nk, tq, tk, tile)
    count = total[...]
    count = jnp.where(count > 0.0, count, 1.0)
    lse[0] = top[...] + jnp.log(count)
    whole = jnp.concatenate([acc[:HEAD, :] / count[0:1, :], acc[HEAD:, :] / count[1:2, :]], axis=0)
    out[...] = whole.T.astype(out.dtype)


def _attend_back_kernel(chunks, tq, tk, causal, own_delta, act, seg_q, seg_k, q, *refs):
    keys, values = refs[:chunks], refs[chunks : 2 * chunks]
    grad_out, stats = refs[2 * chunks : 2 * chunks + 2]
    refs = refs[2 * chunks + 2 :]
    extra, (grad_q, *grad_kv, delta, dq, dkv) = refs[0], refs[-(chunks + 4) :]
    rows = q.shape[0]
    nq, nk = rows // tq, keys[0].shape[0] // tk
    if own_delta:
        product = grad_out[...].astype(WIDE) * extra[...].astype(WIDE)
        pick = (
            lax.broadcasted_iota(jnp.int32, (8, LANES), 1) // HEAD
            == lax.broadcasted_iota(jnp.int32, (8, LANES), 0)
        ).astype(WIDE)
        delta[...] = lax.dot_general(
            pick, product, (((1,), (1,)), ((), ())), precision=lax.Precision.HIGHEST, preferred_element_type=WIDE
        )
    else:
        delta[0:2, :] = stats[0, 2:4, :]
    dq[...] = jnp.zeros(dq.shape, WIDE)
    for c in range(chunks):
        dkv[...] = jnp.zeros(dkv.shape, WIDE)

        def tile(row0, col0, r, s, c=c):
            qs = q[r, :] * jnp.asarray(HEAD**-0.5, HALF)
            go = grad_out[r, :]
            kk, vv = keys[c][s, :], values[c][s, :]
            ok = _allowed(seg_k[c, s, 0:1], seg_q[0:1, r], causal, col0, row0)
            heads = range(2)
            mine = [_head_lanes(qs.shape, h) for h in heads]
            mine_k = [_head_lanes(kk.shape, h) for h in heads]
            from_keys = kk if own_delta else extra[s, :]
            qh = [jnp.where(m, qs, jnp.zeros_like(qs)) for m in mine]
            gh = [jnp.where(m, go, jnp.zeros_like(go)) for m in mine]
            kh = [jnp.where(m, from_keys, jnp.zeros_like(kk)) for m in mine_k]
            raw = [dot_bt(kk, v) for v in qh]
            grads = [dot_bt(vv, v) for v in gh]
            pr = [jnp.exp(jnp.where(ok, raw[h], NEGATIVE) - stats[0, h : h + 1, r]) for h in heads]
            ds = [(pr[h] * (grads[h] - delta[h : h + 1, r])).astype(HALF) for h in heads]
            pr = [v.astype(HALF) for v in pr]
            dkv[1, s, :] += dot(pr[0], gh[0]) + dot(pr[1], gh[1])
            dkv[0, s, :] += dot(ds[0], qh[0]) + dot(ds[1], qh[1])
            dq[r, :] += dot_ta(ds[0], kh[0]) + dot_ta(ds[1], kh[1])

        _tile_loop(act, chunks, c, nq, nk, tq, tk, tile)
        grad_kv[c][...] = dkv[...].astype(grad_kv[c].dtype)
    grad_q[...] = (dq[...] * HEAD**-0.5).astype(grad_q.dtype)


def _tile_sizes(rows, keys):
    return min(TILE_Q, rows), min(TILE_K, keys)


def _activity(seg_q, seg_k, tq, tk):
    qt = seg_q.reshape(-1, tq)
    kt = seg_k.reshape(-1, tk)
    hit = (qt[:, :1] <= kt[:, -1][None]) & (kt[:, 0][None] <= qt[:, -1:])
    return hit.astype(jnp.int32).reshape(-1)


def tables(seg_q, seg_k):
    rows, (chunks, span) = seg_q.shape[0], seg_k.shape
    tq, tk = _tile_sizes(rows, span)
    return (
        _activity(seg_q, seg_k, tq, tk),
        jnp.broadcast_to(seg_q[None], (8, rows)),
        jnp.broadcast_to(seg_k[:, :, None], (chunks, span, LANES)),
    )


def _specs(rows, span, chunks, masks, blocked, part):
    def block(h):
        return h if part is None else 2 * h + part

    row_block = pl.BlockSpec((rows, LANES), lambda h, act: (0, block(h)))
    if blocked:
        row_block = pl.BlockSpec((None, rows, LANES), lambda h, act: (block(h), 0, 0))
    stat_block = pl.BlockSpec((1, 8, rows), lambda h, act: (block(h), 0, 0))
    heads = [
        pl.BlockSpec((8, rows), lambda h, act: (0, 0)),
        pl.BlockSpec((chunks, span, LANES), lambda h, act: (0, 0, 0)),
        row_block,
    ]
    for side in range(2):
        heads += [
            pl.BlockSpec((None, span, LANES), lambda h, act, m=m, side=side: (side, 0, h ^ m)) for m in masks
        ]
    return row_block, stat_block, heads


def _dimensions(q, key_values, masks, part):
    blocked = q.ndim == 3
    rows, width = (q.shape[1], q.shape[0] * LANES) if blocked else q.shape
    span, chunks, blocks = key_values[0].shape[1], len(key_values), width // LANES
    if part is not None:
        blocks, masks = blocks // 2, [m // 2 for m in masks]
    row_block, stat_block, specs = _specs(rows, span, chunks, masks, blocked, part)
    return rows, span, chunks, blocks, masks, _tile_sizes(rows, span), row_block, stat_block, specs


def attend(q, key_values, segs, masks, causal=False, out_type=WIDE, part=None, into=()):
    rows, span, chunks, blocks, masks, (tq, tk), row_block, stat_block, specs = _dimensions(
        q, key_values, masks, part
    )
    pairs = rows * span * chunks * blocks * LANES
    kept = 4 + 2 * chunks
    stat_blocks = blocks if part is None else 2 * blocks
    return pl.pallas_call(
        partial(_attend_kernel, chunks, tq, tk, causal),
        out_shape=(
            jax.ShapeDtypeStruct(q.shape, out_type),
            jax.ShapeDtypeStruct((stat_blocks, 8, rows), WIDE),
        ),
        grid_spec=pltpu.PrefetchScalarGridSpec(
            num_scalar_prefetch=1,
            grid=(blocks,),
            in_specs=specs + [pl.BlockSpec(memory_space=pl.ANY)] * len(into),
            out_specs=[row_block, stat_block],
            scratch_shapes=[
                pltpu.VMEM((8, rows), WIDE),
                pltpu.VMEM((8, rows), WIDE),
                pltpu.VMEM((LANES, rows), WIDE),
            ],
        ),
        input_output_aliases={kept + i: i for i in range(len(into))},
        compiler_params=pltpu.CompilerParams(vmem_limit_bytes=VMEM_LIMIT),
        cost_estimate=pl.CostEstimate(
            flops=48 * pairs, transcendentals=pairs // HEAD, bytes_accessed=rows * blocks * LANES * 20
        ),
        name="attend",
    )(*segs, q, *key_values, *key_values, *into)


def attend_back(
    q, key_values, grad_out, stats, extra, segs, masks, causal=False, own_delta=True, part=None, into=()
):
    rows, span, chunks, blocks, masks, (tq, tk), row_block, stat_block, specs = _dimensions(
        q, key_values, masks, part
    )
    kv_out = [pl.BlockSpec((2, span, LANES), lambda h, act, m=m: (0, 0, h ^ m)) for m in masks]
    pairs = rows * span * chunks * blocks * LANES
    extra_block = row_block if own_delta else pl.BlockSpec((span, LANES), lambda h, act: (0, h))
    kept = 7 + 2 * chunks
    outs = pl.pallas_call(
        partial(_attend_back_kernel, chunks, tq, tk, causal, own_delta),
        out_shape=[jax.ShapeDtypeStruct(q.shape, HALF)]
        + [jax.ShapeDtypeStruct((2, span, blocks * LANES), HALF)] * chunks,
        grid_spec=pltpu.PrefetchScalarGridSpec(
            num_scalar_prefetch=1,
            grid=(blocks,),
            in_specs=specs
            + [row_block, stat_block, extra_block]
            + [pl.BlockSpec(memory_space=pl.ANY)] * len(into),
            out_specs=[row_block] + kv_out,
            scratch_shapes=[
                pltpu.VMEM((8, rows), WIDE),
                pltpu.VMEM((rows, LANES), WIDE),
                pltpu.VMEM((2, span, LANES), WIDE),
            ],
        ),
        input_output_aliases={kept + i: i for i in range(len(into))},
        compiler_params=pltpu.CompilerParams(vmem_limit_bytes=VMEM_LIMIT),
        cost_estimate=pl.CostEstimate(
            flops=80 * pairs, transcendentals=pairs // HEAD, bytes_accessed=rows * blocks * LANES * 40
        ),
        name="attend_back",
    )(*segs, q, *key_values, *key_values, grad_out, stats, extra, *into)
    return outs[0], outs[1:]


def _row_mean(values):
    return jnp.mean(values, axis=-1, keepdims=True)


def _norm_rows(values, gain, bias):
    center = values - _row_mean(values)
    inv_scale = lax.rsqrt(_row_mean(center * center) + EPSILON)
    normed = center * inv_scale
    return normed * gain + bias, normed, inv_scale


def _norm_rows_back(grad_out, normed, inv_scale, gain):
    grad_normed = grad_out * gain
    grad_in = inv_scale * (
        grad_normed - _row_mean(grad_normed) - normed * _row_mean(grad_normed * normed)
    )
    return (
        grad_in,
        jnp.sum(grad_out * normed, axis=0, keepdims=True),
        jnp.sum(grad_out, axis=0, keepdims=True),
    )


def _forward_rows(total, ins, outs):
    resid, gain, bias = ins
    value, normed, inv_scale = _norm_rows(total + resid[...], gain[...], bias[...])
    outs[0][...] = value
    outs[1][...] = normed
    outs[2][...] = jnp.broadcast_to(inv_scale, outs[2].shape)
    return value


def _turn_rows(total, ins, outs):
    resid, gain, bias, cotangent = ins
    value, normed, inv_scale = _norm_rows(total + resid[...], gain[...], bias[...])
    outs[0][...] = value.astype(outs[0].dtype)
    grad, grad_gain, grad_bias = _norm_rows_back(
        cotangent[...].astype(WIDE), normed, inv_scale, gain[...]
    )
    outs[1][...] = grad
    outs[2][0:1, :] = grad_gain
    outs[2][1:2, :] = grad_bias
    return grad


def _backward_rows(total, ins, outs):
    resid, normed, inv_scale, gain = ins
    grad, grad_gain, grad_bias = _norm_rows_back(
        total + resid[...], normed[...], inv_scale[:, 0:1], gain[...]
    )
    outs[0][...] = grad
    outs[1][0:1, :] = grad_gain
    outs[1][1:2, :] = grad_bias
    return grad


def _rows_kernel(count, scatter, gather, middle, n_in, n_out, *refs):
    refs = list(refs)
    part = refs.pop(0) if scatter else None
    ins, refs = refs[:n_in], refs[n_in:]
    outs, refs = refs[:n_out], refs[n_out:]
    full = refs.pop(0) if gather else None
    landed = refs.pop(0) if scatter else None
    send_sem, recv_sem = refs[:2]
    me = lax.axis_index("tensor")
    steps = range(1, count)
    peers = [lax.rem(me + s, count) for s in steps]
    barrier = pltpu.get_barrier_semaphore()
    for peer in peers:
        pl.semaphore_signal(barrier, inc=1, device_id={"tensor": peer}, device_id_type=MESH)
    pl.semaphore_wait(barrier, count - 1)
    total = None
    if scatter:
        rows = part.shape[0] // count
        copies = []
        for s, peer in zip(steps, peers):
            copy = pltpu.make_async_remote_copy(
                src_ref=part.at[pl.ds(pl.multiple_of(peer * rows, rows), rows)],
                dst_ref=landed.at[s - 1],
                send_sem=send_sem.at[0, s - 1],
                recv_sem=recv_sem.at[0, s - 1],
                device_id={"tensor": peer},
                device_id_type=MESH,
            )
            copy.start()
            copies.append(copy)
        total = part[pl.ds(pl.multiple_of(me * rows, rows), rows), :].astype(WIDE)
        for s, copy in zip(steps, copies):
            copy.wait_recv()
            total = total + landed[s - 1].astype(WIDE)
        for copy in copies:
            copy.wait_send()
    sent = middle(total, ins, outs)
    if gather:
        rows = full.shape[0] // count
        own = pl.ds(pl.multiple_of(me * rows, rows), rows)
        full[own, :] = sent.astype(full.dtype)
        copies = []
        for s, peer in zip(steps, peers):
            copy = pltpu.make_async_remote_copy(
                src_ref=full.at[own],
                dst_ref=full.at[own],
                send_sem=send_sem.at[1, s - 1],
                recv_sem=recv_sem.at[1, s - 1],
                device_id={"tensor": peer},
                device_id_type=MESH,
            )
            copy.start()
            copies.append(copy)
        for copy in copies:
            copy.wait()


def rows_call(middle, number, part, ins, outs, gather=True):
    count = lax.axis_size("tensor")
    scatter = part is not None
    width = (part if scatter else ins[0]).shape[1]
    rows = part.shape[0] // count if scatter else ins[0].shape[0]
    shapes = [jax.ShapeDtypeStruct(shape, kind) for shape, kind in outs]
    if gather:
        shapes.append(jax.ShapeDtypeStruct((rows * count, width), HALF))
    whole = pl.BlockSpec(memory_space=pltpu.VMEM)
    operands = ([part] if scatter else []) + list(ins)
    got = pl.pallas_call(
        partial(_rows_kernel, count, scatter, gather, middle, len(ins), len(outs)),
        out_shape=shapes,
        in_specs=[whole] * len(operands),
        out_specs=[whole] * len(shapes),
        scratch_shapes=([pltpu.VMEM((count - 1, rows, width), HALF)] if scatter else [])
        + [pltpu.SemaphoreType.DMA((2, count - 1))] * 2,
        compiler_params=pltpu.CompilerParams(
            collective_id=number, has_side_effects=True, vmem_limit_bytes=VMEM_LIMIT
        ),
        cost_estimate=pl.CostEstimate(
            flops=0, transcendentals=0, bytes_accessed=1400 * rows * width
        ),
        name=middle.__name__.strip("_"),
    )(*operands)
    return got


def _differ(a, b, count):
    total, bit = 0, 1
    while bit < count:
        total = total + lax.rem(lax.rem(a // bit, 2) + lax.rem(b // bit, 2), 2) * bit
        bit *= 2
    return total


def _slot(difference, count):
    top = count // 2
    return 2 * lax.rem(difference, top) + difference // top


def _enter(peers):
    barrier = pltpu.get_barrier_semaphore()
    for peer in peers:
        pl.semaphore_signal(barrier, inc=1, device_id=peer, device_id_type=MESH)
    pl.semaphore_wait(barrier, len(peers))


def _send(source, dest, send_sem, recv_sem, peer):
    copy = pltpu.make_async_remote_copy(
        src_ref=source,
        dst_ref=dest,
        send_sem=send_sem,
        recv_sem=recv_sem,
        device_id=peer,
        device_id_type=MESH,
    )
    copy.start()
    return copy


def _to_encoder_kernel(count, with_stats, *refs):
    if with_stats:
        value, out, lse, full, stats, own, own_stats, held, other, other_stats, send_sem, recv_sem = refs
    else:
        value, full, own, other, send_sem, recv_sem = refs
    core, me = lax.axis_index("pipe"), lax.axis_index("tensor")
    group = me // (count // 2)
    chips = [lax.rem(me + s, count) for s in range(1, count)]
    _enter([{"tensor": chip} for chip in chips] + [{"pipe": 1 - core}])
    sets = [(value, own, other, full)]
    if with_stats:
        for h in range(2):
            product = value[h].astype(WIDE) * out[h]
            pick = (
                lax.broadcasted_iota(jnp.int32, (8, product.shape[1]), 1) // HEAD
                == lax.broadcasted_iota(jnp.int32, (8, product.shape[1]), 0) - 2
            ).astype(WIDE)
            held[h] = lax.dot_general(
                pick,
                product,
                (((1,), (1,)), ((), ())),
                precision=lax.Precision.HIGHEST,
                preferred_element_type=WIDE,
            )
            held[h, 0:2, :] = lse[h, 0:2, :]
        sets.append((held, own_stats, other_stats, stats))
    copies = []
    for s, chip in enumerate(chips):
        place = _slot(_differ(chip, me, count), count)
        for h in range(2):
            at = lax.rem(h + core, 2) * count + place
            for i, (source, dest, _, _) in enumerate(sets):
                sems = (send_sem.at[i, s, h], recv_sem.at[i, s, h])
                copies.append(_send(source.at[h], dest.at[at], *sems, {"tensor": chip}))
    for h in range(2):
        for source, dest, _, _ in sets:
            dest[lax.rem(h + core, 2) * count] = source[h]
    for copy in copies:
        copy.wait()
    copies = []
    for g in range(2):
        for i, (_, source, dest, _) in enumerate(sets):
            here, there = pl.ds(g * count, count), pl.ds((1 - g) * count, count)
            sems = (send_sem.at[i, count - 1, g], recv_sem.at[i, count - 1, g])
            copies.append(_send(source.at[here], dest.at[there], *sems, {"pipe": 1 - core}))
    for copy in copies:
        copy.wait()
    for _, mine, theirs, dest in sets:

        @pl.when(core == group)
        def _(mine=mine, dest=dest):
            dest[...] = mine[...]

        @pl.when(core != group)
        def _(theirs=theirs, dest=dest):
            dest[...] = theirs[...]


def to_encoder(value, number, out=None, lse=None):
    count = lax.axis_size("tensor")
    _, rows, wide = value.shape
    shapes = [((2 * count, rows, wide), HALF)]
    if out is not None:
        shapes.append(((2 * count, 8, rows), WIDE))
    scratch = [pltpu.VMEM(*s) for s in shapes]
    if out is not None:
        scratch.append(pltpu.VMEM((2, 8, rows), WIDE))
    scratch += [pltpu.VMEM(*s) for s in shapes]
    whole = pl.BlockSpec(memory_space=pltpu.VMEM)
    operands = (value,) if out is None else (value, out, lse)
    return pl.pallas_call(
        partial(_to_encoder_kernel, count, out is not None),
        out_shape=[jax.ShapeDtypeStruct(*s) for s in shapes],
        in_specs=[whole] * len(operands),
        out_specs=[whole] * len(shapes),
        scratch_shapes=scratch + [pltpu.SemaphoreType.DMA((len(shapes), count, 2))] * 2,
        compiler_params=pltpu.CompilerParams(
            collective_id=number, has_side_effects=True, vmem_limit_bytes=VMEM_LIMIT
        ),
        cost_estimate=pl.CostEstimate(flops=0, transcendentals=0, bytes_accessed=60 << 20),
        name="to_encoder",
    )(*operands)


def _over_lanes(weights, wide):
    lanes = lax.broadcasted_iota(jnp.int32, (8, wide), 1) // HEAD
    pick = (lanes == lax.broadcasted_iota(jnp.int32, (8, wide), 0)).astype(HALF)
    high = weights.astype(HALF)
    low = (weights - high.astype(WIDE)).astype(HALF)
    return dot_ta(jnp.concatenate([high, low], axis=0), jnp.concatenate([pick, pick], axis=0))


def _to_decoder_kernel(count, *refs):
    part, lse, heads, out, out_lse = refs[:5]
    other, other_lse, both, both_lse, landed, landed_lse, send_sem, recv_sem = refs[5:]
    core, me = lax.axis_index("pipe"), lax.axis_index("tensor")
    top = count // 2
    chips = [lax.rem(me + s, count) for s in range(1, count)]
    _enter([{"tensor": chip} for chip in chips] + [{"pipe": 1 - core}])
    copies = []
    for g in range(2):
        here, there = pl.ds(g * count, count), pl.ds((1 - g) * count, count)
        for i, (source, dest) in enumerate(((part, other), (lse, other_lse))):
            sems = (send_sem.at[i, count - 1, g], recv_sem.at[i, count - 1, g])
            copies.append(_send(source.at[here], dest.at[there], *sems, {"pipe": 1 - core}))
    for copy in copies:
        copy.wait()
    wide = part.shape[2]
    for i in range(2 * count):
        first, second = lse[i], other_lse[i]
        peak = jnp.maximum(first, second)
        a, b = jnp.exp(first - peak), jnp.exp(second - peak)
        both_lse[i] = peak + jnp.log(a + b)
        share = _over_lanes(b / (a + b), wide)
        mine = part[i].astype(WIDE)
        both[i] = (mine + share * (other[i].astype(WIDE) - mine)).astype(HALF)
    copies = []
    for s, chip in enumerate(chips):
        place = _slot(_differ(chip, me, count), count)
        for h in range(2):
            at = lax.rem(h + core, 2) * count + place
            for i, (source, dest) in enumerate(((both, landed), (both_lse, landed_lse))):
                sems = (send_sem.at[i, s, h], recv_sem.at[i, s, h])
                copies.append(_send(source.at[at], dest.at[s, h], *sems, {"tensor": chip}))
    for copy in copies:
        copy.wait()
    for h in range(2):
        at = lax.rem(h + core, 2) * count
        terms = [(me, both[at], both_lse[at])]
        for s in range(count - 1):
            terms.append((lax.rem(me - s - 1 + count, count), landed[s, h], landed_lse[s, h]))
        logs = [jnp.where(chip // top == core, log, NEGATIVE) for chip, _, log in terms]
        peak = logs[0]
        for log in logs[1:]:
            peak = jnp.maximum(peak, log)
        weights = [jnp.exp(log - peak) for log in logs]
        weights = [
            jnp.where(chip // top == core, w, 0.0) for (chip, _, _), w in zip(terms, weights)
        ]
        total = sum(weights)
        out_lse[h] = peak + jnp.log(total)
        shares = [_over_lanes(w / total, wide) for w in weights]
        value = sum(c * term.astype(WIDE) for c, (_, term, _) in zip(shares, terms)) / sum(shares)
        out[h] = value
        heads[:, h * wide : (h + 1) * wide] = value.astype(HALF)


def to_decoder(part, lse, number):
    count = lax.axis_size("tensor")
    slots, rows, wide = part.shape
    whole = pl.BlockSpec(memory_space=pltpu.VMEM)
    return pl.pallas_call(
        partial(_to_decoder_kernel, count),
        out_shape=[
            jax.ShapeDtypeStruct((rows, 2 * wide), HALF),
            jax.ShapeDtypeStruct((2, rows, wide), WIDE),
            jax.ShapeDtypeStruct((2, 8, rows), WIDE),
        ],
        in_specs=[whole] * 2,
        out_specs=[whole] * 3,
        scratch_shapes=[
            pltpu.VMEM((slots, rows, wide), HALF),
            pltpu.VMEM((slots, 8, rows), WIDE),
            pltpu.VMEM((slots, rows, wide), HALF),
            pltpu.VMEM((slots, 8, rows), WIDE),
            pltpu.VMEM((count - 1, 2, rows, wide), HALF),
            pltpu.VMEM((count - 1, 2, 8, rows), WIDE),
        ]
        + [pltpu.SemaphoreType.DMA((2, count, 2))] * 2,
        compiler_params=pltpu.CompilerParams(
            collective_id=number, has_side_effects=True, vmem_limit_bytes=VMEM_LIMIT
        ),
        cost_estimate=pl.CostEstimate(flops=0, transcendentals=0, bytes_accessed=60 << 20),
        name="to_decoder",
    )(part, lse)


def to_pairs(value):
    slots, rows, wide = value.shape
    each = LANES // wide
    if each == 1:
        return value
    value = value.reshape(slots // each, each, rows, wide)
    return value.transpose(0, 2, 1, 3).reshape(slots // each, rows, LANES)


def from_pairs(value, wide):
    blocks, rows, _ = value.shape
    each = LANES // wide
    if each == 1:
        return value
    value = value.reshape(blocks, rows, each, wide)
    return value.transpose(0, 2, 1, 3).reshape(blocks * each, rows, wide)


def stats_to_pairs(stats, wide):
    each = LANES // wide
    if each == 1:
        return stats
    slots, _, rows = stats.shape
    stats = stats.reshape(slots // each, each, 8, rows)
    return jnp.concatenate(
        [stats[:, :, 0], stats[:, :, 2], jnp.zeros((slots // each, 4, rows), WIDE)], axis=1
    )


def stats_from_pairs(stats, wide):
    each = LANES // wide
    if each == 1:
        return stats
    blocks, _, rows = stats.shape
    value = stats[:, :each].reshape(blocks * each, 1, rows)
    return jnp.concatenate([value, jnp.zeros((blocks * each, 7, rows), WIDE)], axis=1)


def slot_bits():
    count = lax.axis_size("tensor")
    bits, bit = [count // 2], 1
    while bit < count // 2:
        bits.append(bit)
        bit *= 2
    return [b for b in bits if b > 0]


def in_column_halves(values):
    wide = values.shape[2] // 2
    return jnp.stack(
        [
            jnp.concatenate(
                [values[:, k, h * wide : (h + 1) * wide] for k in range(values.shape[1])], axis=1
            ).astype(HALF)
            for h in range(2)
        ]
    )


def _gather_kernel(bits, count, planes, *refs):
    own, refs = refs[:3], refs[3:]
    leaving, dec_rows, *refs = refs
    full, enc_cross, enc_ffn, *refs = refs
    dec, refs = refs[:3], refs[3:]
    rests, refs = refs[:2], refs[2:]
    coming, dec_full, send_sem, recv_sem, local_sem = refs
    core, place, me = lax.axis_index("pipe"), lax.axis_index("dp"), lax.axis_index("tensor")
    wide = own[0].shape[2]
    block = own[0].shape[1] // planes
    sibling = {"pipe": 1 - core}
    chips = {bit: {"tensor": _differ(me, bit, count)} for bit in bits}
    line = [{"tensor": _differ(me, s, count)} for s in range(1, count)]
    dp_bits = [1 << i for i in range(planes.bit_length() - 1)]
    others = {bit: {"dp": _differ(place, bit, planes)} for bit in dp_bits}
    _enter([sibling, *line, *others.values()])
    made = [0]

    def push(source, dest, peer):
        i = made[0]
        made[0] += 1
        return _send(source, dest, send_sem.at[i], recv_sem.at[i], peer)

    def rows_of(difference):
        return pl.ds(pl.multiple_of(_differ(place, difference, planes) * block, block), block)

    enc = [full.at[:, :, pl.ds(0, wide)], enc_cross, enc_ffn]
    shown = []
    for a in range(3):
        i = made[0]
        made[0] += 2
        shown.append(i)

        @pl.when(core == 0)
        def _(a=a, i=i):
            for h in range(2):
                _send(own[a].at[h], enc[a].at[1 - h], send_sem.at[i + h], recv_sem.at[i + h], sibling)
                pltpu.make_async_copy(own[a].at[h], enc[a].at[h], local_sem.at[a, h]).start()

        @pl.when(core == 1)
        def _(a=a, i=i):
            for h in range(2):
                _send(own[a].at[h], dec[a].at[h], send_sem.at[i + h], recv_sem.at[i + h], sibling)
                pltpu.make_async_copy(own[a].at[h], dec[a].at[h], local_sem.at[a, h]).start()

    def arrived(a):
        i = shown[a]
        for h in range(2):
            pltpu.make_async_copy(own[a].at[h], enc[a].at[h], local_sem.at[a, h]).wait()
            pltpu.make_async_copy(own[a].at[h], enc[a].at[h], recv_sem.at[i + h]).wait()

    def line_step(a, n, bit):
        here, size = rows_of(0), own[a].shape[2]
        if a == 0:
            source = full.at[0, here, pl.ds(0, n * size)]
            return [push(source, full.at[0, here, pl.ds(n * size, n * size)], chips[bit])]
        rest = rests[a - 1]
        copies = [
            push(enc[a].at[0, here], rest.at[:, pl.ds((n - 1) * size, size)], chips[bit])
        ]
        if n > 1:
            source = rest.at[:, pl.ds(0, (n - 1) * size)]
            copies.append(push(source, rest.at[:, pl.ds(n * size, (n - 1) * size)], chips[bit]))
        return copies

    def wait(copies):
        for copy in copies:
            copy.wait()

    def advance(chain):
        wait(chain["now"])
        chain["now"] = line_step(chain["array"], *chain["todo"].pop(0)) if chain["todo"] else []

    def columns(part):
        return pl.ds(wide + part * half, half)

    def plane_step(j):
        copies = []
        for part, order in enumerate(orders):
            for m in held[part]:
                at = full.at[0, rows_of(m), columns(part)]
                copies.append((part, m ^ order[j], push(at, at, others[order[j]])))
        return copies

    def share(part, m):
        here = rows_of(m)
        source = full.at[0, here, columns(part)]
        return push(source, full.at[1, here, columns(part)], sibling)

    steps = [(1 << i, bit) for i, bit in enumerate(bits)]
    for_attn, for_cross, for_ffn = [{"array": a, "todo": list(steps), "now": []} for a in range(3)]
    arrived(0)
    advance(for_attn)
    arrived(2)
    advance(for_attn)
    advance(for_ffn)
    while for_attn["now"]:
        advance(for_attn)
    token_sem = made[0]
    made[0] += 1

    @pl.when(core == 1)
    def _():
        _send(leaving, coming, send_sem.at[token_sem], recv_sem.at[token_sem], chips[bits[0]])

    at = pl.ds(pl.multiple_of(me * dec_rows.shape[0], dec_rows.shape[0]), dec_rows.shape[0])
    dec_full[at, :] = dec_rows[...]
    dec_sent = [push(dec_full.at[at], dec_full.at[at], peer) for peer in line]
    half = (count - 1) * wide // 2
    orders, held = (dp_bits, dp_bits[::-1]), ([0], [0])
    moving = plane_step(0)
    shared = [share(part, 0) for part in range(2)]
    advance(for_ffn)
    arrived(1)
    for j in range(len(dp_bits)):
        for _, _, copy in moving:
            copy.wait()
        for part, order in enumerate(orders):
            held[part].extend([m ^ order[j] for m in held[part]])
        following = plane_step(j + 1) if j + 1 < len(dp_bits) else []
        shared += [share(part, m) for part, m, _ in moving]
        moving = following
        advance(for_cross)
    while for_ffn["now"]:
        advance(for_ffn)
    while for_cross["now"]:
        advance(for_cross)

    @pl.when(core == 1)
    def _():
        pltpu.make_async_copy(leaving, leaving, send_sem.at[token_sem]).wait()
        pltpu.make_async_copy(leaving, coming, recv_sem.at[token_sem]).wait()

    wait(dec_sent)
    wait(shared)
    for a in range(3):
        for h in range(2):
            pltpu.make_async_copy(own[a].at[h], own[a].at[h], send_sem.at[shown[a] + h]).wait()


def gather_weights(attn, cross, ffn, leaving, dec_rows):
    own = (attn, cross, ffn)
    count, planes = lax.axis_size("tensor"), lax.axis_size("dp")
    depth = attn.shape[1]
    shapes = [(2, depth, count * attn.shape[2]), cross.shape, ffn.shape]
    shapes += [v.shape for v in own]
    shapes += [(depth // planes, (count - 1) * v.shape[2]) for v in (cross, ffn)]
    shapes += [leaving.shape, (count * dec_rows.shape[0], dec_rows.shape[1])]
    hbm, vmem = pl.BlockSpec(memory_space=pl.ANY), pl.BlockSpec(memory_space=pltpu.VMEM)
    return pl.pallas_call(
        partial(_gather_kernel, slot_bits(), count, planes),
        out_shape=[jax.ShapeDtypeStruct(shape, HALF) for shape in shapes],
        in_specs=[vmem] * 3 + [hbm, vmem],
        out_specs=[hbm] * (len(shapes) - 1) + [vmem],
        scratch_shapes=[pltpu.SemaphoreType.DMA((64,))] * 2 + [pltpu.SemaphoreType.DMA((3, 2))],
        compiler_params=pltpu.CompilerParams(
            collective_id=9, has_side_effects=True, vmem_limit_bytes=VMEM_LIMIT
        ),
        cost_estimate=pl.CostEstimate(flops=0, transcendentals=0, bytes_accessed=280 << 20),
        name="gather_weights",
    )(*own, leaving, dec_rows)


def gather_planes(rest):
    return lax.all_gather(rest, "dp", axis=0, tiled=True)


def fold_cores(mine, other):
    return (mine.astype(WIDE) + swap(other, "pipe", 1).astype(WIDE)).astype(HALF)


def fold_planes(term):
    return lax.psum_scatter(term, "dp", scatter_dimension=0, tiled=True)


def scatter_local(terms):
    core = lax.axis_index("pipe")
    wide = terms[0].shape[1] // 2
    pick = partial(lax.dynamic_slice_in_dim, slice_size=wide, axis=1)
    mine = jnp.concatenate([pick(v.astype(HALF), core * wide) for v in terms], axis=1)
    other = jnp.concatenate([pick(v.astype(HALF), (1 - core) * wide) for v in terms], axis=1)
    term = fold_cores(mine, other)
    return fold_planes(term), term


def _blocks_of(weights, kinds):
    wide = weights.shape[2] // (lax.axis_size("tensor") * kinds)
    each = LANES // wide
    blocks = lax.axis_size("tensor") // each
    spec = pl.BlockSpec(
        (None, weights.shape[1], each * kinds * wide), lambda i: (i // blocks, 0, lax.rem(i, blocks))
    )
    return wide, each, blocks, spec


def _piece(weights, kinds, wide, each, k):
    parts = [weights[:, (j * kinds + k) * wide : (j * kinds + k + 1) * wide] for j in range(each)]
    return parts[0] if each == 1 else jnp.concatenate(parts, axis=1)


def _store_grads(refs, i, blocks, pieces, wide, each):
    columns = [p[:, j * wide : (j + 1) * wide] for j in range(each) for p in pieces]
    for ref, when in zip(refs, (i < blocks, i >= blocks)):

        @pl.when(when)
        def _(ref=ref):
            for n, column in enumerate(columns):
                ref[:, n * wide : (n + 1) * wide] = column.astype(ref.dtype)


def _grad_specs(depth, columns, blocks):
    return [
        pl.BlockSpec((depth, columns), lambda i: (0, jnp.minimum(i, blocks - 1))),
        pl.BlockSpec((depth, columns), lambda i: (0, jnp.maximum(i - blocks, 0))),
    ]


def _spread_kernel(kinds, use, wide, each, blocks, with_grad, pair, x, weights, *refs):
    left = x[...]
    values = [dot(left, _piece(weights, kinds, wide, each, k)) for k in use]
    if with_grad:
        y, *refs = refs
        i = pl.program_id(0)
        _store_grads(refs[-2:], i, blocks, [dot_ta(left, y[...].astype(HALF))], wide, each)
    for n in range(pair):
        ref = refs[len(refs) - pair + n]

        @pl.when(lax.rem(pl.program_id(0), pair) == n)
        def _(ref=ref):
            ref[0] = values[-2].astype(HALF)
            ref[1] = values[-1].astype(HALF)

    values = values[:-2] if pair else values
    for ref, value in zip(refs, values):
        ref[...] = value.astype(HALF)


def spread(x, weights, kinds, use, y=None, pair=0):
    rows, width = x.shape
    wide, each, blocks, spec = _blocks_of(weights, kinds)
    column = pl.BlockSpec((rows, LANES), lambda i: (0, i))
    single = len(use) - (2 if pair else 0)
    shapes, specs = [((rows, width), HALF)] * single, [column] * single
    for _ in range(pair):
        shapes.append(((2, rows, width // pair), HALF))
        specs.append(pl.BlockSpec((2, rows, LANES), lambda i: (0, 0, i // pair)))
    if y is not None:
        shapes += [((width, width // 2), HALF)] * 2
        specs += _grad_specs(width, LANES, blocks)
    return pl.pallas_call(
        partial(_spread_kernel, kinds, use, wide, each, blocks, y is not None, pair),
        out_shape=[jax.ShapeDtypeStruct(*s) for s in shapes],
        grid=(2 * blocks,),
        in_specs=[pl.BlockSpec((rows, width), lambda i: (0, 0)), spec] + [column] * (y is not None),
        out_specs=specs,
        compiler_params=pltpu.CompilerParams(vmem_limit_bytes=VMEM_LIMIT),
        cost_estimate=pl.CostEstimate(
            flops=8 * rows * width * width * (len(use) + (y is not None)),
            transcendentals=0,
            bytes_accessed=2 * width * width * kinds,
        ),
        name="spread",
    )(x, weights, *([] if y is None else [y]))


def _collect_kernel(kinds, use, wide, each, blocks, n_y, split, with_grad, ending, n_extra, *refs):
    refs = list(refs)
    ys, refs = refs[:n_y], refs[n_y:]
    weights, refs = refs[0], refs[1:]
    x = refs.pop(0) if with_grad else None
    extra, refs = refs[:n_extra], refs[n_extra:]
    acc = refs.pop()
    grads = [refs.pop(), refs.pop()][::-1] if with_grad else []
    i = pl.program_id(0)

    @pl.when(i == 0)
    def _():
        acc[...] = jnp.zeros(acc.shape, WIDE)

    values, ys = [], list(ys)
    while ys:
        y = ys.pop(0)
        if len(y.shape) == 2:
            values.append(y[...])
        elif split:
            odd = ys.pop(0)
            values += [jnp.where(lax.rem(i, 2) == 0, y[n], odd[n]) for n in range(2)]
        else:
            values += [y[0], y[1]]
    values = [v.astype(HALF) for v in values]
    for value, k in zip(values, use):
        acc[...] += dot_bt(value, _piece(weights, kinds, wide, each, k))
    if with_grad:
        left = x[...]
        _store_grads(grads, i, blocks, [dot_ta(left, v) for v in values], wide, each)

    @pl.when(i == 2 * blocks - 1)
    def _():
        ending(acc[...], extra, refs)


def collect(ys, weights, kinds, use, ending, extra, outs, x=None):
    rows, width = ys[0].shape[-2], weights.shape[1]
    split = any(y.ndim == 3 and y.shape[2] < width for y in ys)
    wide, each, blocks, spec = _blocks_of(weights, kinds)
    y_specs = [
        pl.BlockSpec((rows, LANES), lambda i: (0, i))
        if y.ndim == 2
        else pl.BlockSpec((2, rows, LANES), lambda i: (0, 0, i // (2 if split else 1)))
        for y in ys
    ]
    fixed = [pl.BlockSpec(v.shape, lambda i: (0, 0)) for v in ([] if x is None else [x]) + extra]
    shapes = list(outs)
    specs = [pl.BlockSpec(shape, lambda i: (0, 0)) for shape, _ in outs]
    if x is not None:
        shapes += [((width, len(use) * width // 2), HALF)] * 2
        specs += _grad_specs(width, len(use) * LANES, blocks)
    return pl.pallas_call(
        partial(
            _collect_kernel, kinds, use, wide, each, blocks, len(ys), split, x is not None, ending, len(extra)
        ),
        out_shape=[jax.ShapeDtypeStruct(*s) for s in shapes],
        grid=(2 * blocks,),
        in_specs=y_specs + [spec] + fixed,
        out_specs=specs,
        scratch_shapes=[pltpu.VMEM((rows, width), WIDE)],
        compiler_params=pltpu.CompilerParams(vmem_limit_bytes=VMEM_LIMIT),
        cost_estimate=pl.CostEstimate(
            flops=8 * rows * width * width * len(use) * (1 + (x is not None)),
            transcendentals=0,
            bytes_accessed=2 * width * width * kinds,
        ),
        name="collect",
    )(*ys, weights, *([] if x is None else [x]), *extra)


def _end_norm(total, ins, outs):
    resid, gain, bias = ins
    value, normed, inv_scale = _norm_rows(total + resid[...], gain[...], bias[...])
    outs[0][...] = value
    outs[1][...] = value.astype(HALF)
    outs[2][...] = normed
    outs[3][...] = jnp.broadcast_to(inv_scale, outs[3].shape)


def _end_norm_back(total, ins, outs):
    *resid, normed, inv_scale, gain = ins
    total = total + resid[0][...] if resid else total
    grad, grad_gain, grad_bias = _norm_rows_back(total, normed[...], inv_scale[:, 0:1], gain[...])
    outs[0][...] = grad
    outs[1][...] = grad.astype(HALF)
    outs[2][0:1, :] = grad_gain
    outs[2][1:2, :] = grad_bias


def _ffn_parts(count, own, mine, other):
    depth, wide = own.shape[1], own.shape[2] // 2
    specs = []
    for k in range(2):
        specs.append(pl.BlockSpec((None, depth, wide), lambda i, k=k: (i // count, 0, k)))
        for first in (0, count):
            specs.append(
                pl.BlockSpec(
                    (depth, wide),
                    lambda i, k=k, first=first: (0, 2 * jnp.clip(i - first - 1, 0, count - 2) + k),
                )
            )
    return wide, specs


def _ffn_cases(count, i, ins, outs):
    local = lax.rem(i, count) == 0
    return [
        (local, ins[0], outs[0]),
        (jnp.logical_and(~local, i < count), ins[1], outs[1]),
        (jnp.logical_and(~local, i > count), ins[2], outs[2]),
    ]


def _ffn_kernel(count, x, resid, gain, bias, *refs):
    ins, outs, refs = refs[:3], refs[3:6], refs[6:]
    value, value_low, normed, inv_scale, active, slope, acc = refs
    i = pl.program_id(0)

    @pl.when(i == 0)
    def _():
        acc[...] = jnp.zeros(acc.shape, WIDE)

    for condition, first, second in _ffn_cases(count, i, ins, outs):

        @pl.when(condition)
        def _(first=first, second=second):
            hidden = dot(x[...], first[...])
            below = 0.5 * (1.0 + lax.erf(hidden * (2.0**-0.5)))
            density = jnp.exp(-0.5 * hidden * hidden) * 0.3989422804014327
            act = (hidden * below).astype(HALF)
            active[...] = act
            slope[...] = (below + hidden * density).astype(HALF)
            acc[...] += dot_bt(act, second[...])

    @pl.when(i == 2 * count - 1)
    def _():
        _end_norm(acc[...], (resid, gain, bias), (value, value_low, normed, inv_scale))


def feed_forward(x, resid, gain, bias, own, mine, other):
    count = lax.axis_size("tensor")
    rows, width = x.shape
    wide, specs = _ffn_parts(count, own, mine, other)
    units = 2 * count * wide
    fixed = [pl.BlockSpec(v.shape, lambda i: (0, 0)) for v in (x, resid, gain, bias)]
    shapes = [((rows, width), WIDE), ((rows, width), HALF), ((rows, width), WIDE), ((rows, LANES), WIDE)]
    column = pl.BlockSpec((rows, wide), lambda i: (0, i))
    return pl.pallas_call(
        partial(_ffn_kernel, count),
        out_shape=[jax.ShapeDtypeStruct(*s) for s in shapes]
        + [jax.ShapeDtypeStruct((rows, units), HALF)] * 2,
        grid=(2 * count,),
        in_specs=fixed + specs,
        out_specs=[pl.BlockSpec(s, lambda i: (0, 0)) for s, _ in shapes] + [column] * 2,
        scratch_shapes=[pltpu.VMEM((rows, width), WIDE)],
        compiler_params=pltpu.CompilerParams(vmem_limit_bytes=VMEM_LIMIT),
        cost_estimate=pl.CostEstimate(
            flops=12 * rows * width * units, transcendentals=2 * rows * units, bytes_accessed=4 * width * units
        ),
        name="feed_forward",
    )(x, resid, gain, bias, own, mine, other, own, mine, other)


def _ffn_back_kernel(count, x, grad, resid, normed, inv_scale, gain, active, slope, *refs):
    ins, outs, refs = refs[:3], refs[3:6], refs[6:]
    result, result_low, terms, *grads, acc = refs
    i = pl.program_id(0)

    @pl.when(i == 0)
    def _():
        acc[...] = jnp.zeros(acc.shape, WIDE)

    for condition, first, second in _ffn_cases(count, i, ins, outs):

        @pl.when(condition)
        def _(first=first, second=second):
            hidden = (dot(grad[...], second[...]) * slope[...].astype(WIDE)).astype(HALF)
            acc[...] += dot_bt(hidden, first[...])
            f1 = dot_ta(x[...], hidden).astype(HALF)
            f2 = dot_ta(grad[...], active[...]).astype(HALF)
            for half, when in enumerate((i < count, i >= count)):

                @pl.when(when)
                def _(half=half):
                    grads[half][...] = f1
                    grads[2 + half][...] = f2

    @pl.when(i == 2 * count - 1)
    def _():
        _end_norm_back(acc[...], (resid, normed, inv_scale, gain), (result, result_low, terms))


def feed_forward_back(x, grad, resid, normed, inv_scale, gain, active, slope, own, mine, other):
    count = lax.axis_size("tensor")
    rows, width = x.shape
    wide, specs = _ffn_parts(count, own, mine, other)
    column = pl.BlockSpec((rows, wide), lambda i: (0, i))
    fixed = [pl.BlockSpec(v.shape, lambda i: (0, 0)) for v in (x, grad, resid, normed, inv_scale, gain)]
    shapes = [((rows, width), WIDE), ((rows, width), HALF), ((8, width), WIDE)]
    grad_specs = [
        pl.BlockSpec((width, wide), lambda i: (0, jnp.minimum(i, count - 1))),
        pl.BlockSpec((width, wide), lambda i: (0, jnp.maximum(i - count, 0))),
    ]
    return pl.pallas_call(
        partial(_ffn_back_kernel, count),
        out_shape=[jax.ShapeDtypeStruct(*s) for s in shapes]
        + [jax.ShapeDtypeStruct((width, count * wide), HALF)] * 4,
        grid=(2 * count,),
        in_specs=fixed + [column] * 2 + specs,
        out_specs=[pl.BlockSpec(s, lambda i: (0, 0)) for s, _ in shapes] + grad_specs * 2,
        scratch_shapes=[pltpu.VMEM((rows, width), WIDE)],
        compiler_params=pltpu.CompilerParams(vmem_limit_bytes=VMEM_LIMIT),
        cost_estimate=pl.CostEstimate(
            flops=32 * rows * width * count * wide, transcendentals=0, bytes_accessed=16 * width * count * wide
        ),
        name="feed_forward_back",
    )(x, grad, resid, normed, inv_scale, gain, active, slope, own, mine, other, own, mine, other)


def _add_rows(dest, first, second):
    rows = 64 if dest.shape[0] % 64 == 0 else dest.shape[0]

    def step(i, carry):
        at = pl.ds(pl.multiple_of(i * rows, rows), rows)
        dest[at, :] = (first[at, :].astype(WIDE) + second[at, :].astype(WIDE)).astype(HALF)
        return carry

    lax.fori_loop(0, dest.shape[0] // rows, step, 0)


def _finish_kernel(bits, count, planes, *refs):
    in_mine, out_mine, in_other, out_other, f1, f2, ckv, dec_ffn, dec_small, tokens = refs[:10]
    norm_terms, refs = refs[10:16], refs[16:]
    attn_out, cross_out, ffn_out, far, near, norm_sum = refs[:6]
    land_in, land_out, term, *refs = refs[6:]
    n_steps = planes.bit_length() - 1
    land_planes, refs = refs[:n_steps], refs[n_steps:]
    folded, landed, refs = refs[:4], refs[4:8], refs[8:]
    enc_ffn, enc_small, got_ffn, got_small, norm_other, norm_land, send_sem, recv_sem = refs
    core, place, me = lax.axis_index("pipe"), lax.axis_index("dp"), lax.axis_index("tensor")
    sibling = {"pipe": 1 - core}
    line = {s: {"tensor": _differ(me, s, count)} for s in range(1, count)}
    cross_over = {"pipe": 1 - core, "tensor": _differ(me, bits[0], count)}
    dp_bits = [1 << i for i in range(n_steps)]
    others = {bit: {"dp": _differ(place, bit, planes)} for bit in dp_bits}
    _enter([sibling, cross_over, *line.values(), *others.values()])
    made = [0]

    def number():
        made[0] += 1
        return made[0] - 1

    def push(source, dest, peer):
        i = number()
        return _send(source, dest, send_sem.at[i], recv_sem.at[i], peer)

    def wait(copies):
        for copy in copies:
            copy.wait()

    for i in range(3):
        at = slice(2 * i, 2 * i + 2)
        enc, dec = norm_terms[i][0:2, :], norm_terms[3 + i][0:2, :]
        norm_sum[at, :] = jnp.where(core == 0, enc, dec)
        norm_other[at, :] = jnp.where(core == 0, dec, enc)
    norm_sum[6:8, :] = jnp.zeros((2, norm_sum.shape[1]), WIDE)
    norm_other[6:8, :] = jnp.zeros((2, norm_sum.shape[1]), WIDE)
    norm_peers = [*others.values(), *(line[bit] for bit in bits)]
    norm_now = [push(norm_other, norm_land.at[0], sibling)]

    def advance_norms():
        if norm_now:
            norm_now.pop().wait()
            n = n_steps + len(bits) - len(norm_peers)
            norm_sum[...] = norm_sum[...] + norm_land[n]
            if norm_peers:
                norm_now.append(push(norm_sum, norm_land.at[n + 1], norm_peers.pop(0)))

    to_core = [push(in_other, land_in, sibling), push(out_other, land_out, sibling)]

    def chain(source, a, at=slice(None)):
        fold, land = (v if at == slice(None) else v.at[at] for v in (folded[a], landed[a]))
        size = folded[a].shape[1] * 2 // count
        return {
            "source": source,
            "fold": fold,
            "land": land,
            "size": size,
            "slots": count,
            "bits": list(reversed(bits)),
            "now": [],
        }

    def advance(c):
        land, size = c["land"], c["size"]
        if c["now"]:
            wait(c["now"])
            c["now"] = []
            kept = c["slots"] // 2 * size
            offset = (count - c["slots"]) * size
            at = pl.ds(0, kept)
            _add_rows(c["fold"].at[:, at], c["source"].at[:, at], land.at[:, pl.ds(offset, kept)])
            c["source"], c["slots"] = c["fold"], c["slots"] // 2
        if c["bits"]:
            kept = c["slots"] // 2 * size
            offset = (count - c["slots"]) * size
            source = c["source"].at[:, pl.ds(kept, kept)]
            c["now"] = [push(source, land.at[:, pl.ds(offset, kept)], line[c["bits"].pop(0)])]

    chains = [chain(f2, 0), chain(f1, 1), chain(ckv, 2)]
    advance(chains[0])

    wait(to_core)
    block = in_mine.shape[0] // planes
    wide = term.shape[1] // count
    inner = in_mine.shape[1] // count

    def sum_step(i, carry):
        at = pl.ds(pl.multiple_of(i * 64, 64), 64)
        for s in range(count):
            first = in_mine[at, s * inner : (s + 1) * inner].astype(WIDE)
            second = land_in[at, s * inner : (s + 1) * inner].astype(WIDE)
            term[at, s * wide : s * wide + inner] = (first + second).astype(HALF)
            outer = wide - inner
            first = out_mine[at, s * outer : (s + 1) * outer].astype(WIDE)
            second = land_out[at, s * outer : (s + 1) * outer].astype(WIDE)
            term[at, s * wide + inner : (s + 1) * wide] = (first + second).astype(HALF)
        return carry

    lax.fori_loop(0, in_mine.shape[0] // 64, sum_step, 0)

    columns = term.shape[1] // 2
    orders = (dp_bits, dp_bits[::-1])
    held = [[list(range(planes)) for _ in orders] for _ in range(2)]
    piece = block // 2

    def rows_of(difference, r):
        first = _differ(place, difference, planes) * block + r * piece
        return pl.ds(pl.multiple_of(first, piece), piece)

    def at_of(p, m, r):
        return term.at[rows_of(m, r), pl.ds(p * columns, columns)]

    def plane_start(j, r):
        copies = []
        for p, order in enumerate(orders):
            bit = order[j]
            kept = [m for m in held[r][p] if not m & bit]
            for n, m in enumerate(kept):
                dest = land_planes[j].at[p, n, pl.ds(r * piece, piece)]
                copies.append((p, m, dest, push(at_of(p, m ^ bit, r), dest, others[bit])))
            held[r][p] = kept
        return copies

    def plane_finish(copies, r):
        for p, m, dest, copy in copies:
            copy.wait()
            _add_rows(at_of(p, m, r), at_of(p, m, r), dest)

    moving = [plane_start(0, r) for r in range(2)]
    for_attn = []
    advance(chains[1])
    advance(chains[2])

    half = tokens.shape[1] // 2
    far_sem, near_sem, same_sem = number(), number(), number()

    @pl.when(core == 1)
    def _():
        _send(tokens.at[:, pl.ds(0, half)], far, send_sem.at[far_sem], recv_sem.at[far_sem], cross_over)
        _send(
            tokens.at[:, pl.ds(half, half)], far, send_sem.at[same_sem], recv_sem.at[far_sem], line[bits[0]]
        )

    @pl.when(core == 0)
    def _():
        _send(tokens.at[:, pl.ds(half, half)], near, send_sem.at[near_sem], recv_sem.at[near_sem], sibling)

    for j in range(n_steps):
        for r in range(2):
            plane_finish(moving[r], r)
            if j + 1 < n_steps:
                moving[r] = plane_start(j + 1, r)
            else:
                for_attn.append(chain(term.at[rows_of(0, r)], 3, pl.ds(r * piece, piece)))
                advance(for_attn[-1])
            advance(chains[(2 * j + r) % 3])
            advance_norms()
    while any(c["now"] or c["bits"] for c in chains + for_attn):
        for c in for_attn + chains:
            advance(c)
        advance_norms()
    while norm_now:
        advance_norms()

    size = [fold.shape[1] * 2 // count for fold in folded]
    enc_ffn[:, : size[1]] = folded[1][:, : size[1]]
    enc_ffn[:, size[1] :] = folded[0][:, : size[0]]
    enc_small[:, : size[3]] = folded[3][:, : size[3]]
    enc_small[:, size[3] :] = folded[2][:, : size[2]]
    swap_sem = [number(), number()]

    @pl.when(core == 0)
    def _():
        _send(dec_ffn, got_ffn, send_sem.at[swap_sem[0]], recv_sem.at[swap_sem[0]], sibling)
        _send(dec_small, got_small, send_sem.at[swap_sem[1]], recv_sem.at[swap_sem[1]], sibling)

    @pl.when(core == 1)
    def _():
        _send(enc_ffn, got_ffn, send_sem.at[swap_sem[0]], recv_sem.at[swap_sem[0]], sibling)
        _send(enc_small, got_small, send_sem.at[swap_sem[1]], recv_sem.at[swap_sem[1]], sibling)

    for i, (mine, got) in enumerate(((enc_ffn, got_ffn), (enc_small, got_small))):
        pltpu.make_async_copy(mine, got, send_sem.at[swap_sem[i]]).wait()
        pltpu.make_async_copy(mine, got, recv_sem.at[swap_sem[i]]).wait()

    def write(first, second):
        for h, (ffn, small) in enumerate((first, second)):
            c = ffn.shape[1] // 2
            for k in range(2):
                ffn_out[k, :, h * c : (h + 1) * c] = ffn[:, k * c : (k + 1) * c].astype(WIDE)
            c = small.shape[1] // 6
            for k in range(6):
                dest = attn_out.at[k] if k < 4 else cross_out.at[k - 4]
                dest[:, h * c : (h + 1) * c] = small[:, k * c : (k + 1) * c].astype(WIDE)

    @pl.when(core == 0)
    def _():
        write((enc_ffn, enc_small), (got_ffn, got_small))

    @pl.when(core == 1)
    def _():
        write((got_ffn, got_small), (dec_ffn, dec_small))

    pltpu.make_async_copy(far, far, recv_sem.at[far_sem]).wait()

    @pl.when(core == 1)
    def _():
        pltpu.make_async_copy(far, far, send_sem.at[far_sem]).wait()
        pltpu.make_async_copy(far, far, send_sem.at[same_sem]).wait()
        pltpu.make_async_copy(near, near, recv_sem.at[near_sem]).wait()

    @pl.when(core == 0)
    def _():
        pltpu.make_async_copy(near, near, send_sem.at[near_sem]).wait()


def finish(in_grads, out_grads, f1, f2, ckv, dec_ffn, dec_small, tokens, norm_terms):
    count, planes = lax.axis_size("tensor"), lax.axis_size("dp")
    depth = in_grads[0].shape[0]
    rows = depth // planes
    attn_columns = in_grads[0].shape[1] + out_grads[0].shape[1]
    wide = 2 * dec_small.shape[1] // 6
    vmem = pl.BlockSpec(memory_space=pltpu.VMEM)
    operands = (in_grads[0], out_grads[0], in_grads[1], out_grads[1], f1, f2, ckv, dec_ffn, dec_small, tokens)
    operands += tuple(norm_terms)
    lines = [f2.shape[1], f1.shape[1], ckv.shape[1], attn_columns]
    scratch = [in_grads[0].shape, out_grads[0].shape, (depth, attn_columns)]
    blocks = planes // 2
    while blocks >= 1:
        scratch.append((2, blocks, rows, attn_columns // 2))
        blocks //= 2
    scratch += [(rows, c // 2) for c in lines]
    scratch += [(rows, c - c // count) for c in lines]
    scratch += [dec_ffn.shape, dec_small.shape] * 2
    norm_steps = count.bit_length() + planes.bit_length() - 1
    norm_shapes = [norm_terms[0].shape, (norm_steps, *norm_terms[0].shape)]
    token_piece = ((tokens.shape[0], tokens.shape[1] // 2), HALF)
    outs = [((4, rows, wide), WIDE), ((2, rows, wide), WIDE), ((2, rows, dec_ffn.shape[1]), WIDE)]
    outs += [token_piece, token_piece, (norm_terms[0].shape, WIDE)]
    return pl.pallas_call(
        partial(_finish_kernel, slot_bits(), count, planes),
        out_shape=[jax.ShapeDtypeStruct(*o) for o in outs],
        in_specs=[vmem] * len(operands),
        out_specs=[vmem] * len(outs),
        scratch_shapes=[pltpu.VMEM(shape, HALF) for shape in scratch]
        + [pltpu.VMEM(shape, WIDE) for shape in norm_shapes]
        + [pltpu.SemaphoreType.DMA((64,))] * 2,
        compiler_params=pltpu.CompilerParams(
            collective_id=5, has_side_effects=True, vmem_limit_bytes=VMEM_LIMIT
        ),
        cost_estimate=pl.CostEstimate(flops=0, transcendentals=0, bytes_accessed=200 << 20),
        name="finish",
    )(*operands)


def per_device(
    enc_input,
    dec_input,
    dec_cotangent,
    enc_lengths,
    dec_lengths,
    attn_weights,
    cross_weights,
    ffn_weights,
    norm_gains,
    norm_biases,
):
    core, place = lax.axis_index("pipe"), lax.axis_index("tensor")
    count = lax.axis_size("tensor")
    top_bit = count // 2
    group = place // top_bit
    block = jnp.where(core == 0, place, place ^ top_bit)
    span, width = enc_input.shape[1:]
    dec_span = dec_input.shape[1]
    local_width = attn_weights.shape[3]
    is_first = core == 0
    chips = range(count)
    sources = [(s // top_bit, s % top_bit) for s in range(2 * top_bit)]
    half = width // 2
    half_local = local_width // 2

    def owner(t):
        return t // top_bit

    norms = jnp.concatenate([norm_gains[0], norm_biases[0]], axis=0)
    norms_other = swap(norms, "pipe", 1)
    enc_norms = jnp.where(is_first, norms, norms_other)
    dec_norms = jnp.where(is_first, norms_other, norms)
    eg, eb, dg, db = enc_norms[:3], enc_norms[3:], dec_norms[:3], dec_norms[3:]

    pick = partial(lax.dynamic_index_in_dim, index=core, axis=0, keepdims=False)
    start_low = pick(dec_input)
    (
        w_attn,
        own_cross,
        own_ffn,
        dec_attn_halves,
        dec_cross_halves,
        dec_ffn_halves,
        cross_rest,
        ffn_rest,
        got,
        start_full,
    ) = gather_weights(
        *[in_column_halves(v[0]) for v in (after(attn_weights, norms_other), cross_weights, ffn_weights)],
        lax.dynamic_index_in_dim(enc_input, 1 - group, 0, False),
        start_low,
    )
    kept = lax.dynamic_index_in_dim(enc_input, group, 0, False)
    tokens = jnp.where(is_first, kept, got).astype(WIDE)
    mine_ffn = gather_planes(ffn_rest)

    def natural(halves, kinds):
        wide = halves.shape[2] // kinds
        return [
            jnp.concatenate([halves[h][:, k * wide : (k + 1) * wide] for h in range(2)], axis=1)
            for k in range(kinds)
        ]

    dec_attn, dec_cross, dec_ffn = [
        natural(v, k) for v, k in ((dec_attn_halves, 4), (dec_cross_halves, 2), (dec_ffn_halves, 2))
    ]
    blocks = width // LANES
    masks = [a * (blocks // 2) + c * (blocks // 2 // top_bit) for a, c in sources]

    def gain_of(i):
        return enc_norms[i : i + 1]

    def bias_of(i):
        return enc_norms[3 + i : 4 + i]

    embed, start_normed, start_scale = norm_forward(tokens, eg[0], eb[0])
    start_scale = jnp.broadcast_to(start_scale, (span, LANES))
    embed_low = embed.astype(HALF)
    parts = 2 if all(m % 2 == 0 for m in masks) else 1
    query, *key_value = spread(embed_low, w_attn, 4, (0, 1, 2), pair=parts)

    def across_chips(value):
        held, bit = [value], 1
        while bit < top_bit:
            held = held + [swap(v, "tensor", bit) for v in held]
            bit *= 2
        return held

    def exchange(held, *earlier):
        if earlier:
            held = after(tuple(held), *earlier)
        return list(held) + [swap(v, "pipe", 1) for v in held]

    key_values = [across_chips(v) for v in key_value]
    mine_cross = gather_planes(after(cross_rest, query))

    enc_lengths, dec_lengths = [after(v, query) for v in (enc_lengths, dec_lengths)]
    enc_row = lax.dynamic_index_in_dim(enc_lengths, group, 0, False)
    dec_row_of_group = lax.dynamic_index_in_dim(dec_lengths, group, 0, False)
    dec_row = lax.dynamic_index_in_dim(dec_lengths, core, 0, False)
    spots = jnp.arange(span, dtype=jnp.int32)
    own_seg = table_of(block * span + spots, enc_row)
    key_seg = jnp.stack(
        [table_of((block ^ (a * top_bit) ^ c) * span + spots, enc_row) for a, c in sources]
    )
    dec_spots = jnp.arange(dec_span * count, dtype=jnp.int32)
    dec_seg = table_of(dec_spots, dec_row)
    enc_segs = tables(own_seg, key_seg)
    dec_segs = tables(dec_seg, dec_seg[None])
    cross_segs = tables(table_of(dec_spots, dec_row_of_group), own_seg[None])

    start_full = after(start_full, key_value)
    start = start_low.astype(WIDE)
    rows_full = dec_span * count
    wide_rows = ((dec_span, width), WIDE)
    kept_rows = [wide_rows, wide_rows, ((dec_span, LANES), WIDE)]
    norm_terms = ((8, width), WIDE)
    dec_in_w = [dec_attn[k] for k in range(3)]
    dec_query = dot(start_full, dec_in_w[0]).astype(HALF)
    dec_kv = jnp.stack([dot(start_full, w).astype(HALF) for w in dec_in_w[1:]])
    dec_heads_wide, dec_lse = attend(dec_query, [dec_kv], dec_segs, [0], True)
    dec_heads = dec_heads_wide.astype(HALF)
    term = dot_bt(dec_heads, dec_attn[3]).astype(HALF)

    attended = ()
    for n in range(parts):
        key_values[n] = exchange(key_values[n], *attended, *((term,) if n else ()))
        attended = attend(
            query, key_values[n], enc_segs, masks, part=n if parts == 2 else None, into=attended
        )
    heads_wide, lse = attended

    def sum_to_owner(term, resid, *earlier):
        total = after(resid, *earlier)
        for s in range(count):
            rows = lax.dynamic_slice_in_dim(term, (place ^ s) * dec_span, dec_span, 0)
            total = total + (swap(rows, "tensor", s) if s else rows).astype(WIDE)
        return total

    self_norm, self_normed, self_scale = norm_forward(sum_to_owner(term, start, lse), dg[0:1], db[0:1])
    self_scale = jnp.broadcast_to(self_scale, (dec_span, LANES))
    self_low = self_norm.astype(HALF)
    self_rows = [swap(self_low, "tensor", s) if s else self_low for s in range(count)]

    heads = heads_wide.astype(HALF)
    mine_ffn = after(mine_ffn, heads_wide)
    other_ffn = swap(mine_ffn, "pipe", 1)
    mine_cross = after(mine_cross, other_ffn)
    w_cross = jnp.stack(
        [
            jnp.concatenate([own_cross[0], mine_cross], axis=1),
            jnp.concatenate([own_cross[1], swap(mine_cross, "pipe", 1)], axis=1),
        ]
    )
    kept_tokens = [((span, width), WIDE), ((span, width), HALF), ((span, width), WIDE), ((span, LANES), WIDE)]
    attn_norm, attn_norm_low, attn_normed, attn_scale = collect(
        [heads], w_attn, 4, (3,), _end_norm, [embed, gain_of(1), bias_of(1)], kept_tokens
    )
    _, memory_low, mem_normed, mem_scale, active, slope = feed_forward(
        attn_norm_low, attn_norm, gain_of(2), bias_of(2), own_ffn, mine_ffn, other_ffn
    )
    self_full = after(jnp.zeros((rows_full, width), HALF), mem_scale)
    for s in range(count):
        self_full = lax.dynamic_update_slice_in_dim(self_full, self_rows[s], (place ^ s) * dec_span, 0)
    cross_query = dot(self_full, dec_cross[0]).astype(HALF)

    def in_halves(value):
        return jnp.stack([value[:, :half_local], value[:, half_local:]])

    [cross_q_enc] = to_encoder(in_halves(cross_query), 6)
    cross_q_enc = to_pairs(cross_q_enc)

    [cross_kv] = spread(memory_low, w_cross, 2, (0, 1), pair=1)

    tables_of_keys = enc_lengths.shape[1]
    at_table = (own_seg[:, None] == jnp.arange(tables_of_keys)[None]).astype(HALF)
    sums = dot_ta(at_table, cross_kv[0])
    bit = 1
    while bit < top_bit:
        sums = sums + swap_columns(sums, "tensor", bit, masks[bit])
        bit *= 2
    sums = sums + swap_columns(sums, "pipe", 1, masks[top_bit])
    means = sums / enc_row.astype(WIDE)[:, None]
    centers = sum(
        jnp.where((own_seg == j)[:, None], means[j : j + 1], 0.0) for j in range(tables_of_keys)
    )
    centered = (cross_kv[0].astype(WIDE) - centers).astype(HALF)

    part_out, part_lse = attend(cross_q_enc, [cross_kv], cross_segs, [0], False, HALF)
    cross_heads, cross_out_wide, cross_lse = to_decoder(
        from_pairs(part_out, half_local), stats_from_pairs(part_lse, half_local), 7
    )
    cross_norm, cross_normed, cross_scale, cross_full = rows_call(
        _forward_rows,
        2,
        dot_bt(cross_heads, dec_cross[1]).astype(HALF),
        [self_norm, dg[1:2], db[1:2]],
        kept_rows,
    )
    dec_hidden = dot(cross_full, dec_ffn[0])
    dec_active = gelu(dec_hidden).astype(HALF)
    result, resid, dec_terms2, grad_full = rows_call(
        _turn_rows,
        3,
        dot_bt(dec_active, dec_ffn[1]).astype(HALF),
        [cross_norm, dg[2:3], db[2:3], pick(dec_cotangent)],
        [((dec_span, width), HALF), wide_rows, norm_terms],
    )
    grad_hidden = (dot(grad_full, dec_ffn[1]) * gelu_slope(dec_hidden)).astype(HALF)
    resid, dec_terms1, cross_grad_full = rows_call(
        _backward_rows,
        4,
        dot_bt(grad_hidden, dec_ffn[0]).astype(HALF),
        [resid, cross_normed, cross_scale, dg[1:2]],
        [wide_rows, norm_terms],
    )
    cross_heads_grad = dot(cross_grad_full, dec_cross[1]).astype(HALF)
    dec_f2_grad = dot_ta(grad_full, dec_active)
    dec_f1_grad = dot_ta(cross_full, grad_hidden)
    dec_ffn_rows, dec_ffn_term = scatter_local([dec_f1_grad, dec_f2_grad])
    heads_grad_enc, stats_enc = to_encoder(
        in_halves(after(cross_heads_grad, dec_ffn_term)), 8, cross_out_wide, cross_lse
    )
    cross_q_term, [cross_kv_grad] = attend_back(
        cross_q_enc,
        [cross_kv],
        to_pairs(heads_grad_enc),
        stats_to_pairs(stats_enc, half_local),
        centered,
        cross_segs,
        [0],
        False,
        False,
    )

    def to_chip(value):
        theirs = joint(value, [((1 - owner(t), t), (owner(t), t)) for t in chips])
        theirs = theirs.reshape(2, count, *theirs.shape[1:])
        chip = value.reshape(theirs.shape).astype(WIDE) + theirs[::-1].astype(WIDE)
        return jnp.where(is_first, chip, chip[::-1]).astype(HALF)

    def to_owner(chip):
        terms = []
        for s in range(top_bit):
            near, far = 2 * s, 2 * s + 1
            near_pairs = [((owner(t), t), (owner(t), t ^ s)) for t in chips]
            far_pairs = [((owner(t), t), (owner(t), t ^ s ^ top_bit)) for t in chips]
            near_got = chip[:, near] if s == 0 else joint(chip[:, near], near_pairs)
            far_got = joint(chip[:, far], far_pairs)
            terms.append(jnp.where(core == group, near_got, far_got).astype(WIDE))
        return sum(terms)

    cross_q_chip = to_chip(from_pairs(cross_q_term, half_local))
    cross_q_grad = to_owner(cross_q_chip).astype(HALF)
    cross_q_grad = jnp.concatenate([cross_q_grad[0], cross_q_grad[1]], axis=1)

    back_tokens = [((span, width), WIDE), ((span, width), HALF), ((8, width), WIDE)]
    resid_enc, resid_low, enc_terms2, *cross_grads = collect(
        [cross_kv_grad],
        w_cross,
        2,
        (0, 1),
        _end_norm_back,
        [mem_normed, mem_scale, gain_of(2)],
        back_tokens,
        memory_low,
    )
    ckv_term = fold_cores(*cross_grads)
    resid_enc, resid_low, enc_terms1, *ffn_grads = feed_forward_back(
        attn_norm_low,
        after(resid_low, dec_ffn_rows, cross_q_chip),
        resid_enc,
        attn_normed,
        attn_scale,
        gain_of(1),
        active,
        slope,
        own_ffn,
        mine_ffn,
        other_ffn,
    )
    heads_grad, *out_grads = spread(resid_low, w_attn, 4, (3,), heads)
    f2_term = fold_cores(after(ffn_grads[2], heads_grad), ffn_grads[3])
    enc_f2 = fold_planes(f2_term)
    f1_term = fold_cores(*ffn_grads[:2])
    enc_f1 = fold_planes(f1_term)
    enc_ckv = fold_planes(ckv_term)
    def join(a, b):
        return (a.astype(WIDE) + b.astype(WIDE)).astype(HALF)

    cross_q_grad = after(cross_q_grad, f2_term)
    resid, dec_terms0, self_grad_full = rows_call(
        _backward_rows,
        4,
        dot_bt(cross_q_grad, dec_cross[0]).astype(HALF),
        [resid, self_normed, self_scale, dg[0:1]],
        [wide_rows, norm_terms],
    )
    dec_heads_grad = dot(self_grad_full, dec_attn[3]).astype(HALF)
    dec_q_grad, [dec_kv_grad] = attend_back(
        dec_query, [dec_kv], dec_heads_grad, dec_lse, dec_heads_wide, dec_segs, [0], True
    )
    dec_proj_grad = [dec_q_grad, dec_kv_grad[0], dec_kv_grad[1]]
    dec_part = sum(dot_bt(g, w) for g, w in zip(dec_proj_grad, dec_in_w)).astype(HALF)
    dec_left = [start_full] * 3 + [self_grad_full, self_full, cross_grad_full]
    dec_right = dec_proj_grad + [dec_heads, cross_q_grad, cross_heads]
    dec_small = [dot_ta(a, b) for a, b in zip(dec_left, dec_right)]
    dec_small_rows, dec_small_term = scatter_local(dec_small)
    grads_in = after(heads_grad, f1_term, dec_small_term)
    def send_chips(held):
        pairs, bit = [(v,) for v in held], top_bit // 2
        while bit >= 1:
            held = [join(*v) if len(v) == 2 else v[0] for v in pairs]
            pairs = [(a, swap(b, "tensor", bit)) for a, b in zip(held[:bit], held[bit:])]
            bit //= 2
        return pairs[0]

    def sum_pair(pair, *earlier):
        return join(after(pair[0], *earlier), pair[1]) if len(pair) == 2 else pair[0]

    q_grad, kv_grad, held = (), [], []
    for n in range(parts):
        q_grad, terms = attend_back(
            query,
            key_values[n],
            after(grads_in, *held),
            lse,
            heads_wide,
            enc_segs,
            masks,
            part=n if parts == 2 else None,
            into=q_grad,
        )
        q_grad = (q_grad,)
        if n:
            kv_grad.append(sum_pair(moving, terms[0]))
            terms = after(tuple(terms), kv_grad[0])
        held = [join(a, swap(b, "pipe", 1)) for a, b in zip(terms[:top_bit], terms[top_bit:])]
        moving = send_chips(held)
    [q_grad] = q_grad

    kv_grad.append(after(sum_pair(moving), enc_ckv, enc_f1, enc_f2))

    enc_grad, enc_low, enc_terms0, *in_grads = collect(
        [q_grad, *kv_grad],
        w_attn,
        4,
        (0, 1, 2),
        _end_norm_back,
        [resid_enc, start_normed, start_scale, gain_of(0)],
        back_tokens,
        embed_low,
    )
    dec_grad = sum_to_owner(after(dec_part, kv_grad[-1]), resid, enc_low)
    attn_out, cross_out, ffn_out_grad, there, near_second, norm_sums = finish(
        in_grads,
        out_grads,
        enc_f1,
        enc_f2,
        enc_ckv,
        dec_ffn_rows,
        dec_small_rows,
        after(enc_low, dec_grad),
        [enc_terms0, enc_terms1, enc_terms2, dec_terms0, dec_terms1, dec_terms2],
    )

    attn_out, cross_out, ffn_out_grad = [
        v.transpose(1, 0, 2)[None] for v in (attn_out, cross_out, ffn_out_grad)
    ]
    own_columns = width // (lax.axis_size("dp") * count)
    norm_sums = lax.dynamic_slice_in_dim(
        norm_sums[:6].reshape(3, 2, width), (lax.axis_index("dp") * count + place) * own_columns, own_columns, 2
    )

    dec_pair = jnp.stack([result, dec_grad.astype(HALF)])
    dec_halves = dec_pair.reshape(2, dec_span, 2, half)
    dec_got = swap(lax.dynamic_index_in_dim(dec_halves, 1 - core, 2, False), "pipe", 1)
    own_result = lax.dynamic_slice_in_dim(result, core * half, half, 1)
    own_grad = lax.dynamic_slice_in_dim(dec_grad, core * half, half, 1)
    dec_output = jnp.where(
        is_first, jnp.stack([own_result, dec_got[0]]), jnp.stack([dec_got[0], own_result])
    )
    got_grad = dec_got[1].astype(WIDE)
    dec_input_grad = jnp.where(
        is_first, jnp.stack([own_grad, got_grad]), jnp.stack([got_grad, own_grad])
    )

    here = jnp.where(is_first, enc_grad[:, :half], near_second.astype(WIDE))
    there = there.astype(WIDE)
    enc_input_grad = jnp.where(group == 0, jnp.stack([here, there]), jnp.stack([there, here]))
    return (
        dec_output,
        enc_input_grad,
        dec_input_grad,
        attn_out,
        cross_out,
        ffn_out_grad,
        norm_sums[None, :, 0],
        norm_sums[None, :, 1],
    )


def solution(mesh):
    rows = P("dp", "tensor", None)
    weights = P("pipe", None, None, "tensor")
    half_rows = P("dp", "tensor", "pipe")
    weight_grads = P("pipe", "dp", None, "tensor")
    norm_grads = P("pipe", None, ("dp", "tensor"))
    return jax.shard_map(
        per_device,
        mesh=mesh,
        in_specs=(rows, rows, rows, P("dp", None), P("dp", None))
        + (weights,) * 3
        + (P("pipe", None, None),) * 2,
        out_specs=(half_rows,) * 3 + (weight_grads,) * 3 + (norm_grads,) * 2,
        check_vma=False,
    )
```

```python
from functools import partial

import jax
import jax.numpy as jnp
from jax import lax
from jax.experimental import pallas as pl
from jax.experimental.pallas import tpu as pltpu
from jax.sharding import PartitionSpec as P

HEAD = 64
LANES = 128
EPSILON = 1e-05
NEGATIVE = -1e30
HALF = jnp.bfloat16
WIDE = jnp.float32
VMEM_LIMIT = 56 << 20
MESH = pl.DeviceIdType.MESH
TILE_Q = 256
TILE_K = 512


def dot(left, right):
    return jnp.dot(left, right, preferred_element_type=WIDE)


def dot_bt(left, right):
    return lax.dot_general(left, right, (((1,), (1,)), ((), ())), preferred_element_type=WIDE)


def dot_ta(left, right):
    return lax.dot_general(left, right, (((0,), (0,)), ((), ())), preferred_element_type=WIDE)


def swap(value, axis, mask):
    return lax.ppermute(value, axis, [(i, i ^ mask) for i in range(lax.axis_size(axis))])


def joint(value, pairs):
    count = lax.axis_size("tensor")
    return lax.ppermute(
        value,
        ("pipe", "tensor"),
        [(a[0] * count + a[1], b[0] * count + b[1]) for a, b in pairs],
    )


def after(value, *earlier):
    return lax.optimization_barrier((value, *earlier))[0]


def swap_columns(value, axis, mask, difference):
    got = swap(value, axis, mask).reshape(value.shape[0], -1, LANES)
    order = [b ^ difference for b in range(got.shape[1])]
    return jnp.concatenate([got[:, b] for b in order], axis=1)


def table_of(places, lengths):
    total = jnp.zeros((), jnp.int32)
    table = jnp.zeros(places.shape, jnp.int32)
    for j in range(lengths.shape[0]):
        total = total + lengths[j]
        table = table + (places >= total).astype(jnp.int32)
    return table


def norm_forward(values, gain, bias):
    center = values - jnp.mean(values, axis=-1, keepdims=True)
    inv_scale = lax.rsqrt(jnp.mean(center * center, axis=-1, keepdims=True) + EPSILON)
    normed = center * inv_scale
    return normed * gain + bias, normed, inv_scale


def norm_backward(grad_out, normed, inv_scale, gain):
    grad_gain = jnp.sum(grad_out * normed, axis=0)
    grad_bias = jnp.sum(grad_out, axis=0)
    grad_normed = grad_out * gain
    grad_in = inv_scale * (
        grad_normed
        - jnp.mean(grad_normed, axis=-1, keepdims=True)
        - normed * jnp.mean(grad_normed * normed, axis=-1, keepdims=True)
    )
    return grad_in, grad_gain, grad_bias


def gelu(hidden):
    return 0.5 * hidden * (1.0 + lax.erf(hidden * (2.0**-0.5)))


def gelu_slope(hidden):
    density = jnp.exp(-0.5 * hidden * hidden) * 0.3989422804014327
    return 0.5 * (1.0 + lax.erf(hidden * (2.0**-0.5))) + hidden * density


def _allowed(seg_k, seg_q, causal, col0, row0):
    ok = seg_k == seg_q
    if causal:
        keys = col0 + lax.broadcasted_iota(jnp.int32, ok.shape, 0)
        queries = row0 + lax.broadcasted_iota(jnp.int32, ok.shape, 1)
        ok = ok & (queries >= keys)
    return ok


def _tile_loop(act, chunks, c, nq, nk, tq, tk, body):
    def step(i, carry):
        iq, ik = i // nk, i % nk

        @pl.when(act[iq * (chunks * nk) + c * nk + ik] > 0)
        def _():
            body(iq * tq, ik * tk, pl.ds(pl.multiple_of(iq * tq, tq), tq), pl.ds(pl.multiple_of(ik * tk, tk), tk))

        return carry

    lax.fori_loop(0, nq * nk, step, 0)


def _head_lanes(shape, head):
    lanes = lax.broadcasted_iota(jnp.int32, shape, 1)
    return (lanes < HEAD) if head == 0 else (lanes >= HEAD)


def _attend_kernel(chunks, tq, tk, causal, act, seg_q, seg_k, q, *refs):
    keys, values = refs[:chunks], refs[chunks : 2 * chunks]
    out, lse, top, total, acc = refs[-5:]
    rows = q.shape[0]
    nq, nk = rows // tq, keys[0].shape[0] // tk
    top[...] = jnp.full(top.shape, NEGATIVE, WIDE)
    total[...] = jnp.zeros(total.shape, WIDE)
    acc[...] = jnp.zeros(acc.shape, WIDE)
    for c in range(chunks):

        def tile(row0, col0, r, s, c=c):
            qs = q[r, :] * jnp.asarray(HEAD**-0.5, HALF)
            kk, vt = keys[c][s, :], values[c][s, :].T
            ok = _allowed(seg_k[c, s, 0:1], seg_q[0:1, r], causal, col0, row0)
            ones = jnp.ones((8, vt.shape[1]), HALF)
            heads = range(2)
            raw = [
                dot_bt(kk, jnp.where(_head_lanes(qs.shape, h), qs, jnp.zeros_like(qs))) for h in heads
            ]
            scores = [jnp.where(ok, sc, NEGATIVE) for sc in raw]
            before = [top[h : h + 1, r] for h in heads]
            after_ = [jnp.maximum(b, jnp.max(sc, axis=0, keepdims=True)) for b, sc in zip(before, scores)]
            terms = [jnp.exp(sc - a).astype(HALF) for sc, a in zip(scores, after_)]
            for h in heads:
                fade = jnp.exp(before[h] - after_[h])
                span = slice(h * HEAD, (h + 1) * HEAD)
                sums = dot(jnp.concatenate([vt[span, :], ones], axis=0), terms[h])
                acc[span, r] = acc[span, r] * fade + sums[:HEAD]
                total[h : h + 1, r] = total[h : h + 1, r] * fade + sums[HEAD : HEAD + 1]
                top[h : h + 1, r] = after_[h]

        _tile_loop(act, chunks, c, nq, nk, tq, tk, tile)
    count = total[...]
    count = jnp.where(count > 0.0, count, 1.0)
    lse[0] = top[...] + jnp.log(count)
    whole = jnp.concatenate([acc[:HEAD, :] / count[0:1, :], acc[HEAD:, :] / count[1:2, :]], axis=0)
    out[...] = whole.T.astype(out.dtype)


def _attend_back_kernel(chunks, tq, tk, causal, own_delta, act, seg_q, seg_k, q, *refs):
    keys, values = refs[:chunks], refs[chunks : 2 * chunks]
    grad_out, stats = refs[2 * chunks : 2 * chunks + 2]
    refs = refs[2 * chunks + 2 :]
    extra, (grad_q, *grad_kv, delta, dq, dkv) = refs[0], refs[-(chunks + 4) :]
    rows = q.shape[0]
    nq, nk = rows // tq, keys[0].shape[0] // tk
    if own_delta:
        product = grad_out[...].astype(WIDE) * extra[...].astype(WIDE)
        pick = (
            lax.broadcasted_iota(jnp.int32, (8, LANES), 1) // HEAD
            == lax.broadcasted_iota(jnp.int32, (8, LANES), 0)
        ).astype(WIDE)
        delta[...] = lax.dot_general(
            pick, product, (((1,), (1,)), ((), ())), precision=lax.Precision.HIGHEST, preferred_element_type=WIDE
        )
    else:
        delta[0:2, :] = stats[0, 2:4, :]
    dq[...] = jnp.zeros(dq.shape, WIDE)
    for c in range(chunks):
        dkv[...] = jnp.zeros(dkv.shape, WIDE)

        def tile(row0, col0, r, s, c=c):
            qs = q[r, :] * jnp.asarray(HEAD**-0.5, HALF)
            go = grad_out[r, :]
            kk, vv = keys[c][s, :], values[c][s, :]
            ok = _allowed(seg_k[c, s, 0:1], seg_q[0:1, r], causal, col0, row0)
            heads = range(2)
            mine = [_head_lanes(qs.shape, h) for h in heads]
            mine_k = [_head_lanes(kk.shape, h) for h in heads]
            from_keys = kk if own_delta else extra[s, :]
            qh = [jnp.where(m, qs, jnp.zeros_like(qs)) for m in mine]
            gh = [jnp.where(m, go, jnp.zeros_like(go)) for m in mine]
            kh = [jnp.where(m, from_keys, jnp.zeros_like(kk)) for m in mine_k]
            raw = [dot_bt(kk, v) for v in qh]
            grads = [dot_bt(vv, v) for v in gh]
            pr = [jnp.exp(jnp.where(ok, raw[h], NEGATIVE) - stats[0, h : h + 1, r]) for h in heads]
            ds = [(pr[h] * (grads[h] - delta[h : h + 1, r])).astype(HALF) for h in heads]
            pr = [v.astype(HALF) for v in pr]
            dkv[1, s, :] += dot(pr[0], gh[0]) + dot(pr[1], gh[1])
            dkv[0, s, :] += dot(ds[0], qh[0]) + dot(ds[1], qh[1])
            dq[r, :] += dot_ta(ds[0], kh[0]) + dot_ta(ds[1], kh[1])

        _tile_loop(act, chunks, c, nq, nk, tq, tk, tile)
        grad_kv[c][...] = dkv[...].astype(grad_kv[c].dtype)
    grad_q[...] = (dq[...] * HEAD**-0.5).astype(grad_q.dtype)


def _tile_sizes(rows, keys):
    return min(TILE_Q, rows), min(TILE_K, keys)


def _activity(seg_q, seg_k, tq, tk):
    qt = seg_q.reshape(-1, tq)
    kt = seg_k.reshape(-1, tk)
    hit = (qt[:, :1] <= kt[:, -1][None]) & (kt[:, 0][None] <= qt[:, -1:])
    return hit.astype(jnp.int32).reshape(-1)


def tables(seg_q, seg_k):
    rows, (chunks, span) = seg_q.shape[0], seg_k.shape
    tq, tk = _tile_sizes(rows, span)
    return (
        _activity(seg_q, seg_k, tq, tk),
        jnp.broadcast_to(seg_q[None], (8, rows)),
        jnp.broadcast_to(seg_k[:, :, None], (chunks, span, LANES)),
    )


def _specs(rows, span, chunks, masks, blocked, part):
    def block(h):
        return h if part is None else 2 * h + part

    row_block = pl.BlockSpec((rows, LANES), lambda h, act: (0, block(h)))
    if blocked:
        row_block = pl.BlockSpec((None, rows, LANES), lambda h, act: (block(h), 0, 0))
    stat_block = pl.BlockSpec((1, 8, rows), lambda h, act: (block(h), 0, 0))
    heads = [
        pl.BlockSpec((8, rows), lambda h, act: (0, 0)),
        pl.BlockSpec((chunks, span, LANES), lambda h, act: (0, 0, 0)),
        row_block,
    ]
    for side in range(2):
        heads += [
            pl.BlockSpec((None, span, LANES), lambda h, act, m=m, side=side: (side, 0, h ^ m)) for m in masks
        ]
    return row_block, stat_block, heads


def _dimensions(q, key_values, masks, part):
    blocked = q.ndim == 3
    rows, width = (q.shape[1], q.shape[0] * LANES) if blocked else q.shape
    span, chunks, blocks = key_values[0].shape[1], len(key_values), width // LANES
    if part is not None:
        blocks, masks = blocks // 2, [m // 2 for m in masks]
    row_block, stat_block, specs = _specs(rows, span, chunks, masks, blocked, part)
    return rows, span, chunks, blocks, masks, _tile_sizes(rows, span), row_block, stat_block, specs


def attend(q, key_values, segs, masks, causal=False, out_type=WIDE, part=None, into=()):
    rows, span, chunks, blocks, masks, (tq, tk), row_block, stat_block, specs = _dimensions(
        q, key_values, masks, part
    )
    pairs = rows * span * chunks * blocks * LANES
    kept = 4 + 2 * chunks
    stat_blocks = blocks if part is None else 2 * blocks
    return pl.pallas_call(
        partial(_attend_kernel, chunks, tq, tk, causal),
        out_shape=(
            jax.ShapeDtypeStruct(q.shape, out_type),
            jax.ShapeDtypeStruct((stat_blocks, 8, rows), WIDE),
        ),
        grid_spec=pltpu.PrefetchScalarGridSpec(
            num_scalar_prefetch=1,
            grid=(blocks,),
            in_specs=specs + [pl.BlockSpec(memory_space=pl.ANY)] * len(into),
            out_specs=[row_block, stat_block],
            scratch_shapes=[
                pltpu.VMEM((8, rows), WIDE),
                pltpu.VMEM((8, rows), WIDE),
                pltpu.VMEM((LANES, rows), WIDE),
            ],
        ),
        input_output_aliases={kept + i: i for i in range(len(into))},
        compiler_params=pltpu.CompilerParams(vmem_limit_bytes=VMEM_LIMIT),
        cost_estimate=pl.CostEstimate(
            flops=48 * pairs, transcendentals=pairs // HEAD, bytes_accessed=rows * blocks * LANES * 20
        ),
        name="attend",
    )(*segs, q, *key_values, *key_values, *into)


def attend_back(
    q, key_values, grad_out, stats, extra, segs, masks, causal=False, own_delta=True, part=None, into=()
):
    rows, span, chunks, blocks, masks, (tq, tk), row_block, stat_block, specs = _dimensions(
        q, key_values, masks, part
    )
    kv_out = [pl.BlockSpec((2, span, LANES), lambda h, act, m=m: (0, 0, h ^ m)) for m in masks]
    pairs = rows * span * chunks * blocks * LANES
    extra_block = row_block if own_delta else pl.BlockSpec((span, LANES), lambda h, act: (0, h))
    kept = 7 + 2 * chunks
    outs = pl.pallas_call(
        partial(_attend_back_kernel, chunks, tq, tk, causal, own_delta),
        out_shape=[jax.ShapeDtypeStruct(q.shape, HALF)]
        + [jax.ShapeDtypeStruct((2, span, blocks * LANES), HALF)] * chunks,
        grid_spec=pltpu.PrefetchScalarGridSpec(
            num_scalar_prefetch=1,
            grid=(blocks,),
            in_specs=specs
            + [row_block, stat_block, extra_block]
            + [pl.BlockSpec(memory_space=pl.ANY)] * len(into),
            out_specs=[row_block] + kv_out,
            scratch_shapes=[
                pltpu.VMEM((8, rows), WIDE),
                pltpu.VMEM((rows, LANES), WIDE),
                pltpu.VMEM((2, span, LANES), WIDE),
            ],
        ),
        input_output_aliases={kept + i: i for i in range(len(into))},
        compiler_params=pltpu.CompilerParams(vmem_limit_bytes=VMEM_LIMIT),
        cost_estimate=pl.CostEstimate(
            flops=80 * pairs, transcendentals=pairs // HEAD, bytes_accessed=rows * blocks * LANES * 40
        ),
        name="attend_back",
    )(*segs, q, *key_values, *key_values, grad_out, stats, extra, *into)
    return outs[0], outs[1:]


def _row_mean(values):
    return jnp.mean(values, axis=-1, keepdims=True)


def _norm_rows(values, gain, bias):
    center = values - _row_mean(values)
    inv_scale = lax.rsqrt(_row_mean(center * center) + EPSILON)
    normed = center * inv_scale
    return normed * gain + bias, normed, inv_scale


def _norm_rows_back(grad_out, normed, inv_scale, gain):
    grad_normed = grad_out * gain
    grad_in = inv_scale * (
        grad_normed - _row_mean(grad_normed) - normed * _row_mean(grad_normed * normed)
    )
    return (
        grad_in,
        jnp.sum(grad_out * normed, axis=0, keepdims=True),
        jnp.sum(grad_out, axis=0, keepdims=True),
    )


def _forward_rows(total, ins, outs):
    resid, gain, bias = ins
    value, normed, inv_scale = _norm_rows(total + resid[...], gain[...], bias[...])
    outs[0][...] = value
    outs[1][...] = normed
    outs[2][...] = jnp.broadcast_to(inv_scale, outs[2].shape)
    return value


def _turn_rows(total, ins, outs):
    resid, gain, bias, cotangent = ins
    value, normed, inv_scale = _norm_rows(total + resid[...], gain[...], bias[...])
    outs[0][...] = value.astype(outs[0].dtype)
    grad, grad_gain, grad_bias = _norm_rows_back(
        cotangent[...].astype(WIDE), normed, inv_scale, gain[...]
    )
    outs[1][...] = grad
    outs[2][0:1, :] = grad_gain
    outs[2][1:2, :] = grad_bias
    return grad


def _backward_rows(total, ins, outs):
    resid, normed, inv_scale, gain = ins
    grad, grad_gain, grad_bias = _norm_rows_back(
        total + resid[...], normed[...], inv_scale[:, 0:1], gain[...]
    )
    outs[0][...] = grad
    outs[1][0:1, :] = grad_gain
    outs[1][1:2, :] = grad_bias
    return grad


def _rows_kernel(count, scatter, gather, middle, n_in, n_out, *refs):
    refs = list(refs)
    part = refs.pop(0) if scatter else None
    ins, refs = refs[:n_in], refs[n_in:]
    outs, refs = refs[:n_out], refs[n_out:]
    full = refs.pop(0) if gather else None
    landed = refs.pop(0) if scatter else None
    send_sem, recv_sem = refs[:2]
    me = lax.axis_index("tensor")
    steps = range(1, count)
    peers = [lax.rem(me + s, count) for s in steps]
    barrier = pltpu.get_barrier_semaphore()
    for peer in peers:
        pl.semaphore_signal(barrier, inc=1, device_id={"tensor": peer}, device_id_type=MESH)
    pl.semaphore_wait(barrier, count - 1)
    total = None
    if scatter:
        rows = part.shape[0] // count
        copies = []
        for s, peer in zip(steps, peers):
            copy = pltpu.make_async_remote_copy(
                src_ref=part.at[pl.ds(pl.multiple_of(peer * rows, rows), rows)],
                dst_ref=landed.at[s - 1],
                send_sem=send_sem.at[0, s - 1],
                recv_sem=recv_sem.at[0, s - 1],
                device_id={"tensor": peer},
                device_id_type=MESH,
            )
            copy.start()
            copies.append(copy)
        total = part[pl.ds(pl.multiple_of(me * rows, rows), rows), :].astype(WIDE)
        for s, copy in zip(steps, copies):
            copy.wait_recv()
            total = total + landed[s - 1].astype(WIDE)
        for copy in copies:
            copy.wait_send()
    sent = middle(total, ins, outs)
    if gather:
        rows = full.shape[0] // count
        own = pl.ds(pl.multiple_of(me * rows, rows), rows)
        full[own, :] = sent.astype(full.dtype)
        copies = []
        for s, peer in zip(steps, peers):
            copy = pltpu.make_async_remote_copy(
                src_ref=full.at[own],
                dst_ref=full.at[own],
                send_sem=send_sem.at[1, s - 1],
                recv_sem=recv_sem.at[1, s - 1],
                device_id={"tensor": peer},
                device_id_type=MESH,
            )
            copy.start()
            copies.append(copy)
        for copy in copies:
            copy.wait()


def rows_call(middle, number, part, ins, outs, gather=True):
    count = lax.axis_size("tensor")
    scatter = part is not None
    width = (part if scatter else ins[0]).shape[1]
    rows = part.shape[0] // count if scatter else ins[0].shape[0]
    shapes = [jax.ShapeDtypeStruct(shape, kind) for shape, kind in outs]
    if gather:
        shapes.append(jax.ShapeDtypeStruct((rows * count, width), HALF))
    whole = pl.BlockSpec(memory_space=pltpu.VMEM)
    operands = ([part] if scatter else []) + list(ins)
    got = pl.pallas_call(
        partial(_rows_kernel, count, scatter, gather, middle, len(ins), len(outs)),
        out_shape=shapes,
        in_specs=[whole] * len(operands),
        out_specs=[whole] * len(shapes),
        scratch_shapes=([pltpu.VMEM((count - 1, rows, width), HALF)] if scatter else [])
        + [pltpu.SemaphoreType.DMA((2, count - 1))] * 2,
        compiler_params=pltpu.CompilerParams(
            collective_id=number, has_side_effects=True, vmem_limit_bytes=VMEM_LIMIT
        ),
        cost_estimate=pl.CostEstimate(
            flops=0, transcendentals=0, bytes_accessed=1400 * rows * width
        ),
        name=middle.__name__.strip("_"),
    )(*operands)
    return got


def _differ(a, b, count):
    total, bit = 0, 1
    while bit < count:
        total = total + lax.rem(lax.rem(a // bit, 2) + lax.rem(b // bit, 2), 2) * bit
        bit *= 2
    return total


def _slot(difference, count):
    top = count // 2
    return 2 * lax.rem(difference, top) + difference // top


def _enter(peers):
    barrier = pltpu.get_barrier_semaphore()
    for peer in peers:
        pl.semaphore_signal(barrier, inc=1, device_id=peer, device_id_type=MESH)
    pl.semaphore_wait(barrier, len(peers))


def _send(source, dest, send_sem, recv_sem, peer):
    copy = pltpu.make_async_remote_copy(
        src_ref=source,
        dst_ref=dest,
        send_sem=send_sem,
        recv_sem=recv_sem,
        device_id=peer,
        device_id_type=MESH,
    )
    copy.start()
    return copy


def _to_encoder_kernel(count, with_stats, *refs):
    if with_stats:
        value, out, lse, full, stats, own, own_stats, held, other, other_stats, send_sem, recv_sem = refs
    else:
        value, full, own, other, send_sem, recv_sem = refs
    core, me = lax.axis_index("pipe"), lax.axis_index("tensor")
    group = me // (count // 2)
    chips = [lax.rem(me + s, count) for s in range(1, count)]
    _enter([{"tensor": chip} for chip in chips] + [{"pipe": 1 - core}])
    sets = [(value, own, other, full)]
    if with_stats:
        for h in range(2):
            product = value[h].astype(WIDE) * out[h]
            pick = (
                lax.broadcasted_iota(jnp.int32, (8, product.shape[1]), 1) // HEAD
                == lax.broadcasted_iota(jnp.int32, (8, product.shape[1]), 0) - 2
            ).astype(WIDE)
            held[h] = lax.dot_general(
                pick,
                product,
                (((1,), (1,)), ((), ())),
                precision=lax.Precision.HIGHEST,
                preferred_element_type=WIDE,
            )
            held[h, 0:2, :] = lse[h, 0:2, :]
        sets.append((held, own_stats, other_stats, stats))
    copies = []
    for s, chip in enumerate(chips):
        place = _slot(_differ(chip, me, count), count)
        for h in range(2):
            at = lax.rem(h + core, 2) * count + place
            for i, (source, dest, _, _) in enumerate(sets):
                sems = (send_sem.at[i, s, h], recv_sem.at[i, s, h])
                copies.append(_send(source.at[h], dest.at[at], *sems, {"tensor": chip}))
    for h in range(2):
        for source, dest, _, _ in sets:
            dest[lax.rem(h + core, 2) * count] = source[h]
    for copy in copies:
        copy.wait()
    copies = []
    for g in range(2):
        for i, (_, source, dest, _) in enumerate(sets):
            here, there = pl.ds(g * count, count), pl.ds((1 - g) * count, count)
            sems = (send_sem.at[i, count - 1, g], recv_sem.at[i, count - 1, g])
            copies.append(_send(source.at[here], dest.at[there], *sems, {"pipe": 1 - core}))
    for copy in copies:
        copy.wait()
    for _, mine, theirs, dest in sets:

        @pl.when(core == group)
        def _(mine=mine, dest=dest):
            dest[...] = mine[...]

        @pl.when(core != group)
        def _(theirs=theirs, dest=dest):
            dest[...] = theirs[...]


def to_encoder(value, number, out=None, lse=None):
    count = lax.axis_size("tensor")
    _, rows, wide = value.shape
    shapes = [((2 * count, rows, wide), HALF)]
    if out is not None:
        shapes.append(((2 * count, 8, rows), WIDE))
    scratch = [pltpu.VMEM(*s) for s in shapes]
    if out is not None:
        scratch.append(pltpu.VMEM((2, 8, rows), WIDE))
    scratch += [pltpu.VMEM(*s) for s in shapes]
    whole = pl.BlockSpec(memory_space=pltpu.VMEM)
    operands = (value,) if out is None else (value, out, lse)
    return pl.pallas_call(
        partial(_to_encoder_kernel, count, out is not None),
        out_shape=[jax.ShapeDtypeStruct(*s) for s in shapes],
        in_specs=[whole] * len(operands),
        out_specs=[whole] * len(shapes),
        scratch_shapes=scratch + [pltpu.SemaphoreType.DMA((len(shapes), count, 2))] * 2,
        compiler_params=pltpu.CompilerParams(
            collective_id=number, has_side_effects=True, vmem_limit_bytes=VMEM_LIMIT
        ),
        cost_estimate=pl.CostEstimate(flops=0, transcendentals=0, bytes_accessed=60 << 20),
        name="to_encoder",
    )(*operands)


def _over_lanes(weights, wide):
    lanes = lax.broadcasted_iota(jnp.int32, (8, wide), 1) // HEAD
    pick = (lanes == lax.broadcasted_iota(jnp.int32, (8, wide), 0)).astype(HALF)
    high = weights.astype(HALF)
    low = (weights - high.astype(WIDE)).astype(HALF)
    return dot_ta(jnp.concatenate([high, low], axis=0), jnp.concatenate([pick, pick], axis=0))


def _to_decoder_kernel(count, *refs):
    part, lse, heads, out, out_lse = refs[:5]
    other, other_lse, both, both_lse, landed, landed_lse, send_sem, recv_sem = refs[5:]
    core, me = lax.axis_index("pipe"), lax.axis_index("tensor")
    top = count // 2
    chips = [lax.rem(me + s, count) for s in range(1, count)]
    _enter([{"tensor": chip} for chip in chips] + [{"pipe": 1 - core}])
    copies = []
    for g in range(2):
        here, there = pl.ds(g * count, count), pl.ds((1 - g) * count, count)
        for i, (source, dest) in enumerate(((part, other), (lse, other_lse))):
            sems = (send_sem.at[i, count - 1, g], recv_sem.at[i, count - 1, g])
            copies.append(_send(source.at[here], dest.at[there], *sems, {"pipe": 1 - core}))
    for copy in copies:
        copy.wait()
    wide = part.shape[2]
    for i in range(2 * count):
        first, second = lse[i], other_lse[i]
        peak = jnp.maximum(first, second)
        a, b = jnp.exp(first - peak), jnp.exp(second - peak)
        both_lse[i] = peak + jnp.log(a + b)
        share = _over_lanes(b / (a + b), wide)
        mine = part[i].astype(WIDE)
        both[i] = (mine + share * (other[i].astype(WIDE) - mine)).astype(HALF)
    copies = []
    for s, chip in enumerate(chips):
        place = _slot(_differ(chip, me, count), count)
        for h in range(2):
            at = lax.rem(h + core, 2) * count + place
            for i, (source, dest) in enumerate(((both, landed), (both_lse, landed_lse))):
                sems = (send_sem.at[i, s, h], recv_sem.at[i, s, h])
                copies.append(_send(source.at[at], dest.at[s, h], *sems, {"tensor": chip}))
    for copy in copies:
        copy.wait()
    for h in range(2):
        at = lax.rem(h + core, 2) * count
        terms = [(me, both[at], both_lse[at])]
        for s in range(count - 1):
            terms.append((lax.rem(me - s - 1 + count, count), landed[s, h], landed_lse[s, h]))
        logs = [jnp.where(chip // top == core, log, NEGATIVE) for chip, _, log in terms]
        peak = logs[0]
        for log in logs[1:]:
            peak = jnp.maximum(peak, log)
        weights = [jnp.exp(log - peak) for log in logs]
        weights = [
            jnp.where(chip // top == core, w, 0.0) for (chip, _, _), w in zip(terms, weights)
        ]
        total = sum(weights)
        out_lse[h] = peak + jnp.log(total)
        shares = [_over_lanes(w / total, wide) for w in weights]
        value = sum(c * term.astype(WIDE) for c, (_, term, _) in zip(shares, terms)) / sum(shares)
        out[h] = value
        heads[:, h * wide : (h + 1) * wide] = value.astype(HALF)


def to_decoder(part, lse, number):
    count = lax.axis_size("tensor")
    slots, rows, wide = part.shape
    whole = pl.BlockSpec(memory_space=pltpu.VMEM)
    return pl.pallas_call(
        partial(_to_decoder_kernel, count),
        out_shape=[
            jax.ShapeDtypeStruct((rows, 2 * wide), HALF),
            jax.ShapeDtypeStruct((2, rows, wide), WIDE),
            jax.ShapeDtypeStruct((2, 8, rows), WIDE),
        ],
        in_specs=[whole] * 2,
        out_specs=[whole] * 3,
        scratch_shapes=[
            pltpu.VMEM((slots, rows, wide), HALF),
            pltpu.VMEM((slots, 8, rows), WIDE),
            pltpu.VMEM((slots, rows, wide), HALF),
            pltpu.VMEM((slots, 8, rows), WIDE),
            pltpu.VMEM((count - 1, 2, rows, wide), HALF),
            pltpu.VMEM((count - 1, 2, 8, rows), WIDE),
        ]
        + [pltpu.SemaphoreType.DMA((2, count, 2))] * 2,
        compiler_params=pltpu.CompilerParams(
            collective_id=number, has_side_effects=True, vmem_limit_bytes=VMEM_LIMIT
        ),
        cost_estimate=pl.CostEstimate(flops=0, transcendentals=0, bytes_accessed=60 << 20),
        name="to_decoder",
    )(part, lse)


def to_pairs(value):
    slots, rows, wide = value.shape
    each = LANES // wide
    if each == 1:
        return value
    value = value.reshape(slots // each, each, rows, wide)
    return value.transpose(0, 2, 1, 3).reshape(slots // each, rows, LANES)


def from_pairs(value, wide):
    blocks, rows, _ = value.shape
    each = LANES // wide
    if each == 1:
        return value
    value = value.reshape(blocks, rows, each, wide)
    return value.transpose(0, 2, 1, 3).reshape(blocks * each, rows, wide)


def stats_to_pairs(stats, wide):
    each = LANES // wide
    if each == 1:
        return stats
    slots, _, rows = stats.shape
    stats = stats.reshape(slots // each, each, 8, rows)
    return jnp.concatenate(
        [stats[:, :, 0], stats[:, :, 2], jnp.zeros((slots // each, 4, rows), WIDE)], axis=1
    )


def stats_from_pairs(stats, wide):
    each = LANES // wide
    if each == 1:
        return stats
    blocks, _, rows = stats.shape
    value = stats[:, :each].reshape(blocks * each, 1, rows)
    return jnp.concatenate([value, jnp.zeros((blocks * each, 7, rows), WIDE)], axis=1)


def slot_bits():
    count = lax.axis_size("tensor")
    bits, bit = [count // 2], 1
    while bit < count // 2:
        bits.append(bit)
        bit *= 2
    return [b for b in bits if b > 0]


def in_column_halves(values):
    wide = values.shape[2] // 2
    return jnp.stack(
        [
            jnp.concatenate(
                [values[:, k, h * wide : (h + 1) * wide] for k in range(values.shape[1])], axis=1
            ).astype(HALF)
            for h in range(2)
        ]
    )


def _gather_kernel(bits, count, planes, *refs):
    own, refs = refs[:3], refs[3:]
    leaving, dec_rows, *refs = refs
    full, enc_cross, enc_ffn, *refs = refs
    dec, refs = refs[:3], refs[3:]
    rests, refs = refs[:2], refs[2:]
    coming, dec_full, send_sem, recv_sem, local_sem = refs
    core, place, me = lax.axis_index("pipe"), lax.axis_index("dp"), lax.axis_index("tensor")
    wide = own[0].shape[2]
    block = own[0].shape[1] // planes
    sibling = {"pipe": 1 - core}
    chips = {bit: {"tensor": _differ(me, bit, count)} for bit in bits}
    line = [{"tensor": _differ(me, s, count)} for s in range(1, count)]
    dp_bits = [1 << i for i in range(planes.bit_length() - 1)]
    others = {bit: {"dp": _differ(place, bit, planes)} for bit in dp_bits}
    _enter([sibling, *line, *others.values()])
    made = [0]

    def push(source, dest, peer):
        i = made[0]
        made[0] += 1
        return _send(source, dest, send_sem.at[i], recv_sem.at[i], peer)

    def rows_of(difference):
        return pl.ds(pl.multiple_of(_differ(place, difference, planes) * block, block), block)

    enc = [full.at[:, :, pl.ds(0, wide)], enc_cross, enc_ffn]
    shown = []
    for a in range(3):
        i = made[0]
        made[0] += 2
        shown.append(i)

        @pl.when(core == 0)
        def _(a=a, i=i):
            for h in range(2):
                _send(own[a].at[h], enc[a].at[1 - h], send_sem.at[i + h], recv_sem.at[i + h], sibling)
                pltpu.make_async_copy(own[a].at[h], enc[a].at[h], local_sem.at[a, h]).start()

        @pl.when(core == 1)
        def _(a=a, i=i):
            for h in range(2):
                _send(own[a].at[h], dec[a].at[h], send_sem.at[i + h], recv_sem.at[i + h], sibling)
                pltpu.make_async_copy(own[a].at[h], dec[a].at[h], local_sem.at[a, h]).start()

    def arrived(a):
        i = shown[a]
        for h in range(2):
            pltpu.make_async_copy(own[a].at[h], enc[a].at[h], local_sem.at[a, h]).wait()
            pltpu.make_async_copy(own[a].at[h], enc[a].at[h], recv_sem.at[i + h]).wait()

    def line_step(a, n, bit):
        here, size = rows_of(0), own[a].shape[2]
        if a == 0:
            source = full.at[0, here, pl.ds(0, n * size)]
            return [push(source, full.at[0, here, pl.ds(n * size, n * size)], chips[bit])]
        rest = rests[a - 1]
        copies = [
            push(enc[a].at[0, here], rest.at[:, pl.ds((n - 1) * size, size)], chips[bit])
        ]
        if n > 1:
            source = rest.at[:, pl.ds(0, (n - 1) * size)]
            copies.append(push(source, rest.at[:, pl.ds(n * size, (n - 1) * size)], chips[bit]))
        return copies

    def wait(copies):
        for copy in copies:
            copy.wait()

    def advance(chain):
        wait(chain["now"])
        chain["now"] = line_step(chain["array"], *chain["todo"].pop(0)) if chain["todo"] else []

    def columns(part):
        return pl.ds(wide + part * half, half)

    def plane_step(j):
        copies = []
        for part, order in enumerate(orders):
            for m in held[part]:
                at = full.at[0, rows_of(m), columns(part)]
                copies.append((part, m ^ order[j], push(at, at, others[order[j]])))
        return copies

    def share(part, m):
        here = rows_of(m)
        source = full.at[0, here, columns(part)]
        return push(source, full.at[1, here, columns(part)], sibling)

    steps = [(1 << i, bit) for i, bit in enumerate(bits)]
    for_attn, for_cross, for_ffn = [{"array": a, "todo": list(steps), "now": []} for a in range(3)]
    arrived(0)
    advance(for_attn)
    arrived(2)
    advance(for_attn)
    advance(for_ffn)
    while for_attn["now"]:
        advance(for_attn)
    token_sem = made[0]
    made[0] += 1

    @pl.when(core == 1)
    def _():
        _send(leaving, coming, send_sem.at[token_sem], recv_sem.at[token_sem], chips[bits[0]])

    at = pl.ds(pl.multiple_of(me * dec_rows.shape[0], dec_rows.shape[0]), dec_rows.shape[0])
    dec_full[at, :] = dec_rows[...]
    dec_sent = [push(dec_full.at[at], dec_full.at[at], peer) for peer in line]
    half = (count - 1) * wide // 2
    orders, held = (dp_bits, dp_bits[::-1]), ([0], [0])
    moving = plane_step(0)
    shared = [share(part, 0) for part in range(2)]
    advance(for_ffn)
    arrived(1)
    for j in range(len(dp_bits)):
        for _, _, copy in moving:
            copy.wait()
        for part, order in enumerate(orders):
            held[part].extend([m ^ order[j] for m in held[part]])
        following = plane_step(j + 1) if j + 1 < len(dp_bits) else []
        shared += [share(part, m) for part, m, _ in moving]
        moving = following
        advance(for_cross)
    while for_ffn["now"]:
        advance(for_ffn)
    while for_cross["now"]:
        advance(for_cross)

    @pl.when(core == 1)
    def _():
        pltpu.make_async_copy(leaving, leaving, send_sem.at[token_sem]).wait()
        pltpu.make_async_copy(leaving, coming, recv_sem.at[token_sem]).wait()

    wait(dec_sent)
    wait(shared)
    for a in range(3):
        for h in range(2):
            pltpu.make_async_copy(own[a].at[h], own[a].at[h], send_sem.at[shown[a] + h]).wait()


def gather_weights(attn, cross, ffn, leaving, dec_rows):
    own = (attn, cross, ffn)
    count, planes = lax.axis_size("tensor"), lax.axis_size("dp")
    depth = attn.shape[1]
    shapes = [(2, depth, count * attn.shape[2]), cross.shape, ffn.shape]
    shapes += [v.shape for v in own]
    shapes += [(depth // planes, (count - 1) * v.shape[2]) for v in (cross, ffn)]
    shapes += [leaving.shape, (count * dec_rows.shape[0], dec_rows.shape[1])]
    hbm, vmem = pl.BlockSpec(memory_space=pl.ANY), pl.BlockSpec(memory_space=pltpu.VMEM)
    return pl.pallas_call(
        partial(_gather_kernel, slot_bits(), count, planes),
        out_shape=[jax.ShapeDtypeStruct(shape, HALF) for shape in shapes],
        in_specs=[vmem] * 3 + [hbm, vmem],
        out_specs=[hbm] * (len(shapes) - 1) + [vmem],
        scratch_shapes=[pltpu.SemaphoreType.DMA((64,))] * 2 + [pltpu.SemaphoreType.DMA((3, 2))],
        compiler_params=pltpu.CompilerParams(
            collective_id=9, has_side_effects=True, vmem_limit_bytes=VMEM_LIMIT
        ),
        cost_estimate=pl.CostEstimate(flops=0, transcendentals=0, bytes_accessed=280 << 20),
        name="gather_weights",
    )(*own, leaving, dec_rows)


def gather_planes(rest):
    return lax.all_gather(rest, "dp", axis=0, tiled=True)


def fold_cores(mine, other):
    return (mine.astype(WIDE) + swap(other, "pipe", 1).astype(WIDE)).astype(HALF)


def fold_planes(term):
    return lax.psum_scatter(term, "dp", scatter_dimension=0, tiled=True)


def scatter_local(terms):
    core = lax.axis_index("pipe")
    wide = terms[0].shape[1] // 2
    pick = partial(lax.dynamic_slice_in_dim, slice_size=wide, axis=1)
    mine = jnp.concatenate([pick(v.astype(HALF), core * wide) for v in terms], axis=1)
    other = jnp.concatenate([pick(v.astype(HALF), (1 - core) * wide) for v in terms], axis=1)
    term = fold_cores(mine, other)
    return fold_planes(term), term


def _blocks_of(weights, kinds):
    wide = weights.shape[2] // (lax.axis_size("tensor") * kinds)
    each = LANES // wide
    blocks = lax.axis_size("tensor") // each
    spec = pl.BlockSpec(
        (None, weights.shape[1], each * kinds * wide), lambda i: (i // blocks, 0, lax.rem(i, blocks))
    )
    return wide, each, blocks, spec


def _piece(weights, kinds, wide, each, k):
    parts = [weights[:, (j * kinds + k) * wide : (j * kinds + k + 1) * wide] for j in range(each)]
    return parts[0] if each == 1 else jnp.concatenate(parts, axis=1)


def _store_grads(refs, i, blocks, pieces, wide, each):
    columns = [p[:, j * wide : (j + 1) * wide] for j in range(each) for p in pieces]
    for ref, when in zip(refs, (i < blocks, i >= blocks)):

        @pl.when(when)
        def _(ref=ref):
            for n, column in enumerate(columns):
                ref[:, n * wide : (n + 1) * wide] = column.astype(ref.dtype)


def _grad_specs(depth, columns, blocks):
    return [
        pl.BlockSpec((depth, columns), lambda i: (0, jnp.minimum(i, blocks - 1))),
        pl.BlockSpec((depth, columns), lambda i: (0, jnp.maximum(i - blocks, 0))),
    ]


def _spread_kernel(kinds, use, wide, each, blocks, with_grad, pair, x, weights, *refs):
    left = x[...]
    values = [dot(left, _piece(weights, kinds, wide, each, k)) for k in use]
    if with_grad:
        y, *refs = refs
        i = pl.program_id(0)
        _store_grads(refs[-2:], i, blocks, [dot_ta(left, y[...].astype(HALF))], wide, each)
    for n in range(pair):
        ref = refs[len(refs) - pair + n]

        @pl.when(lax.rem(pl.program_id(0), pair) == n)
        def _(ref=ref):
            ref[0] = values[-2].astype(HALF)
            ref[1] = values[-1].astype(HALF)

    values = values[:-2] if pair else values
    for ref, value in zip(refs, values):
        ref[...] = value.astype(HALF)


def spread(x, weights, kinds, use, y=None, pair=0):
    rows, width = x.shape
    wide, each, blocks, spec = _blocks_of(weights, kinds)
    column = pl.BlockSpec((rows, LANES), lambda i: (0, i))
    single = len(use) - (2 if pair else 0)
    shapes, specs = [((rows, width), HALF)] * single, [column] * single
    for _ in range(pair):
        shapes.append(((2, rows, width // pair), HALF))
        specs.append(pl.BlockSpec((2, rows, LANES), lambda i: (0, 0, i // pair)))
    if y is not None:
        shapes += [((width, width // 2), HALF)] * 2
        specs += _grad_specs(width, LANES, blocks)
    return pl.pallas_call(
        partial(_spread_kernel, kinds, use, wide, each, blocks, y is not None, pair),
        out_shape=[jax.ShapeDtypeStruct(*s) for s in shapes],
        grid=(2 * blocks,),
        in_specs=[pl.BlockSpec((rows, width), lambda i: (0, 0)), spec] + [column] * (y is not None),
        out_specs=specs,
        compiler_params=pltpu.CompilerParams(vmem_limit_bytes=VMEM_LIMIT),
        cost_estimate=pl.CostEstimate(
            flops=8 * rows * width * width * (len(use) + (y is not None)),
            transcendentals=0,
            bytes_accessed=2 * width * width * kinds,
        ),
        name="spread",
    )(x, weights, *([] if y is None else [y]))


def _collect_kernel(kinds, use, wide, each, blocks, n_y, split, with_grad, ending, n_extra, *refs):
    refs = list(refs)
    ys, refs = refs[:n_y], refs[n_y:]
    weights, refs = refs[0], refs[1:]
    x = refs.pop(0) if with_grad else None
    extra, refs = refs[:n_extra], refs[n_extra:]
    acc = refs.pop()
    grads = [refs.pop(), refs.pop()][::-1] if with_grad else []
    i = pl.program_id(0)

    @pl.when(i == 0)
    def _():
        acc[...] = jnp.zeros(acc.shape, WIDE)

    values, ys = [], list(ys)
    while ys:
        y = ys.pop(0)
        if len(y.shape) == 2:
            values.append(y[...])
        elif split:
            odd = ys.pop(0)
            values += [jnp.where(lax.rem(i, 2) == 0, y[n], odd[n]) for n in range(2)]
        else:
            values += [y[0], y[1]]
    values = [v.astype(HALF) for v in values]
    for value, k in zip(values, use):
        acc[...] += dot_bt(value, _piece(weights, kinds, wide, each, k))
    if with_grad:
        left = x[...]
        _store_grads(grads, i, blocks, [dot_ta(left, v) for v in values], wide, each)

    @pl.when(i == 2 * blocks - 1)
    def _():
        ending(acc[...], extra, refs)


def collect(ys, weights, kinds, use, ending, extra, outs, x=None):
    rows, width = ys[0].shape[-2], weights.shape[1]
    split = any(y.ndim == 3 and y.shape[2] < width for y in ys)
    wide, each, blocks, spec = _blocks_of(weights, kinds)
    y_specs = [
        pl.BlockSpec((rows, LANES), lambda i: (0, i))
        if y.ndim == 2
        else pl.BlockSpec((2, rows, LANES), lambda i: (0, 0, i // (2 if split else 1)))
        for y in ys
    ]
    fixed = [pl.BlockSpec(v.shape, lambda i: (0, 0)) for v in ([] if x is None else [x]) + extra]
    shapes = list(outs)
    specs = [pl.BlockSpec(shape, lambda i: (0, 0)) for shape, _ in outs]
    if x is not None:
        shapes += [((width, len(use) * width // 2), HALF)] * 2
        specs += _grad_specs(width, len(use) * LANES, blocks)
    return pl.pallas_call(
        partial(
            _collect_kernel, kinds, use, wide, each, blocks, len(ys), split, x is not None, ending, len(extra)
        ),
        out_shape=[jax.ShapeDtypeStruct(*s) for s in shapes],
        grid=(2 * blocks,),
        in_specs=y_specs + [spec] + fixed,
        out_specs=specs,
        scratch_shapes=[pltpu.VMEM((rows, width), WIDE)],
        compiler_params=pltpu.CompilerParams(vmem_limit_bytes=VMEM_LIMIT),
        cost_estimate=pl.CostEstimate(
            flops=8 * rows * width * width * len(use) * (1 + (x is not None)),
            transcendentals=0,
            bytes_accessed=2 * width * width * kinds,
        ),
        name="collect",
    )(*ys, weights, *([] if x is None else [x]), *extra)


def _end_norm(total, ins, outs):
    resid, gain, bias = ins
    value, normed, inv_scale = _norm_rows(total + resid[...], gain[...], bias[...])
    outs[0][...] = value
    outs[1][...] = value.astype(HALF)
    outs[2][...] = normed
    outs[3][...] = jnp.broadcast_to(inv_scale, outs[3].shape)


def _end_norm_back(total, ins, outs):
    *resid, normed, inv_scale, gain = ins
    total = total + resid[0][...] if resid else total
    grad, grad_gain, grad_bias = _norm_rows_back(total, normed[...], inv_scale[:, 0:1], gain[...])
    outs[0][...] = grad
    outs[1][...] = grad.astype(HALF)
    outs[2][0:1, :] = grad_gain
    outs[2][1:2, :] = grad_bias


def _ffn_parts(count, own, mine, other):
    depth, wide = own.shape[1], own.shape[2] // 2
    specs = []
    for k in range(2):
        specs.append(pl.BlockSpec((None, depth, wide), lambda i, k=k: (i // count, 0, k)))
        for first in (0, count):
            specs.append(
                pl.BlockSpec(
                    (depth, wide),
                    lambda i, k=k, first=first: (0, 2 * jnp.clip(i - first - 1, 0, count - 2) + k),
                )
            )
    return wide, specs


def _ffn_cases(count, i, ins, outs):
    local = lax.rem(i, count) == 0
    return [
        (local, ins[0], outs[0]),
        (jnp.logical_and(~local, i < count), ins[1], outs[1]),
        (jnp.logical_and(~local, i > count), ins[2], outs[2]),
    ]


def _ffn_kernel(count, x, resid, gain, bias, *refs):
    ins, outs, refs = refs[:3], refs[3:6], refs[6:]
    value, value_low, normed, inv_scale, active, slope, acc = refs
    i = pl.program_id(0)

    @pl.when(i == 0)
    def _():
        acc[...] = jnp.zeros(acc.shape, WIDE)

    for condition, first, second in _ffn_cases(count, i, ins, outs):

        @pl.when(condition)
        def _(first=first, second=second):
            hidden = dot(x[...], first[...])
            below = 0.5 * (1.0 + lax.erf(hidden * (2.0**-0.5)))
            density = jnp.exp(-0.5 * hidden * hidden) * 0.3989422804014327
            act = (hidden * below).astype(HALF)
            active[...] = act
            slope[...] = (below + hidden * density).astype(HALF)
            acc[...] += dot_bt(act, second[...])

    @pl.when(i == 2 * count - 1)
    def _():
        _end_norm(acc[...], (resid, gain, bias), (value, value_low, normed, inv_scale))


def feed_forward(x, resid, gain, bias, own, mine, other):
    count = lax.axis_size("tensor")
    rows, width = x.shape
    wide, specs = _ffn_parts(count, own, mine, other)
    units = 2 * count * wide
    fixed = [pl.BlockSpec(v.shape, lambda i: (0, 0)) for v in (x, resid, gain, bias)]
    shapes = [((rows, width), WIDE), ((rows, width), HALF), ((rows, width), WIDE), ((rows, LANES), WIDE)]
    column = pl.BlockSpec((rows, wide), lambda i: (0, i))
    return pl.pallas_call(
        partial(_ffn_kernel, count),
        out_shape=[jax.ShapeDtypeStruct(*s) for s in shapes]
        + [jax.ShapeDtypeStruct((rows, units), HALF)] * 2,
        grid=(2 * count,),
        in_specs=fixed + specs,
        out_specs=[pl.BlockSpec(s, lambda i: (0, 0)) for s, _ in shapes] + [column] * 2,
        scratch_shapes=[pltpu.VMEM((rows, width), WIDE)],
        compiler_params=pltpu.CompilerParams(vmem_limit_bytes=VMEM_LIMIT),
        cost_estimate=pl.CostEstimate(
            flops=12 * rows * width * units, transcendentals=2 * rows * units, bytes_accessed=4 * width * units
        ),
        name="feed_forward",
    )(x, resid, gain, bias, own, mine, other, own, mine, other)


def _ffn_back_kernel(count, x, grad, resid, normed, inv_scale, gain, active, slope, *refs):
    ins, outs, refs = refs[:3], refs[3:6], refs[6:]
    result, result_low, terms, *grads, acc = refs
    i = pl.program_id(0)

    @pl.when(i == 0)
    def _():
        acc[...] = jnp.zeros(acc.shape, WIDE)

    for condition, first, second in _ffn_cases(count, i, ins, outs):

        @pl.when(condition)
        def _(first=first, second=second):
            hidden = (dot(grad[...], second[...]) * slope[...].astype(WIDE)).astype(HALF)
            acc[...] += dot_bt(hidden, first[...])
            f1 = dot_ta(x[...], hidden).astype(HALF)
            f2 = dot_ta(grad[...], active[...]).astype(HALF)
            for half, when in enumerate((i < count, i >= count)):

                @pl.when(when)
                def _(half=half):
                    grads[half][...] = f1
                    grads[2 + half][...] = f2

    @pl.when(i == 2 * count - 1)
    def _():
        _end_norm_back(acc[...], (resid, normed, inv_scale, gain), (result, result_low, terms))


def feed_forward_back(x, grad, resid, normed, inv_scale, gain, active, slope, own, mine, other):
    count = lax.axis_size("tensor")
    rows, width = x.shape
    wide, specs = _ffn_parts(count, own, mine, other)
    column = pl.BlockSpec((rows, wide), lambda i: (0, i))
    fixed = [pl.BlockSpec(v.shape, lambda i: (0, 0)) for v in (x, grad, resid, normed, inv_scale, gain)]
    shapes = [((rows, width), WIDE), ((rows, width), HALF), ((8, width), WIDE)]
    grad_specs = [
        pl.BlockSpec((width, wide), lambda i: (0, jnp.minimum(i, count - 1))),
        pl.BlockSpec((width, wide), lambda i: (0, jnp.maximum(i - count, 0))),
    ]
    return pl.pallas_call(
        partial(_ffn_back_kernel, count),
        out_shape=[jax.ShapeDtypeStruct(*s) for s in shapes]
        + [jax.ShapeDtypeStruct((width, count * wide), HALF)] * 4,
        grid=(2 * count,),
        in_specs=fixed + [column] * 2 + specs,
        out_specs=[pl.BlockSpec(s, lambda i: (0, 0)) for s, _ in shapes] + grad_specs * 2,
        scratch_shapes=[pltpu.VMEM((rows, width), WIDE)],
        compiler_params=pltpu.CompilerParams(vmem_limit_bytes=VMEM_LIMIT),
        cost_estimate=pl.CostEstimate(
            flops=32 * rows * width * count * wide, transcendentals=0, bytes_accessed=16 * width * count * wide
        ),
        name="feed_forward_back",
    )(x, grad, resid, normed, inv_scale, gain, active, slope, own, mine, other, own, mine, other)


def _add_rows(dest, first, second):
    rows = 64 if dest.shape[0] % 64 == 0 else dest.shape[0]

    def step(i, carry):
        at = pl.ds(pl.multiple_of(i * rows, rows), rows)
        dest[at, :] = (first[at, :].astype(WIDE) + second[at, :].astype(WIDE)).astype(HALF)
        return carry

    lax.fori_loop(0, dest.shape[0] // rows, step, 0)


def _finish_kernel(bits, count, planes, *refs):
    in_mine, out_mine, in_other, out_other, f1, f2, ckv, dec_ffn, dec_small, tokens = refs[:10]
    norm_terms, refs = refs[10:16], refs[16:]
    attn_out, cross_out, ffn_out, far, near, norm_sum = refs[:6]
    land_in, land_out, term, *refs = refs[6:]
    n_steps = planes.bit_length() - 1
    land_planes, refs = refs[:n_steps], refs[n_steps:]
    folded, landed, refs = refs[:4], refs[4:8], refs[8:]
    enc_ffn, enc_small, got_ffn, got_small, norm_other, norm_land, send_sem, recv_sem = refs
    core, place, me = lax.axis_index("pipe"), lax.axis_index("dp"), lax.axis_index("tensor")
    sibling = {"pipe": 1 - core}
    line = {s: {"tensor": _differ(me, s, count)} for s in range(1, count)}
    cross_over = {"pipe": 1 - core, "tensor": _differ(me, bits[0], count)}
    dp_bits = [1 << i for i in range(n_steps)]
    others = {bit: {"dp": _differ(place, bit, planes)} for bit in dp_bits}
    _enter([sibling, cross_over, *line.values(), *others.values()])
    made = [0]

    def number():
        made[0] += 1
        return made[0] - 1

    def push(source, dest, peer):
        i = number()
        return _send(source, dest, send_sem.at[i], recv_sem.at[i], peer)

    def wait(copies):
        for copy in copies:
            copy.wait()

    for i in range(3):
        at = slice(2 * i, 2 * i + 2)
        enc, dec = norm_terms[i][0:2, :], norm_terms[3 + i][0:2, :]
        norm_sum[at, :] = jnp.where(core == 0, enc, dec)
        norm_other[at, :] = jnp.where(core == 0, dec, enc)
    norm_sum[6:8, :] = jnp.zeros((2, norm_sum.shape[1]), WIDE)
    norm_other[6:8, :] = jnp.zeros((2, norm_sum.shape[1]), WIDE)
    norm_peers = [*others.values(), *(line[bit] for bit in bits)]
    norm_now = [push(norm_other, norm_land.at[0], sibling)]

    def advance_norms():
        if norm_now:
            norm_now.pop().wait()
            n = n_steps + len(bits) - len(norm_peers)
            norm_sum[...] = norm_sum[...] + norm_land[n]
            if norm_peers:
                norm_now.append(push(norm_sum, norm_land.at[n + 1], norm_peers.pop(0)))

    to_core = [push(in_other, land_in, sibling), push(out_other, land_out, sibling)]

    def chain(source, a, at=slice(None)):
        fold, land = (v if at == slice(None) else v.at[at] for v in (folded[a], landed[a]))
        size = folded[a].shape[1] * 2 // count
        return {
            "source": source,
            "fold": fold,
            "land": land,
            "size": size,
            "slots": count,
            "bits": list(reversed(bits)),
            "now": [],
        }

    def advance(c):
        land, size = c["land"], c["size"]
        if c["now"]:
            wait(c["now"])
            c["now"] = []
            kept = c["slots"] // 2 * size
            offset = (count - c["slots"]) * size
            at = pl.ds(0, kept)
            _add_rows(c["fold"].at[:, at], c["source"].at[:, at], land.at[:, pl.ds(offset, kept)])
            c["source"], c["slots"] = c["fold"], c["slots"] // 2
        if c["bits"]:
            kept = c["slots"] // 2 * size
            offset = (count - c["slots"]) * size
            source = c["source"].at[:, pl.ds(kept, kept)]
            c["now"] = [push(source, land.at[:, pl.ds(offset, kept)], line[c["bits"].pop(0)])]

    chains = [chain(f2, 0), chain(f1, 1), chain(ckv, 2)]
    advance(chains[0])

    wait(to_core)
    block = in_mine.shape[0] // planes
    wide = term.shape[1] // count
    inner = in_mine.shape[1] // count

    def sum_step(i, carry):
        at = pl.ds(pl.multiple_of(i * 64, 64), 64)
        for s in range(count):
            first = in_mine[at, s * inner : (s + 1) * inner].astype(WIDE)
            second = land_in[at, s * inner : (s + 1) * inner].astype(WIDE)
            term[at, s * wide : s * wide + inner] = (first + second).astype(HALF)
            outer = wide - inner
            first = out_mine[at, s * outer : (s + 1) * outer].astype(WIDE)
            second = land_out[at, s * outer : (s + 1) * outer].astype(WIDE)
            term[at, s * wide + inner : (s + 1) * wide] = (first + second).astype(HALF)
        return carry

    lax.fori_loop(0, in_mine.shape[0] // 64, sum_step, 0)

    columns = term.shape[1] // 2
    orders = (dp_bits, dp_bits[::-1])
    held = [[list(range(planes)) for _ in orders] for _ in range(2)]
    piece = block // 2

    def rows_of(difference, r):
        first = _differ(place, difference, planes) * block + r * piece
        return pl.ds(pl.multiple_of(first, piece), piece)

    def at_of(p, m, r):
        return term.at[rows_of(m, r), pl.ds(p * columns, columns)]

    def plane_start(j, r):
        copies = []
        for p, order in enumerate(orders):
            bit = order[j]
            kept = [m for m in held[r][p] if not m & bit]
            for n, m in enumerate(kept):
                dest = land_planes[j].at[p, n, pl.ds(r * piece, piece)]
                copies.append((p, m, dest, push(at_of(p, m ^ bit, r), dest, others[bit])))
            held[r][p] = kept
        return copies

    def plane_finish(copies, r):
        for p, m, dest, copy in copies:
            copy.wait()
            _add_rows(at_of(p, m, r), at_of(p, m, r), dest)

    moving = [plane_start(0, r) for r in range(2)]
    for_attn = []
    advance(chains[1])
    advance(chains[2])

    half = tokens.shape[1] // 2
    far_sem, near_sem, same_sem = number(), number(), number()

    @pl.when(core == 1)
    def _():
        _send(tokens.at[:, pl.ds(0, half)], far, send_sem.at[far_sem], recv_sem.at[far_sem], cross_over)
        _send(
            tokens.at[:, pl.ds(half, half)], far, send_sem.at[same_sem], recv_sem.at[far_sem], line[bits[0]]
        )

    @pl.when(core == 0)
    def _():
        _send(tokens.at[:, pl.ds(half, half)], near, send_sem.at[near_sem], recv_sem.at[near_sem], sibling)

    for j in range(n_steps):
        for r in range(2):
            plane_finish(moving[r], r)
            if j + 1 < n_steps:
                moving[r] = plane_start(j + 1, r)
            else:
                for_attn.append(chain(term.at[rows_of(0, r)], 3, pl.ds(r * piece, piece)))
                advance(for_attn[-1])
            advance(chains[(2 * j + r) % 3])
            advance_norms()
    while any(c["now"] or c["bits"] for c in chains + for_attn):
        for c in for_attn + chains:
            advance(c)
        advance_norms()
    while norm_now:
        advance_norms()

    size = [fold.shape[1] * 2 // count for fold in folded]
    enc_ffn[:, : size[1]] = folded[1][:, : size[1]]
    enc_ffn[:, size[1] :] = folded[0][:, : size[0]]
    enc_small[:, : size[3]] = folded[3][:, : size[3]]
    enc_small[:, size[3] :] = folded[2][:, : size[2]]
    swap_sem = [number(), number()]

    @pl.when(core == 0)
    def _():
        _send(dec_ffn, got_ffn, send_sem.at[swap_sem[0]], recv_sem.at[swap_sem[0]], sibling)
        _send(dec_small, got_small, send_sem.at[swap_sem[1]], recv_sem.at[swap_sem[1]], sibling)

    @pl.when(core == 1)
    def _():
        _send(enc_ffn, got_ffn, send_sem.at[swap_sem[0]], recv_sem.at[swap_sem[0]], sibling)
        _send(enc_small, got_small, send_sem.at[swap_sem[1]], recv_sem.at[swap_sem[1]], sibling)

    for i, (mine, got) in enumerate(((enc_ffn, got_ffn), (enc_small, got_small))):
        pltpu.make_async_copy(mine, got, send_sem.at[swap_sem[i]]).wait()
        pltpu.make_async_copy(mine, got, recv_sem.at[swap_sem[i]]).wait()

    def write(first, second):
        for h, (ffn, small) in enumerate((first, second)):
            c = ffn.shape[1] // 2
            for k in range(2):
                ffn_out[k, :, h * c : (h + 1) * c] = ffn[:, k * c : (k + 1) * c].astype(WIDE)
            c = small.shape[1] // 6
            for k in range(6):
                dest = attn_out.at[k] if k < 4 else cross_out.at[k - 4]
                dest[:, h * c : (h + 1) * c] = small[:, k * c : (k + 1) * c].astype(WIDE)

    @pl.when(core == 0)
    def _():
        write((enc_ffn, enc_small), (got_ffn, got_small))

    @pl.when(core == 1)
    def _():
        write((got_ffn, got_small), (dec_ffn, dec_small))

    pltpu.make_async_copy(far, far, recv_sem.at[far_sem]).wait()

    @pl.when(core == 1)
    def _():
        pltpu.make_async_copy(far, far, send_sem.at[far_sem]).wait()
        pltpu.make_async_copy(far, far, send_sem.at[same_sem]).wait()
        pltpu.make_async_copy(near, near, recv_sem.at[near_sem]).wait()

    @pl.when(core == 0)
    def _():
        pltpu.make_async_copy(near, near, send_sem.at[near_sem]).wait()


def finish(in_grads, out_grads, f1, f2, ckv, dec_ffn, dec_small, tokens, norm_terms):
    count, planes = lax.axis_size("tensor"), lax.axis_size("dp")
    depth = in_grads[0].shape[0]
    rows = depth // planes
    attn_columns = in_grads[0].shape[1] + out_grads[0].shape[1]
    wide = 2 * dec_small.shape[1] // 6
    vmem = pl.BlockSpec(memory_space=pltpu.VMEM)
    operands = (in_grads[0], out_grads[0], in_grads[1], out_grads[1], f1, f2, ckv, dec_ffn, dec_small, tokens)
    operands += tuple(norm_terms)
    lines = [f2.shape[1], f1.shape[1], ckv.shape[1], attn_columns]
    scratch = [in_grads[0].shape, out_grads[0].shape, (depth, attn_columns)]
    blocks = planes // 2
    while blocks >= 1:
        scratch.append((2, blocks, rows, attn_columns // 2))
        blocks //= 2
    scratch += [(rows, c // 2) for c in lines]
    scratch += [(rows, c - c // count) for c in lines]
    scratch += [dec_ffn.shape, dec_small.shape] * 2
    norm_steps = count.bit_length() + planes.bit_length() - 1
    norm_shapes = [norm_terms[0].shape, (norm_steps, *norm_terms[0].shape)]
    token_piece = ((tokens.shape[0], tokens.shape[1] // 2), HALF)
    outs = [((4, rows, wide), WIDE), ((2, rows, wide), WIDE), ((2, rows, dec_ffn.shape[1]), WIDE)]
    outs += [token_piece, token_piece, (norm_terms[0].shape, WIDE)]
    return pl.pallas_call(
        partial(_finish_kernel, slot_bits(), count, planes),
        out_shape=[jax.ShapeDtypeStruct(*o) for o in outs],
        in_specs=[vmem] * len(operands),
        out_specs=[vmem] * len(outs),
        scratch_shapes=[pltpu.VMEM(shape, HALF) for shape in scratch]
        + [pltpu.VMEM(shape, WIDE) for shape in norm_shapes]
        + [pltpu.SemaphoreType.DMA((64,))] * 2,
        compiler_params=pltpu.CompilerParams(
            collective_id=5, has_side_effects=True, vmem_limit_bytes=VMEM_LIMIT
        ),
        cost_estimate=pl.CostEstimate(flops=0, transcendentals=0, bytes_accessed=200 << 20),
        name="finish",
    )(*operands)


def per_device(
    enc_input,
    dec_input,
    dec_cotangent,
    enc_lengths,
    dec_lengths,
    attn_weights,
    cross_weights,
    ffn_weights,
    norm_gains,
    norm_biases,
):
    core, place = lax.axis_index("pipe"), lax.axis_index("tensor")
    count = lax.axis_size("tensor")
    top_bit = count // 2
    group = place // top_bit
    block = jnp.where(core == 0, place, place ^ top_bit)
    span, width = enc_input.shape[1:]
    dec_span = dec_input.shape[1]
    local_width = attn_weights.shape[3]
    is_first = core == 0
    chips = range(count)
    sources = [(s // top_bit, s % top_bit) for s in range(2 * top_bit)]
    half = width // 2
    half_local = local_width // 2

    def owner(t):
        return t // top_bit

    norms = jnp.concatenate([norm_gains[0], norm_biases[0]], axis=0)
    norms_other = swap(norms, "pipe", 1)
    enc_norms = jnp.where(is_first, norms, norms_other)
    dec_norms = jnp.where(is_first, norms_other, norms)
    eg, eb, dg, db = enc_norms[:3], enc_norms[3:], dec_norms[:3], dec_norms[3:]

    pick = partial(lax.dynamic_index_in_dim, index=core, axis=0, keepdims=False)
    start_low = pick(dec_input)
    (
        w_attn,
        own_cross,
        own_ffn,
        dec_attn_halves,
        dec_cross_halves,
        dec_ffn_halves,
        cross_rest,
        ffn_rest,
        got,
        start_full,
    ) = gather_weights(
        *[in_column_halves(v[0]) for v in (after(attn_weights, norms_other), cross_weights, ffn_weights)],
        lax.dynamic_index_in_dim(enc_input, 1 - group, 0, False),
        start_low,
    )
    kept = lax.dynamic_index_in_dim(enc_input, group, 0, False)
    tokens = jnp.where(is_first, kept, got).astype(WIDE)
    mine_ffn = gather_planes(ffn_rest)

    def natural(halves, kinds):
        wide = halves.shape[2] // kinds
        return [
            jnp.concatenate([halves[h][:, k * wide : (k + 1) * wide] for h in range(2)], axis=1)
            for k in range(kinds)
        ]

    dec_attn, dec_cross, dec_ffn = [
        natural(v, k) for v, k in ((dec_attn_halves, 4), (dec_cross_halves, 2), (dec_ffn_halves, 2))
    ]
    blocks = width // LANES
    masks = [a * (blocks // 2) + c * (blocks // 2 // top_bit) for a, c in sources]

    def gain_of(i):
        return enc_norms[i : i + 1]

    def bias_of(i):
        return enc_norms[3 + i : 4 + i]

    embed, start_normed, start_scale = norm_forward(tokens, eg[0], eb[0])
    start_scale = jnp.broadcast_to(start_scale, (span, LANES))
    embed_low = embed.astype(HALF)
    parts = 2 if all(m % 2 == 0 for m in masks) else 1
    query, *key_value = spread(embed_low, w_attn, 4, (0, 1, 2), pair=parts)

    def across_chips(value):
        held, bit = [value], 1
        while bit < top_bit:
            held = held + [swap(v, "tensor", bit) for v in held]
            bit *= 2
        return held

    def exchange(held, *earlier):
        if earlier:
            held = after(tuple(held), *earlier)
        return list(held) + [swap(v, "pipe", 1) for v in held]

    key_values = [across_chips(v) for v in key_value]
    mine_cross = gather_planes(after(cross_rest, query))

    enc_lengths, dec_lengths = [after(v, query) for v in (enc_lengths, dec_lengths)]
    enc_row = lax.dynamic_index_in_dim(enc_lengths, group, 0, False)
    dec_row_of_group = lax.dynamic_index_in_dim(dec_lengths, group, 0, False)
    dec_row = lax.dynamic_index_in_dim(dec_lengths, core, 0, False)
    spots = jnp.arange(span, dtype=jnp.int32)
    own_seg = table_of(block * span + spots, enc_row)
    key_seg = jnp.stack(
        [table_of((block ^ (a * top_bit) ^ c) * span + spots, enc_row) for a, c in sources]
    )
    dec_spots = jnp.arange(dec_span * count, dtype=jnp.int32)
    dec_seg = table_of(dec_spots, dec_row)
    enc_segs = tables(own_seg, key_seg)
    dec_segs = tables(dec_seg, dec_seg[None])
    cross_segs = tables(table_of(dec_spots, dec_row_of_group), own_seg[None])

    start_full = after(start_full, key_value)
    start = start_low.astype(WIDE)
    rows_full = dec_span * count
    wide_rows = ((dec_span, width), WIDE)
    kept_rows = [wide_rows, wide_rows, ((dec_span, LANES), WIDE)]
    norm_terms = ((8, width), WIDE)
    dec_in_w = [dec_attn[k] for k in range(3)]
    dec_query = dot(start_full, dec_in_w[0]).astype(HALF)
    dec_kv = jnp.stack([dot(start_full, w).astype(HALF) for w in dec_in_w[1:]])
    dec_heads_wide, dec_lse = attend(dec_query, [dec_kv], dec_segs, [0], True)
    dec_heads = dec_heads_wide.astype(HALF)
    term = dot_bt(dec_heads, dec_attn[3]).astype(HALF)

    attended = ()
    for n in range(parts):
        key_values[n] = exchange(key_values[n], *attended, *((term,) if n else ()))
        attended = attend(
            query, key_values[n], enc_segs, masks, part=n if parts == 2 else None, into=attended
        )
    heads_wide, lse = attended

    def sum_to_owner(term, resid, *earlier):
        total = after(resid, *earlier)
        for s in range(count):
            rows = lax.dynamic_slice_in_dim(term, (place ^ s) * dec_span, dec_span, 0)
            total = total + (swap(rows, "tensor", s) if s else rows).astype(WIDE)
        return total

    self_norm, self_normed, self_scale = norm_forward(sum_to_owner(term, start, lse), dg[0:1], db[0:1])
    self_scale = jnp.broadcast_to(self_scale, (dec_span, LANES))
    self_low = self_norm.astype(HALF)
    self_rows = [swap(self_low, "tensor", s) if s else self_low for s in range(count)]

    heads = heads_wide.astype(HALF)
    mine_ffn = after(mine_ffn, heads_wide)
    other_ffn = swap(mine_ffn, "pipe", 1)
    mine_cross = after(mine_cross, other_ffn)
    w_cross = jnp.stack(
        [
            jnp.concatenate([own_cross[0], mine_cross], axis=1),
            jnp.concatenate([own_cross[1], swap(mine_cross, "pipe", 1)], axis=1),
        ]
    )
    kept_tokens = [((span, width), WIDE), ((span, width), HALF), ((span, width), WIDE), ((span, LANES), WIDE)]
    attn_norm, attn_norm_low, attn_normed, attn_scale = collect(
        [heads], w_attn, 4, (3,), _end_norm, [embed, gain_of(1), bias_of(1)], kept_tokens
    )
    _, memory_low, mem_normed, mem_scale, active, slope = feed_forward(
        attn_norm_low, attn_norm, gain_of(2), bias_of(2), own_ffn, mine_ffn, other_ffn
    )
    self_full = after(jnp.zeros((rows_full, width), HALF), mem_scale)
    for s in range(count):
        self_full = lax.dynamic_update_slice_in_dim(self_full, self_rows[s], (place ^ s) * dec_span, 0)
    cross_query = dot(self_full, dec_cross[0]).astype(HALF)

    def in_halves(value):
        return jnp.stack([value[:, :half_local], value[:, half_local:]])

    [cross_q_enc] = to_encoder(in_halves(cross_query), 6)
    cross_q_enc = to_pairs(cross_q_enc)

    [cross_kv] = spread(memory_low, w_cross, 2, (0, 1), pair=1)

    tables_of_keys = enc_lengths.shape[1]
    at_table = (own_seg[:, None] == jnp.arange(tables_of_keys)[None]).astype(HALF)
    sums = dot_ta(at_table, cross_kv[0])
    bit = 1
    while bit < top_bit:
        sums = sums + swap_columns(sums, "tensor", bit, masks[bit])
        bit *= 2
    sums = sums + swap_columns(sums, "pipe", 1, masks[top_bit])
    means = sums / enc_row.astype(WIDE)[:, None]
    centers = sum(
        jnp.where((own_seg == j)[:, None], means[j : j + 1], 0.0) for j in range(tables_of_keys)
    )
    centered = (cross_kv[0].astype(WIDE) - centers).astype(HALF)

    part_out, part_lse = attend(cross_q_enc, [cross_kv], cross_segs, [0], False, HALF)
    cross_heads, cross_out_wide, cross_lse = to_decoder(
        from_pairs(part_out, half_local), stats_from_pairs(part_lse, half_local), 7
    )
    cross_norm, cross_normed, cross_scale, cross_full = rows_call(
        _forward_rows,
        2,
        dot_bt(cross_heads, dec_cross[1]).astype(HALF),
        [self_norm, dg[1:2], db[1:2]],
        kept_rows,
    )
    dec_hidden = dot(cross_full, dec_ffn[0])
    dec_active = gelu(dec_hidden).astype(HALF)
    result, resid, dec_terms2, grad_full = rows_call(
        _turn_rows,
        3,
        dot_bt(dec_active, dec_ffn[1]).astype(HALF),
        [cross_norm, dg[2:3], db[2:3], pick(dec_cotangent)],
        [((dec_span, width), HALF), wide_rows, norm_terms],
    )
    grad_hidden = (dot(grad_full, dec_ffn[1]) * gelu_slope(dec_hidden)).astype(HALF)
    resid, dec_terms1, cross_grad_full = rows_call(
        _backward_rows,
        4,
        dot_bt(grad_hidden, dec_ffn[0]).astype(HALF),
        [resid, cross_normed, cross_scale, dg[1:2]],
        [wide_rows, norm_terms],
    )
    cross_heads_grad = dot(cross_grad_full, dec_cross[1]).astype(HALF)
    dec_f2_grad = dot_ta(grad_full, dec_active)
    dec_f1_grad = dot_ta(cross_full, grad_hidden)
    dec_ffn_rows, dec_ffn_term = scatter_local([dec_f1_grad, dec_f2_grad])
    heads_grad_enc, stats_enc = to_encoder(
        in_halves(after(cross_heads_grad, dec_ffn_term)), 8, cross_out_wide, cross_lse
    )
    cross_q_term, [cross_kv_grad] = attend_back(
        cross_q_enc,
        [cross_kv],
        to_pairs(heads_grad_enc),
        stats_to_pairs(stats_enc, half_local),
        centered,
        cross_segs,
        [0],
        False,
        False,
    )

    def to_chip(value):
        theirs = joint(value, [((1 - owner(t), t), (owner(t), t)) for t in chips])
        theirs = theirs.reshape(2, count, *theirs.shape[1:])
        chip = value.reshape(theirs.shape).astype(WIDE) + theirs[::-1].astype(WIDE)
        return jnp.where(is_first, chip, chip[::-1]).astype(HALF)

    def to_owner(chip):
        terms = []
        for s in range(top_bit):
            near, far = 2 * s, 2 * s + 1
            near_pairs = [((owner(t), t), (owner(t), t ^ s)) for t in chips]
            far_pairs = [((owner(t), t), (owner(t), t ^ s ^ top_bit)) for t in chips]
            near_got = chip[:, near] if s == 0 else joint(chip[:, near], near_pairs)
            far_got = joint(chip[:, far], far_pairs)
            terms.append(jnp.where(core == group, near_got, far_got).astype(WIDE))
        return sum(terms)

    cross_q_chip = to_chip(from_pairs(cross_q_term, half_local))
    cross_q_grad = to_owner(cross_q_chip).astype(HALF)
    cross_q_grad = jnp.concatenate([cross_q_grad[0], cross_q_grad[1]], axis=1)

    back_tokens = [((span, width), WIDE), ((span, width), HALF), ((8, width), WIDE)]
    resid_enc, resid_low, enc_terms2, *cross_grads = collect(
        [cross_kv_grad],
        w_cross,
        2,
        (0, 1),
        _end_norm_back,
        [mem_normed, mem_scale, gain_of(2)],
        back_tokens,
        memory_low,
    )
    ckv_term = fold_cores(*cross_grads)
    resid_enc, resid_low, enc_terms1, *ffn_grads = feed_forward_back(
        attn_norm_low,
        after(resid_low, dec_ffn_rows, cross_q_chip),
        resid_enc,
        attn_normed,
        attn_scale,
        gain_of(1),
        active,
        slope,
        own_ffn,
        mine_ffn,
        other_ffn,
    )
    heads_grad, *out_grads = spread(resid_low, w_attn, 4, (3,), heads)
    f2_term = fold_cores(after(ffn_grads[2], heads_grad), ffn_grads[3])
    enc_f2 = fold_planes(f2_term)
    f1_term = fold_cores(*ffn_grads[:2])
    enc_f1 = fold_planes(f1_term)
    enc_ckv = fold_planes(ckv_term)
    def join(a, b):
        return (a.astype(WIDE) + b.astype(WIDE)).astype(HALF)

    cross_q_grad = after(cross_q_grad, f2_term)
    resid, dec_terms0, self_grad_full = rows_call(
        _backward_rows,
        4,
        dot_bt(cross_q_grad, dec_cross[0]).astype(HALF),
        [resid, self_normed, self_scale, dg[0:1]],
        [wide_rows, norm_terms],
    )
    dec_heads_grad = dot(self_grad_full, dec_attn[3]).astype(HALF)
    dec_q_grad, [dec_kv_grad] = attend_back(
        dec_query, [dec_kv], dec_heads_grad, dec_lse, dec_heads_wide, dec_segs, [0], True
    )
    dec_proj_grad = [dec_q_grad, dec_kv_grad[0], dec_kv_grad[1]]
    dec_part = sum(dot_bt(g, w) for g, w in zip(dec_proj_grad, dec_in_w)).astype(HALF)
    dec_left = [start_full] * 3 + [self_grad_full, self_full, cross_grad_full]
    dec_right = dec_proj_grad + [dec_heads, cross_q_grad, cross_heads]
    dec_small = [dot_ta(a, b) for a, b in zip(dec_left, dec_right)]
    dec_small_rows, dec_small_term = scatter_local(dec_small)
    grads_in = after(heads_grad, f1_term, dec_small_term)
    def send_chips(held):
        pairs, bit = [(v,) for v in held], top_bit // 2
        while bit >= 1:
            held = [join(*v) if len(v) == 2 else v[0] for v in pairs]
            pairs = [(a, swap(b, "tensor", bit)) for a, b in zip(held[:bit], held[bit:])]
            bit //= 2
        return pairs[0]

    def sum_pair(pair, *earlier):
        return join(after(pair[0], *earlier), pair[1]) if len(pair) == 2 else pair[0]

    q_grad, kv_grad, held = (), [], ()
    for n in range(parts):
        q_grad, terms = attend_back(
            query,
            key_values[n],
            after(grads_in, *held, dec_grad) if n else grads_in,
            lse,
            heads_wide,
            enc_segs,
            masks,
            part=n if parts == 2 else None,
            into=q_grad,
        )
        q_grad = (q_grad,)
        if n == 0:
            dec_grad = sum_to_owner(dec_part, resid, terms[0])
        if n:
            kv_grad.append(sum_pair(moving, terms[0]))
            terms = after(tuple(terms), kv_grad[0])
        held = [join(a, swap(b, "pipe", 1)) for a, b in zip(terms[:top_bit], terms[top_bit:])]
        moving = send_chips(held)
    [q_grad] = q_grad

    kv_grad.append(after(sum_pair(moving), enc_ckv, enc_f1, enc_f2))

    enc_grad, enc_low, enc_terms0, *in_grads = collect(
        [q_grad, *kv_grad],
        w_attn,
        4,
        (0, 1, 2),
        _end_norm_back,
        [resid_enc, start_normed, start_scale, gain_of(0)],
        back_tokens,
        embed_low,
    )
    attn_out, cross_out, ffn_out_grad, there, near_second, norm_sums = finish(
        in_grads,
        out_grads,
        enc_f1,
        enc_f2,
        enc_ckv,
        dec_ffn_rows,
        dec_small_rows,
        enc_low,
        [enc_terms0, enc_terms1, enc_terms2, dec_terms0, dec_terms1, dec_terms2],
    )

    attn_out, cross_out, ffn_out_grad = [
        v.transpose(1, 0, 2)[None] for v in (attn_out, cross_out, ffn_out_grad)
    ]
    own_columns = width // (lax.axis_size("dp") * count)
    norm_sums = lax.dynamic_slice_in_dim(
        norm_sums[:6].reshape(3, 2, width), (lax.axis_index("dp") * count + place) * own_columns, own_columns, 2
    )

    dec_pair = jnp.stack([result, dec_grad.astype(HALF)])
    dec_halves = dec_pair.reshape(2, dec_span, 2, half)
    dec_got = swap(lax.dynamic_index_in_dim(dec_halves, 1 - core, 2, False), "pipe", 1)
    own_result = lax.dynamic_slice_in_dim(result, core * half, half, 1)
    own_grad = lax.dynamic_slice_in_dim(dec_grad, core * half, half, 1)
    dec_output = jnp.where(
        is_first, jnp.stack([own_result, dec_got[0]]), jnp.stack([dec_got[0], own_result])
    )
    got_grad = dec_got[1].astype(WIDE)
    dec_input_grad = jnp.where(
        is_first, jnp.stack([own_grad, got_grad]), jnp.stack([got_grad, own_grad])
    )

    here = jnp.where(is_first, enc_grad[:, :half], near_second.astype(WIDE))
    there = there.astype(WIDE)
    enc_input_grad = jnp.where(group == 0, jnp.stack([here, there]), jnp.stack([there, here]))
    return (
        dec_output,
        enc_input_grad,
        dec_input_grad,
        attn_out,
        cross_out,
        ffn_out_grad,
        norm_sums[None, :, 0],
        norm_sums[None, :, 1],
    )


def solution(mesh):
    rows = P("dp", "tensor", None)
    weights = P("pipe", None, None, "tensor")
    half_rows = P("dp", "tensor", "pipe")
    weight_grads = P("pipe", "dp", None, "tensor")
    norm_grads = P("pipe", None, ("dp", "tensor"))
    return jax.shard_map(
        per_device,
        mesh=mesh,
        in_specs=(rows, rows, rows, P("dp", None), P("dp", None))
        + (weights,) * 3
        + (P("pipe", None, None),) * 2,
        out_specs=(half_rows,) * 3 + (weight_grads,) * 3 + (norm_grads,) * 2,
        check_vma=False,
    )
```

```python
from functools import partial

import jax
import jax.numpy as jnp
from jax import lax
from jax.experimental import pallas as pl
from jax.experimental.pallas import tpu as pltpu
from jax.sharding import PartitionSpec as P

HEAD = 64
LANES = 128
EPSILON = 1e-05
NEGATIVE = -1e30
HALF = jnp.bfloat16
WIDE = jnp.float32
VMEM_LIMIT = 56 << 20
MESH = pl.DeviceIdType.MESH
TILE_Q = 256
TILE_K = 512


def dot(left, right):
    return jnp.dot(left, right, preferred_element_type=WIDE)


def dot_bt(left, right):
    return lax.dot_general(left, right, (((1,), (1,)), ((), ())), preferred_element_type=WIDE)


def dot_ta(left, right):
    return lax.dot_general(left, right, (((0,), (0,)), ((), ())), preferred_element_type=WIDE)


def swap(value, axis, mask):
    return lax.ppermute(value, axis, [(i, i ^ mask) for i in range(lax.axis_size(axis))])


def joint(value, pairs):
    count = lax.axis_size("tensor")
    return lax.ppermute(
        value,
        ("pipe", "tensor"),
        [(a[0] * count + a[1], b[0] * count + b[1]) for a, b in pairs],
    )


def after(value, *earlier):
    return lax.optimization_barrier((value, *earlier))[0]


def swap_columns(value, axis, mask, difference):
    got = swap(value, axis, mask).reshape(value.shape[0], -1, LANES)
    order = [b ^ difference for b in range(got.shape[1])]
    return jnp.concatenate([got[:, b] for b in order], axis=1)


def table_of(places, lengths):
    total = jnp.zeros((), jnp.int32)
    table = jnp.zeros(places.shape, jnp.int32)
    for j in range(lengths.shape[0]):
        total = total + lengths[j]
        table = table + (places >= total).astype(jnp.int32)
    return table


def norm_forward(values, gain, bias):
    center = values - jnp.mean(values, axis=-1, keepdims=True)
    inv_scale = lax.rsqrt(jnp.mean(center * center, axis=-1, keepdims=True) + EPSILON)
    normed = center * inv_scale
    return normed * gain + bias, normed, inv_scale


def norm_backward(grad_out, normed, inv_scale, gain):
    grad_gain = jnp.sum(grad_out * normed, axis=0)
    grad_bias = jnp.sum(grad_out, axis=0)
    grad_normed = grad_out * gain
    grad_in = inv_scale * (
        grad_normed
        - jnp.mean(grad_normed, axis=-1, keepdims=True)
        - normed * jnp.mean(grad_normed * normed, axis=-1, keepdims=True)
    )
    return grad_in, grad_gain, grad_bias


def gelu(hidden):
    return 0.5 * hidden * (1.0 + lax.erf(hidden * (2.0**-0.5)))


def gelu_slope(hidden):
    density = jnp.exp(-0.5 * hidden * hidden) * 0.3989422804014327
    return 0.5 * (1.0 + lax.erf(hidden * (2.0**-0.5))) + hidden * density


def _allowed(seg_k, seg_q, causal, col0, row0):
    ok = seg_k == seg_q
    if causal:
        keys = col0 + lax.broadcasted_iota(jnp.int32, ok.shape, 0)
        queries = row0 + lax.broadcasted_iota(jnp.int32, ok.shape, 1)
        ok = ok & (queries >= keys)
    return ok


def _tile_loop(act, chunks, c, nq, nk, tq, tk, body):
    def step(i, carry):
        iq, ik = i // nk, i % nk

        @pl.when(act[iq * (chunks * nk) + c * nk + ik] > 0)
        def _():
            body(iq * tq, ik * tk, pl.ds(pl.multiple_of(iq * tq, tq), tq), pl.ds(pl.multiple_of(ik * tk, tk), tk))

        return carry

    lax.fori_loop(0, nq * nk, step, 0)


def _head_lanes(shape, head):
    lanes = lax.broadcasted_iota(jnp.int32, shape, 1)
    return (lanes < HEAD) if head == 0 else (lanes >= HEAD)


def _attend_kernel(chunks, tq, tk, causal, act, seg_q, seg_k, q, *refs):
    keys, values = refs[:chunks], refs[chunks : 2 * chunks]
    out, lse, top, total, acc = refs[-5:]
    rows = q.shape[0]
    nq, nk = rows // tq, keys[0].shape[0] // tk
    top[...] = jnp.full(top.shape, NEGATIVE, WIDE)
    total[...] = jnp.zeros(total.shape, WIDE)
    acc[...] = jnp.zeros(acc.shape, WIDE)
    for c in range(chunks):

        def tile(row0, col0, r, s, c=c):
            qs = q[r, :] * jnp.asarray(HEAD**-0.5, HALF)
            kk, vt = keys[c][s, :], values[c][s, :].T
            ok = _allowed(seg_k[c, s, 0:1], seg_q[0:1, r], causal, col0, row0)
            ones = jnp.ones((8, vt.shape[1]), HALF)
            heads = range(2)
            raw = [
                dot_bt(kk, jnp.where(_head_lanes(qs.shape, h), qs, jnp.zeros_like(qs))) for h in heads
            ]
            scores = [jnp.where(ok, sc, NEGATIVE) for sc in raw]
            before = [top[h : h + 1, r] for h in heads]
            after_ = [jnp.maximum(b, jnp.max(sc, axis=0, keepdims=True)) for b, sc in zip(before, scores)]
            terms = [jnp.exp(sc - a).astype(HALF) for sc, a in zip(scores, after_)]
            for h in heads:
                fade = jnp.exp(before[h] - after_[h])
                span = slice(h * HEAD, (h + 1) * HEAD)
                sums = dot(jnp.concatenate([vt[span, :], ones], axis=0), terms[h])
                acc[span, r] = acc[span, r] * fade + sums[:HEAD]
                total[h : h + 1, r] = total[h : h + 1, r] * fade + sums[HEAD : HEAD + 1]
                top[h : h + 1, r] = after_[h]

        _tile_loop(act, chunks, c, nq, nk, tq, tk, tile)
    count = total[...]
    count = jnp.where(count > 0.0, count, 1.0)
    lse[0] = top[...] + jnp.log(count)
    whole = jnp.concatenate([acc[:HEAD, :] / count[0:1, :], acc[HEAD:, :] / count[1:2, :]], axis=0)
    out[...] = whole.T.astype(out.dtype)


def _attend_back_kernel(chunks, tq, tk, causal, own_delta, act, seg_q, seg_k, q, *refs):
    keys, values = refs[:chunks], refs[chunks : 2 * chunks]
    grad_out, stats = refs[2 * chunks : 2 * chunks + 2]
    refs = refs[2 * chunks + 2 :]
    extra, (grad_q, *grad_kv, delta, dq, dkv) = refs[0], refs[-(chunks + 4) :]
    rows = q.shape[0]
    nq, nk = rows // tq, keys[0].shape[0] // tk
    if own_delta:
        product = grad_out[...].astype(WIDE) * extra[...].astype(WIDE)
        pick = (
            lax.broadcasted_iota(jnp.int32, (8, LANES), 1) // HEAD
            == lax.broadcasted_iota(jnp.int32, (8, LANES), 0)
        ).astype(WIDE)
        delta[...] = lax.dot_general(
            pick, product, (((1,), (1,)), ((), ())), precision=lax.Precision.HIGHEST, preferred_element_type=WIDE
        )
    else:
        delta[0:2, :] = stats[0, 2:4, :]
    dq[...] = jnp.zeros(dq.shape, WIDE)
    for c in range(chunks):
        dkv[...] = jnp.zeros(dkv.shape, WIDE)

        def tile(row0, col0, r, s, c=c):
            qs = q[r, :] * jnp.asarray(HEAD**-0.5, HALF)
            go = grad_out[r, :]
            kk, vv = keys[c][s, :], values[c][s, :]
            ok = _allowed(seg_k[c, s, 0:1], seg_q[0:1, r], causal, col0, row0)
            heads = range(2)
            mine = [_head_lanes(qs.shape, h) for h in heads]
            mine_k = [_head_lanes(kk.shape, h) for h in heads]
            from_keys = kk if own_delta else extra[s, :]
            qh = [jnp.where(m, qs, jnp.zeros_like(qs)) for m in mine]
            gh = [jnp.where(m, go, jnp.zeros_like(go)) for m in mine]
            kh = [jnp.where(m, from_keys, jnp.zeros_like(kk)) for m in mine_k]
            raw = [dot_bt(kk, v) for v in qh]
            grads = [dot_bt(vv, v) for v in gh]
            pr = [jnp.exp(jnp.where(ok, raw[h], NEGATIVE) - stats[0, h : h + 1, r]) for h in heads]
            ds = [(pr[h] * (grads[h] - delta[h : h + 1, r])).astype(HALF) for h in heads]
            pr = [v.astype(HALF) for v in pr]
            dkv[1, s, :] += dot(pr[0], gh[0]) + dot(pr[1], gh[1])
            dkv[0, s, :] += dot(ds[0], qh[0]) + dot(ds[1], qh[1])
            dq[r, :] += dot_ta(ds[0], kh[0]) + dot_ta(ds[1], kh[1])

        _tile_loop(act, chunks, c, nq, nk, tq, tk, tile)
        grad_kv[c][...] = dkv[...].astype(grad_kv[c].dtype)
    grad_q[...] = (dq[...] * HEAD**-0.5).astype(grad_q.dtype)


def _tile_sizes(rows, keys):
    return min(TILE_Q, rows), min(TILE_K, keys)


def _activity(seg_q, seg_k, tq, tk):
    qt = seg_q.reshape(-1, tq)
    kt = seg_k.reshape(-1, tk)
    hit = (qt[:, :1] <= kt[:, -1][None]) & (kt[:, 0][None] <= qt[:, -1:])
    return hit.astype(jnp.int32).reshape(-1)


def tables(seg_q, seg_k):
    rows, (chunks, span) = seg_q.shape[0], seg_k.shape
    tq, tk = _tile_sizes(rows, span)
    return (
        _activity(seg_q, seg_k, tq, tk),
        jnp.broadcast_to(seg_q[None], (8, rows)),
        jnp.broadcast_to(seg_k[:, :, None], (chunks, span, LANES)),
    )


def _specs(rows, span, chunks, masks, blocked, part):
    def block(h):
        return h if part is None else 2 * h + part

    row_block = pl.BlockSpec((rows, LANES), lambda h, act: (0, block(h)))
    if blocked:
        row_block = pl.BlockSpec((None, rows, LANES), lambda h, act: (block(h), 0, 0))
    stat_block = pl.BlockSpec((1, 8, rows), lambda h, act: (block(h), 0, 0))
    heads = [
        pl.BlockSpec((8, rows), lambda h, act: (0, 0)),
        pl.BlockSpec((chunks, span, LANES), lambda h, act: (0, 0, 0)),
        row_block,
    ]
    for side in range(2):
        heads += [
            pl.BlockSpec((None, span, LANES), lambda h, act, m=m, side=side: (side, 0, h ^ m)) for m in masks
        ]
    return row_block, stat_block, heads


def _dimensions(q, key_values, masks, part):
    blocked = q.ndim == 3
    rows, width = (q.shape[1], q.shape[0] * LANES) if blocked else q.shape
    span, chunks, blocks = key_values[0].shape[1], len(key_values), width // LANES
    if part is not None:
        blocks, masks = blocks // 2, [m // 2 for m in masks]
    row_block, stat_block, specs = _specs(rows, span, chunks, masks, blocked, part)
    return rows, span, chunks, blocks, masks, _tile_sizes(rows, span), row_block, stat_block, specs


def attend(q, key_values, segs, masks, causal=False, out_type=WIDE, part=None, into=()):
    rows, span, chunks, blocks, masks, (tq, tk), row_block, stat_block, specs = _dimensions(
        q, key_values, masks, part
    )
    pairs = rows * span * chunks * blocks * LANES
    kept = 4 + 2 * chunks
    stat_blocks = blocks if part is None else 2 * blocks
    return pl.pallas_call(
        partial(_attend_kernel, chunks, tq, tk, causal),
        out_shape=(
            jax.ShapeDtypeStruct(q.shape, out_type),
            jax.ShapeDtypeStruct((stat_blocks, 8, rows), WIDE),
        ),
        grid_spec=pltpu.PrefetchScalarGridSpec(
            num_scalar_prefetch=1,
            grid=(blocks,),
            in_specs=specs + [pl.BlockSpec(memory_space=pl.ANY)] * len(into),
            out_specs=[row_block, stat_block],
            scratch_shapes=[
                pltpu.VMEM((8, rows), WIDE),
                pltpu.VMEM((8, rows), WIDE),
                pltpu.VMEM((LANES, rows), WIDE),
            ],
        ),
        input_output_aliases={kept + i: i for i in range(len(into))},
        compiler_params=pltpu.CompilerParams(vmem_limit_bytes=VMEM_LIMIT),
        cost_estimate=pl.CostEstimate(
            flops=48 * pairs, transcendentals=pairs // HEAD, bytes_accessed=rows * blocks * LANES * 20
        ),
        name="attend",
    )(*segs, q, *key_values, *key_values, *into)


def attend_back(
    q, key_values, grad_out, stats, extra, segs, masks, causal=False, own_delta=True, part=None, into=()
):
    rows, span, chunks, blocks, masks, (tq, tk), row_block, stat_block, specs = _dimensions(
        q, key_values, masks, part
    )
    kv_out = [pl.BlockSpec((2, span, LANES), lambda h, act, m=m: (0, 0, h ^ m)) for m in masks]
    pairs = rows * span * chunks * blocks * LANES
    extra_block = row_block if own_delta else pl.BlockSpec((span, LANES), lambda h, act: (0, h))
    kept = 7 + 2 * chunks
    outs = pl.pallas_call(
        partial(_attend_back_kernel, chunks, tq, tk, causal, own_delta),
        out_shape=[jax.ShapeDtypeStruct(q.shape, HALF)]
        + [jax.ShapeDtypeStruct((2, span, blocks * LANES), HALF)] * chunks,
        grid_spec=pltpu.PrefetchScalarGridSpec(
            num_scalar_prefetch=1,
            grid=(blocks,),
            in_specs=specs
            + [row_block, stat_block, extra_block]
            + [pl.BlockSpec(memory_space=pl.ANY)] * len(into),
            out_specs=[row_block] + kv_out,
            scratch_shapes=[
                pltpu.VMEM((8, rows), WIDE),
                pltpu.VMEM((rows, LANES), WIDE),
                pltpu.VMEM((2, span, LANES), WIDE),
            ],
        ),
        input_output_aliases={kept + i: i for i in range(len(into))},
        compiler_params=pltpu.CompilerParams(vmem_limit_bytes=VMEM_LIMIT),
        cost_estimate=pl.CostEstimate(
            flops=80 * pairs, transcendentals=pairs // HEAD, bytes_accessed=rows * blocks * LANES * 40
        ),
        name="attend_back",
    )(*segs, q, *key_values, *key_values, grad_out, stats, extra, *into)
    return outs[0], outs[1:]


def _row_mean(values):
    return jnp.mean(values, axis=-1, keepdims=True)


def _norm_rows(values, gain, bias):
    center = values - _row_mean(values)
    inv_scale = lax.rsqrt(_row_mean(center * center) + EPSILON)
    normed = center * inv_scale
    return normed * gain + bias, normed, inv_scale


def _norm_rows_back(grad_out, normed, inv_scale, gain):
    grad_normed = grad_out * gain
    grad_in = inv_scale * (
        grad_normed - _row_mean(grad_normed) - normed * _row_mean(grad_normed * normed)
    )
    return (
        grad_in,
        jnp.sum(grad_out * normed, axis=0, keepdims=True),
        jnp.sum(grad_out, axis=0, keepdims=True),
    )


def _forward_rows(total, ins, outs):
    resid, gain, bias = ins
    value, normed, inv_scale = _norm_rows(total + resid[...], gain[...], bias[...])
    outs[0][...] = value
    outs[1][...] = normed
    outs[2][...] = jnp.broadcast_to(inv_scale, outs[2].shape)
    return value


def _turn_rows(total, ins, outs):
    resid, gain, bias, cotangent = ins
    value, normed, inv_scale = _norm_rows(total + resid[...], gain[...], bias[...])
    outs[0][...] = value.astype(outs[0].dtype)
    grad, grad_gain, grad_bias = _norm_rows_back(
        cotangent[...].astype(WIDE), normed, inv_scale, gain[...]
    )
    outs[1][...] = grad
    outs[2][0:1, :] = grad_gain
    outs[2][1:2, :] = grad_bias
    return grad


def _backward_rows(total, ins, outs):
    resid, normed, inv_scale, gain = ins
    grad, grad_gain, grad_bias = _norm_rows_back(
        total + resid[...], normed[...], inv_scale[:, 0:1], gain[...]
    )
    outs[0][...] = grad
    outs[1][0:1, :] = grad_gain
    outs[1][1:2, :] = grad_bias
    return grad


def _rows_kernel(count, scatter, gather, middle, n_in, n_out, *refs):
    refs = list(refs)
    part = refs.pop(0) if scatter else None
    ins, refs = refs[:n_in], refs[n_in:]
    outs, refs = refs[:n_out], refs[n_out:]
    full = refs.pop(0) if gather else None
    landed = refs.pop(0) if scatter else None
    send_sem, recv_sem = refs[:2]
    me = lax.axis_index("tensor")
    steps = range(1, count)
    peers = [lax.rem(me + s, count) for s in steps]
    barrier = pltpu.get_barrier_semaphore()
    for peer in peers:
        pl.semaphore_signal(barrier, inc=1, device_id={"tensor": peer}, device_id_type=MESH)
    pl.semaphore_wait(barrier, count - 1)
    total = None
    if scatter:
        rows = part.shape[0] // count
        copies = []
        for s, peer in zip(steps, peers):
            copy = pltpu.make_async_remote_copy(
                src_ref=part.at[pl.ds(pl.multiple_of(peer * rows, rows), rows)],
                dst_ref=landed.at[s - 1],
                send_sem=send_sem.at[0, s - 1],
                recv_sem=recv_sem.at[0, s - 1],
                device_id={"tensor": peer},
                device_id_type=MESH,
            )
            copy.start()
            copies.append(copy)
        total = part[pl.ds(pl.multiple_of(me * rows, rows), rows), :].astype(WIDE)
        for s, copy in zip(steps, copies):
            copy.wait_recv()
            total = total + landed[s - 1].astype(WIDE)
        for copy in copies:
            copy.wait_send()
    sent = middle(total, ins, outs)
    if gather:
        rows = full.shape[0] // count
        own = pl.ds(pl.multiple_of(me * rows, rows), rows)
        full[own, :] = sent.astype(full.dtype)
        copies = []
        for s, peer in zip(steps, peers):
            copy = pltpu.make_async_remote_copy(
                src_ref=full.at[own],
                dst_ref=full.at[own],
                send_sem=send_sem.at[1, s - 1],
                recv_sem=recv_sem.at[1, s - 1],
                device_id={"tensor": peer},
                device_id_type=MESH,
            )
            copy.start()
            copies.append(copy)
        for copy in copies:
            copy.wait()


def rows_call(middle, number, part, ins, outs, gather=True):
    count = lax.axis_size("tensor")
    scatter = part is not None
    width = (part if scatter else ins[0]).shape[1]
    rows = part.shape[0] // count if scatter else ins[0].shape[0]
    shapes = [jax.ShapeDtypeStruct(shape, kind) for shape, kind in outs]
    if gather:
        shapes.append(jax.ShapeDtypeStruct((rows * count, width), HALF))
    whole = pl.BlockSpec(memory_space=pltpu.VMEM)
    operands = ([part] if scatter else []) + list(ins)
    got = pl.pallas_call(
        partial(_rows_kernel, count, scatter, gather, middle, len(ins), len(outs)),
        out_shape=shapes,
        in_specs=[whole] * len(operands),
        out_specs=[whole] * len(shapes),
        scratch_shapes=([pltpu.VMEM((count - 1, rows, width), HALF)] if scatter else [])
        + [pltpu.SemaphoreType.DMA((2, count - 1))] * 2,
        compiler_params=pltpu.CompilerParams(
            collective_id=number, has_side_effects=True, vmem_limit_bytes=VMEM_LIMIT
        ),
        cost_estimate=pl.CostEstimate(
            flops=0, transcendentals=0, bytes_accessed=1400 * rows * width
        ),
        name=middle.__name__.strip("_"),
    )(*operands)
    return got


def _differ(a, b, count):
    total, bit = 0, 1
    while bit < count:
        total = total + lax.rem(lax.rem(a // bit, 2) + lax.rem(b // bit, 2), 2) * bit
        bit *= 2
    return total


def _slot(difference, count):
    top = count // 2
    return 2 * lax.rem(difference, top) + difference // top


def _enter(peers):
    barrier = pltpu.get_barrier_semaphore()
    for peer in peers:
        pl.semaphore_signal(barrier, inc=1, device_id=peer, device_id_type=MESH)
    pl.semaphore_wait(barrier, len(peers))


def _send(source, dest, send_sem, recv_sem, peer):
    copy = pltpu.make_async_remote_copy(
        src_ref=source,
        dst_ref=dest,
        send_sem=send_sem,
        recv_sem=recv_sem,
        device_id=peer,
        device_id_type=MESH,
    )
    copy.start()
    return copy


def _to_encoder_kernel(count, with_stats, *refs):
    if with_stats:
        value, out, lse, full, stats, own, own_stats, held, other, other_stats, send_sem, recv_sem = refs
    else:
        value, full, own, other, send_sem, recv_sem = refs
    core, me = lax.axis_index("pipe"), lax.axis_index("tensor")
    group = me // (count // 2)
    chips = [lax.rem(me + s, count) for s in range(1, count)]
    _enter([{"tensor": chip} for chip in chips] + [{"pipe": 1 - core}])
    sets = [(value, own, other, full)]
    if with_stats:
        for h in range(2):
            product = value[h].astype(WIDE) * out[h]
            pick = (
                lax.broadcasted_iota(jnp.int32, (8, product.shape[1]), 1) // HEAD
                == lax.broadcasted_iota(jnp.int32, (8, product.shape[1]), 0) - 2
            ).astype(WIDE)
            held[h] = lax.dot_general(
                pick,
                product,
                (((1,), (1,)), ((), ())),
                precision=lax.Precision.HIGHEST,
                preferred_element_type=WIDE,
            )
            held[h, 0:2, :] = lse[h, 0:2, :]
        sets.append((held, own_stats, other_stats, stats))
    copies = []
    for s, chip in enumerate(chips):
        place = _slot(_differ(chip, me, count), count)
        for h in range(2):
            at = lax.rem(h + core, 2) * count + place
            for i, (source, dest, _, _) in enumerate(sets):
                sems = (send_sem.at[i, s, h], recv_sem.at[i, s, h])
                copies.append(_send(source.at[h], dest.at[at], *sems, {"tensor": chip}))
    for h in range(2):
        for source, dest, _, _ in sets:
            dest[lax.rem(h + core, 2) * count] = source[h]
    for copy in copies:
        copy.wait()
    copies = []
    for g in range(2):
        for i, (_, source, dest, _) in enumerate(sets):
            here, there = pl.ds(g * count, count), pl.ds((1 - g) * count, count)
            sems = (send_sem.at[i, count - 1, g], recv_sem.at[i, count - 1, g])
            copies.append(_send(source.at[here], dest.at[there], *sems, {"pipe": 1 - core}))
    for copy in copies:
        copy.wait()
    for _, mine, theirs, dest in sets:

        @pl.when(core == group)
        def _(mine=mine, dest=dest):
            dest[...] = mine[...]

        @pl.when(core != group)
        def _(theirs=theirs, dest=dest):
            dest[...] = theirs[...]


def to_encoder(value, number, out=None, lse=None):
    count = lax.axis_size("tensor")
    _, rows, wide = value.shape
    shapes = [((2 * count, rows, wide), HALF)]
    if out is not None:
        shapes.append(((2 * count, 8, rows), WIDE))
    scratch = [pltpu.VMEM(*s) for s in shapes]
    if out is not None:
        scratch.append(pltpu.VMEM((2, 8, rows), WIDE))
    scratch += [pltpu.VMEM(*s) for s in shapes]
    whole = pl.BlockSpec(memory_space=pltpu.VMEM)
    operands = (value,) if out is None else (value, out, lse)
    return pl.pallas_call(
        partial(_to_encoder_kernel, count, out is not None),
        out_shape=[jax.ShapeDtypeStruct(*s) for s in shapes],
        in_specs=[whole] * len(operands),
        out_specs=[whole] * len(shapes),
        scratch_shapes=scratch + [pltpu.SemaphoreType.DMA((len(shapes), count, 2))] * 2,
        compiler_params=pltpu.CompilerParams(
            collective_id=number, has_side_effects=True, vmem_limit_bytes=VMEM_LIMIT
        ),
        cost_estimate=pl.CostEstimate(flops=0, transcendentals=0, bytes_accessed=60 << 20),
        name="to_encoder",
    )(*operands)


def _over_lanes(weights, wide):
    lanes = lax.broadcasted_iota(jnp.int32, (8, wide), 1) // HEAD
    pick = (lanes == lax.broadcasted_iota(jnp.int32, (8, wide), 0)).astype(HALF)
    high = weights.astype(HALF)
    low = (weights - high.astype(WIDE)).astype(HALF)
    return dot_ta(jnp.concatenate([high, low], axis=0), jnp.concatenate([pick, pick], axis=0))


def _to_decoder_kernel(count, *refs):
    part, lse, heads, out, out_lse = refs[:5]
    other, other_lse, both, both_lse, landed, landed_lse, send_sem, recv_sem = refs[5:]
    core, me = lax.axis_index("pipe"), lax.axis_index("tensor")
    top = count // 2
    chips = [lax.rem(me + s, count) for s in range(1, count)]
    _enter([{"tensor": chip} for chip in chips] + [{"pipe": 1 - core}])
    copies = []
    for g in range(2):
        here, there = pl.ds(g * count, count), pl.ds((1 - g) * count, count)
        for i, (source, dest) in enumerate(((part, other), (lse, other_lse))):
            sems = (send_sem.at[i, count - 1, g], recv_sem.at[i, count - 1, g])
            copies.append(_send(source.at[here], dest.at[there], *sems, {"pipe": 1 - core}))
    for copy in copies:
        copy.wait()
    wide = part.shape[2]
    for i in range(2 * count):
        first, second = lse[i], other_lse[i]
        peak = jnp.maximum(first, second)
        a, b = jnp.exp(first - peak), jnp.exp(second - peak)
        both_lse[i] = peak + jnp.log(a + b)
        share = _over_lanes(b / (a + b), wide)
        mine = part[i].astype(WIDE)
        both[i] = (mine + share * (other[i].astype(WIDE) - mine)).astype(HALF)
    copies = []
    for s, chip in enumerate(chips):
        place = _slot(_differ(chip, me, count), count)
        for h in range(2):
            at = lax.rem(h + core, 2) * count + place
            for i, (source, dest) in enumerate(((both, landed), (both_lse, landed_lse))):
                sems = (send_sem.at[i, s, h], recv_sem.at[i, s, h])
                copies.append(_send(source.at[at], dest.at[s, h], *sems, {"tensor": chip}))
    for copy in copies:
        copy.wait()
    for h in range(2):
        at = lax.rem(h + core, 2) * count
        terms = [(me, both[at], both_lse[at])]
        for s in range(count - 1):
            terms.append((lax.rem(me - s - 1 + count, count), landed[s, h], landed_lse[s, h]))
        logs = [jnp.where(chip // top == core, log, NEGATIVE) for chip, _, log in terms]
        peak = logs[0]
        for log in logs[1:]:
            peak = jnp.maximum(peak, log)
        weights = [jnp.exp(log - peak) for log in logs]
        weights = [
            jnp.where(chip // top == core, w, 0.0) for (chip, _, _), w in zip(terms, weights)
        ]
        total = sum(weights)
        out_lse[h] = peak + jnp.log(total)
        shares = [_over_lanes(w / total, wide) for w in weights]
        value = sum(c * term.astype(WIDE) for c, (_, term, _) in zip(shares, terms)) / sum(shares)
        out[h] = value
        heads[:, h * wide : (h + 1) * wide] = value.astype(HALF)


def to_decoder(part, lse, number):
    count = lax.axis_size("tensor")
    slots, rows, wide = part.shape
    whole = pl.BlockSpec(memory_space=pltpu.VMEM)
    return pl.pallas_call(
        partial(_to_decoder_kernel, count),
        out_shape=[
            jax.ShapeDtypeStruct((rows, 2 * wide), HALF),
            jax.ShapeDtypeStruct((2, rows, wide), WIDE),
            jax.ShapeDtypeStruct((2, 8, rows), WIDE),
        ],
        in_specs=[whole] * 2,
        out_specs=[whole] * 3,
        scratch_shapes=[
            pltpu.VMEM((slots, rows, wide), HALF),
            pltpu.VMEM((slots, 8, rows), WIDE),
            pltpu.VMEM((slots, rows, wide), HALF),
            pltpu.VMEM((slots, 8, rows), WIDE),
            pltpu.VMEM((count - 1, 2, rows, wide), HALF),
            pltpu.VMEM((count - 1, 2, 8, rows), WIDE),
        ]
        + [pltpu.SemaphoreType.DMA((2, count, 2))] * 2,
        compiler_params=pltpu.CompilerParams(
            collective_id=number, has_side_effects=True, vmem_limit_bytes=VMEM_LIMIT
        ),
        cost_estimate=pl.CostEstimate(flops=0, transcendentals=0, bytes_accessed=60 << 20),
        name="to_decoder",
    )(part, lse)


def to_pairs(value):
    slots, rows, wide = value.shape
    each = LANES // wide
    if each == 1:
        return value
    value = value.reshape(slots // each, each, rows, wide)
    return value.transpose(0, 2, 1, 3).reshape(slots // each, rows, LANES)


def from_pairs(value, wide):
    blocks, rows, _ = value.shape
    each = LANES // wide
    if each == 1:
        return value
    value = value.reshape(blocks, rows, each, wide)
    return value.transpose(0, 2, 1, 3).reshape(blocks * each, rows, wide)


def stats_to_pairs(stats, wide):
    each = LANES // wide
    if each == 1:
        return stats
    slots, _, rows = stats.shape
    stats = stats.reshape(slots // each, each, 8, rows)
    return jnp.concatenate(
        [stats[:, :, 0], stats[:, :, 2], jnp.zeros((slots // each, 4, rows), WIDE)], axis=1
    )


def stats_from_pairs(stats, wide):
    each = LANES // wide
    if each == 1:
        return stats
    blocks, _, rows = stats.shape
    value = stats[:, :each].reshape(blocks * each, 1, rows)
    return jnp.concatenate([value, jnp.zeros((blocks * each, 7, rows), WIDE)], axis=1)


def slot_bits():
    count = lax.axis_size("tensor")
    bits, bit = [count // 2], 1
    while bit < count // 2:
        bits.append(bit)
        bit *= 2
    return [b for b in bits if b > 0]


def in_column_halves(values):
    wide = values.shape[2] // 2
    return jnp.stack(
        [
            jnp.concatenate(
                [values[:, k, h * wide : (h + 1) * wide] for k in range(values.shape[1])], axis=1
            ).astype(HALF)
            for h in range(2)
        ]
    )


def _gather_kernel(bits, count, planes, *refs):
    own, refs = refs[:3], refs[3:]
    leaving, dec_rows, *refs = refs
    full, enc_cross, enc_ffn, *refs = refs
    dec, refs = refs[:3], refs[3:]
    rests, refs = refs[:2], refs[2:]
    coming, dec_full, send_sem, recv_sem, local_sem = refs
    core, place, me = lax.axis_index("pipe"), lax.axis_index("dp"), lax.axis_index("tensor")
    wide = own[0].shape[2]
    block = own[0].shape[1] // planes
    sibling = {"pipe": 1 - core}
    chips = {bit: {"tensor": _differ(me, bit, count)} for bit in bits}
    line = [{"tensor": _differ(me, s, count)} for s in range(1, count)]
    dp_bits = [1 << i for i in range(planes.bit_length() - 1)]
    others = {bit: {"dp": _differ(place, bit, planes)} for bit in dp_bits}
    _enter([sibling, *line, *others.values()])
    made = [0]

    def push(source, dest, peer):
        i = made[0]
        made[0] += 1
        return _send(source, dest, send_sem.at[i], recv_sem.at[i], peer)

    def rows_of(difference):
        return pl.ds(pl.multiple_of(_differ(place, difference, planes) * block, block), block)

    enc = [full.at[:, :, pl.ds(0, wide)], enc_cross, enc_ffn]
    shown = []
    for a in range(3):
        i = made[0]
        made[0] += 2
        shown.append(i)

        @pl.when(core == 0)
        def _(a=a, i=i):
            for h in range(2):
                _send(own[a].at[h], enc[a].at[1 - h], send_sem.at[i + h], recv_sem.at[i + h], sibling)
                pltpu.make_async_copy(own[a].at[h], enc[a].at[h], local_sem.at[a, h]).start()

        @pl.when(core == 1)
        def _(a=a, i=i):
            for h in range(2):
                _send(own[a].at[h], dec[a].at[h], send_sem.at[i + h], recv_sem.at[i + h], sibling)
                pltpu.make_async_copy(own[a].at[h], dec[a].at[h], local_sem.at[a, h]).start()

    def arrived(a):
        i = shown[a]
        for h in range(2):
            pltpu.make_async_copy(own[a].at[h], enc[a].at[h], local_sem.at[a, h]).wait()
            pltpu.make_async_copy(own[a].at[h], enc[a].at[h], recv_sem.at[i + h]).wait()

    def line_step(a, n, bit):
        here, size = rows_of(0), own[a].shape[2]
        if a == 0:
            source = full.at[0, here, pl.ds(0, n * size)]
            return [push(source, full.at[0, here, pl.ds(n * size, n * size)], chips[bit])]
        rest = rests[a - 1]
        copies = [
            push(enc[a].at[0, here], rest.at[:, pl.ds((n - 1) * size, size)], chips[bit])
        ]
        if n > 1:
            source = rest.at[:, pl.ds(0, (n - 1) * size)]
            copies.append(push(source, rest.at[:, pl.ds(n * size, (n - 1) * size)], chips[bit]))
        return copies

    def wait(copies):
        for copy in copies:
            copy.wait()

    def advance(chain):
        wait(chain["now"])
        chain["now"] = line_step(chain["array"], *chain["todo"].pop(0)) if chain["todo"] else []

    def columns(part):
        return pl.ds(wide + part * half, half)

    def plane_step(j):
        copies = []
        for part, order in enumerate(orders):
            for m in held[part]:
                at = full.at[0, rows_of(m), columns(part)]
                copies.append((part, m ^ order[j], push(at, at, others[order[j]])))
        return copies

    def share(part, m):
        here = rows_of(m)
        source = full.at[0, here, columns(part)]
        return push(source, full.at[1, here, columns(part)], sibling)

    steps = [(1 << i, bit) for i, bit in enumerate(bits)]
    for_attn, for_cross, for_ffn = [{"array": a, "todo": list(steps), "now": []} for a in range(3)]
    at = pl.ds(pl.multiple_of(me * dec_rows.shape[0], dec_rows.shape[0]), dec_rows.shape[0])
    dec_full[at, :] = dec_rows[...]
    dec_sent = [push(dec_full.at[at], dec_full.at[at], peer) for peer in line]
    arrived(0)
    advance(for_attn)
    arrived(2)
    advance(for_attn)
    advance(for_ffn)
    while for_attn["now"]:
        advance(for_attn)
    token_sem = made[0]
    made[0] += 1

    @pl.when(core == 1)
    def _():
        _send(leaving, coming, send_sem.at[token_sem], recv_sem.at[token_sem], chips[bits[0]])

    half = (count - 1) * wide // 2
    orders, held = (dp_bits, dp_bits[::-1]), ([0], [0])
    moving = plane_step(0)
    shared = [share(part, 0) for part in range(2)]
    advance(for_ffn)
    arrived(1)
    for j in range(len(dp_bits)):
        for _, _, copy in moving:
            copy.wait()
        for part, order in enumerate(orders):
            held[part].extend([m ^ order[j] for m in held[part]])
        following = plane_step(j + 1) if j + 1 < len(dp_bits) else []
        shared += [share(part, m) for part, m, _ in moving]
        moving = following
        advance(for_cross)
    while for_ffn["now"]:
        advance(for_ffn)
    while for_cross["now"]:
        advance(for_cross)

    @pl.when(core == 1)
    def _():
        pltpu.make_async_copy(leaving, leaving, send_sem.at[token_sem]).wait()
        pltpu.make_async_copy(leaving, coming, recv_sem.at[token_sem]).wait()

    wait(dec_sent)
    wait(shared)
    for a in range(3):
        for h in range(2):
            pltpu.make_async_copy(own[a].at[h], own[a].at[h], send_sem.at[shown[a] + h]).wait()


def gather_weights(attn, cross, ffn, leaving, dec_rows):
    own = (attn, cross, ffn)
    count, planes = lax.axis_size("tensor"), lax.axis_size("dp")
    depth = attn.shape[1]
    shapes = [(2, depth, count * attn.shape[2]), cross.shape, ffn.shape]
    shapes += [v.shape for v in own]
    shapes += [(depth // planes, (count - 1) * v.shape[2]) for v in (cross, ffn)]
    shapes += [leaving.shape, (count * dec_rows.shape[0], dec_rows.shape[1])]
    hbm, vmem = pl.BlockSpec(memory_space=pl.ANY), pl.BlockSpec(memory_space=pltpu.VMEM)
    return pl.pallas_call(
        partial(_gather_kernel, slot_bits(), count, planes),
        out_shape=[jax.ShapeDtypeStruct(shape, HALF) for shape in shapes],
        in_specs=[vmem] * 3 + [hbm, vmem],
        out_specs=[hbm] * (len(shapes) - 1) + [vmem],
        scratch_shapes=[pltpu.SemaphoreType.DMA((64,))] * 2 + [pltpu.SemaphoreType.DMA((3, 2))],
        compiler_params=pltpu.CompilerParams(
            collective_id=9, has_side_effects=True, vmem_limit_bytes=VMEM_LIMIT
        ),
        cost_estimate=pl.CostEstimate(flops=0, transcendentals=0, bytes_accessed=280 << 20),
        name="gather_weights",
    )(*own, leaving, dec_rows)


def gather_planes(rest):
    return lax.all_gather(rest, "dp", axis=0, tiled=True)


def fold_cores(mine, other):
    return (mine.astype(WIDE) + swap(other, "pipe", 1).astype(WIDE)).astype(HALF)


def fold_planes(term):
    return lax.psum_scatter(term, "dp", scatter_dimension=0, tiled=True)


def scatter_local(terms):
    core = lax.axis_index("pipe")
    wide = terms[0].shape[1] // 2
    pick = partial(lax.dynamic_slice_in_dim, slice_size=wide, axis=1)
    mine = jnp.concatenate([pick(v.astype(HALF), core * wide) for v in terms], axis=1)
    other = jnp.concatenate([pick(v.astype(HALF), (1 - core) * wide) for v in terms], axis=1)
    term = fold_cores(mine, other)
    return fold_planes(term), term


def _blocks_of(weights, kinds):
    wide = weights.shape[2] // (lax.axis_size("tensor") * kinds)
    each = LANES // wide
    blocks = lax.axis_size("tensor") // each
    spec = pl.BlockSpec(
        (None, weights.shape[1], each * kinds * wide), lambda i: (i // blocks, 0, lax.rem(i, blocks))
    )
    return wide, each, blocks, spec


def _piece(weights, kinds, wide, each, k):
    parts = [weights[:, (j * kinds + k) * wide : (j * kinds + k + 1) * wide] for j in range(each)]
    return parts[0] if each == 1 else jnp.concatenate(parts, axis=1)


def _store_grads(refs, i, blocks, pieces, wide, each):
    columns = [p[:, j * wide : (j + 1) * wide] for j in range(each) for p in pieces]
    for ref, when in zip(refs, (i < blocks, i >= blocks)):

        @pl.when(when)
        def _(ref=ref):
            for n, column in enumerate(columns):
                ref[:, n * wide : (n + 1) * wide] = column.astype(ref.dtype)


def _grad_specs(depth, columns, blocks):
    return [
        pl.BlockSpec((depth, columns), lambda i: (0, jnp.minimum(i, blocks - 1))),
        pl.BlockSpec((depth, columns), lambda i: (0, jnp.maximum(i - blocks, 0))),
    ]


def _spread_kernel(kinds, use, wide, each, blocks, with_grad, pair, x, weights, *refs):
    left = x[...]
    values = [dot(left, _piece(weights, kinds, wide, each, k)) for k in use]
    if with_grad:
        y, *refs = refs
        i = pl.program_id(0)
        _store_grads(refs[-2:], i, blocks, [dot_ta(left, y[...].astype(HALF))], wide, each)
    for n in range(pair):
        ref = refs[len(refs) - pair + n]

        @pl.when(lax.rem(pl.program_id(0), pair) == n)
        def _(ref=ref):
            ref[0] = values[-2].astype(HALF)
            ref[1] = values[-1].astype(HALF)

    values = values[:-2] if pair else values
    for ref, value in zip(refs, values):
        ref[...] = value.astype(HALF)


def spread(x, weights, kinds, use, y=None, pair=0):
    rows, width = x.shape
    wide, each, blocks, spec = _blocks_of(weights, kinds)
    column = pl.BlockSpec((rows, LANES), lambda i: (0, i))
    single = len(use) - (2 if pair else 0)
    shapes, specs = [((rows, width), HALF)] * single, [column] * single
    for _ in range(pair):
        shapes.append(((2, rows, width // pair), HALF))
        specs.append(pl.BlockSpec((2, rows, LANES), lambda i: (0, 0, i // pair)))
    if y is not None:
        shapes += [((width, width // 2), HALF)] * 2
        specs += _grad_specs(width, LANES, blocks)
    return pl.pallas_call(
        partial(_spread_kernel, kinds, use, wide, each, blocks, y is not None, pair),
        out_shape=[jax.ShapeDtypeStruct(*s) for s in shapes],
        grid=(2 * blocks,),
        in_specs=[pl.BlockSpec((rows, width), lambda i: (0, 0)), spec] + [column] * (y is not None),
        out_specs=specs,
        compiler_params=pltpu.CompilerParams(vmem_limit_bytes=VMEM_LIMIT),
        cost_estimate=pl.CostEstimate(
            flops=8 * rows * width * width * (len(use) + (y is not None)),
            transcendentals=0,
            bytes_accessed=2 * width * width * kinds,
        ),
        name="spread",
    )(x, weights, *([] if y is None else [y]))


def _collect_kernel(kinds, use, wide, each, blocks, n_y, split, with_grad, ending, n_extra, *refs):
    refs = list(refs)
    ys, refs = refs[:n_y], refs[n_y:]
    weights, refs = refs[0], refs[1:]
    x = refs.pop(0) if with_grad else None
    extra, refs = refs[:n_extra], refs[n_extra:]
    acc = refs.pop()
    grads = [refs.pop(), refs.pop()][::-1] if with_grad else []
    i = pl.program_id(0)

    @pl.when(i == 0)
    def _():
        acc[...] = jnp.zeros(acc.shape, WIDE)

    values, ys = [], list(ys)
    while ys:
        y = ys.pop(0)
        if len(y.shape) == 2:
            values.append(y[...])
        elif split:
            odd = ys.pop(0)
            values += [jnp.where(lax.rem(i, 2) == 0, y[n], odd[n]) for n in range(2)]
        else:
            values += [y[0], y[1]]
    values = [v.astype(HALF) for v in values]
    for value, k in zip(values, use):
        acc[...] += dot_bt(value, _piece(weights, kinds, wide, each, k))
    if with_grad:
        left = x[...]
        _store_grads(grads, i, blocks, [dot_ta(left, v) for v in values], wide, each)

    @pl.when(i == 2 * blocks - 1)
    def _():
        ending(acc[...], extra, refs)


def collect(ys, weights, kinds, use, ending, extra, outs, x=None):
    rows, width = ys[0].shape[-2], weights.shape[1]
    split = any(y.ndim == 3 and y.shape[2] < width for y in ys)
    wide, each, blocks, spec = _blocks_of(weights, kinds)
    y_specs = [
        pl.BlockSpec((rows, LANES), lambda i: (0, i))
        if y.ndim == 2
        else pl.BlockSpec((2, rows, LANES), lambda i: (0, 0, i // (2 if split else 1)))
        for y in ys
    ]
    fixed = [pl.BlockSpec(v.shape, lambda i: (0, 0)) for v in ([] if x is None else [x]) + extra]
    shapes = list(outs)
    specs = [pl.BlockSpec(shape, lambda i: (0, 0)) for shape, _ in outs]
    if x is not None:
        shapes += [((width, len(use) * width // 2), HALF)] * 2
        specs += _grad_specs(width, len(use) * LANES, blocks)
    return pl.pallas_call(
        partial(
            _collect_kernel, kinds, use, wide, each, blocks, len(ys), split, x is not None, ending, len(extra)
        ),
        out_shape=[jax.ShapeDtypeStruct(*s) for s in shapes],
        grid=(2 * blocks,),
        in_specs=y_specs + [spec] + fixed,
        out_specs=specs,
        scratch_shapes=[pltpu.VMEM((rows, width), WIDE)],
        compiler_params=pltpu.CompilerParams(vmem_limit_bytes=VMEM_LIMIT),
        cost_estimate=pl.CostEstimate(
            flops=8 * rows * width * width * len(use) * (1 + (x is not None)),
            transcendentals=0,
            bytes_accessed=2 * width * width * kinds,
        ),
        name="collect",
    )(*ys, weights, *([] if x is None else [x]), *extra)


def _end_norm(total, ins, outs):
    resid, gain, bias = ins
    value, normed, inv_scale = _norm_rows(total + resid[...], gain[...], bias[...])
    outs[0][...] = value
    outs[1][...] = value.astype(HALF)
    outs[2][...] = normed
    outs[3][...] = jnp.broadcast_to(inv_scale, outs[3].shape)


def _end_norm_back(total, ins, outs):
    *resid, normed, inv_scale, gain = ins
    total = total + resid[0][...] if resid else total
    grad, grad_gain, grad_bias = _norm_rows_back(total, normed[...], inv_scale[:, 0:1], gain[...])
    outs[0][...] = grad
    outs[1][...] = grad.astype(HALF)
    outs[2][0:1, :] = grad_gain
    outs[2][1:2, :] = grad_bias


def _ffn_parts(count, own, mine, other):
    depth, wide = own.shape[1], own.shape[2] // 2
    specs = []
    for k in range(2):
        specs.append(pl.BlockSpec((None, depth, wide), lambda i, k=k: (i // count, 0, k)))
        for first in (0, count):
            specs.append(
                pl.BlockSpec(
                    (depth, wide),
                    lambda i, k=k, first=first: (0, 2 * jnp.clip(i - first - 1, 0, count - 2) + k),
                )
            )
    return wide, specs


def _ffn_cases(count, i, ins, outs):
    local = lax.rem(i, count) == 0
    return [
        (local, ins[0], outs[0]),
        (jnp.logical_and(~local, i < count), ins[1], outs[1]),
        (jnp.logical_and(~local, i > count), ins[2], outs[2]),
    ]


def _ffn_kernel(count, x, resid, gain, bias, *refs):
    ins, outs, refs = refs[:3], refs[3:6], refs[6:]
    value, value_low, normed, inv_scale, active, slope, acc = refs
    i = pl.program_id(0)

    @pl.when(i == 0)
    def _():
        acc[...] = jnp.zeros(acc.shape, WIDE)

    for condition, first, second in _ffn_cases(count, i, ins, outs):

        @pl.when(condition)
        def _(first=first, second=second):
            hidden = dot(x[...], first[...])
            below = 0.5 * (1.0 + lax.erf(hidden * (2.0**-0.5)))
            density = jnp.exp(-0.5 * hidden * hidden) * 0.3989422804014327
            act = (hidden * below).astype(HALF)
            active[...] = act
            slope[...] = (below + hidden * density).astype(HALF)
            acc[...] += dot_bt(act, second[...])

    @pl.when(i == 2 * count - 1)
    def _():
        _end_norm(acc[...], (resid, gain, bias), (value, value_low, normed, inv_scale))


def feed_forward(x, resid, gain, bias, own, mine, other):
    count = lax.axis_size("tensor")
    rows, width = x.shape
    wide, specs = _ffn_parts(count, own, mine, other)
    units = 2 * count * wide
    fixed = [pl.BlockSpec(v.shape, lambda i: (0, 0)) for v in (x, resid, gain, bias)]
    shapes = [((rows, width), WIDE), ((rows, width), HALF), ((rows, width), WIDE), ((rows, LANES), WIDE)]
    column = pl.BlockSpec((rows, wide), lambda i: (0, i))
    return pl.pallas_call(
        partial(_ffn_kernel, count),
        out_shape=[jax.ShapeDtypeStruct(*s) for s in shapes]
        + [jax.ShapeDtypeStruct((rows, units), HALF)] * 2,
        grid=(2 * count,),
        in_specs=fixed + specs,
        out_specs=[pl.BlockSpec(s, lambda i: (0, 0)) for s, _ in shapes] + [column] * 2,
        scratch_shapes=[pltpu.VMEM((rows, width), WIDE)],
        compiler_params=pltpu.CompilerParams(vmem_limit_bytes=VMEM_LIMIT),
        cost_estimate=pl.CostEstimate(
            flops=12 * rows * width * units, transcendentals=2 * rows * units, bytes_accessed=4 * width * units
        ),
        name="feed_forward",
    )(x, resid, gain, bias, own, mine, other, own, mine, other)


def _ffn_back_kernel(count, x, grad, resid, normed, inv_scale, gain, active, slope, *refs):
    ins, outs, refs = refs[:3], refs[3:6], refs[6:]
    result, result_low, terms, *grads, acc = refs
    i = pl.program_id(0)

    @pl.when(i == 0)
    def _():
        acc[...] = jnp.zeros(acc.shape, WIDE)

    for condition, first, second in _ffn_cases(count, i, ins, outs):

        @pl.when(condition)
        def _(first=first, second=second):
            hidden = (dot(grad[...], second[...]) * slope[...].astype(WIDE)).astype(HALF)
            acc[...] += dot_bt(hidden, first[...])
            f1 = dot_ta(x[...], hidden).astype(HALF)
            f2 = dot_ta(grad[...], active[...]).astype(HALF)
            for half, when in enumerate((i < count, i >= count)):

                @pl.when(when)
                def _(half=half):
                    grads[half][...] = f1
                    grads[2 + half][...] = f2

    @pl.when(i == 2 * count - 1)
    def _():
        _end_norm_back(acc[...], (resid, normed, inv_scale, gain), (result, result_low, terms))


def feed_forward_back(x, grad, resid, normed, inv_scale, gain, active, slope, own, mine, other):
    count = lax.axis_size("tensor")
    rows, width = x.shape
    wide, specs = _ffn_parts(count, own, mine, other)
    column = pl.BlockSpec((rows, wide), lambda i: (0, i))
    fixed = [pl.BlockSpec(v.shape, lambda i: (0, 0)) for v in (x, grad, resid, normed, inv_scale, gain)]
    shapes = [((rows, width), WIDE), ((rows, width), HALF), ((8, width), WIDE)]
    grad_specs = [
        pl.BlockSpec((width, wide), lambda i: (0, jnp.minimum(i, count - 1))),
        pl.BlockSpec((width, wide), lambda i: (0, jnp.maximum(i - count, 0))),
    ]
    return pl.pallas_call(
        partial(_ffn_back_kernel, count),
        out_shape=[jax.ShapeDtypeStruct(*s) for s in shapes]
        + [jax.ShapeDtypeStruct((width, count * wide), HALF)] * 4,
        grid=(2 * count,),
        in_specs=fixed + [column] * 2 + specs,
        out_specs=[pl.BlockSpec(s, lambda i: (0, 0)) for s, _ in shapes] + grad_specs * 2,
        scratch_shapes=[pltpu.VMEM((rows, width), WIDE)],
        compiler_params=pltpu.CompilerParams(vmem_limit_bytes=VMEM_LIMIT),
        cost_estimate=pl.CostEstimate(
            flops=32 * rows * width * count * wide, transcendentals=0, bytes_accessed=16 * width * count * wide
        ),
        name="feed_forward_back",
    )(x, grad, resid, normed, inv_scale, gain, active, slope, own, mine, other, own, mine, other)


def _add_rows(dest, first, second):
    rows = 64 if dest.shape[0] % 64 == 0 else dest.shape[0]

    def step(i, carry):
        at = pl.ds(pl.multiple_of(i * rows, rows), rows)
        dest[at, :] = (first[at, :].astype(WIDE) + second[at, :].astype(WIDE)).astype(HALF)
        return carry

    lax.fori_loop(0, dest.shape[0] // rows, step, 0)


def _finish_kernel(bits, count, planes, *refs):
    in_mine, out_mine, in_other, out_other, f1, f2, ckv, dec_ffn, dec_small, tokens = refs[:10]
    norm_terms, refs = refs[10:16], refs[16:]
    attn_out, cross_out, ffn_out, far, near, norm_sum = refs[:6]
    land_in, land_out, term, *refs = refs[6:]
    n_steps = planes.bit_length() - 1
    land_planes, refs = refs[:n_steps], refs[n_steps:]
    folded, landed, refs = refs[:4], refs[4:8], refs[8:]
    enc_ffn, enc_small, got_ffn, got_small, norm_other, norm_land, send_sem, recv_sem = refs
    core, place, me = lax.axis_index("pipe"), lax.axis_index("dp"), lax.axis_index("tensor")
    sibling = {"pipe": 1 - core}
    line = {s: {"tensor": _differ(me, s, count)} for s in range(1, count)}
    cross_over = {"pipe": 1 - core, "tensor": _differ(me, bits[0], count)}
    dp_bits = [1 << i for i in range(n_steps)]
    others = {bit: {"dp": _differ(place, bit, planes)} for bit in dp_bits}
    _enter([sibling, cross_over, *line.values(), *others.values()])
    made = [0]

    def number():
        made[0] += 1
        return made[0] - 1

    def push(source, dest, peer):
        i = number()
        return _send(source, dest, send_sem.at[i], recv_sem.at[i], peer)

    def wait(copies):
        for copy in copies:
            copy.wait()

    for i in range(3):
        at = slice(2 * i, 2 * i + 2)
        enc, dec = norm_terms[i][0:2, :], norm_terms[3 + i][0:2, :]
        norm_sum[at, :] = jnp.where(core == 0, enc, dec)
        norm_other[at, :] = jnp.where(core == 0, dec, enc)
    norm_sum[6:8, :] = jnp.zeros((2, norm_sum.shape[1]), WIDE)
    norm_other[6:8, :] = jnp.zeros((2, norm_sum.shape[1]), WIDE)
    norm_peers = [*others.values(), *(line[bit] for bit in bits)]
    norm_now = [push(norm_other, norm_land.at[0], sibling)]

    def advance_norms():
        if norm_now:
            norm_now.pop().wait()
            n = n_steps + len(bits) - len(norm_peers)
            norm_sum[...] = norm_sum[...] + norm_land[n]
            if norm_peers:
                norm_now.append(push(norm_sum, norm_land.at[n + 1], norm_peers.pop(0)))

    to_core = [push(in_other, land_in, sibling), push(out_other, land_out, sibling)]

    def chain(source, a, at=slice(None)):
        fold, land = (v if at == slice(None) else v.at[at] for v in (folded[a], landed[a]))
        size = folded[a].shape[1] * 2 // count
        return {
            "source": source,
            "fold": fold,
            "land": land,
            "size": size,
            "slots": count,
            "bits": list(reversed(bits)),
            "now": [],
        }

    def advance(c):
        land, size = c["land"], c["size"]
        if c["now"]:
            wait(c["now"])
            c["now"] = []
            kept = c["slots"] // 2 * size
            offset = (count - c["slots"]) * size
            at = pl.ds(0, kept)
            _add_rows(c["fold"].at[:, at], c["source"].at[:, at], land.at[:, pl.ds(offset, kept)])
            c["source"], c["slots"] = c["fold"], c["slots"] // 2
        if c["bits"]:
            kept = c["slots"] // 2 * size
            offset = (count - c["slots"]) * size
            source = c["source"].at[:, pl.ds(kept, kept)]
            c["now"] = [push(source, land.at[:, pl.ds(offset, kept)], line[c["bits"].pop(0)])]

    chains = [chain(f2, 0), chain(f1, 1), chain(ckv, 2)]
    advance(chains[0])

    wait(to_core)
    block = in_mine.shape[0] // planes
    wide = term.shape[1] // count
    inner = in_mine.shape[1] // count

    def sum_step(i, carry):
        at = pl.ds(pl.multiple_of(i * 64, 64), 64)
        for s in range(count):
            first = in_mine[at, s * inner : (s + 1) * inner].astype(WIDE)
            second = land_in[at, s * inner : (s + 1) * inner].astype(WIDE)
            term[at, s * wide : s * wide + inner] = (first + second).astype(HALF)
            outer = wide - inner
            first = out_mine[at, s * outer : (s + 1) * outer].astype(WIDE)
            second = land_out[at, s * outer : (s + 1) * outer].astype(WIDE)
            term[at, s * wide + inner : (s + 1) * wide] = (first + second).astype(HALF)
        return carry

    lax.fori_loop(0, in_mine.shape[0] // 64, sum_step, 0)

    columns = term.shape[1] // 2
    orders = (dp_bits, dp_bits[::-1])
    held = [[list(range(planes)) for _ in orders] for _ in range(2)]
    piece = block // 2

    def rows_of(difference, r):
        first = _differ(place, difference, planes) * block + r * piece
        return pl.ds(pl.multiple_of(first, piece), piece)

    def at_of(p, m, r):
        return term.at[rows_of(m, r), pl.ds(p * columns, columns)]

    def plane_start(j, r):
        copies = []
        for p, order in enumerate(orders):
            bit = order[j]
            kept = [m for m in held[r][p] if not m & bit]
            for n, m in enumerate(kept):
                dest = land_planes[j].at[p, n, pl.ds(r * piece, piece)]
                copies.append((p, m, dest, push(at_of(p, m ^ bit, r), dest, others[bit])))
            held[r][p] = kept
        return copies

    def plane_finish(copies, r):
        for p, m, dest, copy in copies:
            copy.wait()
            _add_rows(at_of(p, m, r), at_of(p, m, r), dest)

    moving = [plane_start(0, r) for r in range(2)]
    for_attn = []

    half = tokens.shape[1] // 2
    far_sem, near_sem, same_sem = number(), number(), number()

    @pl.when(core == 1)
    def _():
        _send(tokens.at[:, pl.ds(0, half)], far, send_sem.at[far_sem], recv_sem.at[far_sem], cross_over)
        _send(
            tokens.at[:, pl.ds(half, half)], far, send_sem.at[same_sem], recv_sem.at[far_sem], line[bits[0]]
        )

    @pl.when(core == 0)
    def _():
        _send(tokens.at[:, pl.ds(half, half)], near, send_sem.at[near_sem], recv_sem.at[near_sem], sibling)

    advance(chains[1])
    advance(chains[2])

    for j in range(n_steps):
        for r in range(2):
            plane_finish(moving[r], r)
            if j + 1 < n_steps:
                moving[r] = plane_start(j + 1, r)
            else:
                for_attn.append(chain(term.at[rows_of(0, r)], 3, pl.ds(r * piece, piece)))
                advance(for_attn[-1])
            advance(chains[(2 * j + r) % 3])
            advance_norms()
    while any(c["now"] or c["bits"] for c in chains + for_attn):
        for c in for_attn + chains:
            advance(c)
        advance_norms()
    while norm_now:
        advance_norms()

    size = [fold.shape[1] * 2 // count for fold in folded]
    enc_ffn[:, : size[1]] = folded[1][:, : size[1]]
    enc_ffn[:, size[1] :] = folded[0][:, : size[0]]
    enc_small[:, : size[3]] = folded[3][:, : size[3]]
    enc_small[:, size[3] :] = folded[2][:, : size[2]]
    swap_sem = [number(), number()]

    @pl.when(core == 0)
    def _():
        _send(dec_ffn, got_ffn, send_sem.at[swap_sem[0]], recv_sem.at[swap_sem[0]], sibling)
        _send(dec_small, got_small, send_sem.at[swap_sem[1]], recv_sem.at[swap_sem[1]], sibling)

    @pl.when(core == 1)
    def _():
        _send(enc_ffn, got_ffn, send_sem.at[swap_sem[0]], recv_sem.at[swap_sem[0]], sibling)
        _send(enc_small, got_small, send_sem.at[swap_sem[1]], recv_sem.at[swap_sem[1]], sibling)

    for i, (mine, got) in enumerate(((enc_ffn, got_ffn), (enc_small, got_small))):
        pltpu.make_async_copy(mine, got, send_sem.at[swap_sem[i]]).wait()
        pltpu.make_async_copy(mine, got, recv_sem.at[swap_sem[i]]).wait()

    def write(first, second):
        for h, (ffn, small) in enumerate((first, second)):
            c = ffn.shape[1] // 2
            for k in range(2):
                ffn_out[k, :, h * c : (h + 1) * c] = ffn[:, k * c : (k + 1) * c].astype(WIDE)
            c = small.shape[1] // 6
            for k in range(6):
                dest = attn_out.at[k] if k < 4 else cross_out.at[k - 4]
                dest[:, h * c : (h + 1) * c] = small[:, k * c : (k + 1) * c].astype(WIDE)

    @pl.when(core == 0)
    def _():
        write((enc_ffn, enc_small), (got_ffn, got_small))

    @pl.when(core == 1)
    def _():
        write((got_ffn, got_small), (dec_ffn, dec_small))

    pltpu.make_async_copy(far, far, recv_sem.at[far_sem]).wait()

    @pl.when(core == 1)
    def _():
        pltpu.make_async_copy(far, far, send_sem.at[far_sem]).wait()
        pltpu.make_async_copy(far, far, send_sem.at[same_sem]).wait()
        pltpu.make_async_copy(near, near, recv_sem.at[near_sem]).wait()

    @pl.when(core == 0)
    def _():
        pltpu.make_async_copy(near, near, send_sem.at[near_sem]).wait()


def finish(in_grads, out_grads, f1, f2, ckv, dec_ffn, dec_small, tokens, norm_terms):
    count, planes = lax.axis_size("tensor"), lax.axis_size("dp")
    depth = in_grads[0].shape[0]
    rows = depth // planes
    attn_columns = in_grads[0].shape[1] + out_grads[0].shape[1]
    wide = 2 * dec_small.shape[1] // 6
    vmem = pl.BlockSpec(memory_space=pltpu.VMEM)
    operands = (in_grads[0], out_grads[0], in_grads[1], out_grads[1], f1, f2, ckv, dec_ffn, dec_small, tokens)
    operands += tuple(norm_terms)
    lines = [f2.shape[1], f1.shape[1], ckv.shape[1], attn_columns]
    scratch = [in_grads[0].shape, out_grads[0].shape, (depth, attn_columns)]
    blocks = planes // 2
    while blocks >= 1:
        scratch.append((2, blocks, rows, attn_columns // 2))
        blocks //= 2
    scratch += [(rows, c // 2) for c in lines]
    scratch += [(rows, c - c // count) for c in lines]
    scratch += [dec_ffn.shape, dec_small.shape] * 2
    norm_steps = count.bit_length() + planes.bit_length() - 1
    norm_shapes = [norm_terms[0].shape, (norm_steps, *norm_terms[0].shape)]
    token_piece = ((tokens.shape[0], tokens.shape[1] // 2), HALF)
    outs = [((4, rows, wide), WIDE), ((2, rows, wide), WIDE), ((2, rows, dec_ffn.shape[1]), WIDE)]
    outs += [token_piece, token_piece, (norm_terms[0].shape, WIDE)]
    return pl.pallas_call(
        partial(_finish_kernel, slot_bits(), count, planes),
        out_shape=[jax.ShapeDtypeStruct(*o) for o in outs],
        in_specs=[vmem] * len(operands),
        out_specs=[vmem] * len(outs),
        scratch_shapes=[pltpu.VMEM(shape, HALF) for shape in scratch]
        + [pltpu.VMEM(shape, WIDE) for shape in norm_shapes]
        + [pltpu.SemaphoreType.DMA((64,))] * 2,
        compiler_params=pltpu.CompilerParams(
            collective_id=5, has_side_effects=True, vmem_limit_bytes=VMEM_LIMIT
        ),
        cost_estimate=pl.CostEstimate(flops=0, transcendentals=0, bytes_accessed=200 << 20),
        name="finish",
    )(*operands)


def per_device(
    enc_input,
    dec_input,
    dec_cotangent,
    enc_lengths,
    dec_lengths,
    attn_weights,
    cross_weights,
    ffn_weights,
    norm_gains,
    norm_biases,
):
    core, place = lax.axis_index("pipe"), lax.axis_index("tensor")
    count = lax.axis_size("tensor")
    top_bit = count // 2
    group = place // top_bit
    block = jnp.where(core == 0, place, place ^ top_bit)
    span, width = enc_input.shape[1:]
    dec_span = dec_input.shape[1]
    local_width = attn_weights.shape[3]
    is_first = core == 0
    chips = range(count)
    sources = [(s // top_bit, s % top_bit) for s in range(2 * top_bit)]
    half = width // 2
    half_local = local_width // 2

    def owner(t):
        return t // top_bit

    norms = jnp.concatenate([norm_gains[0], norm_biases[0]], axis=0)
    norms_other = swap(norms, "pipe", 1)
    enc_norms = jnp.where(is_first, norms, norms_other)
    dec_norms = jnp.where(is_first, norms_other, norms)
    eg, eb, dg, db = enc_norms[:3], enc_norms[3:], dec_norms[:3], dec_norms[3:]

    pick = partial(lax.dynamic_index_in_dim, index=core, axis=0, keepdims=False)
    start_low = pick(dec_input)
    (
        w_attn,
        own_cross,
        own_ffn,
        dec_attn_halves,
        dec_cross_halves,
        dec_ffn_halves,
        cross_rest,
        ffn_rest,
        got,
        start_full,
    ) = gather_weights(
        *[in_column_halves(v[0]) for v in (after(attn_weights, norms_other), cross_weights, ffn_weights)],
        lax.dynamic_index_in_dim(enc_input, 1 - group, 0, False),
        start_low,
    )
    kept = lax.dynamic_index_in_dim(enc_input, group, 0, False)
    tokens = jnp.where(is_first, kept, got).astype(WIDE)
    mine_ffn = gather_planes(ffn_rest)

    def natural(halves, kinds):
        wide = halves.shape[2] // kinds
        return [
            jnp.concatenate([halves[h][:, k * wide : (k + 1) * wide] for h in range(2)], axis=1)
            for k in range(kinds)
        ]

    dec_attn, dec_cross, dec_ffn = [
        natural(v, k) for v, k in ((dec_attn_halves, 4), (dec_cross_halves, 2), (dec_ffn_halves, 2))
    ]
    blocks = width // LANES
    masks = [a * (blocks // 2) + c * (blocks // 2 // top_bit) for a, c in sources]

    def gain_of(i):
        return enc_norms[i : i + 1]

    def bias_of(i):
        return enc_norms[3 + i : 4 + i]

    embed, start_normed, start_scale = norm_forward(tokens, eg[0], eb[0])
    start_scale = jnp.broadcast_to(start_scale, (span, LANES))
    embed_low = embed.astype(HALF)
    parts = 2 if all(m % 2 == 0 for m in masks) else 1
    query, *key_value = spread(embed_low, w_attn, 4, (0, 1, 2), pair=parts)

    def across_chips(value):
        held, bit = [value], 1
        while bit < top_bit:
            held = held + [swap(v, "tensor", bit) for v in held]
            bit *= 2
        return held

    def exchange(held, *earlier):
        if earlier:
            held = after(tuple(held), *earlier)
        return list(held) + [swap(v, "pipe", 1) for v in held]

    key_values = [across_chips(v) for v in key_value]
    mine_cross = gather_planes(after(cross_rest, query))

    enc_lengths, dec_lengths = [after(v, query) for v in (enc_lengths, dec_lengths)]
    enc_row = lax.dynamic_index_in_dim(enc_lengths, group, 0, False)
    dec_row_of_group = lax.dynamic_index_in_dim(dec_lengths, group, 0, False)
    dec_row = lax.dynamic_index_in_dim(dec_lengths, core, 0, False)
    spots = jnp.arange(span, dtype=jnp.int32)
    own_seg = table_of(block * span + spots, enc_row)
    key_seg = jnp.stack(
        [table_of((block ^ (a * top_bit) ^ c) * span + spots, enc_row) for a, c in sources]
    )
    dec_spots = jnp.arange(dec_span * count, dtype=jnp.int32)
    dec_seg = table_of(dec_spots, dec_row)
    enc_segs = tables(own_seg, key_seg)
    dec_segs = tables(dec_seg, dec_seg[None])
    cross_segs = tables(table_of(dec_spots, dec_row_of_group), own_seg[None])

    start_full = after(start_full, key_value)
    start = start_low.astype(WIDE)
    rows_full = dec_span * count
    wide_rows = ((dec_span, width), WIDE)
    kept_rows = [wide_rows, wide_rows, ((dec_span, LANES), WIDE)]
    norm_terms = ((8, width), WIDE)
    dec_in_w = [dec_attn[k] for k in range(3)]
    dec_query = dot(start_full, dec_in_w[0]).astype(HALF)
    dec_kv = jnp.stack([dot(start_full, w).astype(HALF) for w in dec_in_w[1:]])
    dec_heads_wide, dec_lse = attend(dec_query, [dec_kv], dec_segs, [0], True)
    dec_heads = dec_heads_wide.astype(HALF)
    term = dot_bt(dec_heads, dec_attn[3]).astype(HALF)

    attended = ()
    for n in range(parts):
        key_values[n] = exchange(key_values[n], *attended, *((term,) if n else ()))
        attended = attend(
            query, key_values[n], enc_segs, masks, part=n if parts == 2 else None, into=attended
        )
    heads_wide, lse = attended

    def sum_to_owner(term, resid, *earlier):
        total = after(resid, *earlier)
        for s in range(count):
            rows = lax.dynamic_slice_in_dim(term, (place ^ s) * dec_span, dec_span, 0)
            total = total + (swap(rows, "tensor", s) if s else rows).astype(WIDE)
        return total

    self_norm, self_normed, self_scale = norm_forward(sum_to_owner(term, start, lse), dg[0:1], db[0:1])
    self_scale = jnp.broadcast_to(self_scale, (dec_span, LANES))
    self_low = self_norm.astype(HALF)
    self_rows = [swap(self_low, "tensor", s) if s else self_low for s in range(count)]

    heads = heads_wide.astype(HALF)
    mine_ffn = after(mine_ffn, heads_wide)
    other_ffn = swap(mine_ffn, "pipe", 1)
    mine_cross = after(mine_cross, other_ffn)
    w_cross = jnp.stack(
        [
            jnp.concatenate([own_cross[0], mine_cross], axis=1),
            jnp.concatenate([own_cross[1], swap(mine_cross, "pipe", 1)], axis=1),
        ]
    )
    kept_tokens = [((span, width), WIDE), ((span, width), HALF), ((span, width), WIDE), ((span, LANES), WIDE)]
    attn_norm, attn_norm_low, attn_normed, attn_scale = collect(
        [heads], w_attn, 4, (3,), _end_norm, [embed, gain_of(1), bias_of(1)], kept_tokens
    )
    _, memory_low, mem_normed, mem_scale, active, slope = feed_forward(
        attn_norm_low, attn_norm, gain_of(2), bias_of(2), own_ffn, mine_ffn, other_ffn
    )
    self_full = after(jnp.zeros((rows_full, width), HALF), mem_scale)
    for s in range(count):
        self_full = lax.dynamic_update_slice_in_dim(self_full, self_rows[s], (place ^ s) * dec_span, 0)
    cross_query = dot(self_full, dec_cross[0]).astype(HALF)

    def in_halves(value):
        return jnp.stack([value[:, :half_local], value[:, half_local:]])

    [cross_q_enc] = to_encoder(in_halves(cross_query), 6)
    cross_q_enc = to_pairs(cross_q_enc)

    [cross_kv] = spread(memory_low, w_cross, 2, (0, 1), pair=1)

    tables_of_keys = enc_lengths.shape[1]
    at_table = (own_seg[:, None] == jnp.arange(tables_of_keys)[None]).astype(HALF)
    sums = dot_ta(at_table, cross_kv[0])
    bit = 1
    while bit < top_bit:
        sums = sums + swap_columns(sums, "tensor", bit, masks[bit])
        bit *= 2
    sums = sums + swap_columns(sums, "pipe", 1, masks[top_bit])
    means = sums / enc_row.astype(WIDE)[:, None]
    centers = sum(
        jnp.where((own_seg == j)[:, None], means[j : j + 1], 0.0) for j in range(tables_of_keys)
    )
    centered = (cross_kv[0].astype(WIDE) - centers).astype(HALF)

    part_out, part_lse = attend(cross_q_enc, [cross_kv], cross_segs, [0], False, HALF)
    cross_heads, cross_out_wide, cross_lse = to_decoder(
        from_pairs(part_out, half_local), stats_from_pairs(part_lse, half_local), 7
    )
    cross_norm, cross_normed, cross_scale, cross_full = rows_call(
        _forward_rows,
        2,
        dot_bt(cross_heads, dec_cross[1]).astype(HALF),
        [self_norm, dg[1:2], db[1:2]],
        kept_rows,
    )
    dec_hidden = dot(cross_full, dec_ffn[0])
    dec_active = gelu(dec_hidden).astype(HALF)
    result, resid, dec_terms2, grad_full = rows_call(
        _turn_rows,
        3,
        dot_bt(dec_active, dec_ffn[1]).astype(HALF),
        [cross_norm, dg[2:3], db[2:3], pick(dec_cotangent)],
        [((dec_span, width), HALF), wide_rows, norm_terms],
    )
    grad_hidden = (dot(grad_full, dec_ffn[1]) * gelu_slope(dec_hidden)).astype(HALF)
    resid, dec_terms1, cross_grad_full = rows_call(
        _backward_rows,
        4,
        dot_bt(grad_hidden, dec_ffn[0]).astype(HALF),
        [resid, cross_normed, cross_scale, dg[1:2]],
        [wide_rows, norm_terms],
    )
    cross_heads_grad = dot(cross_grad_full, dec_cross[1]).astype(HALF)
    dec_f2_grad = dot_ta(grad_full, dec_active)
    dec_f1_grad = dot_ta(cross_full, grad_hidden)
    dec_ffn_rows, dec_ffn_term = scatter_local([dec_f1_grad, dec_f2_grad])
    heads_grad_enc, stats_enc = to_encoder(
        in_halves(after(cross_heads_grad, dec_ffn_term)), 8, cross_out_wide, cross_lse
    )
    cross_q_term, [cross_kv_grad] = attend_back(
        cross_q_enc,
        [cross_kv],
        to_pairs(heads_grad_enc),
        stats_to_pairs(stats_enc, half_local),
        centered,
        cross_segs,
        [0],
        False,
        False,
    )

    def to_chip(value):
        theirs = joint(value, [((1 - owner(t), t), (owner(t), t)) for t in chips])
        theirs = theirs.reshape(2, count, *theirs.shape[1:])
        chip = value.reshape(theirs.shape).astype(WIDE) + theirs[::-1].astype(WIDE)
        return jnp.where(is_first, chip, chip[::-1]).astype(HALF)

    def to_owner(chip):
        terms = []
        for s in range(top_bit):
            near, far = 2 * s, 2 * s + 1
            near_pairs = [((owner(t), t), (owner(t), t ^ s)) for t in chips]
            far_pairs = [((owner(t), t), (owner(t), t ^ s ^ top_bit)) for t in chips]
            near_got = chip[:, near] if s == 0 else joint(chip[:, near], near_pairs)
            far_got = joint(chip[:, far], far_pairs)
            terms.append(jnp.where(core == group, near_got, far_got).astype(WIDE))
        return sum(terms)

    cross_q_chip = to_chip(from_pairs(cross_q_term, half_local))
    cross_q_grad = to_owner(cross_q_chip).astype(HALF)
    cross_q_grad = jnp.concatenate([cross_q_grad[0], cross_q_grad[1]], axis=1)

    back_tokens = [((span, width), WIDE), ((span, width), HALF), ((8, width), WIDE)]
    resid_enc, resid_low, enc_terms2, *cross_grads = collect(
        [cross_kv_grad],
        w_cross,
        2,
        (0, 1),
        _end_norm_back,
        [mem_normed, mem_scale, gain_of(2)],
        back_tokens,
        memory_low,
    )
    ckv_term = fold_cores(*cross_grads)
    resid_enc, resid_low, enc_terms1, *ffn_grads = feed_forward_back(
        attn_norm_low,
        after(resid_low, dec_ffn_rows, cross_q_chip),
        resid_enc,
        attn_normed,
        attn_scale,
        gain_of(1),
        active,
        slope,
        own_ffn,
        mine_ffn,
        other_ffn,
    )
    heads_grad, *out_grads = spread(resid_low, w_attn, 4, (3,), heads)
    f2_term = fold_cores(after(ffn_grads[2], heads_grad), ffn_grads[3])
    enc_f2 = fold_planes(f2_term)
    f1_term = fold_cores(*ffn_grads[:2])
    enc_f1 = fold_planes(f1_term)
    enc_ckv = fold_planes(ckv_term)
    def join(a, b):
        return (a.astype(WIDE) + b.astype(WIDE)).astype(HALF)

    cross_q_grad = after(cross_q_grad, f2_term)
    resid, dec_terms0, self_grad_full = rows_call(
        _backward_rows,
        4,
        dot_bt(cross_q_grad, dec_cross[0]).astype(HALF),
        [resid, self_normed, self_scale, dg[0:1]],
        [wide_rows, norm_terms],
    )
    dec_heads_grad = dot(self_grad_full, dec_attn[3]).astype(HALF)
    dec_q_grad, [dec_kv_grad] = attend_back(
        dec_query, [dec_kv], dec_heads_grad, dec_lse, dec_heads_wide, dec_segs, [0], True
    )
    dec_proj_grad = [dec_q_grad, dec_kv_grad[0], dec_kv_grad[1]]
    dec_part = sum(dot_bt(g, w) for g, w in zip(dec_proj_grad, dec_in_w)).astype(HALF)
    dec_left = [start_full] * 3 + [self_grad_full, self_full, cross_grad_full]
    dec_right = dec_proj_grad + [dec_heads, cross_q_grad, cross_heads]
    dec_small = [dot_ta(a, b) for a, b in zip(dec_left, dec_right)]
    dec_small_rows, dec_small_term = scatter_local(dec_small)
    grads_in = after(heads_grad, f1_term, dec_small_term)
    def send_chips(held):
        pairs, bit = [(v,) for v in held], top_bit // 2
        while bit >= 1:
            held = [join(*v) if len(v) == 2 else v[0] for v in pairs]
            pairs = [(a, swap(b, "tensor", bit)) for a, b in zip(held[:bit], held[bit:])]
            bit //= 2
        return pairs[0]

    def sum_pair(pair, *earlier):
        return join(after(pair[0], *earlier), pair[1]) if len(pair) == 2 else pair[0]

    q_grad, kv_grad, held = (), [], []
    for n in range(parts):
        q_grad, terms = attend_back(
            query,
            key_values[n],
            after(grads_in, *held),
            lse,
            heads_wide,
            enc_segs,
            masks,
            part=n if parts == 2 else None,
            into=q_grad,
        )
        q_grad = (q_grad,)
        if n:
            kv_grad.append(sum_pair(moving, terms[0]))
            terms = after(tuple(terms), kv_grad[0])
        held = [join(a, swap(b, "pipe", 1)) for a, b in zip(terms[:top_bit], terms[top_bit:])]
        moving = send_chips(held)
    [q_grad] = q_grad

    kv_grad.append(after(sum_pair(moving), enc_ckv, enc_f1, enc_f2))

    enc_grad, enc_low, enc_terms0, *in_grads = collect(
        [q_grad, *kv_grad],
        w_attn,
        4,
        (0, 1, 2),
        _end_norm_back,
        [resid_enc, start_normed, start_scale, gain_of(0)],
        back_tokens,
        embed_low,
    )
    dec_grad = sum_to_owner(after(dec_part, kv_grad[-1]), resid, enc_low)
    attn_out, cross_out, ffn_out_grad, there, near_second, norm_sums = finish(
        in_grads,
        out_grads,
        enc_f1,
        enc_f2,
        enc_ckv,
        dec_ffn_rows,
        dec_small_rows,
        after(enc_low, dec_grad),
        [enc_terms0, enc_terms1, enc_terms2, dec_terms0, dec_terms1, dec_terms2],
    )

    attn_out, cross_out, ffn_out_grad = [
        v.transpose(1, 0, 2)[None] for v in (attn_out, cross_out, ffn_out_grad)
    ]
    own_columns = width // (lax.axis_size("dp") * count)
    norm_sums = lax.dynamic_slice_in_dim(
        norm_sums[:6].reshape(3, 2, width), (lax.axis_index("dp") * count + place) * own_columns, own_columns, 2
    )

    dec_pair = jnp.stack([result, dec_grad.astype(HALF)])
    dec_halves = dec_pair.reshape(2, dec_span, 2, half)
    dec_got = swap(lax.dynamic_index_in_dim(dec_halves, 1 - core, 2, False), "pipe", 1)
    own_result = lax.dynamic_slice_in_dim(result, core * half, half, 1)
    own_grad = lax.dynamic_slice_in_dim(dec_grad, core * half, half, 1)
    dec_output = jnp.where(
        is_first, jnp.stack([own_result, dec_got[0]]), jnp.stack([dec_got[0], own_result])
    )
    got_grad = dec_got[1].astype(WIDE)
    dec_input_grad = jnp.where(
        is_first, jnp.stack([own_grad, got_grad]), jnp.stack([got_grad, own_grad])
    )

    here = jnp.where(is_first, enc_grad[:, :half], near_second.astype(WIDE))
    there = there.astype(WIDE)
    enc_input_grad = jnp.where(group == 0, jnp.stack([here, there]), jnp.stack([there, here]))
    return (
        dec_output,
        enc_input_grad,
        dec_input_grad,
        attn_out,
        cross_out,
        ffn_out_grad,
        norm_sums[None, :, 0],
        norm_sums[None, :, 1],
    )


def solution(mesh):
    rows = P("dp", "tensor", None)
    weights = P("pipe", None, None, "tensor")
    half_rows = P("dp", "tensor", "pipe")
    weight_grads = P("pipe", "dp", None, "tensor")
    norm_grads = P("pipe", None, ("dp", "tensor"))
    return jax.shard_map(
        per_device,
        mesh=mesh,
        in_specs=(rows, rows, rows, P("dp", None), P("dp", None))
        + (weights,) * 3
        + (P("pipe", None, None),) * 2,
        out_specs=(half_rows,) * 3 + (weight_grads,) * 3 + (norm_grads,) * 2,
        check_vma=False,
    )
```
